32 devices in a mesh: group: 8 (over z, y), row: 2 (over x), col: 2 (over core).
Axes of the slice: x: 2, y: 2, z: 4, core: 2. Of those that a mesh axis runs over, the one named last changes fastest.
Arguments:
- tokens: bfloat16 [5120, 2048], P(('group', 'col'), 'row'), may hold values from -6 to 6
- lengths: int32 [24], P('group'), may hold values from 1 to 512, as said below
- norm_gain: float32 [2048], P('row'), may hold values from 0.25 to 1.75
- w_query: bfloat16 [2048, 2048], P('row', 'col'), may hold values from -0.125 to 0.125
- w_key: bfloat16 [2048, 1024], P('row', 'col'), may hold values from -0.125 to 0.125
- w_value: bfloat16 [2048, 1024], P('row', 'col'), may hold values from -0.125 to 0.125
- w_head_gate: bfloat16 [2048, 16], P('row', 'col'), may hold values from -0.25 to 0.25
- query_gain: float32 [128], replicated, may hold values from 1 to 2
- key_gain: float32 [128], replicated, may hold values from 1 to 2
- w_out: bfloat16 [2048, 2048], P('col', 'row'), may hold values from -1.5 to 1.5
- ffn_gain: float32 [2048], P('row'), may hold values from 0.25 to 1.75
- w_gate: bfloat16 [2048, 6144], P('row', 'col'), may hold values from -0.125 to 0.125
- w_up: bfloat16 [2048, 6144], P('row', 'col'), may hold values from -0.125 to 0.125
- w_down: bfloat16 [6144, 2048], P('col', 'row'), may hold values from -0.15625 to 0.15625
- grad_out: bfloat16 [5120, 2048], P(('group', 'col'), 'row'), may hold values from -6 to 6
Outputs:
- output: bfloat16 [5120, 2048], P(('group', 'col'), 'row')
- input_grad: float32 [5120, 2048], P(('group', 'col'), 'row')
- grad_norm_gain: float32 [2048], P('row')
- grad_w_query: float32 [2048, 2048], P('row', 'col')
- grad_w_key: float32 [2048, 1024], P('row', 'col')
- grad_w_value: float32 [2048, 1024], P('row', 'col')
- grad_w_head_gate: float32 [2048, 16], P('row', 'col')
- grad_query_gain: float32 [128], replicated
- grad_key_gain: float32 [128], replicated
- grad_w_out: float32 [2048, 2048], P('col', 'row')
- grad_ffn_gain: float32 [2048], P('row')
- grad_w_gate: float32 [2048, 6144], P('row', 'col')
- grad_w_up: float32 [2048, 6144], P('row', 'col')
- grad_w_down: float32 [6144, 2048], P('col', 'row')
The draws below stay inside these ranges and needn't reach their ends.
Inputs may be any that keep to these rules, and one draw needn't show every extreme that they name: Each group's 3 entries are the lengths of its sequences in token order; they sum to 640.
All inputs are finite; a program needn't handle non-finite values.
Results may differ from the reference program's by a relative error of at most 0.024.
Values may be sent and summed in bfloat16 or wider, within the bound.
A program may use at most 256 MiB of HBM per device.

```python
import math
import jax
import jax.numpy as jnp
from jax import lax

D = 2048
HEADS = 16
HEAD_DIM = 128
FF = 6144
SEQ_GROUP = 3
GROUP_TOK = 640
MAXLEN = 512
TOKENS = 5120
QW = 2048
KVW = 1024


def group_lengths(base_key, group_at):
    parts = SEQ_GROUP - 1
    rest = GROUP_TOK - MAXLEN
    group_key = jax.random.fold_in(base_key, group_at)
    key_share, key_shuffle = jax.random.split(group_key)
    shares = jax.random.randint(key_share, (parts,), 1, 1000).astype(jnp.int32)
    pieces = ((rest - parts) * shares // jnp.sum(shares) + 1).astype(jnp.int32)
    pieces = pieces.at[0].add((rest - jnp.sum(pieces)).astype(jnp.int32))
    row_values = jnp.concatenate([jnp.full((1,), MAXLEN, jnp.int32), pieces])
    return jax.random.permutation(key_shuffle, row_values).astype(jnp.int32)


def draw_lengths(key, part):
    groups = TOKENS // GROUP_TOK
    base_key = jax.random.fold_in(key, 4242)
    return jnp.concatenate([group_lengths(base_key, group_at) for group_at in range(groups)])


def steps_of(rng, dims, cuts, smallest, largest):
    def one(dim, blocks):
        heights = jax.random.uniform(jax.random.fold_in(jax.random.fold_in(rng, 6), dim), (blocks,), jnp.float32, smallest / len(cuts), largest / len(cuts))
        return jnp.repeat(jnp.exp(heights), dims[dim] // blocks).reshape((-1,) + (1,) * (len(dims) - dim - 1))

    level = one(*cuts[0])
    for cut in cuts[1:]:
        level = level * one(*cut)
    return level


def normal_values(stream_key, extent, deviation, most, cuts=(), held_as=jnp.bfloat16):
    array = deviation * jax.random.normal(stream_key, extent, jnp.float32)
    if cuts:
        array = array * steps_of(stream_key, extent, cuts, -0.22, 0.18)
    return jnp.clip(array, -most, most).astype(held_as)


def setup_inputs(seed: int = 0) -> dict:
    seeds = jax.random.split(jax.random.key(seed), 16)
    return {
        "tokens": normal_values(seeds[0], (TOKENS, D), 1.0, 6.0, ((0, 16), (1, 2))),
        "lengths": draw_lengths(jax.random.fold_in(seeds[15], 71), 0),
        "norm_gain": jnp.clip(1.0 + 0.15 * jax.random.normal(seeds[2], (D,), jnp.float32), 0.25, 1.75),
        "w_query": normal_values(seeds[3], (D, QW), D ** -0.5, 0.125, ((0, 2), (1, 2))),
        "w_key": normal_values(seeds[4], (D, KVW), D ** -0.5, 0.125, ((0, 2), (1, 2))),
        "w_value": normal_values(seeds[5], (D, KVW), D ** -0.5, 0.125, ((0, 2), (1, 2))),
        "w_head_gate": normal_values(seeds[6], (D, HEADS), (D // 4) ** -0.5, 0.25, ((0, 2), (1, 2))),
        "query_gain": jnp.clip(jnp.exp(jax.random.uniform(seeds[7], (HEAD_DIM,), jnp.float32, math.log(1.0), math.log(2.0))), 1.0, 2.0),
        "key_gain": jnp.clip(jnp.exp(jax.random.uniform(seeds[8], (HEAD_DIM,), jnp.float32, math.log(1.0), math.log(2.0))), 1.0, 2.0),
        "w_out": normal_values(seeds[9], (QW, D), (QW // 128) ** -0.5, 1.5, ((0, 2), (1, 2))),
        "ffn_gain": jnp.clip(1.0 + 0.15 * jax.random.normal(seeds[10], (D,), jnp.float32), 0.25, 1.75),
        "w_gate": normal_values(seeds[11], (D, FF), D ** -0.5, 0.125, ((0, 2), (1, 2))),
        "w_up": normal_values(seeds[12], (D, FF), D ** -0.5, 0.125, ((0, 2), (1, 2))),
        "w_down": normal_values(seeds[13], (FF, D), (FF // 4) ** -0.5, 0.15625, ((0, 2), (1, 2))),
        "grad_out": normal_values(seeds[14], (TOKENS, D), 1.0, 6.0, ((0, 16), (1, 2))),
    }


EPS = 1e-06
THETA = 1000000.0
HIGH = lax.Precision.HIGHEST

@jax.custom_vjp
def low(v):
    return lax.optimization_barrier(v.astype(jnp.bfloat16)).astype(jnp.float32)

@jax.custom_vjp
def low_back(v):
    return v

def low_keep(v):
    return (low(v), None)

def low_pass(kept, grad):
    return (grad,)

def back_keep(v):
    return (v, None)

def back_low(kept, grad):
    return (low(grad),)
low.defvjp(low_keep, low_pass)
low_back.defvjp(back_keep, back_low)

def places(lengths_group, count):
    ends = jnp.cumsum(lengths_group).astype(jnp.int32)
    index = jnp.arange(count, dtype=jnp.int32)
    passed = (index[:, None] >= ends[None, :]).astype(jnp.int32)
    segment = lax.optimization_barrier(jnp.sum(passed, axis=1)).astype(jnp.int32)
    place = (index - lax.optimization_barrier(jnp.sum(passed * lengths_group[None, :], axis=1))).astype(jnp.int32)
    return (segment, place)

def rope_tables(place, width):
    half = width // 2
    freq = THETA ** (-(jnp.arange(half, dtype=jnp.float32) * 2.0 / width))
    angle = place.astype(jnp.float32)[:, None] * freq[None, :]
    cosines = jnp.concatenate([jnp.cos(angle), jnp.cos(angle)], axis=1)
    sines = jnp.concatenate([jnp.sin(angle), jnp.sin(angle)], axis=1)
    return (cosines, sines)

def rotate(values, cosines, sines):
    half = values.shape[-1] // 2
    turned = jnp.concatenate([-values[..., half:], values[..., :half]], axis=-1)
    return values * cosines + turned * sines

def rms_norm(values, gain):
    return values * lax.rsqrt(lax.optimization_barrier(jnp.mean(values * values, axis=-1, keepdims=True)) + EPS) * gain

def attend(query, key_rows, value_rows, segment, place):
    repeat = query.shape[1] // key_rows.shape[1]
    keys = jnp.repeat(key_rows, repeat, axis=1)
    values = jnp.repeat(value_rows, repeat, axis=1)
    scores = jnp.einsum('qhd,khd->hqk', query, keys, precision=HIGH) * query.shape[2] ** (-0.5)
    scores = low_back(scores)
    allowed = (segment[:, None] == segment[None, :]) & (place[None, :] <= place[:, None])
    scores = jnp.where(allowed[None], scores, -1e+30)
    top = lax.optimization_barrier(jnp.max(scores, axis=-1, keepdims=True))
    raised = jnp.exp(scores - top)
    probs = raised / lax.optimization_barrier(jnp.sum(raised, axis=-1, keepdims=True))
    return jnp.einsum('hqk,khd->qhd', low(probs), values, precision=HIGH)

def group_layer(x_group, segment, place, norm_gain, w_query, w_key, w_value, w_head_gate, query_gain, key_gain, w_out, ffn_gain, w_gate, w_up, w_down):
    count = x_group.shape[0]
    permuted = low(rms_norm(x_group, norm_gain))
    w_first = jnp.concatenate([w_query, w_key, w_value, w_head_gate], axis=1)
    projected = low_back(jnp.dot(permuted, w_first, precision=HIGH))
    q_cols = w_query.shape[1]
    kv_cols = w_key.shape[1]
    head_dim = query_gain.shape[0]
    raw_query = projected[:, :q_cols].reshape(count, q_cols // head_dim, head_dim)
    raw_key = projected[:, q_cols:q_cols + kv_cols].reshape(count, kv_cols // head_dim, head_dim)
    raw_value = projected[:, q_cols + kv_cols:q_cols + 2 * kv_cols].reshape(count, kv_cols // head_dim, head_dim)
    logit = projected[:, q_cols + 2 * kv_cols:]
    cosines, sines = rope_tables(place, head_dim)
    query = low(rotate(rms_norm(raw_query, query_gain), cosines[:, None, :], sines[:, None, :]))
    keys = low(rotate(rms_norm(raw_key, key_gain), cosines[:, None, :], sines[:, None, :]))
    values = low(raw_value)
    attended = jax.checkpoint(attend)(query, keys, values, segment, place)
    attended = low_back(attended)
    gated = low((attended * jax.nn.sigmoid(logit)[:, :, None]).reshape(count, q_cols))
    attn_branch = low_back(jnp.dot(gated, w_out, precision=HIGH))
    resid = x_group + attn_branch
    normed_two = low(rms_norm(resid, ffn_gain))
    gate_part = low_back(jnp.dot(normed_two, w_gate, precision=HIGH))
    up_part = low_back(jnp.dot(normed_two, w_up, precision=HIGH))
    inner = low(jax.nn.silu(gate_part) * up_part)
    branch = low_back(jnp.dot(inner, w_down, precision=HIGH))
    return resid + branch

def reference(tokens, lengths, norm_gain, w_query, w_key, w_value, w_head_gate, query_gain, key_gain, w_out, ffn_gain, w_gate, w_up, w_down, grad_out):
    groups = TOKENS // GROUP_TOK
    x_all = tokens.astype(jnp.float32).reshape(groups, GROUP_TOK, D)
    lens = lengths.reshape(groups, SEQ_GROUP)
    segments, positions = jax.vmap(lambda item: places(item, GROUP_TOK))(lens)
    params = tuple((w.astype(jnp.float32) for w in (norm_gain, w_query, w_key, w_value, w_head_gate, query_gain, key_gain, w_out, ffn_gain, w_gate, w_up, w_down)))
    layer = jax.checkpoint(group_layer)

    def forward(x_all, params):

        def step(carry, item):
            return (carry, layer(item[0], item[1], item[2], *params))
        _, result = lax.scan(step, jnp.zeros((), jnp.float32), (x_all, segments, positions))
        return result
    result, pullback = jax.vjp(forward, x_all, params)
    d_x, d_params = pullback(grad_out.astype(jnp.float32).reshape(groups, GROUP_TOK, D))
    return (result.reshape(TOKENS, D).astype(jnp.bfloat16), d_x.reshape(TOKENS, D), d_params[0], d_params[1], d_params[2], d_params[3], d_params[4], d_params[5], d_params[6], d_params[7], d_params[8], d_params[9], d_params[10], d_params[11])
```

```python
import functools

import jax
import jax.numpy as jnp
from jax import lax
from jax.experimental import pallas as pl
from jax.experimental.pallas import tpu as pltpu
from jax.sharding import PartitionSpec as P

EPS = 1e-06
THETA = 1000000.0
NEGATIVE = -1e30
MESH = pl.DeviceIdType.MESH
F32 = jnp.float32
BF16 = jnp.bfloat16


def swap(values, axis):
    return lax.ppermute(values, axis, [(0, 1), (1, 0)])


def swap_groups(values):
    count = lax.axis_size("group")
    return lax.ppermute(values, "group", [(i, i ^ 1) for i in range(count)])


def halves(values, axis, at):
    low, high = jnp.split(values, 2, axis=axis)
    first = at == 0
    return jnp.where(first, low, high), jnp.where(first, high, low)


def ordered(own, other, axis, at):
    first = at == 0
    return jnp.concatenate(
        [jnp.where(first, own, other), jnp.where(first, other, own)], axis=axis
    )


def places(lengths_group, index):
    ends = jnp.cumsum(lengths_group)
    passed = (index[:, None] >= ends[None, :]).astype(jnp.int32)
    segment = jnp.sum(passed, axis=1)
    place = index - jnp.sum(passed * lengths_group[None, :], axis=1)
    return (segment, place)


def rope_tables(place, width):
    half = width // 2
    freq = THETA ** (-(jnp.arange(half, dtype=F32) * 2.0 / width))
    angle = place.astype(F32)[:, None] * freq[None, :]
    cosines = jnp.concatenate([jnp.cos(angle), jnp.cos(angle)], axis=1)
    sines = jnp.concatenate([jnp.sin(angle), jnp.sin(angle)], axis=1)
    return (cosines, sines)


def rotate(values, cosines, sines):
    half = values.shape[-1] // 2
    turned = jnp.concatenate([-values[..., half:], values[..., :half]], axis=-1)
    return values * cosines + turned * sines


def unrotate(grads, cosines, sines):
    half = grads.shape[-1] // 2
    scaled = grads * sines
    return grads * cosines + jnp.concatenate([scaled[..., half:], -scaled[..., :half]], axis=-1)


def head_norm_back(d_normed, raw_values, inverse, gain):
    scaled = d_normed * gain
    gain_part = jnp.sum(d_normed * raw_values * inverse, axis=(0, 1))
    d_raw = inverse * scaled - raw_values * inverse**3 * jnp.mean(
        scaled * raw_values, axis=-1, keepdims=True
    )
    return (d_raw, gain_part)


TILE = 256


def nt(a, b):
    return lax.dot_general(a, b, (((1,), (1,)), ((), ())), preferred_element_type=F32)


def nn(a, b):
    return jnp.dot(a, b, preferred_element_type=F32)


def ffn_kernel(
    count, chunks, h_ref, goal_ref, inner_grad_ref, gate_ref, up_ref, down_ref,
    grads_ref, low_ref, high_ref, branch_ref, back_ref,
    h_all, h_turned, sent, came, w_pair, w_down, acc_branch, acc_back, parts, total,
    stage, reduce_recv,
    gather_send, gather_recv, x_send, x_recv, chain_send, low_recv, high_recv,
    final_up, final_down, final_recv, pass_send, pass_recv, load_sem, weight_sem, keep_sem, fold_send, fold_recv,
):
    rows = h_ref.shape[0]
    tokens = h_all.shape[0]
    tiles = tokens // TILE
    width = h_ref.shape[1]
    wide = w_down.shape[0] // chunks
    line = count // 2
    root = (line - 1) // 2
    root_lag = max(root, line - 1 - root)
    group = lax.axis_index("group")
    at = group // 2
    side = group % 2
    x_peer = {"row": 1 - lax.axis_index("row")}
    core_peer = {"col": 1 - lax.axis_index("col")}
    y_peer = {"group": group + 1 - 2 * side}
    above = {"group": jnp.minimum(group + 2, count - 1)}
    below = {"group": jnp.maximum(group - 2, 0)}
    has_above = at < line - 1
    has_below = at > 0

    def weight_copies(j):
        cols = pl.ds(pl.multiple_of(side * wide * chunks + j * wide, wide), wide)
        mine = pl.ds(pl.multiple_of(j * wide, wide), wide)
        return (
            pltpu.make_async_copy(
                gate_ref.at[:, cols], w_pair.at[j, :, pl.ds(0, wide)], weight_sem.at[0, j]
            ),
            pltpu.make_async_copy(
                up_ref.at[:, cols], w_pair.at[j, :, pl.ds(wide, wide)], weight_sem.at[1, j]
            ),
            pltpu.make_async_copy(down_ref.at[cols, :], w_down.at[mine, :], weight_sem.at[2, j]),
        )

    @pl.loop(0, chunks)
    def _(j):
        for copy in weight_copies(j):
            copy.start()

    barrier = pltpu.get_barrier_semaphore()
    for peer in (x_peer, core_peer, y_peer):
        pl.semaphore_signal(barrier, inc=1, device_id=peer, device_id_type=MESH)

    @pl.when(has_above)
    def _():
        pl.semaphore_signal(barrier, inc=1, device_id=above, device_id_type=MESH)

    @pl.when(has_below)
    def _():
        pl.semaphore_signal(barrier, inc=1, device_id=below, device_id_type=MESH)

    pl.semaphore_wait(barrier, 3 + has_above.astype(jnp.int32) + has_below.astype(jnp.int32))

    def slot(i):
        return pl.ds(i * rows, rows)

    def send(src, dst, s_sem, r_sem, peer):
        return pltpu.make_async_remote_copy(
            src_ref=src, dst_ref=dst, send_sem=s_sem, recv_sem=r_sem,
            device_id=peer, device_id_type=MESH,
        )

    to_y = send(h_ref, h_all.at[slot(2)], gather_send.at[0], gather_recv.at[0], y_peer)
    to_core = send(h_ref, h_all.at[slot(1)], gather_send.at[1], gather_recv.at[1], core_peer)
    forward = send(
        h_all.at[slot(2)], h_all.at[slot(3)], gather_send.at[2], gather_recv.at[2], core_peer
    )
    to_y.start()
    to_core.start()
    h_all[slot(0), :] = h_ref[...]
    acc_branch[...] = jnp.zeros_like(acc_branch)
    acc_back[...] = jnp.zeros_like(acc_back)
    to_y.wait_recv()
    forward.start()
    to_core.wait_recv()
    forward.wait_recv()

    def exchange(j):
        return send(
            sent.at[lax.rem(j, 3)], came.at[j], x_send.at[j], x_recv.at[j], x_peer
        )

    def project(j):
        for copy in weight_copies(j):
            copy.wait()

        @pl.loop(0, tiles)
        def _(i):
            at_rows = pl.ds(pl.multiple_of(i * TILE, TILE), TILE)
            sent[lax.rem(j, 3), at_rows, :] = nn(h_all[at_rows, :], w_pair[j]).astype(BF16)

        exchange(j).start()

    def work(j):
        exchange(j).wait_recv()
        mine = pl.ds(pl.multiple_of(j * wide, wide), wide)

        @pl.loop(0, tiles)
        def _(i):
            at_rows = pl.ds(pl.multiple_of(i * TILE, TILE), TILE)
            pair = sent[lax.rem(j, 3), at_rows, :].astype(F32) + came[j, at_rows, :].astype(F32)
            gate, up = pair[:, :wide], pair[:, wide:]
            grad = inner_grad_ref[at_rows, mine].astype(F32)
            sig = 1.0 / (1.0 + jnp.exp(-gate))
            silu = gate * sig
            parts[at_rows, pl.ds(0, wide)] = (
                grad * up * (sig * (1.0 + gate * (1.0 - sig)))
            ).astype(BF16)
            parts[at_rows, pl.ds(wide, wide)] = (grad * silu).astype(BF16)
            parts[at_rows, pl.ds(2 * wide, wide)] = (silu * up).astype(BF16)
            acc_branch[at_rows, :] += nn(parts[at_rows, pl.ds(2 * wide, wide)], w_down[mine, :])
            acc_back[at_rows, :] += nt(parts[at_rows, pl.ds(0, 2 * wide)], w_pair[j])

        @pl.loop(0, width // TILE)
        def _(i):
            at_rows = pl.ds(pl.multiple_of(i * TILE, TILE), TILE)
            pair = nn(h_turned[at_rows, :], parts[:, pl.ds(0, 2 * wide)])
            total[3 * j, at_rows, :] = pair[:, :wide].astype(BF16)
            total[3 * j + 1, at_rows, :] = pair[:, wide:].astype(BF16)
            total[3 * j + 2, at_rows, :] = nn(
                goal_ref[at_rows, :], parts[:, pl.ds(2 * wide, wide)]
            ).astype(BF16)

    def up_copy(p):
        return send(total.at[p], low_ref.at[p], chain_send.at[p], low_recv.at[p], above)

    def down_copy(p):
        return send(total.at[p], high_ref.at[p], chain_send.at[p], high_recv.at[p], below)

    def home(c, k, of=side):
        start = pl.multiple_of((of * chunks + c) * wide, wide)
        return grads_ref.at[k, :, pl.ds(start, wide)]

    def to_pair(c, k, from_total):
        p = 3 * c + k
        src = total.at[p] if from_total else home(c, k)
        return send(src, home(c, k), pass_send.at[p], pass_recv.at[p], y_peer)

    def from_pair(c, k):
        p = 3 * c + k
        return send(
            home(c, k), home(c, k, 1 - side), pass_send.at[p], pass_recv.at[p], y_peer
        )

    def add(p, which):
        copy = pltpu.make_async_copy(
            (low_ref if which == 0 else high_ref).at[p], stage.at[which], load_sem.at[which]
        )
        copy.start()
        copy.wait()

        @pl.loop(0, width // TILE)
        def _(i):
            at_rows = pl.ds(pl.multiple_of(i * TILE, TILE), TILE)
            total[p, at_rows, :] = (
                total[p, at_rows, :].astype(F32) + stage[which, at_rows, :].astype(F32)
            ).astype(BF16)

    def keep(c, k):
        return pltpu.make_async_copy(total.at[3 * c + k], home(c, k), keep_sem.at[3 * c + k])

    def finals(c, k, upward, from_total):
        p = 3 * c + k
        src = total.at[p] if from_total else home(c, k)
        if upward:
            return send(src, home(c, k), final_up.at[p], final_recv.at[p], above)
        return send(src, home(c, k), final_down.at[p], final_recv.at[p], below)

    lag = jnp.where(at < root, at, jnp.where(at > root, line - 1 - at, root_lag))
    far = jnp.abs(at - root)

    def chain(t):
        c = t - lag
        live = (c >= 0) & (c < chunks)
        for k in range(3):
            p = 3 * c + k

            @pl.when(live & (at < root))
            def _():
                @pl.when(has_below)
                def _():
                    down_wait = up_copy(p)
                    down_wait.wait_recv()
                    add(p, 0)

                up_copy(p).start()

            @pl.when(live & (at > root))
            def _():
                @pl.when(has_above)
                def _():
                    down_copy(p).wait_recv()
                    add(p, 1)

                down_copy(p).start()

            @pl.when(live & (at == root))
            def _():
                if root > 0:
                    up_copy(p).wait_recv()
                    add(p, 0)
                if root < line - 1:
                    down_copy(p).wait_recv()
                    add(p, 1)
                if root > 0:
                    finals(c, k, False, True).start()
                if root < line - 1:
                    finals(c, k, True, True).start()
                to_pair(c, k, True).start()
                keep(c, k).start()

        c = t - root_lag - far
        for k in range(3):

            @pl.when((c >= 0) & (c < chunks) & (at != root))
            def _():
                finals(c, k, True, False).wait_recv()

                @pl.when((at > root) & has_above)
                def _():
                    finals(c, k, True, False).start()

                @pl.when((at < root) & has_below)
                def _():
                    finals(c, k, False, False).start()

                to_pair(c, k, False).start()

    for j in range(min(2, chunks)):
        project(j)

    @pl.loop(0, tiles)
    def _(i):
        at_rows = pl.ds(pl.multiple_of(i * TILE, TILE), TILE)
        h_turned[:, at_rows] = h_all[at_rows, :].T

    @pl.loop(0, chunks)
    def _(t):
        @pl.when(t + 2 < chunks)
        def _():
            @pl.when(t >= 1)
            def _():
                exchange(t - 1).wait_send()

            project(t + 2)

        work(t)
        chain(t)

    folded = ((acc_back, back_ref), (acc_branch, branch_ref))

    def fold_source(n, i):
        if i == 2:
            return w_down.at[slot(n), :]
        return h_all.at[slot(2 * n + i), :]

    def fold_one(n, i):
        return send(
            fold_source(n, i), reduce_recv.at[n, i], fold_send.at[n, i], fold_recv.at[n, i],
            core_peer,
        )

    def fold_two(n):
        return send(
            fold_source(n, 2), reduce_recv.at[n, 2], fold_send.at[n, 2], fold_recv.at[n, 2],
            y_peer,
        )

    to_y.wait_send()
    to_core.wait_send()
    forward.wait_send()
    for n, (acc, _) in enumerate(folded):
        for i in (1, 0):
            fold_source(n, i)[...] = acc[slot(2 * i + 1), :].astype(BF16)
            fold_one(n, i).start()
    for n, (acc, _) in enumerate(folded):
        fold_one(n, 1).wait_recv()
        fold_source(n, 2)[...] = (acc[slot(2), :] + reduce_recv[n, 1].astype(F32)).astype(BF16)
        fold_two(n).start()
    chain(chunks)
    for n, (acc, out) in enumerate(folded):
        fold_one(n, 0).wait_recv()
        fold_two(n).wait_recv()
        out[...] = acc[slot(0), :] + reduce_recv[n, 0].astype(F32) + reduce_recv[n, 2].astype(F32)

    @pl.loop(chunks + 1, chunks + 2 * root_lag + 1)
    def _(t):
        chain(t)

    @pl.loop(0, chunks)
    def _(c):
        for k in range(3):
            p = 3 * c + k
            from_pair(c, k).wait_recv()
            from_pair(c, k).wait_send()

            @pl.when(at == root)
            def _():
                keep(c, k).wait()
                if root > 0:
                    finals(c, k, False, True).wait_send()
                if root < line - 1:
                    finals(c, k, True, True).wait_send()

            @pl.when(at < root)
            def _():
                up_copy(p).wait_send()

                @pl.when(has_below)
                def _():
                    finals(c, k, False, False).wait_send()

            @pl.when(at > root)
            def _():
                down_copy(p).wait_send()

                @pl.when(has_above)
                def _():
                    finals(c, k, True, False).wait_send()

    @pl.loop(max(chunks - 3, 0), chunks)
    def _(j):
        exchange(j).wait_send()

    for n in range(2):
        for i in range(2):
            fold_one(n, i).wait_send()
        fold_two(n).wait_send()


def ffn(h, goal, inner_grad, w_gate, w_up, w_down):
    count = lax.axis_size("group")
    rows, width = h.shape
    hidden = w_gate.shape[1] // 2
    wide = 128
    chunks = hidden // wide
    tokens = 4 * rows
    anywhere = pl.BlockSpec(memory_space=pl.ANY)
    local = pl.BlockSpec(memory_space=pltpu.VMEM)
    dma = pltpu.SemaphoreType.DMA
    pieces = 3 * chunks
    flops = 2 * tokens * width * hidden * 8
    return pl.pallas_call(
        functools.partial(ffn_kernel, count, chunks),
        out_shape=(
            jax.ShapeDtypeStruct((3, width, 2 * hidden), BF16),
            jax.ShapeDtypeStruct((pieces, width, wide), BF16),
            jax.ShapeDtypeStruct((pieces, width, wide), BF16),
            jax.ShapeDtypeStruct((rows, width), F32),
            jax.ShapeDtypeStruct((rows, width), F32),
        ),
        in_specs=[local, local, local, anywhere, anywhere, anywhere],
        out_specs=(anywhere, anywhere, anywhere, local, local),
        scratch_shapes=[
            pltpu.VMEM((tokens, width), BF16),
            pltpu.VMEM((width, tokens), BF16),
            pltpu.VMEM((3, tokens, 2 * wide), BF16),
            pltpu.VMEM((chunks, tokens, 2 * wide), BF16),
            pltpu.VMEM((chunks, width, 2 * wide), BF16),
            pltpu.VMEM((hidden, width), BF16),
            pltpu.VMEM((tokens, width), F32),
            pltpu.VMEM((tokens, width), F32),
            pltpu.VMEM((tokens, 3 * wide), BF16),
            pltpu.VMEM((pieces, width, wide), BF16),
            pltpu.VMEM((2, width, wide), BF16),
            pltpu.VMEM((2, 3, rows, width), BF16),
            dma((3,)), dma((3,)), dma((chunks,)), dma((chunks,)),
            dma((pieces,)), dma((pieces,)), dma((pieces,)),
            dma((pieces,)), dma((pieces,)), dma((pieces,)), dma((pieces,)), dma((pieces,)),
            dma((2,)), dma((3, chunks)), dma((pieces,)), dma((2, 3)), dma((2, 3)),
        ],
        compiler_params=pltpu.CompilerParams(
            collective_id=1, has_side_effects=True, vmem_limit_bytes=63 << 20
        ),
        cost_estimate=pl.CostEstimate(
            flops=flops, bytes_accessed=200 << 20, transcendentals=tokens * hidden
        ),
    )(h, goal, inner_grad, w_gate, w_up, w_down)


def masked_scores(query, keys, segment, place, scale):
    scores = jnp.einsum("qkgd,skd->kgqs", query, keys, preferred_element_type=F32) * scale
    allowed = (segment[:, None] == segment[None, :]) & (place[None, :] <= place[:, None])
    return jnp.where(allowed, scores, NEGATIVE)


def body(
    tokens, lengths, norm_gain, w_query, w_key, w_value, w_head_gate, query_gain, key_gain,
    w_out, ffn_gain, w_gate, w_up, w_down, grad_out,
):
    row_count = lax.axis_size("row")
    rows, d_loc = tokens.shape
    group_tok = 2 * rows
    width = d_loc * row_count
    head_dim = query_gain.shape[0]
    q_half = w_query.shape[1] // 2
    kv_half = w_key.shape[1] // 2
    gate_half = w_head_gate.shape[1] // 2
    heads = q_half // head_dim
    kv_heads = kv_half // head_dim
    share = heads // kv_heads
    main = q_half + 2 * kv_half
    half_hidden = w_gate.shape[1] // 2
    scale = head_dim ** (-0.5)
    row_at = lax.axis_index("row")
    col_at = lax.axis_index("col")
    side = lax.axis_index("group") % 2

    steps = jnp.arange(rows, dtype=jnp.int32)
    index = jnp.concatenate([col_at * rows + steps, (1 - col_at) * rows + steps])
    segment, place = places(lengths, index)

    grad_group = jnp.concatenate([grad_out, swap(grad_out, "col")])
    grad_all = jnp.concatenate([grad_group, swap_groups(grad_group)])
    down_half = lax.dynamic_slice_in_dim(w_down, side * half_hidden, half_hidden, axis=0)
    inner_part = nt(grad_all, down_half)
    inner_grad = (inner_part + swap(inner_part.astype(BF16), "row").astype(F32)).astype(BF16)
    grad_turned = grad_all.T

    x_in = tokens.astype(F32)
    squares = jnp.sum(x_in * x_in, axis=1)
    inverse_one = lax.rsqrt((squares + swap(squares, "row")) / width + EPS)
    normed_one = (x_in * inverse_one[:, None] * norm_gain).astype(BF16)
    permuted = jnp.concatenate([normed_one, swap(normed_one, "col")])
    splits = [halves(w, 1, row_at) for w in (w_query, w_key, w_value, w_head_gate)]
    w_first = jnp.concatenate(
        [own for own, _ in splits[:3]] + [other for _, other in splits[:3]] + list(splits[3]),
        axis=1,
    )
    partial = nn(permuted, w_first)
    away = jnp.concatenate(
        [partial[:, main : 2 * main], partial[:, 2 * main + gate_half :]], axis=1
    ).astype(BF16)
    stay = jnp.concatenate(
        [partial[:, :main], partial[:, 2 * main : 2 * main + gate_half]], axis=1
    )
    projected = stay + swap(away, "row").astype(F32)
    raw_query = projected[:, :q_half].reshape(group_tok, heads, head_dim)
    raw_key = projected[:, q_half : q_half + kv_half].reshape(group_tok, kv_heads, head_dim)
    raw_value = projected[:, q_half + kv_half : main].reshape(group_tok, kv_heads, head_dim)
    logit = projected[:, main:]
    query_inverse = lax.rsqrt(jnp.mean(raw_query * raw_query, axis=-1, keepdims=True) + EPS)
    key_inverse = lax.rsqrt(jnp.mean(raw_key * raw_key, axis=-1, keepdims=True) + EPS)
    cosines, sines = rope_tables(place, head_dim)
    cos_heads = cosines[:, None, :]
    sin_heads = sines[:, None, :]
    query = rotate(raw_query * query_inverse * query_gain, cos_heads, sin_heads).astype(BF16)
    keys = rotate(raw_key * key_inverse * key_gain, cos_heads, sin_heads).astype(BF16)
    values = raw_value.astype(BF16)
    query = query.reshape(group_tok, kv_heads, share, head_dim)

    scores = masked_scores(query, keys, segment, place, scale)
    top = jnp.max(scores, axis=-1, keepdims=True)
    raised = jnp.exp(scores - top)
    probs = raised / jnp.sum(raised, axis=-1, keepdims=True)
    probs_low = probs.astype(BF16)
    attended = jnp.einsum("kgqs,skd->qkgd", probs_low, values, preferred_element_type=F32)
    attended = attended.reshape(group_tok, heads, head_dim)
    gate_sigmoid = jax.nn.sigmoid(logit)
    gated = (attended * gate_sigmoid[:, :, None]).reshape(group_tok, q_half).astype(BF16)
    gated_all = jnp.concatenate([gated, swap(gated, "row")], axis=1)
    w_back = jnp.concatenate(halves(w_out, 0, row_at))

    def sum_cores(values):
        return values[:rows] + swap(values[rows:].astype(BF16), "col").astype(F32)

    resid = x_in + sum_cores(nn(gated_all, w_back))
    squares = jnp.sum(resid * resid, axis=1)
    inverse_two = lax.rsqrt((squares + swap(squares, "row")) / width + EPS)
    normed_two = (resid * inverse_two[:, None] * ffn_gain).astype(BF16)

    ffn_sum, _, _, branch, d_normed_two = ffn(
        normed_two, grad_turned, inner_grad, w_gate, w_up, w_down
    )
    output = (resid + branch).astype(BF16)

    d_top = grad_out.astype(F32)
    ffn_gain_part = jnp.sum(d_normed_two * resid * inverse_two[:, None], axis=0)
    scaled_two = d_normed_two * ffn_gain
    inner_two = jnp.sum(scaled_two * resid, axis=1)
    inner_two = inner_two + swap(inner_two, "row")
    d_resid = (
        d_top
        + inverse_two[:, None] * scaled_two
        - resid * (inverse_two**3 * inner_two / width)[:, None]
    )
    d_branch = d_resid.astype(BF16)
    branch_all = jnp.concatenate([d_branch, swap(d_branch, "col")])
    grad_out_w = lax.dot_general(
        gated_all, branch_all, (((0,), (0,)), ((), ())), preferred_element_type=F32
    )
    d_gated_part = nt(branch_all, w_back)
    d_gated = d_gated_part[:, :q_half] + swap(
        d_gated_part[:, q_half:].astype(BF16), "row"
    ).astype(F32)
    d_gated = d_gated.reshape(group_tok, heads, head_dim)
    d_attended = (d_gated * gate_sigmoid[:, :, None]).astype(BF16)
    d_logit = jnp.sum(d_gated * attended, axis=-1) * gate_sigmoid * (1.0 - gate_sigmoid)
    d_attended = d_attended.reshape(group_tok, kv_heads, share, head_dim)

    d_probs = jnp.einsum("qkgd,skd->kgqs", d_attended, values, preferred_element_type=F32)
    d_scores = (probs * (d_probs - jnp.sum(d_probs * probs, axis=-1, keepdims=True))).astype(BF16)
    d_query = jnp.einsum("kgqs,skd->qkgd", d_scores, keys, preferred_element_type=F32) * scale
    d_keys = jnp.einsum("kgqs,qkgd->skd", d_scores, query, preferred_element_type=F32) * scale
    d_values = jnp.einsum("kgqs,qkgd->skd", probs_low, d_attended, preferred_element_type=F32)
    d_query = d_query.reshape(group_tok, heads, head_dim)
    d_raw_query, query_gain_part = head_norm_back(
        unrotate(d_query, cos_heads, sin_heads), raw_query, query_inverse, query_gain
    )
    d_raw_key, key_gain_part = head_norm_back(
        unrotate(d_keys, cos_heads, sin_heads), raw_key, key_inverse, key_gain
    )
    d_projected = jnp.concatenate(
        [
            d_raw_query.reshape(group_tok, q_half),
            d_raw_key.reshape(group_tok, kv_half),
            d_values.reshape(group_tok, kv_half),
            d_logit,
        ],
        axis=1,
    ).astype(BF16)
    came = swap(d_projected, "row")
    d_first = jnp.concatenate(
        [d_projected[:, :main], came[:, :main], d_projected[:, main:], came[:, main:]], axis=1
    )
    grad_first = lax.dot_general(
        permuted, d_first, (((0,), (0,)), ((), ())), preferred_element_type=F32
    )
    d_normed_one = sum_cores(nt(d_first, w_first))
    norm_gain_part = jnp.sum(d_normed_one * x_in * inverse_one[:, None], axis=0)
    scaled_one = d_normed_one * norm_gain
    inner_one = jnp.sum(scaled_one * x_in, axis=1)
    inner_one = inner_one + swap(inner_one, "row")
    input_grad = (
        d_resid
        + inverse_one[:, None] * scaled_one
        - x_in * (inverse_one**3 * inner_one / width)[:, None]
    )
    grad_norm_gain, grad_ffn_gain = lax.psum((norm_gain_part, ffn_gain_part), ("group", "col"))
    grad_query_gain, grad_key_gain = lax.psum(
        (query_gain_part, key_gain_part), ("group", "row", "col")
    )
    first_sum = lax.psum(grad_first.astype(BF16), "group")
    out_sum = lax.psum(grad_out_w.astype(BF16), "group")

    def piece(start, size):
        own = first_sum[:, start : start + size]
        other = first_sum[:, main + start : main + start + size]
        return ordered(own, other, 1, row_at).astype(F32)

    gates = first_sum[:, 2 * main :]
    grad_head_gate = ordered(gates[:, :gate_half], gates[:, gate_half:], 1, row_at).astype(F32)
    grad_out_full = ordered(*jnp.split(out_sum, 2, axis=0), 0, row_at).astype(F32)
    grad_gate, grad_up, grad_down = (ffn_sum[k].astype(F32) for k in range(3))
    return (
        output,
        input_grad,
        grad_norm_gain,
        piece(0, q_half),
        piece(q_half, kv_half),
        piece(q_half + kv_half, kv_half),
        grad_head_gate,
        grad_query_gain,
        grad_key_gain,
        grad_out_full,
        grad_ffn_gain,
        grad_gate,
        grad_up,
        grad_down.T,
    )


def solution(mesh):
    shards = P(("group", "col"), "row")
    in_specs = (
        shards,
        P("group"),
        P("row"),
        P("row", "col"),
        P("row", "col"),
        P("row", "col"),
        P("row", "col"),
        P(),
        P(),
        P("col", "row"),
        P("row"),
        P("row", "col"),
        P("row", "col"),
        P("col", "row"),
        shards,
    )
    out_specs = (
        shards,
        shards,
        P("row"),
        P("row", "col"),
        P("row", "col"),
        P("row", "col"),
        P("row", "col"),
        P(),
        P(),
        P("col", "row"),
        P("row"),
        P("row", "col"),
        P("row", "col"),
        P("col", "row"),
    )
    return jax.shard_map(body, mesh=mesh, in_specs=in_specs, out_specs=out_specs, check_vma=False)
```

```python
import functools

import jax
import jax.numpy as jnp
from jax import lax
from jax.experimental import pallas as pl
from jax.experimental.pallas import tpu as pltpu
from jax.sharding import PartitionSpec as P

EPS = 1e-06
THETA = 1000000.0
NEGATIVE = -1e30
MESH = pl.DeviceIdType.MESH
F32 = jnp.float32
BF16 = jnp.bfloat16


def swap(values, axis):
    return lax.ppermute(values, axis, [(0, 1), (1, 0)])


def swap_groups(values):
    count = lax.axis_size("group")
    return lax.ppermute(values, "group", [(i, i ^ 1) for i in range(count)])


def halves(values, axis, at):
    low, high = jnp.split(values, 2, axis=axis)
    first = at == 0
    return jnp.where(first, low, high), jnp.where(first, high, low)


def ordered(own, other, axis, at):
    first = at == 0
    return jnp.concatenate(
        [jnp.where(first, own, other), jnp.where(first, other, own)], axis=axis
    )


def places(lengths_group, index):
    ends = jnp.cumsum(lengths_group)
    passed = (index[:, None] >= ends[None, :]).astype(jnp.int32)
    segment = jnp.sum(passed, axis=1)
    place = index - jnp.sum(passed * lengths_group[None, :], axis=1)
    return (segment, place)


def rope_tables(place, width):
    half = width // 2
    freq = THETA ** (-(jnp.arange(half, dtype=F32) * 2.0 / width))
    angle = place.astype(F32)[:, None] * freq[None, :]
    cosines = jnp.concatenate([jnp.cos(angle), jnp.cos(angle)], axis=1)
    sines = jnp.concatenate([jnp.sin(angle), jnp.sin(angle)], axis=1)
    return (cosines, sines)


def rotate(values, cosines, sines):
    half = values.shape[-1] // 2
    turned = jnp.concatenate([-values[..., half:], values[..., :half]], axis=-1)
    return values * cosines + turned * sines


def unrotate(grads, cosines, sines):
    half = grads.shape[-1] // 2
    scaled = grads * sines
    return grads * cosines + jnp.concatenate([scaled[..., half:], -scaled[..., :half]], axis=-1)


def head_norm_back(d_normed, raw_values, inverse, gain):
    scaled = d_normed * gain
    gain_part = jnp.sum(d_normed * raw_values * inverse, axis=(0, 1))
    d_raw = inverse * scaled - raw_values * inverse**3 * jnp.mean(
        scaled * raw_values, axis=-1, keepdims=True
    )
    return (d_raw, gain_part)


TILE = 256


def nt(a, b):
    return lax.dot_general(a, b, (((1,), (1,)), ((), ())), preferred_element_type=F32)


def nn(a, b):
    return jnp.dot(a, b, preferred_element_type=F32)


def copy_to(src, dst, send_sem, recv_sem, peer):
    return pltpu.make_async_remote_copy(
        src_ref=src, dst_ref=dst, send_sem=send_sem, recv_sem=recv_sem,
        device_id=peer, device_id_type=MESH,
    )


def tile(i, size=TILE):
    return pl.ds(pl.multiple_of(i * size, size), size)


class Place:
    def __init__(self, count):
        group = lax.axis_index("group")
        self.line = count // 2
        self.root = (self.line - 1) // 2
        self.deep = max(self.root, self.line - 1 - self.root)
        self.at = group // 2
        self.side = group % 2
        self.x_peer = {"row": 1 - lax.axis_index("row")}
        self.core_peer = {"col": 1 - lax.axis_index("col")}
        self.y_peer = {"group": group + 1 - 2 * self.side}
        self.above = {"group": jnp.minimum(group + 2, count - 1)}
        self.below = {"group": jnp.maximum(group - 2, 0)}
        self.has_above = self.at < self.line - 1
        self.has_below = self.at > 0

    def meet(self):
        barrier = pltpu.get_barrier_semaphore()

        def greet(peer):
            pl.semaphore_signal(barrier, inc=1, device_id=peer, device_id_type=MESH)

        for peer in (self.x_peer, self.core_peer, self.y_peer):
            greet(peer)
        pl.when(self.has_above)(lambda: greet(self.above))
        pl.when(self.has_below)(lambda: greet(self.below))
        met = 3 + self.has_above.astype(jnp.int32) + self.has_below.astype(jnp.int32)
        pl.semaphore_wait(barrier, met)


class Chain:
    def __init__(self, place, chunks, kinds, total, came, home, add, sems, share=True):
        self.place, self.chunks, self.kinds = place, chunks, kinds
        self.total, self.came, self.home, self.add = total, came, home, add
        self.sems, self.share = sems, share

    def part_copy(self, c, k, upward):
        sent, low, high = self.sems[:3]
        p = self.kinds * c + k
        peer, which, arrived = (
            (self.place.above, 0, low) if upward else (self.place.below, 1, high)
        )
        return copy_to(
            self.total(c, k), self.came(c, k, which), sent.at[p], arrived.at[p], peer
        )

    def final_copy(self, c, k, upward, first):
        up, down, arrived = self.sems[3:6]
        p = self.kinds * c + k
        src = self.total(c, k) if first else self.home(c, k, self.place.side)
        peer, sent = (self.place.above, up) if upward else (self.place.below, down)
        return copy_to(src, self.home(c, k, self.place.side), sent.at[p], arrived.at[p], peer)

    def keep_copy(self, c, k):
        return pltpu.make_async_copy(
            self.total(c, k), self.home(c, k, self.place.side),
            self.sems[6].at[self.kinds * c + k],
        )

    def share_copy(self, c, k, first, of=None):
        p = self.kinds * c + k
        of = self.place.side if of is None else of
        src = self.total(c, k) if first else self.home(c, k, self.place.side)
        return copy_to(
            src, self.home(c, k, of), self.sems[7].at[p], self.sems[8].at[p], self.place.y_peer
        )

    def step(self, t):
        at, line, root, deep = self.place.at, self.place.line, self.place.root, self.place.deep
        c = t - jnp.where(at < root, at, jnp.where(at > root, line - 1 - at, deep))
        live = (c >= 0) & (c < self.chunks)
        for k in range(self.kinds):

            @pl.when(live & (at < root))
            def _():
                @pl.when(self.place.has_below)
                def _():
                    self.part_copy(c, k, True).wait_recv()
                    self.add(c, k, 0)

                self.part_copy(c, k, True).start()

            @pl.when(live & (at > root))
            def _():
                @pl.when(self.place.has_above)
                def _():
                    self.part_copy(c, k, False).wait_recv()
                    self.add(c, k, 1)

                self.part_copy(c, k, False).start()

            @pl.when(live & (at == root))
            def _():
                if root > 0:
                    self.part_copy(c, k, True).wait_recv()
                    self.add(c, k, 0)
                if root < line - 1:
                    self.part_copy(c, k, False).wait_recv()
                    self.add(c, k, 1)
                if root > 0:
                    self.final_copy(c, k, False, True).start()
                if root < line - 1:
                    self.final_copy(c, k, True, True).start()
                if self.share:
                    self.share_copy(c, k, True).start()
                self.keep_copy(c, k).start()

        c = t - deep - jnp.abs(at - root)
        for k in range(self.kinds):

            @pl.when((c >= 0) & (c < self.chunks) & (at != root))
            def _():
                self.final_copy(c, k, True, False).wait_recv()

                @pl.when((at > root) & self.place.has_above)
                def _():
                    self.final_copy(c, k, True, False).start()

                @pl.when((at < root) & self.place.has_below)
                def _():
                    self.final_copy(c, k, False, False).start()

                if self.share:
                    self.share_copy(c, k, False).start()

    def steps(self):
        return self.chunks + 2 * self.place.deep

    def drain(self):
        at, line, root = self.place.at, self.place.line, self.place.root

        @pl.loop(0, self.chunks)
        def _(c):
            for k in range(self.kinds):
                if self.share:
                    self.share_copy(c, k, False, 1 - self.place.side).wait_recv()
                    self.share_copy(c, k, False).wait_send()

                @pl.when(at == root)
                def _():
                    self.keep_copy(c, k).wait()
                    if root > 0:
                        self.final_copy(c, k, False, True).wait_send()
                    if root < line - 1:
                        self.final_copy(c, k, True, True).wait_send()

                @pl.when(at < root)
                def _():
                    self.part_copy(c, k, True).wait_send()

                    @pl.when(self.place.has_below)
                    def _():
                        self.final_copy(c, k, False, False).wait_send()

                @pl.when(at > root)
                def _():
                    self.part_copy(c, k, False).wait_send()

                    @pl.when(self.place.has_above)
                    def _():
                        self.final_copy(c, k, True, False).wait_send()


def chain_semaphores(pieces):
    return [pltpu.SemaphoreType.DMA((pieces,)) for _ in range(9)]


def ffn_kernel(
    count, chunks, h_ref, top_ref, inner_grad_ref, gate_ref, up_ref, down_ref,
    pair_grads_ref, down_grads_ref, pair_came_ref, down_came_ref, branch_ref, back_ref,
    h_all, h_turned, sent, came, w_pair, w_down, acc_branch, acc_back, parts, inner_turned,
    pair_total, down_total, pair_stage, down_stage, reduce_recv,
    gather_send, gather_recv, x_send, x_recv, load_sem, weight_sem, fold_send, fold_recv,
    *chain_sems,
):
    place = Place(count)
    rows, width = h_ref.shape
    tokens = h_all.shape[0]
    tiles = tokens // TILE
    wide = w_down.shape[0] // chunks
    side = place.side

    def weight_copies(j):
        cols = tile(side * chunks + j, wide)
        return (
            pltpu.make_async_copy(
                gate_ref.at[:, cols], w_pair.at[j, :, pl.ds(0, wide)], weight_sem.at[0, j]
            ),
            pltpu.make_async_copy(
                up_ref.at[:, cols], w_pair.at[j, :, pl.ds(wide, wide)], weight_sem.at[1, j]
            ),
            pltpu.make_async_copy(
                down_ref.at[cols, :], w_down.at[tile(j, wide), :], weight_sem.at[2, j]
            ),
        )

    @pl.loop(0, chunks)
    def _(j):
        for copy in weight_copies(j):
            copy.start()

    place.meet()

    def slot(i):
        return pl.ds(i * rows, rows)

    to_y = copy_to(h_ref, h_all.at[slot(2)], gather_send.at[0], gather_recv.at[0], place.y_peer)
    to_core = copy_to(
        h_ref, h_all.at[slot(1)], gather_send.at[1], gather_recv.at[1], place.core_peer
    )
    forward = copy_to(
        h_all.at[slot(2)], h_all.at[slot(3)], gather_send.at[2], gather_recv.at[2],
        place.core_peer,
    )
    to_y.start()
    to_core.start()
    h_all[slot(0), :] = h_ref[...]
    acc_branch[...] = jnp.zeros_like(acc_branch)
    acc_back[...] = jnp.zeros_like(acc_back)
    to_y.wait_recv()
    forward.start()
    to_core.wait_recv()
    forward.wait_recv()

    def exchange(j):
        return copy_to(
            sent.at[lax.rem(j, 3)], came.at[j], x_send.at[j], x_recv.at[j], place.x_peer
        )

    def project(j):
        for copy in weight_copies(j):
            copy.wait()

        @pl.loop(0, tiles)
        def _(i):
            sent[lax.rem(j, 3), tile(i), :] = nn(h_all[tile(i), :], w_pair[j]).astype(BF16)

        exchange(j).start()

    def work(j):
        exchange(j).wait_recv()

        @pl.loop(0, tiles)
        def _(i):
            at_rows = tile(i)
            pair = sent[lax.rem(j, 3), at_rows, :].astype(F32) + came[j, at_rows, :].astype(F32)
            gate, up = pair[:, :wide], pair[:, wide:]
            grad = inner_grad_ref[at_rows, tile(j, wide)].astype(F32)
            sig = 1.0 / (1.0 + jnp.exp(-gate))
            silu = gate * sig
            parts[at_rows, pl.ds(0, wide)] = (
                grad * up * (sig * (1.0 + gate * (1.0 - sig)))
            ).astype(BF16)
            parts[at_rows, pl.ds(wide, wide)] = (grad * silu).astype(BF16)
            inner = (silu * up).astype(BF16)
            inner_turned[:, at_rows] = inner.T
            acc_branch[at_rows, :] += nn(inner, w_down[tile(j, wide), :])
            acc_back[at_rows, :] += nt(parts[at_rows, :], w_pair[j])

        @pl.loop(0, width // TILE)
        def _(i):
            pair = nn(h_turned[tile(i), :], parts[...])
            pair_total[j, 0, tile(i), :] = pair[:, :wide].astype(BF16)
            pair_total[j, 1, tile(i), :] = pair[:, wide:].astype(BF16)
            down_total[j, :, tile(i)] = nn(inner_turned[...], top_ref[:, tile(i)]).astype(BF16)

    def total(c, k):
        return down_total.at[c] if k == 2 else pair_total.at[c, k]

    def landed(c, k, which):
        return down_came_ref.at[which, c] if k == 2 else pair_came_ref.at[which, c, k]

    def home(c, k, of):
        at_cols = tile(of * chunks + c, wide)
        return down_grads_ref.at[at_cols, :] if k == 2 else pair_grads_ref.at[k, :, at_cols]

    def add(c, k, which):
        stage = (down_stage if k == 2 else pair_stage).at[which]
        copy = pltpu.make_async_copy(landed(c, k, which), stage, load_sem.at[which])
        copy.start()
        copy.wait()
        into = total(c, k)

        @pl.loop(0, into.shape[0] // wide)
        def _(i):
            at_rows = tile(i, wide)
            into[at_rows, :] = (
                into[at_rows, :].astype(F32) + stage[at_rows, :].astype(F32)
            ).astype(BF16)

    chain = Chain(place, chunks, 3, total, landed, home, add, chain_sems)

    for j in range(min(2, chunks)):
        project(j)

    @pl.loop(0, tiles)
    def _(i):
        h_turned[:, tile(i)] = h_all[tile(i), :].T

    @pl.loop(0, chunks)
    def _(t):
        @pl.when(t + 2 < chunks)
        def _():
            @pl.when(t >= 1)
            def _():
                exchange(t - 1).wait_send()

            project(t + 2)

        work(t)
        chain.step(t)

    folded = ((acc_back, back_ref), (acc_branch, branch_ref))

    def fold_source(n, i):
        if i == 2:
            return w_down.at[slot(n), :]
        return h_all.at[slot(2 * n + i), :]

    def fold(n, i):
        return copy_to(
            fold_source(n, i), reduce_recv.at[n, i], fold_send.at[n, i], fold_recv.at[n, i],
            place.y_peer if i == 2 else place.core_peer,
        )

    to_y.wait_send()
    to_core.wait_send()
    forward.wait_send()
    for n, (acc, _) in enumerate(folded):
        for i in (1, 0):
            fold_source(n, i)[...] = acc[slot(2 * i + 1), :].astype(BF16)
            fold(n, i).start()
    for n, (acc, _) in enumerate(folded):
        fold(n, 1).wait_recv()
        fold_source(n, 2)[...] = (acc[slot(2), :] + reduce_recv[n, 1].astype(F32)).astype(BF16)
        fold(n, 2).start()
    chain.step(chunks)
    for n, (acc, out) in enumerate(folded):
        fold(n, 0).wait_recv()
        fold(n, 2).wait_recv()
        out[...] = acc[slot(0), :] + reduce_recv[n, 0].astype(F32) + reduce_recv[n, 2].astype(F32)

    @pl.loop(chunks + 1, chain.steps())
    def _(t):
        chain.step(t)

    chain.drain()

    @pl.loop(max(chunks - 3, 0), chunks)
    def _(j):
        exchange(j).wait_send()

    for n in range(2):
        for i in range(3):
            fold(n, i).wait_send()


def ffn(h, top, inner_grad, w_gate, w_up, w_down):
    count = lax.axis_size("group")
    rows, width = h.shape
    hidden = w_gate.shape[1] // 2
    wide = 128
    chunks = hidden // wide
    tokens = 4 * rows
    anywhere = pl.BlockSpec(memory_space=pl.ANY)
    local = pl.BlockSpec(memory_space=pltpu.VMEM)
    dma = pltpu.SemaphoreType.DMA
    pieces = 3 * chunks
    flops = 2 * tokens * width * hidden * 8
    return pl.pallas_call(
        functools.partial(ffn_kernel, count, chunks),
        out_shape=(
            jax.ShapeDtypeStruct((2, width, 2 * hidden), BF16),
            jax.ShapeDtypeStruct((2 * hidden, width), BF16),
            jax.ShapeDtypeStruct((2, chunks, 2, width, wide), BF16),
            jax.ShapeDtypeStruct((2, chunks, wide, width), BF16),
            jax.ShapeDtypeStruct((rows, width), F32),
            jax.ShapeDtypeStruct((rows, width), F32),
        ),
        in_specs=[local, local, local, anywhere, anywhere, anywhere],
        out_specs=(anywhere, anywhere, anywhere, anywhere, local, local),
        scratch_shapes=[
            pltpu.VMEM((tokens, width), BF16),
            pltpu.VMEM((width, tokens), BF16),
            pltpu.VMEM((3, tokens, 2 * wide), BF16),
            pltpu.VMEM((chunks, tokens, 2 * wide), BF16),
            pltpu.VMEM((chunks, width, 2 * wide), BF16),
            pltpu.VMEM((hidden, width), BF16),
            pltpu.VMEM((tokens, width), F32),
            pltpu.VMEM((tokens, width), F32),
            pltpu.VMEM((tokens, 2 * wide), BF16),
            pltpu.VMEM((wide, tokens), BF16),
            pltpu.VMEM((chunks, 2, width, wide), BF16),
            pltpu.VMEM((chunks, wide, width), BF16),
            pltpu.VMEM((2, width, wide), BF16),
            pltpu.VMEM((2, wide, width), BF16),
            pltpu.VMEM((2, 3, rows, width), BF16),
            dma((3,)), dma((3,)), dma((chunks,)), dma((chunks,)),
            dma((2,)), dma((3, chunks)), dma((2, 3)), dma((2, 3)),
            *chain_semaphores(pieces),
        ],
        compiler_params=pltpu.CompilerParams(
            collective_id=1, has_side_effects=True, vmem_limit_bytes=63 << 20
        ),
        cost_estimate=pl.CostEstimate(
            flops=flops, bytes_accessed=200 << 20, transcendentals=tokens * hidden
        ),
    )(h, top, inner_grad, w_gate, w_up, w_down)


MISC = 88


def back_kernel(
    count, own_ref, turned_ref, w_main_ref, gates_ref, w_gates_ref, gated_ref, branch_ref,
    hat_ref, scale_ref, misc_ref,
    grads_ref, back_ref, inner_ref, sums_ref,
    came, across, total, landed, misc, misc_came, misc_landed, misc_home, acc, fold_src, fold_dst,
    inner_src, inner_dst,
    x_send, x_recv, y_send, y_recv, small_send, small_recv, *chain_sems,
):
    place = Place(count)
    side = place.side
    tokens, main = own_ref.shape
    rows = tokens // 2
    cols = 256
    parts = main // cols
    width = turned_ref.shape[0]
    high = gated_ref.shape[0]
    pieces = total.shape[0]
    place.meet()

    def cut(j):
        return pl.ds(j * cols, cols) if isinstance(j, int) else tile(j, cols)

    def over_x(j):
        return copy_to(
            own_ref.at[:, cut(j)], came.at[j], x_send.at[j], x_recv.at[j], place.x_peer
        )

    def over_y(j, mine):
        src = own_ref.at[:, cut(j)] if mine else came.at[j]
        return copy_to(src, across.at[j], y_send.at[j], y_recv.at[j], place.y_peer)

    for j in range(parts):
        over_x(j).start()

    @pl.when(side == 1)
    def _():
        for j in range(parts):
            over_y(j, True).start()

    def add(c, k, which):
        total[c] = (total[c].astype(F32) + landed[which, c].astype(F32)).astype(BF16)

    chain = Chain(
        place, pieces, 1,
        lambda c, k: total.at[c],
        lambda c, k, which: landed.at[which, c],
        lambda c, k, of: grads_ref.at[of * pieces + c],
        add, chain_sems[:9],
    )

    def add_misc(c, k, which):
        misc[...] += misc_landed[which]

    small = Chain(
        place, 1, 1,
        lambda c, k: misc,
        lambda c, k, which: misc_landed.at[which],
        lambda c, k, of: misc_home,
        add_misc, chain_sems[9:], share=False,
    )

    misc[...] = misc_ref[...]
    acc[...] = nt(gates_ref[...], w_gates_ref[...])

    @pl.loop(0, parts)
    def _(t):
        total[t] = nn(gated_ref[...], branch_ref[:, cut(t)]).astype(BF16)
        chain.step(t)
        over_x(t).wait_recv()

        @pl.when(side == 0)
        def _():
            over_y(t, False).start()

        acc[...] += nt(own_ref[:, cut(t)], w_main_ref[:, cut(t)])
        acc[...] += nt(came[t], w_main_ref[:, cut(parts + t)])

    fold = copy_to(fold_src, fold_dst, small_send.at[0], small_recv.at[0], place.core_peer)
    fold_src[...] = acc[rows:, :].astype(BF16)
    fold.start()

    def inner_copy():
        return copy_to(inner_src, inner_dst, small_send.at[1], small_recv.at[1], place.x_peer)

    def misc_copy(n, peer):
        return copy_to(
            misc, misc_came.at[n], small_send.at[2 + n], small_recv.at[2 + n], peer
        )

    row_at = lax.broadcasted_iota(jnp.int32, (MISC, 128), 0)

    def block(j, i):
        if i == 0:
            over_y(j, True).wait_recv()
        at_rows = pl.ds(i * high, high)
        first = jnp.where(side == 0, own_ref[:, cut(j)], came[j])
        total[parts + 2 * j + i] = (
            nn(turned_ref[at_rows, pl.ds(0, tokens)], first)
            + nn(turned_ref[at_rows, pl.ds(tokens, tokens)], across[j])
        ).astype(BF16)

    for n in range(2 * parts):
        block(n // 2, n % 2)
        chain.step(parts + n)
        if n == 0:
            fold.wait_recv()
            grad = acc[:rows, :] + fold_dst[...].astype(F32)
            back_ref[...] = grad
            found = grad * hat_ref[...]
            inner = jnp.sum(found * scale_ref[...], axis=1, keepdims=True)
            inner_src[...] = jnp.broadcast_to(inner, (rows, 128))
            inner_copy().start()
            gain = jnp.sum(found, axis=0, keepdims=True)
            for i in range(width // 128):
                misc[i : i + 1, :] = gain[:, i * 128 : (i + 1) * 128]
            misc_copy(0, place.core_peer).start()
        if n == 1:
            misc_copy(0, place.core_peer).wait()
            both = (row_at < 16) | (row_at >= 80)
            misc[...] += jnp.where(both, misc_came[0], 0.0)
            misc_copy(1, place.x_peer).start()
        if n == 2:
            misc_copy(1, place.x_peer).wait()
            misc[...] += jnp.where(row_at >= 80, misc_came[1], 0.0)
            misc_copy(2, place.y_peer).start()
        if n == 3:
            misc_copy(2, place.y_peer).wait()
            misc[...] += misc_came[2]
            inner_copy().wait()
            inner_ref[...] = inner_src[...] + inner_dst[...]
        if n > 3:
            small.step(n - 4)

    @pl.loop(3 * parts, chain.steps())
    def _(t):
        chain.step(t)

        @pl.when(t - parts - 4 < small.steps())
        def _():
            small.step(t - parts - 4)

    @pl.loop(chain.steps() - parts - 4, small.steps())
    def _(t):
        small.step(t)

    small.drain()
    sums_ref[...] = misc_home[...]
    chain.drain()
    fold.wait_send()
    for j in range(parts):
        over_x(j).wait_send()
        over_y(j, True).wait_send()


def back(own, turned, w_main, gates, w_gates, gated, branch, hat, scale, misc):
    count = lax.axis_size("group")
    tokens, main = own.shape
    rows = tokens // 2
    width = turned.shape[0]
    high = gated.shape[0]
    cols = 256
    parts = main // cols
    pieces = 3 * parts
    anywhere = pl.BlockSpec(memory_space=pl.ANY)
    local = pl.BlockSpec(memory_space=pltpu.VMEM)
    dma = pltpu.SemaphoreType.DMA
    return pl.pallas_call(
        functools.partial(back_kernel, count),
        out_shape=(
            jax.ShapeDtypeStruct((2 * pieces, high, cols), BF16),
            jax.ShapeDtypeStruct((rows, width), F32),
            jax.ShapeDtypeStruct((rows, 128), F32),
            jax.ShapeDtypeStruct((MISC, 128), F32),
        ),
        in_specs=[local] * 10,
        out_specs=(anywhere, local, local, local),
        scratch_shapes=[
            pltpu.VMEM((parts, tokens, cols), BF16),
            pltpu.VMEM((parts, tokens, cols), BF16),
            pltpu.VMEM((pieces, high, cols), BF16),
            pltpu.VMEM((2, pieces, high, cols), BF16),
            pltpu.VMEM((MISC, 128), F32),
            pltpu.VMEM((3, MISC, 128), F32),
            pltpu.VMEM((2, MISC, 128), F32),
            pltpu.VMEM((MISC, 128), F32),
            pltpu.VMEM((tokens, width), F32),
            pltpu.VMEM((rows, width), BF16),
            pltpu.VMEM((rows, width), BF16),
            pltpu.VMEM((rows, 128), F32),
            pltpu.VMEM((rows, 128), F32),
            dma((parts,)), dma((parts,)), dma((parts,)), dma((parts,)), dma((5,)), dma((5,)),
            *chain_semaphores(pieces), *chain_semaphores(1),
        ],
        compiler_params=pltpu.CompilerParams(
            collective_id=2, has_side_effects=True, vmem_limit_bytes=56 << 20
        ),
        cost_estimate=pl.CostEstimate(
            flops=2 * tokens * width * main * 6, bytes_accessed=100 << 20, transcendentals=0
        ),
    )(own, turned, w_main, gates, w_gates, gated, branch, hat, scale, misc)


def masked_scores(query, keys, segment, place, scale):
    scores = jnp.einsum("qkgd,skd->kgqs", query, keys, preferred_element_type=F32) * scale
    allowed = (segment[:, None] == segment[None, :]) & (place[None, :] <= place[:, None])
    return jnp.where(allowed, scores, NEGATIVE)


def body(
    tokens, lengths, norm_gain, w_query, w_key, w_value, w_head_gate, query_gain, key_gain,
    w_out, ffn_gain, w_gate, w_up, w_down, grad_out,
):
    row_count = lax.axis_size("row")
    rows, d_loc = tokens.shape
    group_tok = 2 * rows
    width = d_loc * row_count
    head_dim = query_gain.shape[0]
    q_half = w_query.shape[1] // 2
    kv_half = w_key.shape[1] // 2
    gate_half = w_head_gate.shape[1] // 2
    heads = q_half // head_dim
    kv_heads = kv_half // head_dim
    share = heads // kv_heads
    main = q_half + 2 * kv_half
    half_hidden = w_gate.shape[1] // 2
    scale = head_dim ** (-0.5)
    row_at = lax.axis_index("row")
    col_at = lax.axis_index("col")
    side = lax.axis_index("group") % 2

    steps = jnp.arange(rows, dtype=jnp.int32)
    index = jnp.concatenate([col_at * rows + steps, (1 - col_at) * rows + steps])
    segment, place = places(lengths, index)

    grad_group = jnp.concatenate([grad_out, swap(grad_out, "col")])
    grad_all = jnp.concatenate([grad_group, swap_groups(grad_group)])
    down_half = lax.dynamic_slice_in_dim(w_down, side * half_hidden, half_hidden, axis=0)
    inner_part = nt(grad_all, down_half)
    inner_grad = (inner_part + swap(inner_part.astype(BF16), "row").astype(F32)).astype(BF16)
    x_in = tokens.astype(F32)
    squares = jnp.sum(x_in * x_in, axis=1)
    inverse_one = lax.rsqrt((squares + swap(squares, "row")) / width + EPS)
    normed_one = (x_in * inverse_one[:, None] * norm_gain).astype(BF16)
    permuted = jnp.concatenate([normed_one, swap(normed_one, "col")])
    splits = [halves(w, 1, row_at) for w in (w_query, w_key, w_value, w_head_gate)]
    w_main = jnp.concatenate(
        [own for own, _ in splits[:3]] + [other for _, other in splits[:3]], axis=1
    )
    w_gates = jnp.pad(jnp.concatenate(splits[3], axis=1), ((0, 0), (0, 128 - 2 * gate_half)))
    partial = nn(permuted, w_main)
    partial_gates = nn(permuted, w_gates)
    away = jnp.concatenate(
        [partial[:, main:], partial_gates[:, gate_half : 2 * gate_half]], axis=1
    ).astype(BF16)
    stay = jnp.concatenate([partial[:, :main], partial_gates[:, :gate_half]], axis=1)
    turned = jnp.concatenate([permuted, swap_groups(permuted)]).T
    projected = stay + swap(away, "row").astype(F32)
    raw_query = projected[:, :q_half].reshape(group_tok, heads, head_dim)
    raw_key = projected[:, q_half : q_half + kv_half].reshape(group_tok, kv_heads, head_dim)
    raw_value = projected[:, q_half + kv_half : main].reshape(group_tok, kv_heads, head_dim)
    logit = projected[:, main:]
    query_inverse = lax.rsqrt(jnp.mean(raw_query * raw_query, axis=-1, keepdims=True) + EPS)
    key_inverse = lax.rsqrt(jnp.mean(raw_key * raw_key, axis=-1, keepdims=True) + EPS)
    cosines, sines = rope_tables(place, head_dim)
    cos_heads = cosines[:, None, :]
    sin_heads = sines[:, None, :]
    query = rotate(raw_query * query_inverse * query_gain, cos_heads, sin_heads).astype(BF16)
    keys = rotate(raw_key * key_inverse * key_gain, cos_heads, sin_heads).astype(BF16)
    values = raw_value.astype(BF16)
    query = query.reshape(group_tok, kv_heads, share, head_dim)

    scores = masked_scores(query, keys, segment, place, scale)
    top = jnp.max(scores, axis=-1, keepdims=True)
    raised = jnp.exp(scores - top)
    probs = raised / jnp.sum(raised, axis=-1, keepdims=True)
    probs_low = probs.astype(BF16)
    attended = jnp.einsum("kgqs,skd->qkgd", probs_low, values, preferred_element_type=F32)
    attended = attended.reshape(group_tok, heads, head_dim)
    gate_sigmoid = jax.nn.sigmoid(logit)
    gated = (attended * gate_sigmoid[:, :, None]).reshape(group_tok, q_half).astype(BF16)
    gated_came = swap(gated, "row")
    gated_all = jnp.concatenate([gated, gated_came], axis=1)
    first_side = side == 0
    gated_pair = jnp.concatenate(
        [
            jnp.where(first_side, gated, gated_came),
            swap_groups(jnp.where(first_side, gated_came, gated)),
        ]
    ).T
    w_back = jnp.concatenate(halves(w_out, 0, row_at))

    def sum_cores(values):
        return values[:rows] + swap(values[rows:].astype(BF16), "col").astype(F32)

    resid = x_in + sum_cores(nn(gated_all, w_back))
    squares = jnp.sum(resid * resid, axis=1)
    inverse_two = lax.rsqrt((squares + swap(squares, "row")) / width + EPS)
    normed_two = (resid * inverse_two[:, None] * ffn_gain).astype(BF16)

    pair_sum, down_sum, _, _, branch, d_normed_two = ffn(
        normed_two, grad_all, inner_grad, w_gate, w_up, w_down
    )
    output = (resid + branch).astype(BF16)

    d_top = grad_out.astype(F32)
    ffn_gain_part = jnp.sum(d_normed_two * resid * inverse_two[:, None], axis=0)
    scaled_two = d_normed_two * ffn_gain
    inner_two = jnp.sum(scaled_two * resid, axis=1)
    inner_two = inner_two + swap(inner_two, "row")
    d_resid = (
        d_top
        + inverse_two[:, None] * scaled_two
        - resid * (inverse_two**3 * inner_two / width)[:, None]
    )
    d_branch = d_resid.astype(BF16)
    branch_all = jnp.concatenate([d_branch, swap(d_branch, "col")])
    branch_across = swap_groups(d_branch)
    branch_pair = jnp.concatenate([branch_all, branch_across, swap(branch_across, "col")])
    d_gated_part = nt(branch_all, w_back)
    d_gated = d_gated_part[:, :q_half] + swap(
        d_gated_part[:, q_half:].astype(BF16), "row"
    ).astype(F32)
    d_gated = d_gated.reshape(group_tok, heads, head_dim)
    d_attended = (d_gated * gate_sigmoid[:, :, None]).astype(BF16)
    d_logit = jnp.sum(d_gated * attended, axis=-1) * gate_sigmoid * (1.0 - gate_sigmoid)
    d_attended = d_attended.reshape(group_tok, kv_heads, share, head_dim)

    d_probs = jnp.einsum("qkgd,skd->kgqs", d_attended, values, preferred_element_type=F32)
    d_scores = (probs * (d_probs - jnp.sum(d_probs * probs, axis=-1, keepdims=True))).astype(BF16)
    d_query = jnp.einsum("kgqs,skd->qkgd", d_scores, keys, preferred_element_type=F32) * scale
    d_keys = jnp.einsum("kgqs,qkgd->skd", d_scores, query, preferred_element_type=F32) * scale
    d_values = jnp.einsum("kgqs,qkgd->skd", probs_low, d_attended, preferred_element_type=F32)
    d_query = d_query.reshape(group_tok, heads, head_dim)
    d_raw_query, query_gain_part = head_norm_back(
        unrotate(d_query, cos_heads, sin_heads), raw_query, query_inverse, query_gain
    )
    d_raw_key, key_gain_part = head_norm_back(
        unrotate(d_keys, cos_heads, sin_heads), raw_key, key_inverse, key_gain
    )
    d_main = jnp.concatenate(
        [
            d_raw_query.reshape(group_tok, q_half),
            d_raw_key.reshape(group_tok, kv_half),
            d_values.reshape(group_tok, kv_half),
        ],
        axis=1,
    ).astype(BF16)
    d_gates = d_logit.astype(BF16)
    d_gates = jnp.concatenate([d_gates, swap(d_gates, "row")], axis=1)
    gates_part = lax.dot_general(
        d_gates, permuted, (((0,), (0,)), ((), ())), preferred_element_type=F32
    )
    misc = jnp.concatenate(
        [
            jnp.zeros((8, 128), F32),
            ffn_gain_part.reshape(8, 128),
            gates_part.reshape(64, 128),
            query_gain_part[None],
            key_gain_part[None],
            jnp.zeros((6, 128), F32),
        ]
    )
    hat = x_in * inverse_one[:, None]
    grads, d_normed_one, inner_one, sums = back(
        d_main, turned, w_main, jnp.pad(d_gates, ((0, 0), (0, 128 - 2 * gate_half))), w_gates,
        gated_pair, branch_pair, hat, norm_gain[None], misc,
    )
    input_grad = d_resid + inverse_one[:, None] * (
        d_normed_one * norm_gain - hat * (inner_one[:, :1] / width)
    )
    grad_norm_gain = sums[:8].reshape(d_loc)
    grad_ffn_gain = sums[8:16].reshape(d_loc)
    grad_gates = sums[16:80].reshape(2 * gate_half, d_loc)
    grad_head_gate = ordered(grad_gates[:gate_half], grad_gates[gate_half:], 0, row_at).T
    grads = grads.reshape(2, -1, q_half, 256)
    count = main // 256
    out_sum = grads[:, :count].transpose(0, 2, 1, 3).reshape(2 * q_half, d_loc)
    first_sum = (
        grads[:, count:]
        .reshape(2, count, 2, q_half, 256)
        .transpose(2, 3, 0, 1, 4)
        .reshape(d_loc, 2 * main)
    )

    def piece(start, size):
        own = first_sum[:, start : start + size]
        other = first_sum[:, main + start : main + start + size]
        return ordered(own, other, 1, row_at).astype(F32)

    grad_out_full = ordered(*jnp.split(out_sum, 2, axis=0), 0, row_at).astype(F32)
    return (
        output,
        input_grad,
        grad_norm_gain,
        piece(0, q_half),
        piece(q_half, kv_half),
        piece(q_half + kv_half, kv_half),
        grad_head_gate,
        sums[80],
        sums[81],
        grad_out_full,
        grad_ffn_gain,
        pair_sum[0].astype(F32),
        pair_sum[1].astype(F32),
        down_sum.astype(F32),
    )


def solution(mesh):
    shards = P(("group", "col"), "row")
    in_specs = (
        shards,
        P("group"),
        P("row"),
        P("row", "col"),
        P("row", "col"),
        P("row", "col"),
        P("row", "col"),
        P(),
        P(),
        P("col", "row"),
        P("row"),
        P("row", "col"),
        P("row", "col"),
        P("col", "row"),
        shards,
    )
    out_specs = (
        shards,
        shards,
        P("row"),
        P("row", "col"),
        P("row", "col"),
        P("row", "col"),
        P("row", "col"),
        P(),
        P(),
        P("col", "row"),
        P("row"),
        P("row", "col"),
        P("row", "col"),
        P("col", "row"),
    )
    return jax.shard_map(body, mesh=mesh, in_specs=in_specs, out_specs=out_specs, check_vma=False)
```

```python
import functools

import jax
import jax.numpy as jnp
from jax import lax
from jax.experimental import pallas as pl
from jax.experimental.pallas import tpu as pltpu
from jax.sharding import PartitionSpec as P

EPS = 1e-06
THETA = 1000000.0
NEGATIVE = -1e30
MESH = pl.DeviceIdType.MESH
F32 = jnp.float32
BF16 = jnp.bfloat16


def swap(values, axis):
    return lax.ppermute(values, axis, [(0, 1), (1, 0)])


def swap_groups(values):
    count = lax.axis_size("group")
    return lax.ppermute(values, "group", [(i, i ^ 1) for i in range(count)])


def halves(values, axis, at):
    low, high = jnp.split(values, 2, axis=axis)
    first = at == 0
    return jnp.where(first, low, high), jnp.where(first, high, low)


def ordered(own, other, axis, at):
    first = at == 0
    return jnp.concatenate(
        [jnp.where(first, own, other), jnp.where(first, other, own)], axis=axis
    )


def places(lengths_group, index):
    ends = jnp.cumsum(lengths_group)
    passed = (index[:, None] >= ends[None, :]).astype(jnp.int32)
    segment = jnp.sum(passed, axis=1)
    place = index - jnp.sum(passed * lengths_group[None, :], axis=1)
    return (segment, place)


def rope_tables(place, width):
    half = width // 2
    freq = THETA ** (-(jnp.arange(half, dtype=F32) * 2.0 / width))
    angle = place.astype(F32)[:, None] * freq[None, :]
    cosines = jnp.concatenate([jnp.cos(angle), jnp.cos(angle)], axis=1)
    sines = jnp.concatenate([jnp.sin(angle), jnp.sin(angle)], axis=1)
    return (cosines, sines)


def rotate(values, cosines, sines):
    half = values.shape[-1] // 2
    turned = jnp.concatenate([-values[..., half:], values[..., :half]], axis=-1)
    return values * cosines + turned * sines


def unrotate(grads, cosines, sines):
    half = grads.shape[-1] // 2
    scaled = grads * sines
    return grads * cosines + jnp.concatenate([scaled[..., half:], -scaled[..., :half]], axis=-1)


def head_norm_back(d_normed, raw_values, inverse, gain):
    scaled = d_normed * gain
    gain_part = jnp.sum(d_normed * raw_values * inverse, axis=(0, 1))
    d_raw = inverse * scaled - raw_values * inverse**3 * jnp.mean(
        scaled * raw_values, axis=-1, keepdims=True
    )
    return (d_raw, gain_part)


TILE = 256
HOP = 1
WIDE = 128
EARLY = 6
AHEAD = 3


def nt(a, b):
    return lax.dot_general(a, b, (((1,), (1,)), ((), ())), preferred_element_type=F32)


def nn(a, b):
    return jnp.dot(a, b, preferred_element_type=F32)


def copy_to(src, dst, send_sem, recv_sem, peer):
    return pltpu.make_async_remote_copy(
        src_ref=src, dst_ref=dst, send_sem=send_sem, recv_sem=recv_sem,
        device_id=peer, device_id_type=MESH,
    )


def tile(i, size=TILE):
    return pl.ds(pl.multiple_of(i * size, size), size)


class Place:
    def __init__(self, count):
        group = lax.axis_index("group")
        self.line = count // 2
        self.root = (self.line - 1) // 2
        self.deep = max(self.root, self.line - 1 - self.root)
        self.at = group // 2
        self.side = group % 2
        self.x_peer = {"row": 1 - lax.axis_index("row")}
        self.core_peer = {"col": 1 - lax.axis_index("col")}
        self.y_peer = {"group": group + 1 - 2 * self.side}
        self.above = {"group": jnp.minimum(group + 2, count - 1)}
        self.below = {"group": jnp.maximum(group - 2, 0)}
        self.has_above = self.at < self.line - 1
        self.has_below = self.at > 0

    def meet(self):
        barrier = pltpu.get_barrier_semaphore()

        def greet(peer):
            pl.semaphore_signal(barrier, inc=1, device_id=peer, device_id_type=MESH)

        for peer in (self.x_peer, self.core_peer, self.y_peer):
            greet(peer)
        pl.when(self.has_above)(lambda: greet(self.above))
        pl.when(self.has_below)(lambda: greet(self.below))
        met = 3 + self.has_above.astype(jnp.int32) + self.has_below.astype(jnp.int32)
        pl.semaphore_wait(barrier, met)


class Chain:
    def __init__(self, place, chunks, kinds, total, came, home, add, sems, share=True):
        self.place, self.chunks, self.kinds = place, chunks, kinds
        self.total, self.came, self.home, self.add = total, came, home, add
        self.sems, self.share = sems, share

    def part_copy(self, c, k, upward):
        sent, low, high = self.sems[:3]
        p = self.kinds * c + k
        peer, which, arrived = (
            (self.place.above, 0, low) if upward else (self.place.below, 1, high)
        )
        return copy_to(
            self.total(c, k), self.came(c, k, which), sent.at[p], arrived.at[p], peer
        )

    def final_copy(self, c, k, upward, first):
        up, down, arrived = self.sems[3:6]
        p = self.kinds * c + k
        src = self.total(c, k) if first else self.home(c, k, self.place.side)
        peer, sent = (self.place.above, up) if upward else (self.place.below, down)
        return copy_to(src, self.home(c, k, self.place.side), sent.at[p], arrived.at[p], peer)

    def keep_copy(self, c, k):
        return pltpu.make_async_copy(
            self.total(c, k), self.home(c, k, self.place.side),
            self.sems[6].at[self.kinds * c + k],
        )

    def share_copy(self, c, k, first, of=None):
        p = self.kinds * c + k
        of = self.place.side if of is None else of
        src = self.total(c, k) if first else self.home(c, k, self.place.side)
        return copy_to(
            src, self.home(c, k, of), self.sems[7].at[p], self.sems[8].at[p], self.place.y_peer
        )

    def step(self, u, hop=1):
        at, line, root, deep = self.place.at, self.place.line, self.place.root, self.place.deep
        behind = jnp.where(at < root, at, jnp.where(at > root, line - 1 - at, deep))
        self.inward(u - hop * behind)
        self.outward(u - hop * (deep + jnp.abs(at - root)))

    def kinds_of(self, p):
        live = (p >= 0) & (p < self.kinds * self.chunks)
        if self.kinds == 1:
            return [(live, p, 0)]
        p = jnp.maximum(p, 0)
        return [
            (live & (lax.rem(p, self.kinds) == k), lax.div(p, self.kinds), k)
            for k in range(self.kinds)
        ]

    def inward(self, piece):
        at, line, root = self.place.at, self.place.line, self.place.root
        for live, c, k in self.kinds_of(piece):

            @pl.when(live & (at < root))
            def _():
                @pl.when(self.place.has_below)
                def _():
                    self.part_copy(c, k, True).wait_recv()
                    self.add(c, k, 0)

                self.part_copy(c, k, True).start()

            @pl.when(live & (at > root))
            def _():
                @pl.when(self.place.has_above)
                def _():
                    self.part_copy(c, k, False).wait_recv()
                    self.add(c, k, 1)

                self.part_copy(c, k, False).start()

            @pl.when(live & (at == root))
            def _():
                if root > 0:
                    self.part_copy(c, k, True).wait_recv()
                    self.add(c, k, 0)
                if root < line - 1:
                    self.part_copy(c, k, False).wait_recv()
                    self.add(c, k, 1)
                if root > 0:
                    self.final_copy(c, k, False, True).start()
                if root < line - 1:
                    self.final_copy(c, k, True, True).start()
                if self.share:
                    self.share_copy(c, k, True).start()
                self.keep_copy(c, k).start()

    def outward(self, piece):
        at, root = self.place.at, self.place.root
        for live, c, k in self.kinds_of(piece):

            @pl.when(live & (at != root))
            def _():
                self.final_copy(c, k, True, False).wait_recv()

                @pl.when((at > root) & self.place.has_above)
                def _():
                    self.final_copy(c, k, True, False).start()

                @pl.when((at < root) & self.place.has_below)
                def _():
                    self.final_copy(c, k, False, False).start()

                if self.share:
                    self.share_copy(c, k, False).start()

    def steps(self, hop=1):
        return self.kinds * self.chunks + 2 * hop * self.place.deep

    def drain(self):
        at, line, root = self.place.at, self.place.line, self.place.root

        @pl.loop(0, self.chunks)
        def _(c):
            for k in range(self.kinds):
                if self.share:
                    self.share_copy(c, k, False, 1 - self.place.side).wait_recv()
                    self.share_copy(c, k, False).wait_send()

                @pl.when(at == root)
                def _():
                    self.keep_copy(c, k).wait()
                    if root > 0:
                        self.final_copy(c, k, False, True).wait_send()
                    if root < line - 1:
                        self.final_copy(c, k, True, True).wait_send()

                @pl.when(at < root)
                def _():
                    self.part_copy(c, k, True).wait_send()

                    @pl.when(self.place.has_below)
                    def _():
                        self.final_copy(c, k, False, False).wait_send()

                @pl.when(at > root)
                def _():
                    self.part_copy(c, k, False).wait_send()

                    @pl.when(self.place.has_above)
                    def _():
                        self.final_copy(c, k, True, False).wait_send()


def chain_semaphores(pieces):
    return [pltpu.SemaphoreType.DMA((pieces,)) for _ in range(9)]


def ffn_kernel(
    count, chunks, h_ref, top_ref, early_ref, gate_ref, up_ref, down_ref,
    pair_grads_ref, down_grads_ref, pair_came_ref, down_came_ref, branch_ref, branch_out_ref,
    back_ref,
    h_all, h_turned, sent, came, top_sent, top_came, grad_part, w_pair, w_down, acc_branch, acc_back, parts, inner_turned,
    pair_total, down_total, pair_stage, down_stage, reduce_recv,
    gather_send, gather_recv, x_send, x_recv, top_send, top_recv, load_sem, weight_sem, fold_send, fold_recv,
    *chain_sems,
):
    place = Place(count)
    rows, width = h_ref.shape
    tokens = h_all.shape[0]
    tiles = tokens // TILE
    wide = w_down.shape[0] // chunks
    side = place.side

    def weight_copies(j):
        cols = tile(side * chunks + j, wide)
        return (
            pltpu.make_async_copy(
                gate_ref.at[:, cols], w_pair.at[j, :, pl.ds(0, wide)], weight_sem.at[0, j]
            ),
            pltpu.make_async_copy(
                up_ref.at[:, cols], w_pair.at[j, :, pl.ds(wide, wide)], weight_sem.at[1, j]
            ),
            pltpu.make_async_copy(
                down_ref.at[cols, :], w_down.at[tile(j, wide), :], weight_sem.at[2, j]
            ),
        )

    @pl.loop(0, chunks)
    def _(j):
        for copy in weight_copies(j):
            copy.start()

    place.meet()

    def slot(i):
        return pl.ds(i * rows, rows)

    to_y = copy_to(h_ref, h_all.at[slot(2)], gather_send.at[0], gather_recv.at[0], place.y_peer)
    to_core = copy_to(
        h_ref, h_all.at[slot(1)], gather_send.at[1], gather_recv.at[1], place.core_peer
    )
    forward = copy_to(
        h_all.at[slot(2)], h_all.at[slot(3)], gather_send.at[2], gather_recv.at[2],
        place.core_peer,
    )
    to_y.start()
    to_core.start()

    def top_exchange(j):
        n = j - EARLY
        return copy_to(
            top_sent.at[n], top_came.at[n], top_send.at[n], top_recv.at[n], place.x_peer
        )

    def top_project(j):
        @pl.loop(0, tiles)
        def _(i):
            top_sent[j - EARLY, tile(i), :] = nt(
                top_ref[tile(i), :], w_down[tile(j, wide), :]
            ).astype(BF16)

        top_exchange(j).start()

    @pl.loop(0, chunks)
    def _(j):
        weight_copies(j)[2].wait()

    @pl.loop(EARLY, min(EARLY + AHEAD, chunks))
    def _(j):
        top_project(j)

    h_all[slot(0), :] = h_ref[...]
    acc_branch[...] = jnp.zeros_like(acc_branch)
    acc_back[...] = jnp.zeros_like(acc_back)
    to_y.wait_recv()
    forward.start()
    to_core.wait_recv()
    forward.wait_recv()

    def exchange(j):
        return copy_to(
            sent.at[lax.rem(j, 3)], came.at[j], x_send.at[j], x_recv.at[j], place.x_peer
        )

    def project(j):
        for copy in weight_copies(j)[:2]:
            copy.wait()

        @pl.loop(0, tiles)
        def _(i):
            sent[lax.rem(j, 3), tile(i), :] = nn(h_all[tile(i), :], w_pair[j]).astype(BF16)

        exchange(j).start()

    def work(j):
        exchange(j).wait_recv()

        @pl.when(j < EARLY)
        def _():
            grad_part[...] = early_ref[:, tile(j, wide)].astype(F32)

        @pl.when(j >= EARLY)
        def _():
            top_exchange(j).wait_recv()
            grad_part[...] = top_sent[j - EARLY].astype(F32) + top_came[j - EARLY].astype(F32)

        @pl.loop(0, tiles)
        def _(i):
            at_rows = tile(i)
            pair = sent[lax.rem(j, 3), at_rows, :].astype(F32) + came[j, at_rows, :].astype(F32)
            gate, up = pair[:, :wide], pair[:, wide:]
            grad = grad_part[at_rows, :]
            sig = 1.0 / (1.0 + jnp.exp(-gate))
            silu = gate * sig
            parts[at_rows, pl.ds(0, wide)] = (
                grad * up * (sig * (1.0 + gate * (1.0 - sig)))
            ).astype(BF16)
            parts[at_rows, pl.ds(wide, wide)] = (grad * silu).astype(BF16)
            inner = (silu * up).astype(BF16)
            inner_turned[:, at_rows] = inner.T
            acc_branch[at_rows, :] += nn(inner, w_down[tile(j, wide), :])
            acc_back[at_rows, :] += nt(parts[at_rows, :], w_pair[j])

    def gradients(j):
        @pl.loop(0, width // TILE)
        def _(i):
            pair = nn(h_turned[tile(i), :], parts[...])
            pair_total[j, 0, tile(i), :] = pair[:, :wide].astype(BF16)
            pair_total[j, 1, tile(i), :] = pair[:, wide:].astype(BF16)
            down_total[j, :, tile(i)] = nn(inner_turned[...], top_ref[:, tile(i)]).astype(BF16)

    def total(c, k):
        return down_total.at[c] if k == 2 else pair_total.at[c, k]

    def landed(c, k, which):
        return down_came_ref.at[which, c] if k == 2 else pair_came_ref.at[which, c, k]

    def home(c, k, of):
        at_cols = tile(of * chunks + c, wide)
        return down_grads_ref.at[at_cols, :] if k == 2 else pair_grads_ref.at[k, :, at_cols]

    def add(c, k, which):
        stage = (down_stage if k == 2 else pair_stage).at[which]
        copy = pltpu.make_async_copy(landed(c, k, which), stage, load_sem.at[which])
        copy.start()
        copy.wait()
        into = total(c, k)

        @pl.loop(0, into.shape[0] // wide)
        def _(i):
            at_rows = tile(i, wide)
            into[at_rows, :] = (
                into[at_rows, :].astype(F32) + stage[at_rows, :].astype(F32)
            ).astype(BF16)

    chain = Chain(place, chunks, 3, total, landed, home, add, chain_sems)

    for j in range(min(2, chunks)):
        project(j)

    @pl.loop(0, tiles)
    def _(i):
        h_turned[:, tile(i)] = h_all[tile(i), :].T

    @pl.loop(0, chunks)
    def _(t):
        work(t)
        chain.step(3 * t - 1, HOP)
        gradients(t)
        chain.step(3 * t, HOP)

        @pl.when(t + 2 < chunks)
        def _():
            @pl.when(t >= 1)
            def _():
                exchange(t - 1).wait_send()

            project(t + 2)

        @pl.when(EARLY + AHEAD + t < chunks)
        def _():
            top_project(EARLY + AHEAD + t)

        chain.step(3 * t + 1, HOP)

    chain.step(3 * chunks - 1, HOP)

    def fold_source(n, i):
        if i == 2:
            return w_down.at[slot(0), :]
        return h_all.at[slot(2 * n + i), :]

    def fold(n, i):
        return copy_to(
            fold_source(n, i), reduce_recv.at[n, i], fold_send.at[n, i], fold_recv.at[n, i],
            place.y_peer if i == 2 else place.core_peer,
        )

    to_y.wait_send()
    to_core.wait_send()
    forward.wait_send()
    for n, acc in enumerate((acc_back, acc_branch)):
        for i in (1, 0):
            fold_source(n, i)[...] = acc[slot(2 * i + 1), :].astype(BF16)
            fold(n, i).start()
    fold(0, 1).wait_recv()
    fold_source(0, 2)[...] = (acc_back[slot(2), :] + reduce_recv[0, 1].astype(F32)).astype(BF16)
    fold(0, 2).start()
    chain.step(3 * chunks, HOP)
    fold(1, 0).wait_recv()
    fold(1, 1).wait_recv()
    branch_ref[...] = acc_branch[slot(0), :] + reduce_recv[1, 0].astype(F32)
    branch_out_ref[...] = (acc_branch[slot(2), :] + reduce_recv[1, 1].astype(F32)).astype(BF16)
    fold(0, 0).wait_recv()
    fold(0, 2).wait_recv()
    back_ref[...] = (
        acc_back[slot(0), :] + reduce_recv[0, 0].astype(F32) + reduce_recv[0, 2].astype(F32)
    )

    @pl.loop(3 * chunks + 1, chain.steps(HOP))
    def _(u):
        chain.step(u, HOP)

    chain.drain()

    @pl.loop(max(chunks - 3, 0), chunks)
    def _(j):
        exchange(j).wait_send()

    @pl.loop(EARLY, chunks)
    def _(j):
        top_exchange(j).wait_send()

    for n, i in ((0, 0), (0, 1), (0, 2), (1, 0), (1, 1)):
        fold(n, i).wait_send()


def ffn(h, top, early, w_gate, w_up, w_down):
    count = lax.axis_size("group")
    rows, width = h.shape
    hidden = w_gate.shape[1] // 2
    wide = WIDE
    chunks = hidden // wide
    tokens = 4 * rows
    anywhere = pl.BlockSpec(memory_space=pl.ANY)
    local = pl.BlockSpec(memory_space=pltpu.VMEM)
    dma = pltpu.SemaphoreType.DMA
    pieces = 3 * chunks
    flops = 2 * tokens * width * hidden * 8
    return pl.pallas_call(
        functools.partial(ffn_kernel, count, chunks),
        out_shape=(
            jax.ShapeDtypeStruct((2, width, 2 * hidden), BF16),
            jax.ShapeDtypeStruct((2 * hidden, width), BF16),
            jax.ShapeDtypeStruct((2, chunks, 2, width, wide), BF16),
            jax.ShapeDtypeStruct((2, chunks, wide, width), BF16),
            jax.ShapeDtypeStruct((rows, width), F32),
            jax.ShapeDtypeStruct((rows, width), BF16),
            jax.ShapeDtypeStruct((rows, width), F32),
        ),
        in_specs=[local, local, local, anywhere, anywhere, anywhere],
        out_specs=(anywhere, anywhere, anywhere, anywhere, local, local, local),
        scratch_shapes=[
            pltpu.VMEM((tokens, width), BF16),
            pltpu.VMEM((width, tokens), BF16),
            pltpu.VMEM((3, tokens, 2 * wide), BF16),
            pltpu.VMEM((chunks, tokens, 2 * wide), BF16),
            pltpu.VMEM((chunks - EARLY, tokens, wide), BF16),
            pltpu.VMEM((chunks - EARLY, tokens, wide), BF16),
            pltpu.VMEM((tokens, wide), F32),
            pltpu.VMEM((chunks, width, 2 * wide), BF16),
            pltpu.VMEM((hidden, width), BF16),
            pltpu.VMEM((tokens, width), F32),
            pltpu.VMEM((tokens, width), F32),
            pltpu.VMEM((tokens, 2 * wide), BF16),
            pltpu.VMEM((wide, tokens), BF16),
            pltpu.VMEM((chunks, 2, width, wide), BF16),
            pltpu.VMEM((chunks, wide, width), BF16),
            pltpu.VMEM((2, width, wide), BF16),
            pltpu.VMEM((2, wide, width), BF16),
            pltpu.VMEM((2, 3, rows, width), BF16),
            dma((3,)), dma((3,)), dma((chunks,)), dma((chunks,)),
            dma((chunks - EARLY,)), dma((chunks - EARLY,)),
            dma((2,)), dma((3, chunks)), dma((2, 3)), dma((2, 3)),
            *chain_semaphores(pieces),
        ],
        compiler_params=pltpu.CompilerParams(
            collective_id=1, has_side_effects=True, vmem_limit_bytes=63 << 20
        ),
        cost_estimate=pl.CostEstimate(
            flops=flops, bytes_accessed=200 << 20, transcendentals=tokens * hidden
        ),
    )(h, top, early, w_gate, w_up, w_down)


ROWS = 128


def sigmoid(v):
    return 1.0 / (1.0 + jnp.exp(-v))


def column(values):
    return jnp.broadcast_to(values, (values.shape[0], 128))


def front_kernel(
    count, heads, kv_heads, tok_ref, top_ref, norm_ref, second_ref, q_gain_ref, k_gain_ref,
    cos_ref, sin_ref, at_ref, start_ref, key_at_ref, w_gates_ref, wq_ref, wk_ref, wv_ref, wo_ref,
    wd_ref,
    h_ref, resid_ref, inv_two_ref, hat_ref, inv_one_ref, normed_ref, tops_ref, early_ref,
    raw_ref, sig_ref, q_ref, k_ref, v_ref, log_ref, attended_ref, gated_ref,
    wq, wk, wv, wo, wd, kv_send, kv_came, q_send, q_came, gates, early_send, early_came,
    ss_send, ss_came, fold_src, fold_dst, acc,
    w_sem, n_send, n_recv, t_send, t_recv, p_send, p_recv, e_send, e_recv, g_send, g_recv,
    s_send, s_recv,
):
    place = Place(count)
    rows, width = tok_ref.shape
    tokens = 2 * rows
    row_at = lax.axis_index("row")
    side = place.side
    hd = 128
    qw, kw = heads * hd, kv_heads * hd
    hidden = wd_ref.shape[0] // 2
    scale = hd**-0.5

    loads = []
    for i, at in enumerate((row_at, 1 - row_at)):
        q_cols, k_cols = tile(at, qw), tile(at, kw)
        loads += [
            pltpu.make_async_copy(wk_ref.at[:, k_cols], wk.at[i], w_sem.at[i, 0]),
            pltpu.make_async_copy(wv_ref.at[:, k_cols], wv.at[i], w_sem.at[i, 1]),
            pltpu.make_async_copy(wq_ref.at[:, q_cols], wq.at[i], w_sem.at[i, 2]),
            pltpu.make_async_copy(wo_ref.at[q_cols, :], wo.at[i], w_sem.at[i, 3]),
        ]
    down_rows = pl.ds(pl.multiple_of(side * hidden, WIDE), wd.shape[0])
    loads.append(pltpu.make_async_copy(wd_ref.at[down_rows, :], wd, w_sem.at[0, 4]))
    for copy in loads:
        copy.start()
    place.meet()

    def slot(i):
        return pl.ds(i * rows, rows)

    def spread(ref, sends, recvs):
        own, core, pair, both = (ref.at[slot(i), :] for i in range(4))
        return (
            copy_to(own, core, sends.at[0], recvs.at[0], place.core_peer),
            copy_to(own, pair, sends.at[1], recvs.at[1], place.y_peer),
            copy_to(pair, both, sends.at[2], recvs.at[2], place.core_peer),
        )

    tops_ref[slot(0), :] = top_ref[...]
    tops = spread(tops_ref, t_send, t_recv)
    tops[0].start()
    tops[1].start()

    def squares(n):
        return copy_to(ss_send.at[n], ss_came.at[n], s_send.at[n], s_recv.at[n], place.x_peer)

    x = tok_ref[...].astype(F32)
    ss_send[0] = column(jnp.sum(x * x, axis=1, keepdims=True))
    squares(0).start()

    def early(i):
        return copy_to(
            early_send.at[slot(i), :], early_came.at[slot(i), :], e_send.at[i], e_recv.at[i],
            place.x_peer,
        )

    def early_start(i):
        early_send[slot(i), :] = nt(tops_ref[slot(i), :], wd[...]).astype(BF16)
        early(i).start()

    loads[-1].wait()
    early_start(0)
    squares(0).wait()
    inv_one = lax.rsqrt((ss_send[0] + ss_came[0]) / (2 * width) + EPS)
    inv_one_ref[...] = inv_one
    hat = tok_ref[...].astype(F32) * inv_one[:, :1]
    hat_ref[...] = hat
    normed_ref[slot(0), :] = (hat * norm_ref[...]).astype(BF16)
    normed = spread(normed_ref, n_send, n_recv)
    normed[0].start()
    normed[1].start()

    kv_copy = copy_to(kv_send, kv_came, p_send.at[0], p_recv.at[0], place.x_peer)
    q_copy = copy_to(q_send, q_came, p_send.at[1], p_recv.at[1], place.x_peer)
    for copy in loads[:-1]:
        copy.wait()
    for i in range(2):
        if i == 1:
            normed[0].wait_recv()
        rows_in = normed_ref[slot(i), :]
        kv_send[slot(i), pl.ds(0, kw)] = nn(rows_in, wk[1]).astype(BF16)
        kv_send[slot(i), pl.ds(kw, kw)] = nn(rows_in, wv[1]).astype(BF16)
    kv_copy.start()
    for i in range(2):
        rows_in = normed_ref[slot(i), :]
        q_send[slot(i), pl.ds(0, qw)] = nn(rows_in, wq[1]).astype(BF16)
        part = nn(rows_in, w_gates_ref[...])
        gates[slot(i), :] = part
        q_send[slot(i), pl.ds(qw, 128)] = part.astype(BF16)
    q_copy.start()
    for i in range(2):
        rows_in = normed_ref[slot(i), :]
        raw_ref[slot(i), pl.ds(0, qw)] = nn(rows_in, wq[0])
        raw_ref[slot(i), pl.ds(qw, kw)] = nn(rows_in, wk[0])
        raw_ref[slot(i), pl.ds(qw + kw, kw)] = nn(rows_in, wv[0])

    def turn(values, gain, at_rows):
        inverse = lax.rsqrt(jnp.mean(values * values, axis=1, keepdims=True) + EPS)
        scaled = values * inverse * gain
        return scaled * cos_ref[at_rows, :] + pltpu.roll(scaled, 64, axis=1) * sin_ref[at_rows, :]

    tops[1].wait_recv()
    tops[2].start()
    normed[1].wait_recv()
    normed[2].start()
    tops[0].wait_recv()
    kv_copy.wait_recv()

    @pl.loop(0, tokens // ROWS)
    def _(i):
        at_rows = tile(i, ROWS)
        for n in range(kv_heads):
            cols = pl.ds(qw + n * hd, hd)
            key = raw_ref[at_rows, cols] + kv_came[at_rows, pl.ds(n * hd, hd)].astype(F32)
            raw_ref[at_rows, cols] = key
            k_ref[at_rows, pl.ds(n * hd, hd)] = turn(key, k_gain_ref[...], at_rows).astype(BF16)
            cols = pl.ds(qw + kw + n * hd, hd)
            value = raw_ref[at_rows, cols] + kv_came[at_rows, pl.ds(kw + n * hd, hd)].astype(F32)
            raw_ref[at_rows, cols] = value
            v_ref[at_rows, pl.ds(n * hd, hd)] = value.astype(BF16)

    q_copy.wait_recv()
    early_start(1)

    @pl.loop(0, tokens // ROWS)
    def _(i):
        at_rows = tile(i, ROWS)
        other = q_came[at_rows, pl.ds(qw, 128)].astype(F32)
        logit = gates[at_rows, :] + pltpu.roll(other, 128 - heads, axis=1)
        sig_ref[at_rows, :] = sigmoid(logit)
        for n in range(heads):
            cols = pl.ds(n * hd, hd)
            query = raw_ref[at_rows, cols] + q_came[at_rows, cols].astype(F32)
            raw_ref[at_rows, cols] = query
            q_ref[at_rows, cols] = turn(query, q_gain_ref[...], at_rows).astype(BF16)

    def head_copy(n):
        cols = pl.ds(n * hd, hd)
        return copy_to(
            gated_ref.at[0, :, cols], gated_ref.at[1, :, cols], g_send.at[n], g_recv.at[n],
            place.x_peer,
        )

    for n in range(heads):
        cols = pl.ds(n * hd, hd)
        kv = pl.ds(n * kv_heads // heads * hd, hd)

        @pl.loop(0, tokens // ROWS)
        def _(i):
            at_rows = tile(i, ROWS)
            scores = nt(q_ref[at_rows, cols], k_ref[:, kv]) * scale
            key_at = key_at_ref[:1, :]
            allowed = (key_at <= at_ref[at_rows, :1]) & (key_at >= start_ref[at_rows, :1])
            scores = jnp.where(allowed, scores, NEGATIVE)
            top = jnp.max(scores, axis=1, keepdims=True)
            raised = jnp.exp(scores - top)
            total = jnp.sum(raised, axis=1, keepdims=True)
            result = nn((raised / total).astype(BF16), v_ref[:, kv])
            log_ref[n, at_rows, :] = column(top + jnp.log(total))
            attended_ref[at_rows, cols] = result
            gated_ref[0, at_rows, cols] = (result * sig_ref[at_rows, n : n + 1]).astype(BF16)

        head_copy(n).start()
        if n == 0:
            tops[2].wait_recv()
            early_start(2)
        if n == 2:
            early_start(3)

    for i in (1, 0):
        acc[slot(i), :] = nn(gated_ref[0, slot(i), :], wo[0])
    for n in range(heads):
        head_copy(n).wait_recv()
    fold = copy_to(fold_src, fold_dst, s_send.at[2], s_recv.at[2], place.core_peer)
    fold_src[...] = (acc[slot(1), :] + nn(gated_ref[1, slot(1), :], wo[1])).astype(BF16)
    fold.start()
    acc[slot(0), :] += nn(gated_ref[1, slot(0), :], wo[1])
    fold.wait_recv()
    resid = tok_ref[...].astype(F32) + acc[slot(0), :] + fold_dst[...].astype(F32)
    resid_ref[...] = resid
    ss_send[1] = column(jnp.sum(resid * resid, axis=1, keepdims=True))
    squares(1).start()
    for i in range(4):
        early(i).wait_recv()
        early_ref[slot(i), :] = (
            early_send[slot(i), :].astype(F32) + early_came[slot(i), :].astype(F32)
        ).astype(BF16)
    squares(1).wait()
    inv_two = lax.rsqrt((ss_send[1] + ss_came[1]) / (2 * width) + EPS)
    inv_two_ref[...] = inv_two
    h_ref[...] = (resid_ref[...] * inv_two[:, :1] * second_ref[...]).astype(BF16)

    normed[2].wait_recv()
    for copy in (*tops, *normed, kv_copy, q_copy, fold):
        copy.wait_send()
    for i in range(4):
        early(i).wait_send()
    for n in range(heads):
        head_copy(n).wait_send()


def front(
    tok, top, norm_gain, ffn_gain, q_gain, k_gain, cos, sin, at, start, key_at, w_gates,
    wq, wk, wv, wo, wd,
):
    count = lax.axis_size("group")
    rows, width = tok.shape
    tokens = 2 * rows
    hd = 128
    heads, kv_heads = wq.shape[1] // 2 // hd, wk.shape[1] // 2 // hd
    qw, kw = heads * hd, kv_heads * hd
    early = EARLY * WIDE
    local = pl.BlockSpec(memory_space=pltpu.VMEM)
    anywhere = pl.BlockSpec(memory_space=pl.ANY)
    dma = pltpu.SemaphoreType.DMA
    struct = jax.ShapeDtypeStruct
    return pl.pallas_call(
        functools.partial(front_kernel, count, heads, kv_heads),
        out_shape=(
            struct((rows, width), BF16),
            struct((rows, width), F32),
            struct((rows, 128), F32),
            struct((rows, width), F32),
            struct((rows, 128), F32),
            struct((4 * rows, width), BF16),
            struct((4 * rows, width), BF16),
            struct((4 * rows, early), BF16),
            struct((tokens, qw + 2 * kw), F32),
            struct((tokens, 128), F32),
            struct((tokens, qw), BF16),
            struct((tokens, kw), BF16),
            struct((tokens, kw), BF16),
            struct((heads, tokens, 128), F32),
            struct((tokens, qw), F32),
            struct((2, tokens, qw), BF16),
        ),
        in_specs=[local] * 12 + [anywhere] * 5,
        out_specs=(local,) * 16,
        scratch_shapes=[
            pltpu.VMEM((2, width, qw), BF16),
            pltpu.VMEM((2, width, kw), BF16),
            pltpu.VMEM((2, width, kw), BF16),
            pltpu.VMEM((2, qw, width), BF16),
            pltpu.VMEM((early, width), BF16),
            pltpu.VMEM((tokens, 2 * kw), BF16),
            pltpu.VMEM((tokens, 2 * kw), BF16),
            pltpu.VMEM((tokens, qw + 128), BF16),
            pltpu.VMEM((tokens, qw + 128), BF16),
            pltpu.VMEM((tokens, 128), F32),
            pltpu.VMEM((4 * rows, early), BF16),
            pltpu.VMEM((4 * rows, early), BF16),
            pltpu.VMEM((2, rows, 128), F32),
            pltpu.VMEM((2, rows, 128), F32),
            pltpu.VMEM((rows, width), BF16),
            pltpu.VMEM((rows, width), BF16),
            pltpu.VMEM((tokens, width), F32),
            dma((2, 5)), dma((3,)), dma((3,)), dma((3,)), dma((3,)), dma((2,)), dma((2,)),
            dma((4,)), dma((4,)), dma((heads,)), dma((heads,)), dma((3,)), dma((3,)),
        ],
        compiler_params=pltpu.CompilerParams(
            collective_id=3, has_side_effects=True, vmem_limit_bytes=60 << 20
        ),
        cost_estimate=pl.CostEstimate(
            flops=6 * tokens * width * (qw + kw) * 4, bytes_accessed=40 << 20,
            transcendentals=heads * tokens * tokens,
        ),
    )(
        tok, top, norm_gain, ffn_gain, q_gain, k_gain, cos, sin, at, start, key_at, w_gates,
        wq, wk, wv, wo, wd,
    )


MISC = 88


def back_kernel(
    count, own_ref, turned_ref, w_main_ref, gates_ref, w_gates_ref, gated_ref, branch_ref,
    hat_ref, scale_ref, misc_ref,
    grads_ref, back_ref, inner_ref, sums_ref,
    came, across, total, landed, misc, misc_came, misc_landed, misc_home, acc, fold_src, fold_dst,
    inner_src, inner_dst,
    x_send, x_recv, y_send, y_recv, small_send, small_recv, *chain_sems,
):
    place = Place(count)
    side = place.side
    tokens, main = own_ref.shape
    rows = tokens // 2
    cols = 256
    parts = main // cols
    width = turned_ref.shape[0]
    high = gated_ref.shape[0]
    pieces = total.shape[0]
    place.meet()

    def cut(j):
        return pl.ds(j * cols, cols) if isinstance(j, int) else tile(j, cols)

    def over_x(j):
        return copy_to(
            own_ref.at[:, cut(j)], came.at[j], x_send.at[j], x_recv.at[j], place.x_peer
        )

    def over_y(j, mine):
        src = own_ref.at[:, cut(j)] if mine else came.at[j]
        return copy_to(src, across.at[j], y_send.at[j], y_recv.at[j], place.y_peer)

    for j in range(parts):
        over_x(j).start()

    @pl.when(side == 1)
    def _():
        for j in range(parts):
            over_y(j, True).start()

    def add(c, k, which):
        total[c] = (total[c].astype(F32) + landed[which, c].astype(F32)).astype(BF16)

    chain = Chain(
        place, pieces, 1,
        lambda c, k: total.at[c],
        lambda c, k, which: landed.at[which, c],
        lambda c, k, of: grads_ref.at[of * pieces + c],
        add, chain_sems[:9],
    )

    def add_misc(c, k, which):
        misc[...] += misc_landed[which]

    small = Chain(
        place, 1, 1,
        lambda c, k: misc,
        lambda c, k, which: misc_landed.at[which],
        lambda c, k, of: misc_home,
        add_misc, chain_sems[9:], share=False,
    )

    misc[...] = misc_ref[...]
    acc[...] = nt(gates_ref[...], w_gates_ref[...])

    @pl.loop(0, parts)
    def _(t):
        total[t] = nn(gated_ref[...], branch_ref[:, cut(t)]).astype(BF16)
        chain.step(t)
        over_x(t).wait_recv()

        @pl.when(side == 0)
        def _():
            over_y(t, False).start()

        acc[...] += nt(own_ref[:, cut(t)], w_main_ref[:, cut(t)])
        acc[...] += nt(came[t], w_main_ref[:, cut(parts + t)])

    fold = copy_to(fold_src, fold_dst, small_send.at[0], small_recv.at[0], place.core_peer)
    fold_src[...] = acc[rows:, :].astype(BF16)
    fold.start()

    def inner_copy():
        return copy_to(inner_src, inner_dst, small_send.at[1], small_recv.at[1], place.x_peer)

    def misc_copy(n, peer):
        return copy_to(
            misc, misc_came.at[n], small_send.at[2 + n], small_recv.at[2 + n], peer
        )

    row_at = lax.broadcasted_iota(jnp.int32, (MISC, 128), 0)

    def block(j, i):
        if i == 0:
            over_y(j, True).wait_recv()
        at_rows = pl.ds(i * high, high)
        first = jnp.where(side == 0, own_ref[:, cut(j)], came[j])
        total[parts + 2 * j + i] = (
            nn(turned_ref[at_rows, pl.ds(0, tokens)], first)
            + nn(turned_ref[at_rows, pl.ds(tokens, tokens)], across[j])
        ).astype(BF16)

    for n in range(2 * parts):
        block(n // 2, n % 2)
        chain.step(parts + n)
        if n == 0:
            fold.wait_recv()
            grad = acc[:rows, :] + fold_dst[...].astype(F32)
            back_ref[...] = grad
            found = grad * hat_ref[...]
            inner = jnp.sum(found * scale_ref[...], axis=1, keepdims=True)
            inner_src[...] = jnp.broadcast_to(inner, (rows, 128))
            inner_copy().start()
            gain = jnp.sum(found, axis=0, keepdims=True)
            for i in range(width // 128):
                misc[i : i + 1, :] = gain[:, i * 128 : (i + 1) * 128]
            misc_copy(0, place.core_peer).start()
        if n == 1:
            misc_copy(0, place.core_peer).wait()
            both = (row_at < 16) | (row_at >= 80)
            misc[...] += jnp.where(both, misc_came[0], 0.0)
            misc_copy(1, place.x_peer).start()
        if n == 2:
            misc_copy(1, place.x_peer).wait()
            misc[...] += jnp.where(row_at >= 80, misc_came[1], 0.0)
            misc_copy(2, place.y_peer).start()
        if n == 3:
            misc_copy(2, place.y_peer).wait()
            misc[...] += misc_came[2]
            inner_copy().wait()
            inner_ref[...] = inner_src[...] + inner_dst[...]
        if n > 3:
            small.step(n - 4)

    @pl.loop(3 * parts, chain.steps())
    def _(t):
        chain.step(t)

        @pl.when(t - parts - 4 < small.steps())
        def _():
            small.step(t - parts - 4)

    @pl.loop(chain.steps() - parts - 4, small.steps())
    def _(t):
        small.step(t)

    small.drain()
    sums_ref[...] = misc_home[...]
    chain.drain()
    fold.wait_send()
    for j in range(parts):
        over_x(j).wait_send()
        over_y(j, True).wait_send()


def back(own, turned, w_main, gates, w_gates, gated, branch, hat, scale, misc):
    count = lax.axis_size("group")
    tokens, main = own.shape
    rows = tokens // 2
    width = turned.shape[0]
    high = gated.shape[0]
    cols = 256
    parts = main // cols
    pieces = 3 * parts
    anywhere = pl.BlockSpec(memory_space=pl.ANY)
    local = pl.BlockSpec(memory_space=pltpu.VMEM)
    dma = pltpu.SemaphoreType.DMA
    return pl.pallas_call(
        functools.partial(back_kernel, count),
        out_shape=(
            jax.ShapeDtypeStruct((2 * pieces, high, cols), BF16),
            jax.ShapeDtypeStruct((rows, width), F32),
            jax.ShapeDtypeStruct((rows, 128), F32),
            jax.ShapeDtypeStruct((MISC, 128), F32),
        ),
        in_specs=[local] * 10,
        out_specs=(anywhere, local, local, local),
        scratch_shapes=[
            pltpu.VMEM((parts, tokens, cols), BF16),
            pltpu.VMEM((parts, tokens, cols), BF16),
            pltpu.VMEM((pieces, high, cols), BF16),
            pltpu.VMEM((2, pieces, high, cols), BF16),
            pltpu.VMEM((MISC, 128), F32),
            pltpu.VMEM((3, MISC, 128), F32),
            pltpu.VMEM((2, MISC, 128), F32),
            pltpu.VMEM((MISC, 128), F32),
            pltpu.VMEM((tokens, width), F32),
            pltpu.VMEM((rows, width), BF16),
            pltpu.VMEM((rows, width), BF16),
            pltpu.VMEM((rows, 128), F32),
            pltpu.VMEM((rows, 128), F32),
            dma((parts,)), dma((parts,)), dma((parts,)), dma((parts,)), dma((5,)), dma((5,)),
            *chain_semaphores(pieces), *chain_semaphores(1),
        ],
        compiler_params=pltpu.CompilerParams(
            collective_id=2, has_side_effects=True, vmem_limit_bytes=56 << 20
        ),
        cost_estimate=pl.CostEstimate(
            flops=2 * tokens * width * main * 6, bytes_accessed=100 << 20, transcendentals=0
        ),
    )(own, turned, w_main, gates, w_gates, gated, branch, hat, scale, misc)


def masked_scores(query, keys, segment, place, scale):
    scores = jnp.einsum("qkgd,skd->kgqs", query, keys, preferred_element_type=F32) * scale
    allowed = (segment[:, None] == segment[None, :]) & (place[None, :] <= place[:, None])
    return jnp.where(allowed, scores, NEGATIVE)


def body(
    tokens, lengths, norm_gain, w_query, w_key, w_value, w_head_gate, query_gain, key_gain,
    w_out, ffn_gain, w_gate, w_up, w_down, grad_out,
):
    row_count = lax.axis_size("row")
    rows, d_loc = tokens.shape
    group_tok = 2 * rows
    width = d_loc * row_count
    head_dim = query_gain.shape[0]
    q_half = w_query.shape[1] // 2
    kv_half = w_key.shape[1] // 2
    gate_half = w_head_gate.shape[1] // 2
    heads = q_half // head_dim
    kv_heads = kv_half // head_dim
    share = heads // kv_heads
    main = q_half + 2 * kv_half
    scale = head_dim ** (-0.5)
    row_at = lax.axis_index("row")
    col_at = lax.axis_index("col")
    side = lax.axis_index("group") % 2

    steps = jnp.arange(rows, dtype=jnp.int32)
    index = jnp.concatenate([col_at * rows + steps, (1 - col_at) * rows + steps])
    segment, place = places(lengths, index)
    cosines, sines = rope_tables(place, head_dim)
    signed = jnp.concatenate([-sines[:, : head_dim // 2], sines[:, head_dim // 2 :]], axis=1)
    cos_heads = cosines[:, None, :]
    sin_heads = sines[:, None, :]
    w_gates = jnp.pad(
        jnp.concatenate(halves(w_head_gate, 1, row_at), axis=1),
        ((0, 0), (0, 128 - 2 * gate_half)),
    )
    (
        normed_two, resid, inverse_two, hat, inverse_one, permuted_pair, grad_all, early_grad,
        raw, gate_sigmoid, query, keys, values, logsum, attended, gated_both,
    ) = front(
        tokens, grad_out, norm_gain[None], ffn_gain[None], query_gain[None], key_gain[None],
        cosines, signed,
        jnp.broadcast_to(index[:, None], (group_tok, 128)),
        jnp.broadcast_to((index - place)[:, None], (group_tok, 128)),
        jnp.broadcast_to(index[None], (8, group_tok)),
        w_gates, w_query, w_key, w_value, w_out, w_down,
    )
    inverse_one, inverse_two = inverse_one[:, 0], inverse_two[:, 0]
    gate_sigmoid = gate_sigmoid[:, :heads]
    permuted = permuted_pair[:group_tok]
    turned = permuted_pair.T
    raw_query = raw[:, :q_half].reshape(group_tok, heads, head_dim)
    raw_key = raw[:, q_half : q_half + kv_half].reshape(group_tok, kv_heads, head_dim)
    query_inverse = lax.rsqrt(jnp.mean(raw_query * raw_query, axis=-1, keepdims=True) + EPS)
    key_inverse = lax.rsqrt(jnp.mean(raw_key * raw_key, axis=-1, keepdims=True) + EPS)
    query = query.reshape(group_tok, kv_heads, share, head_dim)
    keys = keys.reshape(group_tok, kv_heads, head_dim)
    values = values.reshape(group_tok, kv_heads, head_dim)
    attended = attended.reshape(group_tok, heads, head_dim)
    gated, gated_came = gated_both[0], gated_both[1]
    first_side = side == 0
    gated_pair = jnp.concatenate(
        [
            jnp.where(first_side, gated, gated_came),
            swap_groups(jnp.where(first_side, gated_came, gated)),
        ]
    ).T
    splits = [halves(w, 1, row_at) for w in (w_query, w_key, w_value)]
    w_main = jnp.concatenate([own for own, _ in splits] + [other for _, other in splits], axis=1)
    w_back = jnp.concatenate(halves(w_out, 0, row_at))

    def sum_cores(values):
        return values[:rows] + swap(values[rows:].astype(BF16), "col").astype(F32)

    pair_sum, down_sum, _, _, branch, branch_out, d_normed_two = ffn(
        normed_two, grad_all, early_grad, w_gate, w_up, w_down
    )
    output = (resid + branch + swap_groups(branch_out).astype(F32)).astype(BF16)

    d_top = grad_out.astype(F32)
    ffn_gain_part = jnp.sum(d_normed_two * resid * inverse_two[:, None], axis=0)
    scaled_two = d_normed_two * ffn_gain
    inner_two = jnp.sum(scaled_two * resid, axis=1)
    inner_two = inner_two + swap(inner_two, "row")
    d_resid = (
        d_top
        + inverse_two[:, None] * scaled_two
        - resid * (inverse_two**3 * inner_two / width)[:, None]
    )
    d_branch = d_resid.astype(BF16)
    branch_all = jnp.concatenate([d_branch, swap(d_branch, "col")])
    branch_across = swap_groups(d_branch)
    branch_pair = jnp.concatenate([branch_all, branch_across, swap(branch_across, "col")])
    d_gated_part = nt(branch_all, w_back)
    d_gated = d_gated_part[:, :q_half] + swap(
        d_gated_part[:, q_half:].astype(BF16), "row"
    ).astype(F32)
    d_gated = d_gated.reshape(group_tok, heads, head_dim)
    d_attended = (d_gated * gate_sigmoid[:, :, None]).astype(BF16)
    d_logit = jnp.sum(d_gated * attended, axis=-1) * gate_sigmoid * (1.0 - gate_sigmoid)
    d_attended = d_attended.reshape(group_tok, kv_heads, share, head_dim)

    scores = masked_scores(query, keys, segment, place, scale)
    probs = jnp.exp(scores - logsum[:, :, 0].reshape(kv_heads, share, group_tok, 1))
    probs_low = probs.astype(BF16)
    d_probs = jnp.einsum("qkgd,skd->kgqs", d_attended, values, preferred_element_type=F32)
    d_scores = (probs * (d_probs - jnp.sum(d_probs * probs, axis=-1, keepdims=True))).astype(BF16)
    d_query = jnp.einsum("kgqs,skd->qkgd", d_scores, keys, preferred_element_type=F32) * scale
    d_keys = jnp.einsum("kgqs,qkgd->skd", d_scores, query, preferred_element_type=F32) * scale
    d_values = jnp.einsum("kgqs,qkgd->skd", probs_low, d_attended, preferred_element_type=F32)
    d_query = d_query.reshape(group_tok, heads, head_dim)
    d_raw_query, query_gain_part = head_norm_back(
        unrotate(d_query, cos_heads, sin_heads), raw_query, query_inverse, query_gain
    )
    d_raw_key, key_gain_part = head_norm_back(
        unrotate(d_keys, cos_heads, sin_heads), raw_key, key_inverse, key_gain
    )
    d_main = jnp.concatenate(
        [
            d_raw_query.reshape(group_tok, q_half),
            d_raw_key.reshape(group_tok, kv_half),
            d_values.reshape(group_tok, kv_half),
        ],
        axis=1,
    ).astype(BF16)
    d_gates = d_logit.astype(BF16)
    d_gates = jnp.concatenate([d_gates, swap(d_gates, "row")], axis=1)
    gates_part = lax.dot_general(
        d_gates, permuted, (((0,), (0,)), ((), ())), preferred_element_type=F32
    )
    misc = jnp.concatenate(
        [
            jnp.zeros((8, 128), F32),
            ffn_gain_part.reshape(8, 128),
            gates_part.reshape(64, 128),
            query_gain_part[None],
            key_gain_part[None],
            jnp.zeros((6, 128), F32),
        ]
    )
    grads, d_normed_one, inner_one, sums = back(
        d_main, turned, w_main, jnp.pad(d_gates, ((0, 0), (0, 128 - 2 * gate_half))), w_gates,
        gated_pair, branch_pair, hat, norm_gain[None], misc,
    )
    input_grad = d_resid + inverse_one[:, None] * (
        d_normed_one * norm_gain - hat * (inner_one[:, :1] / width)
    )
    grad_norm_gain = sums[:8].reshape(d_loc)
    grad_ffn_gain = sums[8:16].reshape(d_loc)
    grad_gates = sums[16:80].reshape(2 * gate_half, d_loc)
    grad_head_gate = ordered(grad_gates[:gate_half], grad_gates[gate_half:], 0, row_at).T
    grads = grads.reshape(2, -1, q_half, 256)
    count = main // 256
    out_sum = grads[:, :count].transpose(0, 2, 1, 3).reshape(2 * q_half, d_loc)
    first_sum = (
        grads[:, count:]
        .reshape(2, count, 2, q_half, 256)
        .transpose(2, 3, 0, 1, 4)
        .reshape(d_loc, 2 * main)
    )

    def piece(start, size):
        own = first_sum[:, start : start + size]
        other = first_sum[:, main + start : main + start + size]
        return ordered(own, other, 1, row_at).astype(F32)

    grad_out_full = ordered(*jnp.split(out_sum, 2, axis=0), 0, row_at).astype(F32)
    return (
        output,
        input_grad,
        grad_norm_gain,
        piece(0, q_half),
        piece(q_half, kv_half),
        piece(q_half + kv_half, kv_half),
        grad_head_gate,
        sums[80],
        sums[81],
        grad_out_full,
        grad_ffn_gain,
        pair_sum[0].astype(F32),
        pair_sum[1].astype(F32),
        down_sum.astype(F32),
    )


def solution(mesh):
    shards = P(("group", "col"), "row")
    in_specs = (
        shards,
        P("group"),
        P("row"),
        P("row", "col"),
        P("row", "col"),
        P("row", "col"),
        P("row", "col"),
        P(),
        P(),
        P("col", "row"),
        P("row"),
        P("row", "col"),
        P("row", "col"),
        P("col", "row"),
        shards,
    )
    out_specs = (
        shards,
        shards,
        P("row"),
        P("row", "col"),
        P("row", "col"),
        P("row", "col"),
        P("row", "col"),
        P(),
        P(),
        P("col", "row"),
        P("row"),
        P("row", "col"),
        P("row", "col"),
        P("col", "row"),
    )
    return jax.shard_map(body, mesh=mesh, in_specs=in_specs, out_specs=out_specs, check_vma=False)
```

```python
import functools

import jax
import jax.numpy as jnp
from jax import lax
from jax.experimental import pallas as pl
from jax.experimental.pallas import tpu as pltpu
from jax.sharding import PartitionSpec as P

EPS = 1e-06
THETA = 1000000.0
NEGATIVE = -1e30
MESH = pl.DeviceIdType.MESH
F32 = jnp.float32
BF16 = jnp.bfloat16


def swap_groups(values):
    count = lax.axis_size("group")
    return lax.ppermute(values, "group", [(i, i ^ 1) for i in range(count)])


def halves(values, axis, at):
    low, high = jnp.split(values, 2, axis=axis)
    first = at == 0
    return jnp.where(first, low, high), jnp.where(first, high, low)


def ordered(own, other, axis, at):
    first = at == 0
    return jnp.concatenate(
        [jnp.where(first, own, other), jnp.where(first, other, own)], axis=axis
    )


def places(lengths_group, index):
    ends = jnp.cumsum(lengths_group)
    passed = (index[:, None] >= ends[None, :]).astype(jnp.int32)
    segment = jnp.sum(passed, axis=1)
    place = index - jnp.sum(passed * lengths_group[None, :], axis=1)
    return (segment, place)


def rope_tables(place, width):
    half = width // 2
    freq = THETA ** (-(jnp.arange(half, dtype=F32) * 2.0 / width))
    angle = place.astype(F32)[:, None] * freq[None, :]
    cosines = jnp.concatenate([jnp.cos(angle), jnp.cos(angle)], axis=1)
    sines = jnp.concatenate([jnp.sin(angle), jnp.sin(angle)], axis=1)
    return (cosines, sines)


TILE = 256
HOP = 1
WIDE = 128
EARLY = 6
AHEAD = 3


def nt(a, b):
    return lax.dot_general(a, b, (((1,), (1,)), ((), ())), preferred_element_type=F32)


def nn(a, b):
    return jnp.dot(a, b, preferred_element_type=F32)


def copy_to(src, dst, send_sem, recv_sem, peer):
    return pltpu.make_async_remote_copy(
        src_ref=src, dst_ref=dst, send_sem=send_sem, recv_sem=recv_sem,
        device_id=peer, device_id_type=MESH,
    )


def tile(i, size=TILE):
    return pl.ds(pl.multiple_of(i * size, size), size)


class Place:
    def __init__(self, count):
        group = lax.axis_index("group")
        self.line = count // 2
        self.root = (self.line - 1) // 2
        self.deep = max(self.root, self.line - 1 - self.root)
        self.at = group // 2
        self.side = group % 2
        self.x_peer = {"row": 1 - lax.axis_index("row")}
        self.core_peer = {"col": 1 - lax.axis_index("col")}
        self.y_peer = {"group": group + 1 - 2 * self.side}
        self.above = {"group": jnp.minimum(group + 2, count - 1)}
        self.below = {"group": jnp.maximum(group - 2, 0)}
        self.has_above = self.at < self.line - 1
        self.has_below = self.at > 0

    def meet(self):
        barrier = pltpu.get_barrier_semaphore()

        def greet(peer):
            pl.semaphore_signal(barrier, inc=1, device_id=peer, device_id_type=MESH)

        for peer in (self.x_peer, self.core_peer, self.y_peer):
            greet(peer)
        pl.when(self.has_above)(lambda: greet(self.above))
        pl.when(self.has_below)(lambda: greet(self.below))
        met = 3 + self.has_above.astype(jnp.int32) + self.has_below.astype(jnp.int32)
        pl.semaphore_wait(barrier, met)


class Chain:
    def __init__(self, place, chunks, kinds, total, came, home, add, sems, share=True):
        self.place, self.chunks, self.kinds = place, chunks, kinds
        self.total, self.came, self.home, self.add = total, came, home, add
        self.sems, self.share = sems, share

    def part_copy(self, c, k, upward):
        sent, low, high = self.sems[:3]
        p = self.kinds * c + k
        peer, which, arrived = (
            (self.place.above, 0, low) if upward else (self.place.below, 1, high)
        )
        return copy_to(
            self.total(c, k), self.came(c, k, which), sent.at[p], arrived.at[p], peer
        )

    def final_copy(self, c, k, upward, first):
        up, down, arrived = self.sems[3:6]
        p = self.kinds * c + k
        src = self.total(c, k) if first else self.home(c, k, self.place.side)
        peer, sent = (self.place.above, up) if upward else (self.place.below, down)
        return copy_to(src, self.home(c, k, self.place.side), sent.at[p], arrived.at[p], peer)

    def keep_copy(self, c, k):
        return pltpu.make_async_copy(
            self.total(c, k), self.home(c, k, self.place.side),
            self.sems[6].at[self.kinds * c + k],
        )

    def share_copy(self, c, k, first, of=None):
        p = self.kinds * c + k
        of = self.place.side if of is None else of
        src = self.total(c, k) if first else self.home(c, k, self.place.side)
        return copy_to(
            src, self.home(c, k, of), self.sems[7].at[p], self.sems[8].at[p], self.place.y_peer
        )

    def step(self, u, hop=1):
        at, line, root, deep = self.place.at, self.place.line, self.place.root, self.place.deep
        behind = jnp.where(at < root, at, jnp.where(at > root, line - 1 - at, deep))
        self.inward(u - hop * behind)
        self.outward(u - hop * (deep + jnp.abs(at - root)))

    def kinds_of(self, p):
        live = (p >= 0) & (p < self.kinds * self.chunks)
        if self.kinds == 1:
            return [(live, p, 0)]
        p = jnp.maximum(p, 0)
        return [
            (live & (lax.rem(p, self.kinds) == k), lax.div(p, self.kinds), k)
            for k in range(self.kinds)
        ]

    def inward(self, piece):
        at, line, root = self.place.at, self.place.line, self.place.root
        for live, c, k in self.kinds_of(piece):

            @pl.when(live & (at < root))
            def _():
                @pl.when(self.place.has_below)
                def _():
                    self.part_copy(c, k, True).wait_recv()
                    self.add(c, k, 0)

                self.part_copy(c, k, True).start()

            @pl.when(live & (at > root))
            def _():
                @pl.when(self.place.has_above)
                def _():
                    self.part_copy(c, k, False).wait_recv()
                    self.add(c, k, 1)

                self.part_copy(c, k, False).start()

            @pl.when(live & (at == root))
            def _():
                if root > 0:
                    self.part_copy(c, k, True).wait_recv()
                    self.add(c, k, 0)
                if root < line - 1:
                    self.part_copy(c, k, False).wait_recv()
                    self.add(c, k, 1)
                if root > 0:
                    self.final_copy(c, k, False, True).start()
                if root < line - 1:
                    self.final_copy(c, k, True, True).start()
                if self.share:
                    self.share_copy(c, k, True).start()
                self.keep_copy(c, k).start()

    def outward(self, piece):
        at, root = self.place.at, self.place.root
        for live, c, k in self.kinds_of(piece):

            @pl.when(live & (at != root))
            def _():
                self.final_copy(c, k, True, False).wait_recv()

                @pl.when((at > root) & self.place.has_above)
                def _():
                    self.final_copy(c, k, True, False).start()

                @pl.when((at < root) & self.place.has_below)
                def _():
                    self.final_copy(c, k, False, False).start()

                if self.share:
                    self.share_copy(c, k, False).start()

    def steps(self, hop=1):
        return self.kinds * self.chunks + 2 * hop * self.place.deep

    def drain(self):
        at, line, root = self.place.at, self.place.line, self.place.root

        @pl.loop(0, self.chunks)
        def _(c):
            for k in range(self.kinds):
                if self.share:
                    self.share_copy(c, k, False, 1 - self.place.side).wait_recv()
                    self.share_copy(c, k, False).wait_send()

                @pl.when(at == root)
                def _():
                    self.keep_copy(c, k).wait()
                    if root > 0:
                        self.final_copy(c, k, False, True).wait_send()
                    if root < line - 1:
                        self.final_copy(c, k, True, True).wait_send()

                @pl.when(at < root)
                def _():
                    self.part_copy(c, k, True).wait_send()

                    @pl.when(self.place.has_below)
                    def _():
                        self.final_copy(c, k, False, False).wait_send()

                @pl.when(at > root)
                def _():
                    self.part_copy(c, k, False).wait_send()

                    @pl.when(self.place.has_above)
                    def _():
                        self.final_copy(c, k, True, False).wait_send()


def chain_semaphores(pieces):
    return [pltpu.SemaphoreType.DMA((pieces,)) for _ in range(9)]


def ffn_kernel(
    count, chunks, h_ref, top_ref, early_ref, gate_ref, up_ref, down_ref,
    pair_grads_ref, down_grads_ref, pair_came_ref, down_came_ref, branch_ref, branch_out_ref,
    back_ref,
    h_all, h_turned, sent, came, top_sent, top_came, grad_part, w_pair, w_down, acc_branch, acc_back, parts, inner_turned,
    pair_total, down_total, pair_stage, down_stage, reduce_recv,
    gather_send, gather_recv, x_send, x_recv, top_send, top_recv, load_sem, weight_sem, fold_send, fold_recv,
    *chain_sems,
):
    place = Place(count)
    rows, width = h_ref.shape
    tokens = h_all.shape[0]
    tiles = tokens // TILE
    wide = w_down.shape[0] // chunks
    side = place.side

    def weight_copies(j):
        cols = tile(side * chunks + j, wide)
        return (
            pltpu.make_async_copy(
                gate_ref.at[:, cols], w_pair.at[j, :, pl.ds(0, wide)], weight_sem.at[0, j]
            ),
            pltpu.make_async_copy(
                up_ref.at[:, cols], w_pair.at[j, :, pl.ds(wide, wide)], weight_sem.at[1, j]
            ),
            pltpu.make_async_copy(
                down_ref.at[cols, :], w_down.at[tile(j, wide), :], weight_sem.at[2, j]
            ),
        )

    @pl.loop(0, chunks)
    def _(j):
        for copy in weight_copies(j):
            copy.start()

    place.meet()

    def slot(i):
        return pl.ds(i * rows, rows)

    to_y = copy_to(h_ref, h_all.at[slot(2)], gather_send.at[0], gather_recv.at[0], place.y_peer)
    to_core = copy_to(
        h_ref, h_all.at[slot(1)], gather_send.at[1], gather_recv.at[1], place.core_peer
    )
    forward = copy_to(
        h_all.at[slot(2)], h_all.at[slot(3)], gather_send.at[2], gather_recv.at[2],
        place.core_peer,
    )
    to_y.start()
    to_core.start()

    def top_exchange(j):
        n = j - EARLY
        return copy_to(
            top_sent.at[n], top_came.at[n], top_send.at[n], top_recv.at[n], place.x_peer
        )

    def top_project(j):
        @pl.loop(0, tiles)
        def _(i):
            top_sent[j - EARLY, tile(i), :] = nt(
                top_ref[tile(i), :], w_down[tile(j, wide), :]
            ).astype(BF16)

        top_exchange(j).start()

    @pl.loop(0, chunks)
    def _(j):
        weight_copies(j)[2].wait()

    @pl.loop(EARLY, min(EARLY + AHEAD, chunks))
    def _(j):
        top_project(j)

    h_all[slot(0), :] = h_ref[...]
    acc_branch[...] = jnp.zeros_like(acc_branch)
    acc_back[...] = jnp.zeros_like(acc_back)
    to_y.wait_recv()
    forward.start()
    to_core.wait_recv()
    forward.wait_recv()

    def exchange(j):
        return copy_to(
            sent.at[lax.rem(j, 3)], came.at[j], x_send.at[j], x_recv.at[j], place.x_peer
        )

    def project(j):
        for copy in weight_copies(j)[:2]:
            copy.wait()

        @pl.loop(0, tiles)
        def _(i):
            sent[lax.rem(j, 3), tile(i), :] = nn(h_all[tile(i), :], w_pair[j]).astype(BF16)

        exchange(j).start()

    def work(j):
        exchange(j).wait_recv()

        @pl.when(j < EARLY)
        def _():
            grad_part[...] = early_ref[:, tile(j, wide)].astype(F32)

        @pl.when(j >= EARLY)
        def _():
            top_exchange(j).wait_recv()
            grad_part[...] = top_sent[j - EARLY].astype(F32) + top_came[j - EARLY].astype(F32)

        @pl.loop(0, tiles)
        def _(i):
            at_rows = tile(i)
            pair = sent[lax.rem(j, 3), at_rows, :].astype(F32) + came[j, at_rows, :].astype(F32)
            gate, up = pair[:, :wide], pair[:, wide:]
            grad = grad_part[at_rows, :]
            sig = 1.0 / (1.0 + jnp.exp(-gate))
            silu = gate * sig
            parts[at_rows, pl.ds(0, wide)] = (
                grad * up * (sig * (1.0 + gate * (1.0 - sig)))
            ).astype(BF16)
            parts[at_rows, pl.ds(wide, wide)] = (grad * silu).astype(BF16)
            inner = (silu * up).astype(BF16)
            inner_turned[:, at_rows] = inner.T
            acc_branch[at_rows, :] += nn(inner, w_down[tile(j, wide), :])
            acc_back[at_rows, :] += nt(parts[at_rows, :], w_pair[j])

    def gradients(j):
        @pl.loop(0, width // TILE)
        def _(i):
            pair = nn(h_turned[tile(i), :], parts[...])
            pair_total[j, 0, tile(i), :] = pair[:, :wide].astype(BF16)
            pair_total[j, 1, tile(i), :] = pair[:, wide:].astype(BF16)
            down_total[j, :, tile(i)] = nn(inner_turned[...], top_ref[:, tile(i)]).astype(BF16)

    def total(c, k):
        return down_total.at[c] if k == 2 else pair_total.at[c, k]

    def landed(c, k, which):
        return down_came_ref.at[which, c] if k == 2 else pair_came_ref.at[which, c, k]

    def home(c, k, of):
        at_cols = tile(of * chunks + c, wide)
        return down_grads_ref.at[at_cols, :] if k == 2 else pair_grads_ref.at[k, :, at_cols]

    def add(c, k, which):
        stage = (down_stage if k == 2 else pair_stage).at[which]
        copy = pltpu.make_async_copy(landed(c, k, which), stage, load_sem.at[which])
        copy.start()
        copy.wait()
        into = total(c, k)

        @pl.loop(0, into.shape[0] // wide)
        def _(i):
            at_rows = tile(i, wide)
            into[at_rows, :] = (
                into[at_rows, :].astype(F32) + stage[at_rows, :].astype(F32)
            ).astype(BF16)

    chain = Chain(place, chunks, 3, total, landed, home, add, chain_sems)

    for j in range(min(2, chunks)):
        project(j)

    @pl.loop(0, tiles)
    def _(i):
        h_turned[:, tile(i)] = h_all[tile(i), :].T

    @pl.loop(0, chunks)
    def _(t):
        work(t)
        chain.step(3 * t - 1, HOP)
        gradients(t)
        chain.step(3 * t, HOP)

        @pl.when(t + 2 < chunks)
        def _():
            @pl.when(t >= 1)
            def _():
                exchange(t - 1).wait_send()

            project(t + 2)

        @pl.when(EARLY + AHEAD + t < chunks)
        def _():
            top_project(EARLY + AHEAD + t)

        chain.step(3 * t + 1, HOP)

    chain.step(3 * chunks - 1, HOP)

    def fold_source(n, i):
        if i == 2:
            return w_down.at[slot(0), :]
        return h_all.at[slot(2 * n + i), :]

    def fold(n, i):
        return copy_to(
            fold_source(n, i), reduce_recv.at[n, i], fold_send.at[n, i], fold_recv.at[n, i],
            place.y_peer if i == 2 else place.core_peer,
        )

    to_y.wait_send()
    to_core.wait_send()
    forward.wait_send()
    for n, acc in enumerate((acc_back, acc_branch)):
        for i in (1, 0):
            fold_source(n, i)[...] = acc[slot(2 * i + 1), :].astype(BF16)
            fold(n, i).start()
    fold(0, 1).wait_recv()
    fold_source(0, 2)[...] = (acc_back[slot(2), :] + reduce_recv[0, 1].astype(F32)).astype(BF16)
    fold(0, 2).start()
    chain.step(3 * chunks, HOP)
    fold(1, 0).wait_recv()
    fold(1, 1).wait_recv()
    branch_ref[...] = acc_branch[slot(0), :] + reduce_recv[1, 0].astype(F32)
    branch_out_ref[...] = (acc_branch[slot(2), :] + reduce_recv[1, 1].astype(F32)).astype(BF16)
    fold(0, 0).wait_recv()
    fold(0, 2).wait_recv()
    back_ref[...] = (
        acc_back[slot(0), :] + reduce_recv[0, 0].astype(F32) + reduce_recv[0, 2].astype(F32)
    )

    @pl.loop(3 * chunks + 1, chain.steps(HOP))
    def _(u):
        chain.step(u, HOP)

    chain.drain()

    @pl.loop(max(chunks - 3, 0), chunks)
    def _(j):
        exchange(j).wait_send()

    @pl.loop(EARLY, chunks)
    def _(j):
        top_exchange(j).wait_send()

    for n, i in ((0, 0), (0, 1), (0, 2), (1, 0), (1, 1)):
        fold(n, i).wait_send()


def ffn(h, top, early, w_gate, w_up, w_down):
    count = lax.axis_size("group")
    rows, width = h.shape
    hidden = w_gate.shape[1] // 2
    wide = WIDE
    chunks = hidden // wide
    tokens = 4 * rows
    anywhere = pl.BlockSpec(memory_space=pl.ANY)
    local = pl.BlockSpec(memory_space=pltpu.VMEM)
    dma = pltpu.SemaphoreType.DMA
    pieces = 3 * chunks
    flops = 2 * tokens * width * hidden * 8
    return pl.pallas_call(
        functools.partial(ffn_kernel, count, chunks),
        out_shape=(
            jax.ShapeDtypeStruct((2, width, 2 * hidden), BF16),
            jax.ShapeDtypeStruct((2 * hidden, width), BF16),
            jax.ShapeDtypeStruct((2, chunks, 2, width, wide), BF16),
            jax.ShapeDtypeStruct((2, chunks, wide, width), BF16),
            jax.ShapeDtypeStruct((rows, width), F32),
            jax.ShapeDtypeStruct((rows, width), BF16),
            jax.ShapeDtypeStruct((rows, width), F32),
        ),
        in_specs=[local, local, local, anywhere, anywhere, anywhere],
        out_specs=(anywhere, anywhere, anywhere, anywhere, local, local, local),
        scratch_shapes=[
            pltpu.VMEM((tokens, width), BF16),
            pltpu.VMEM((width, tokens), BF16),
            pltpu.VMEM((3, tokens, 2 * wide), BF16),
            pltpu.VMEM((chunks, tokens, 2 * wide), BF16),
            pltpu.VMEM((chunks - EARLY, tokens, wide), BF16),
            pltpu.VMEM((chunks - EARLY, tokens, wide), BF16),
            pltpu.VMEM((tokens, wide), F32),
            pltpu.VMEM((chunks, width, 2 * wide), BF16),
            pltpu.VMEM((hidden, width), BF16),
            pltpu.VMEM((tokens, width), F32),
            pltpu.VMEM((tokens, width), F32),
            pltpu.VMEM((tokens, 2 * wide), BF16),
            pltpu.VMEM((wide, tokens), BF16),
            pltpu.VMEM((chunks, 2, width, wide), BF16),
            pltpu.VMEM((chunks, wide, width), BF16),
            pltpu.VMEM((2, width, wide), BF16),
            pltpu.VMEM((2, wide, width), BF16),
            pltpu.VMEM((2, 3, rows, width), BF16),
            dma((3,)), dma((3,)), dma((chunks,)), dma((chunks,)),
            dma((chunks - EARLY,)), dma((chunks - EARLY,)),
            dma((2,)), dma((3, chunks)), dma((2, 3)), dma((2, 3)),
            *chain_semaphores(pieces),
        ],
        compiler_params=pltpu.CompilerParams(
            collective_id=1, has_side_effects=True, vmem_limit_bytes=63 << 20
        ),
        cost_estimate=pl.CostEstimate(
            flops=flops, bytes_accessed=200 << 20, transcendentals=tokens * hidden
        ),
    )(h, top, early, w_gate, w_up, w_down)


ROWS = 128


def sigmoid(v):
    return 1.0 / (1.0 + jnp.exp(-v))


def column(values):
    return jnp.broadcast_to(values, (values.shape[0], 128))


def front_kernel(
    count, heads, kv_heads, tok_ref, top_ref, norm_ref, second_ref, q_gain_ref, k_gain_ref,
    cos_ref, sin_ref, at_ref, start_ref, key_at_ref, w_gates_ref, wq_ref, wk_ref, wv_ref, wo_ref,
    wd_ref,
    h_ref, resid_ref, inv_two_ref, hat_ref, inv_one_ref, normed_ref, tops_ref, early_ref,
    raw_ref, sig_ref, q_ref, k_ref, v_ref, log_ref, attended_ref, gated_ref,
    wq, wk, wv, wo, wd, kv_send, kv_came, q_send, q_came, gates, early_send, early_came,
    ss_send, ss_came, fold_src, fold_dst, acc,
    w_sem, n_send, n_recv, t_send, t_recv, p_send, p_recv, e_send, e_recv, g_send, g_recv,
    s_send, s_recv,
):
    place = Place(count)
    rows, width = tok_ref.shape
    tokens = 2 * rows
    row_at = lax.axis_index("row")
    side = place.side
    hd = 128
    qw, kw = heads * hd, kv_heads * hd
    hidden = wd_ref.shape[0] // 2
    scale = hd**-0.5

    loads = []
    for i, at in enumerate((row_at, 1 - row_at)):
        q_cols, k_cols = tile(at, qw), tile(at, kw)
        loads += [
            pltpu.make_async_copy(wk_ref.at[:, k_cols], wk.at[i], w_sem.at[i, 0]),
            pltpu.make_async_copy(wv_ref.at[:, k_cols], wv.at[i], w_sem.at[i, 1]),
            pltpu.make_async_copy(wq_ref.at[:, q_cols], wq.at[i], w_sem.at[i, 2]),
            pltpu.make_async_copy(wo_ref.at[q_cols, :], wo.at[i], w_sem.at[i, 3]),
        ]
    down_rows = pl.ds(pl.multiple_of(side * hidden, WIDE), wd.shape[0])
    loads.append(pltpu.make_async_copy(wd_ref.at[down_rows, :], wd, w_sem.at[0, 4]))
    for copy in loads:
        copy.start()
    place.meet()

    def slot(i):
        return pl.ds(i * rows, rows)

    def spread(ref, sends, recvs):
        own, core, pair, both = (ref.at[slot(i), :] for i in range(4))
        return (
            copy_to(own, core, sends.at[0], recvs.at[0], place.core_peer),
            copy_to(own, pair, sends.at[1], recvs.at[1], place.y_peer),
            copy_to(pair, both, sends.at[2], recvs.at[2], place.core_peer),
        )

    tops_ref[slot(0), :] = top_ref[...]
    tops = spread(tops_ref, t_send, t_recv)
    tops[0].start()
    tops[1].start()

    def squares(n):
        return copy_to(ss_send.at[n], ss_came.at[n], s_send.at[n], s_recv.at[n], place.x_peer)

    x = tok_ref[...].astype(F32)
    ss_send[0] = column(jnp.sum(x * x, axis=1, keepdims=True))
    squares(0).start()

    def early(i):
        return copy_to(
            early_send.at[slot(i), :], early_came.at[slot(i), :], e_send.at[i], e_recv.at[i],
            place.x_peer,
        )

    def early_start(i):
        early_send[slot(i), :] = nt(tops_ref[slot(i), :], wd[...]).astype(BF16)
        early(i).start()

    loads[-1].wait()
    early_start(0)
    squares(0).wait()
    inv_one = lax.rsqrt((ss_send[0] + ss_came[0]) / (2 * width) + EPS)
    inv_one_ref[...] = inv_one
    hat = tok_ref[...].astype(F32) * inv_one[:, :1]
    hat_ref[...] = hat
    normed_ref[slot(0), :] = (hat * norm_ref[...]).astype(BF16)
    normed = spread(normed_ref, n_send, n_recv)
    normed[0].start()
    normed[1].start()

    kv_copy = copy_to(kv_send, kv_came, p_send.at[0], p_recv.at[0], place.x_peer)
    q_copy = copy_to(q_send, q_came, p_send.at[1], p_recv.at[1], place.x_peer)
    for copy in loads[:-1]:
        copy.wait()
    for i in range(2):
        if i == 1:
            normed[0].wait_recv()
        rows_in = normed_ref[slot(i), :]
        kv_send[slot(i), pl.ds(0, kw)] = nn(rows_in, wk[1]).astype(BF16)
        kv_send[slot(i), pl.ds(kw, kw)] = nn(rows_in, wv[1]).astype(BF16)
    kv_copy.start()
    for i in range(2):
        rows_in = normed_ref[slot(i), :]
        q_send[slot(i), pl.ds(0, qw)] = nn(rows_in, wq[1]).astype(BF16)
        part = nn(rows_in, w_gates_ref[...])
        gates[slot(i), :] = part
        q_send[slot(i), pl.ds(qw, 128)] = part.astype(BF16)
    q_copy.start()
    for i in range(2):
        rows_in = normed_ref[slot(i), :]
        raw_ref[slot(i), pl.ds(0, qw)] = nn(rows_in, wq[0])
        raw_ref[slot(i), pl.ds(qw, kw)] = nn(rows_in, wk[0])
        raw_ref[slot(i), pl.ds(qw + kw, kw)] = nn(rows_in, wv[0])

    def turn(values, gain, at_rows):
        inverse = lax.rsqrt(jnp.mean(values * values, axis=1, keepdims=True) + EPS)
        scaled = values * inverse * gain
        return scaled * cos_ref[at_rows, :] + pltpu.roll(scaled, 64, axis=1) * sin_ref[at_rows, :]

    tops[1].wait_recv()
    tops[2].start()
    normed[1].wait_recv()
    normed[2].start()
    tops[0].wait_recv()
    kv_copy.wait_recv()

    @pl.loop(0, tokens // ROWS)
    def _(i):
        at_rows = tile(i, ROWS)
        for n in range(kv_heads):
            cols = pl.ds(qw + n * hd, hd)
            key = raw_ref[at_rows, cols] + kv_came[at_rows, pl.ds(n * hd, hd)].astype(F32)
            raw_ref[at_rows, cols] = key
            k_ref[at_rows, pl.ds(n * hd, hd)] = turn(key, k_gain_ref[...], at_rows).astype(BF16)
            cols = pl.ds(qw + kw + n * hd, hd)
            value = raw_ref[at_rows, cols] + kv_came[at_rows, pl.ds(kw + n * hd, hd)].astype(F32)
            raw_ref[at_rows, cols] = value
            v_ref[at_rows, pl.ds(n * hd, hd)] = value.astype(BF16)

    q_copy.wait_recv()
    early_start(1)

    @pl.loop(0, tokens // ROWS)
    def _(i):
        at_rows = tile(i, ROWS)
        other = q_came[at_rows, pl.ds(qw, 128)].astype(F32)
        logit = gates[at_rows, :] + pltpu.roll(other, 128 - heads, axis=1)
        sig_ref[at_rows, :] = sigmoid(logit)
        for n in range(heads):
            cols = pl.ds(n * hd, hd)
            query = raw_ref[at_rows, cols] + q_came[at_rows, cols].astype(F32)
            raw_ref[at_rows, cols] = query
            q_ref[at_rows, cols] = turn(query, q_gain_ref[...], at_rows).astype(BF16)

    def head_copy(n):
        cols = pl.ds(n * hd, hd)
        return copy_to(
            gated_ref.at[0, :, cols], gated_ref.at[1, :, cols], g_send.at[n], g_recv.at[n],
            place.x_peer,
        )

    for n in range(heads):
        cols = pl.ds(n * hd, hd)
        kv = pl.ds(n * kv_heads // heads * hd, hd)

        @pl.loop(0, tokens // ROWS)
        def _(i):
            at_rows = tile(i, ROWS)
            scores = nt(q_ref[at_rows, cols], k_ref[:, kv]) * scale
            key_at = key_at_ref[:1, :]
            allowed = (key_at <= at_ref[at_rows, :1]) & (key_at >= start_ref[at_rows, :1])
            scores = jnp.where(allowed, scores, NEGATIVE)
            top = jnp.max(scores, axis=1, keepdims=True)
            raised = jnp.exp(scores - top)
            total = jnp.sum(raised, axis=1, keepdims=True)
            result = nn((raised / total).astype(BF16), v_ref[:, kv])
            log_ref[n, at_rows, :] = column(top + jnp.log(total))
            attended_ref[at_rows, cols] = result
            gated_ref[0, at_rows, cols] = (result * sig_ref[at_rows, n : n + 1]).astype(BF16)

        head_copy(n).start()
        if n == 0:
            tops[2].wait_recv()
            early_start(2)
        if n == 2:
            early_start(3)

    for i in (1, 0):
        acc[slot(i), :] = nn(gated_ref[0, slot(i), :], wo[0])
    for n in range(heads):
        head_copy(n).wait_recv()
    fold = copy_to(fold_src, fold_dst, s_send.at[2], s_recv.at[2], place.core_peer)
    fold_src[...] = (acc[slot(1), :] + nn(gated_ref[1, slot(1), :], wo[1])).astype(BF16)
    fold.start()
    acc[slot(0), :] += nn(gated_ref[1, slot(0), :], wo[1])
    fold.wait_recv()
    resid = tok_ref[...].astype(F32) + acc[slot(0), :] + fold_dst[...].astype(F32)
    resid_ref[...] = resid
    ss_send[1] = column(jnp.sum(resid * resid, axis=1, keepdims=True))
    squares(1).start()
    for i in range(4):
        early(i).wait_recv()
        early_ref[slot(i), :] = (
            early_send[slot(i), :].astype(F32) + early_came[slot(i), :].astype(F32)
        ).astype(BF16)
    squares(1).wait()
    inv_two = lax.rsqrt((ss_send[1] + ss_came[1]) / (2 * width) + EPS)
    inv_two_ref[...] = inv_two
    h_ref[...] = (resid_ref[...] * inv_two[:, :1] * second_ref[...]).astype(BF16)

    normed[2].wait_recv()
    for copy in (*tops, *normed, kv_copy, q_copy, fold):
        copy.wait_send()
    for i in range(4):
        early(i).wait_send()
    for n in range(heads):
        head_copy(n).wait_send()


def front(
    tok, top, norm_gain, ffn_gain, q_gain, k_gain, cos, sin, at, start, key_at, w_gates,
    wq, wk, wv, wo, wd,
):
    count = lax.axis_size("group")
    rows, width = tok.shape
    tokens = 2 * rows
    hd = 128
    heads, kv_heads = wq.shape[1] // 2 // hd, wk.shape[1] // 2 // hd
    qw, kw = heads * hd, kv_heads * hd
    early = EARLY * WIDE
    local = pl.BlockSpec(memory_space=pltpu.VMEM)
    anywhere = pl.BlockSpec(memory_space=pl.ANY)
    dma = pltpu.SemaphoreType.DMA
    struct = jax.ShapeDtypeStruct
    return pl.pallas_call(
        functools.partial(front_kernel, count, heads, kv_heads),
        out_shape=(
            struct((rows, width), BF16),
            struct((rows, width), F32),
            struct((rows, 128), F32),
            struct((rows, width), F32),
            struct((rows, 128), F32),
            struct((4 * rows, width), BF16),
            struct((4 * rows, width), BF16),
            struct((4 * rows, early), BF16),
            struct((tokens, qw + 2 * kw), F32),
            struct((tokens, 128), F32),
            struct((tokens, qw), BF16),
            struct((tokens, kw), BF16),
            struct((tokens, kw), BF16),
            struct((heads, tokens, 128), F32),
            struct((tokens, qw), F32),
            struct((2, tokens, qw), BF16),
        ),
        in_specs=[local] * 12 + [anywhere] * 5,
        out_specs=(local,) * 16,
        scratch_shapes=[
            pltpu.VMEM((2, width, qw), BF16),
            pltpu.VMEM((2, width, kw), BF16),
            pltpu.VMEM((2, width, kw), BF16),
            pltpu.VMEM((2, qw, width), BF16),
            pltpu.VMEM((early, width), BF16),
            pltpu.VMEM((tokens, 2 * kw), BF16),
            pltpu.VMEM((tokens, 2 * kw), BF16),
            pltpu.VMEM((tokens, qw + 128), BF16),
            pltpu.VMEM((tokens, qw + 128), BF16),
            pltpu.VMEM((tokens, 128), F32),
            pltpu.VMEM((4 * rows, early), BF16),
            pltpu.VMEM((4 * rows, early), BF16),
            pltpu.VMEM((2, rows, 128), F32),
            pltpu.VMEM((2, rows, 128), F32),
            pltpu.VMEM((rows, width), BF16),
            pltpu.VMEM((rows, width), BF16),
            pltpu.VMEM((tokens, width), F32),
            dma((2, 5)), dma((3,)), dma((3,)), dma((3,)), dma((3,)), dma((2,)), dma((2,)),
            dma((4,)), dma((4,)), dma((heads,)), dma((heads,)), dma((3,)), dma((3,)),
        ],
        compiler_params=pltpu.CompilerParams(
            collective_id=3, has_side_effects=True, vmem_limit_bytes=60 << 20
        ),
        cost_estimate=pl.CostEstimate(
            flops=6 * tokens * width * (qw + kw) * 4, bytes_accessed=40 << 20,
            transcendentals=heads * tokens * tokens,
        ),
    )(
        tok, top, norm_gain, ffn_gain, q_gain, k_gain, cos, sin, at, start, key_at, w_gates,
        wq, wk, wv, wo, wd,
    )


MISC = 88


def tn(a, b):
    return lax.dot_general(a, b, (((0,), (0,)), ((), ())), preferred_element_type=F32)


def rear_kernel(
    count, heads, kv_heads, back_ref, resid_ref, inv_two_ref, second_ref, top_ref, raw_ref,
    sig_ref, q_ref, k_ref, v_ref, log_ref, attended_ref, cos_ref, sin_ref, at_ref, start_ref,
    key_at_ref, q_gain_ref, k_gain_ref, turned_ref, gated_ref, w_gates_ref, hat_ref, inv_one_ref,
    norm_ref, wq_ref, wk_ref, wv_ref, wo_ref,
    grads_ref, input_ref, sums_ref,
    w_main, wo, branch, dg_own, dg_send, dg_came, dk, dv, gates, gates_came, own, came, across,
    total, landed, misc, misc_came, misc_landed, misc_home, acc, fold_src, fold_dst, in_send,
    in_came,
    w_sem, b_send, b_recv, d_send, d_recv, x_send, x_recv, y_send, y_recv, s_send, s_recv,
    *chain_sems,
):
    place = Place(count)
    row_at = lax.axis_index("row")
    side = place.side
    rows, width = back_ref.shape
    tokens = 2 * rows
    hd = 128
    cols = 2 * hd
    qw = heads * hd
    parts = heads // 2 + kv_heads
    high = gated_ref.shape[0]
    pieces = total.shape[0]
    scale = hd**-0.5

    loads = []
    for i, at in enumerate((row_at, 1 - row_at)):
        for n in range(kv_heads):
            q_cols, k_cols = tile(at * kv_heads + n, cols), tile(at * kv_heads + n, hd)
            first, second = w_main.at[i * parts + 2 * n], w_main.at[i * parts + 2 * n + 1]
            loads += [
                pltpu.make_async_copy(wq_ref.at[:, q_cols], first, w_sem.at[i, n, 0]),
                pltpu.make_async_copy(
                    wk_ref.at[:, k_cols], second.at[:, pl.ds(0, hd)], w_sem.at[i, n, 1]
                ),
                pltpu.make_async_copy(
                    wv_ref.at[:, k_cols], second.at[:, pl.ds(hd, hd)], w_sem.at[i, n, 2]
                ),
            ]
        loads.append(pltpu.make_async_copy(wo_ref.at[tile(at, qw), :], wo.at[i], w_sem.at[i, 0, 3]))
    for copy in loads:
        copy.start()
    place.meet()

    def slot(i):
        return pl.ds(i * rows, rows)

    def inner_copy(n):
        return copy_to(in_send.at[n], in_came.at[n], s_send.at[n], s_recv.at[n], place.x_peer)

    def store_row(at, values):
        for i in range(width // 128):
            misc[at + i : at + i + 1, :] = values[:, i * 128 : (i + 1) * 128]

    misc[...] = jnp.zeros_like(misc)
    grad = back_ref[...]
    in_send[0] = column(jnp.sum(grad * second_ref[...] * resid_ref[...], axis=1, keepdims=True))
    inner_copy(0).start()
    inv_two = inv_two_ref[:, :1]
    store_row(8, jnp.sum(back_ref[...] * resid_ref[...] * inv_two, axis=0, keepdims=True))
    inner_copy(0).wait()
    inner = (in_send[0, :, :1] + in_came[0, :, :1]) * inv_two * inv_two * inv_two / (2 * width)
    d_resid = (
        top_ref[...].astype(F32)
        + inv_two * (back_ref[...] * second_ref[...])
        - resid_ref[...] * inner
    )
    input_ref[...] = d_resid
    branch[slot(0), :] = d_resid.astype(BF16)
    to_core = copy_to(
        branch.at[slot(0), :], branch.at[slot(1), :], b_send.at[0], b_recv.at[0], place.core_peer
    )
    to_pair = copy_to(
        branch.at[slot(0), :], branch.at[slot(2), :], b_send.at[1], b_recv.at[1], place.y_peer
    )
    forward = copy_to(
        branch.at[slot(2), :], branch.at[slot(3), :], b_send.at[2], b_recv.at[2],
        place.core_peer,
    )
    to_core.start()
    to_pair.start()

    def dg_copy(n):
        at_cols = pl.ds(n * cols, cols)
        return copy_to(
            dg_send.at[:, at_cols], dg_came.at[:, at_cols], d_send.at[n], d_recv.at[n],
            place.x_peer,
        )

    for copy in loads:
        copy.wait()
    halves_of = heads // 2
    dg_send[slot(0), :] = nt(branch[slot(0), :], wo[1]).astype(BF16)
    to_core.wait_recv()
    dg_send[slot(1), :] = nt(branch[slot(1), :], wo[1]).astype(BF16)
    for n in range(halves_of):
        dg_copy(n).start()
    for i in range(2):
        dg_own[slot(i), :] = nt(branch[slot(i), :], wo[0])
    dk[...] = jnp.zeros_like(dk)
    dv[...] = jnp.zeros_like(dv)
    gates[...] = jnp.zeros_like(gates)

    def unturn(values, at_rows):
        return values * cos_ref[at_rows, :] - pltpu.roll(values, 64, axis=1) * sin_ref[at_rows, :]

    def norm_back(values, raw, gain, at_rows, into):
        normed = unturn(values, at_rows)
        inverse = lax.rsqrt(jnp.mean(raw * raw, axis=1, keepdims=True) + EPS)
        misc[into : into + 1, :] += jnp.sum(normed * raw * inverse, axis=0, keepdims=True)
        scaled = normed * gain
        inner = jnp.mean(scaled * raw, axis=1, keepdims=True)
        return inverse * scaled - raw * (inverse * inverse * inverse * inner)

    lane = lax.broadcasted_iota(jnp.int32, (ROWS, 128), 1)

    def head(n):
        at_cols = pl.ds(n * hd, hd)
        kv = n * kv_heads // heads
        kv_cols = pl.ds(kv * hd, hd)

        @pl.loop(0, tokens // ROWS)
        def _(i):
            at_rows = tile(i, ROWS)
            query = q_ref[at_rows, at_cols]
            d_gated = dg_own[at_rows, at_cols] + dg_came[at_rows, at_cols].astype(F32)
            sig = sig_ref[at_rows, n : n + 1]
            d_att = (d_gated * sig).astype(BF16)
            d_logit = jnp.sum(d_gated * attended_ref[at_rows, at_cols], axis=1, keepdims=True)
            d_logit = d_logit * sig * (1.0 - sig)
            gates[at_rows, :] = jnp.where(lane == n, d_logit.astype(BF16), gates[at_rows, :])
            scores = nt(query, k_ref[:, kv_cols]) * scale
            key_at = key_at_ref[:1, :]
            allowed = (key_at <= at_ref[at_rows, :1]) & (key_at >= start_ref[at_rows, :1])
            probs = jnp.exp(jnp.where(allowed, scores, NEGATIVE) - log_ref[n, at_rows, :1])
            d_probs = nt(d_att, v_ref[:, kv_cols])
            mean = jnp.sum(d_probs * probs, axis=1, keepdims=True)
            d_scores = (probs * (d_probs - mean)).astype(BF16)
            dv[:, kv_cols] += tn(probs.astype(BF16), d_att)
            dk[:, kv_cols] += tn(d_scores, query)
            d_query = nn(d_scores, k_ref[:, kv_cols]) * scale
            own[2 * (n // 2), at_rows, pl.ds(n % 2 * hd, hd)] = norm_back(
                d_query, raw_ref[at_rows, at_cols], q_gain_ref[...], at_rows, 80
            ).astype(BF16)

    def key_value(n):
        kv_cols = pl.ds(n * hd, hd)

        @pl.loop(0, tokens // ROWS)
        def _(i):
            at_rows = tile(i, ROWS)
            raw = raw_ref[at_rows, pl.ds(qw + n * hd, hd)]
            own[2 * n + 1, at_rows, pl.ds(0, hd)] = norm_back(
                dk[at_rows, kv_cols] * scale, raw, k_gain_ref[...], at_rows, 81
            ).astype(BF16)
            own[2 * n + 1, at_rows, pl.ds(hd, hd)] = dv[at_rows, kv_cols].astype(BF16)

    def over_x(j):
        return copy_to(own.at[j], came.at[j], x_send.at[j], x_recv.at[j], place.x_peer)

    def over_y(j, mine):
        src = own.at[j] if mine else came.at[j]
        return copy_to(src, across.at[j], y_send.at[j], y_recv.at[j], place.y_peer)

    def send_chunk(j):
        over_x(j).start()

        @pl.when(side == 1)
        def _():
            over_y(j, True).start()

    def take_chunk(j):
        over_x(j).wait_recv()

        @pl.when(side == 0)
        def _():
            over_y(j, False).start()

    def add(c, k, which):
        total[c] = (total[c].astype(F32) + landed[which, c].astype(F32)).astype(BF16)

    chain = Chain(
        place, pieces, 1,
        lambda c, k: total.at[c],
        lambda c, k, which: landed.at[which, c],
        lambda c, k, of: grads_ref.at[of * pieces + c],
        add, chain_sems[:9],
    )

    def add_misc(c, k, which):
        misc[...] += misc_landed[which]

    small = Chain(
        place, 1, 1,
        lambda c, k: misc,
        lambda c, k, which: misc_landed.at[which],
        lambda c, k, of: misc_home,
        add_misc, chain_sems[9:], share=False,
    )

    outs = pieces - 2 * parts

    def out_piece(t):
        at_cols = pl.ds(t * cols, cols)
        total[t] = nn(gated_ref[...], branch[:, at_cols]).astype(BF16)
        chain.step(t)

    def block(j):
        over_y(j, True).wait_recv()
        first = jnp.where(side == 0, own[j], came[j])
        for i in range(2):
            at_rows = pl.ds(i * high, high)
            total[outs + 2 * j + i] = (
                nn(turned_ref[at_rows, pl.ds(0, tokens)], first)
                + nn(turned_ref[at_rows, pl.ds(tokens, tokens)], across[j])
            ).astype(BF16)
            chain.step(outs + 2 * j + i)

    for n in range(kv_heads):
        dg_copy(n).wait_recv()
        head(2 * n)
        if n == 0:
            to_pair.wait_recv()
            forward.start()
        else:
            take_chunk(2 * n - 2)
        head(2 * n + 1)
        key_value(n)
        send_chunk(2 * n)
        send_chunk(2 * n + 1)
        if n == 0:
            forward.wait_recv()
            for t in range(outs):
                out_piece(t)
        else:
            take_chunk(2 * n - 1)
            block(2 * n - 2)
            block(2 * n - 1)

    def gates_copy():
        return copy_to(gates, gates_came, s_send.at[2], s_recv.at[2], place.x_peer)

    gates_copy().start()
    last = 2 * (kv_heads - 1)
    acc[...] = nt(own[0], w_main[0])
    for j in range(1, parts):
        acc[...] += nt(own[j], w_main[j])
    for j in range(last):
        acc[...] += nt(came[j], w_main[parts + j])
    for j in range(last, parts):
        take_chunk(j)
        acc[...] += nt(came[j], w_main[parts + j])
    gates_copy().wait_recv()
    moved = pltpu.roll(gates_came[...].astype(F32), heads, axis=1)
    both = gates[...].astype(F32) + moved
    both = both.astype(BF16)
    acc[...] += nt(both, w_gates_ref[...])
    fold = copy_to(fold_src, fold_dst, s_send.at[3], s_recv.at[3], place.core_peer)
    fold_src[...] = acc[rows:, :].astype(BF16)
    fold.start()
    gate_grads = nn(turned_ref[:, pl.ds(0, tokens)], both).T
    for i in range(width // 128):
        misc[16 + 8 * i : 24 + 8 * i, :] = gate_grads[:8, i * 128 : (i + 1) * 128]

    def misc_copy(n, peer):
        return copy_to(misc, misc_came.at[n], s_send.at[4 + n], s_recv.at[4 + n], peer)

    row_of = lax.broadcasted_iota(jnp.int32, (MISC, 128), 0)
    block(last)
    fold.wait_recv()
    grad = acc[:rows, :] + fold_dst[...].astype(F32)
    found = grad * hat_ref[...]
    in_send[1] = column(jnp.sum(found * norm_ref[...], axis=1, keepdims=True))
    inner_copy(1).start()
    acc[:rows, :] = grad
    store_row(0, jnp.sum(found, axis=0, keepdims=True))
    misc_copy(0, place.core_peer).start()
    block(last + 1)
    misc_copy(0, place.core_peer).wait()
    misc[...] += jnp.where((row_of < 16) | (row_of >= 80), misc_came[0], 0.0)
    misc_copy(1, place.x_peer).start()
    chain.step(pieces)
    misc_copy(1, place.x_peer).wait()
    misc[...] += jnp.where(row_of >= 80, misc_came[1], 0.0)
    misc_copy(2, place.y_peer).start()
    inner_copy(1).wait()
    inner = (in_send[1, :, :1] + in_came[1, :, :1]) / (2 * width)
    input_ref[...] += inv_one_ref[:, :1] * (acc[:rows, :] * norm_ref[...] - hat_ref[...] * inner)
    chain.step(pieces + 1)
    misc_copy(2, place.y_peer).wait()
    misc[...] += misc_came[2]

    @pl.loop(pieces + 2, chain.steps())
    def _(u):
        chain.step(u)
        small.step(u - pieces - 2)

    @pl.loop(chain.steps() - pieces - 2, small.steps())
    def _(u):
        small.step(u)

    small.drain()
    sums_ref[...] = misc_home[...]
    chain.drain()
    for copy in (to_core, to_pair, forward, gates_copy(), fold):
        copy.wait_send()
    for n in range(halves_of):
        dg_copy(n).wait_send()
    for j in range(parts):
        over_x(j).wait_send()
        over_y(j, True).wait_send()


def rear(
    back, resid, inv_two, ffn_gain, top, raw, sig, query, keys, values, log, attended, cos, sin,
    at, start, key_at, q_gain, k_gain, turned, gated, w_gates, hat, inv_one, norm_gain,
    wq, wk, wv, wo,
):
    count = lax.axis_size("group")
    rows, width = back.shape
    tokens = 2 * rows
    hd = 128
    heads, kv_heads = query.shape[1] // hd, keys.shape[1] // hd
    qw, kw = heads * hd, kv_heads * hd
    cols = 2 * hd
    parts = heads // 2 + kv_heads
    high = gated.shape[0]
    pieces = 2 * parts + width // cols
    anywhere = pl.BlockSpec(memory_space=pl.ANY)
    local = pl.BlockSpec(memory_space=pltpu.VMEM)
    dma = pltpu.SemaphoreType.DMA
    struct = jax.ShapeDtypeStruct
    return pl.pallas_call(
        functools.partial(rear_kernel, count, heads, kv_heads),
        out_shape=(
            struct((2 * pieces, high, cols), BF16),
            struct((rows, width), F32),
            struct((MISC, 128), F32),
        ),
        in_specs=[local] * 25 + [anywhere] * 4,
        out_specs=(anywhere, local, local),
        scratch_shapes=[
            pltpu.VMEM((2 * parts, width, cols), BF16),
            pltpu.VMEM((2, qw, width), BF16),
            pltpu.VMEM((4 * rows, width), BF16),
            pltpu.VMEM((tokens, qw), F32),
            pltpu.VMEM((tokens, qw), BF16),
            pltpu.VMEM((tokens, qw), BF16),
            pltpu.VMEM((tokens, kw), F32),
            pltpu.VMEM((tokens, kw), F32),
            pltpu.VMEM((tokens, 128), BF16),
            pltpu.VMEM((tokens, 128), BF16),
            pltpu.VMEM((parts, tokens, cols), BF16),
            pltpu.VMEM((parts, tokens, cols), BF16),
            pltpu.VMEM((parts, tokens, cols), BF16),
            pltpu.VMEM((pieces, high, cols), BF16),
            pltpu.VMEM((2, pieces, high, cols), BF16),
            pltpu.VMEM((MISC, 128), F32),
            pltpu.VMEM((3, MISC, 128), F32),
            pltpu.VMEM((2, MISC, 128), F32),
            pltpu.VMEM((MISC, 128), F32),
            pltpu.VMEM((tokens, width), F32),
            pltpu.VMEM((rows, width), BF16),
            pltpu.VMEM((rows, width), BF16),
            pltpu.VMEM((2, rows, 128), F32),
            pltpu.VMEM((2, rows, 128), F32),
            dma((2, kv_heads, 4)), dma((3,)), dma((3,)), dma((heads // 2,)), dma((heads // 2,)),
            dma((parts,)), dma((parts,)), dma((parts,)), dma((parts,)), dma((7,)), dma((7,)),
            *chain_semaphores(pieces), *chain_semaphores(1),
        ],
        compiler_params=pltpu.CompilerParams(
            collective_id=2, has_side_effects=True, vmem_limit_bytes=60 << 20
        ),
        cost_estimate=pl.CostEstimate(
            flops=2 * tokens * width * (qw + 2 * kw) * 6, bytes_accessed=100 << 20,
            transcendentals=heads * tokens * tokens,
        ),
    )(
        back, resid, inv_two, ffn_gain, top, raw, sig, query, keys, values, log, attended, cos,
        sin, at, start, key_at, q_gain, k_gain, turned, gated, w_gates, hat, inv_one, norm_gain,
        wq, wk, wv, wo,
    )


def body(
    tokens, lengths, norm_gain, w_query, w_key, w_value, w_head_gate, query_gain, key_gain,
    w_out, ffn_gain, w_gate, w_up, w_down, grad_out,
):
    rows, d_loc = tokens.shape
    group_tok = 2 * rows
    head_dim = query_gain.shape[0]
    q_half = w_query.shape[1] // 2
    kv_half = w_key.shape[1] // 2
    gate_half = w_head_gate.shape[1] // 2
    row_at = lax.axis_index("row")
    col_at = lax.axis_index("col")
    side = lax.axis_index("group") % 2

    steps = jnp.arange(rows, dtype=jnp.int32)
    index = jnp.concatenate([col_at * rows + steps, (1 - col_at) * rows + steps])
    place = places(lengths, index)[1]
    cosines, sines = rope_tables(place, head_dim)
    signed = jnp.concatenate([-sines[:, : head_dim // 2], sines[:, head_dim // 2 :]], axis=1)
    positions = (
        jnp.broadcast_to(index[:, None], (group_tok, 128)),
        jnp.broadcast_to((index - place)[:, None], (group_tok, 128)),
        jnp.broadcast_to(index[None], (8, group_tok)),
    )
    w_gates = jnp.pad(
        jnp.concatenate(halves(w_head_gate, 1, row_at), axis=1),
        ((0, 0), (0, 128 - 2 * gate_half)),
    )
    gains = (query_gain[None], key_gain[None])
    (
        normed_two, resid, inverse_two, hat, inverse_one, permuted_pair, grad_all, early_grad,
        raw, gate_sigmoid, query, keys, values, logsum, attended, gated_both,
    ) = front(
        tokens, grad_out, norm_gain[None], ffn_gain[None], *gains, cosines, signed, *positions,
        w_gates, w_query, w_key, w_value, w_out, w_down,
    )
    turned = permuted_pair.T
    gated, gated_came = gated_both[0], gated_both[1]
    first_side = side == 0
    gated_pair = jnp.concatenate(
        [
            jnp.where(first_side, gated, gated_came),
            swap_groups(jnp.where(first_side, gated_came, gated)),
        ]
    ).T

    pair_sum, down_sum, _, _, branch, branch_out, d_normed_two = ffn(
        normed_two, grad_all, early_grad, w_gate, w_up, w_down
    )
    output = (resid + branch + swap_groups(branch_out).astype(F32)).astype(BF16)

    grads, input_grad, sums = rear(
        d_normed_two, resid, inverse_two, ffn_gain[None], grad_out, raw, gate_sigmoid, query,
        keys, values, logsum, attended, cosines, signed, *positions, *gains, turned, gated_pair,
        w_gates, hat, inverse_one, norm_gain[None], w_query, w_key, w_value, w_out,
    )
    grad_norm_gain = sums[:8].reshape(d_loc)
    grad_ffn_gain = sums[8:16].reshape(d_loc)
    grad_gates = sums[16:80].reshape(8, 2 * gate_half, 128).transpose(1, 0, 2)
    grad_gates = grad_gates.reshape(2 * gate_half, d_loc)
    grad_head_gate = ordered(grad_gates[:gate_half], grad_gates[gate_half:], 0, row_at).T

    grads = grads.reshape(2, -1, q_half, 256)
    count = d_loc // 256
    out_sum = grads[:, :count].transpose(0, 2, 1, 3).reshape(2 * q_half, d_loc)
    grad_out_full = ordered(*jnp.split(out_sum, 2, axis=0), 0, row_at).astype(F32)
    chunks = grads[:, count:].reshape(2, kv_half // head_dim, 2, 2, q_half, 256)

    def collect(at, start, size):
        def side_of(n):
            pieces = [
                chunks[n, i, at, :, :, start : start + size].reshape(d_loc, size)
                for i in range(chunks.shape[1])
            ]
            return jnp.concatenate(pieces, axis=1)

        return ordered(side_of(0), side_of(1), 1, row_at).astype(F32)

    return (
        output,
        input_grad,
        grad_norm_gain,
        collect(0, 0, 256),
        collect(1, 0, 128),
        collect(1, 128, 128),
        grad_head_gate,
        sums[80],
        sums[81],
        grad_out_full,
        grad_ffn_gain,
        pair_sum[0].astype(F32),
        pair_sum[1].astype(F32),
        down_sum.astype(F32),
    )


def solution(mesh):
    shards = P(("group", "col"), "row")
    in_specs = (
        shards,
        P("group"),
        P("row"),
        P("row", "col"),
        P("row", "col"),
        P("row", "col"),
        P("row", "col"),
        P(),
        P(),
        P("col", "row"),
        P("row"),
        P("row", "col"),
        P("row", "col"),
        P("col", "row"),
        shards,
    )
    out_specs = (
        shards,
        shards,
        P("row"),
        P("row", "col"),
        P("row", "col"),
        P("row", "col"),
        P("row", "col"),
        P(),
        P(),
        P("col", "row"),
        P("row"),
        P("row", "col"),
        P("row", "col"),
        P("col", "row"),
    )
    return jax.shard_map(body, mesh=mesh, in_specs=in_specs, out_specs=out_specs, check_vma=False)
```

```python
import functools

import jax
import jax.numpy as jnp
from jax import lax
from jax.experimental import pallas as pl
from jax.experimental.pallas import tpu as pltpu
from jax.sharding import PartitionSpec as P

EPS = 1e-06
THETA = 1000000.0
NEGATIVE = -1e30
MESH = pl.DeviceIdType.MESH
F32 = jnp.float32
BF16 = jnp.bfloat16


def swap_groups(values):
    count = lax.axis_size("group")
    return lax.ppermute(values, "group", [(i, i ^ 1) for i in range(count)])


def halves(values, axis, at):
    low, high = jnp.split(values, 2, axis=axis)
    first = at == 0
    return jnp.where(first, low, high), jnp.where(first, high, low)


def ordered(own, other, axis, at):
    first = at == 0
    return jnp.concatenate(
        [jnp.where(first, own, other), jnp.where(first, other, own)], axis=axis
    )


def places(lengths_group, index):
    ends = jnp.cumsum(lengths_group)
    passed = (index[:, None] >= ends[None, :]).astype(jnp.int32)
    segment = jnp.sum(passed, axis=1)
    place = index - jnp.sum(passed * lengths_group[None, :], axis=1)
    return (segment, place)


def rope_tables(place, width):
    half = width // 2
    freq = THETA ** (-(jnp.arange(half, dtype=F32) * 2.0 / width))
    angle = place.astype(F32)[:, None] * freq[None, :]
    cosines = jnp.concatenate([jnp.cos(angle), jnp.cos(angle)], axis=1)
    sines = jnp.concatenate([jnp.sin(angle), jnp.sin(angle)], axis=1)
    return (cosines, sines)


TILE = 256
HOP = 2
WIDE = 128
EARLY = 6
AHEAD = 2
LATE = 3


def nt(a, b):
    return lax.dot_general(a, b, (((1,), (1,)), ((), ())), preferred_element_type=F32)


def nn(a, b):
    return jnp.dot(a, b, preferred_element_type=F32)


def copy_to(src, dst, send_sem, recv_sem, peer):
    return pltpu.make_async_remote_copy(
        src_ref=src, dst_ref=dst, send_sem=send_sem, recv_sem=recv_sem,
        device_id=peer, device_id_type=MESH,
    )


def tile(i, size=TILE):
    return pl.ds(pl.multiple_of(i * size, size), size)


class Place:
    def __init__(self, count):
        group = lax.axis_index("group")
        self.line = count // 2
        self.root = (self.line - 1) // 2
        self.deep = max(self.root, self.line - 1 - self.root)
        self.at = group // 2
        self.side = group % 2
        self.x_peer = {"row": 1 - lax.axis_index("row")}
        self.core_peer = {"col": 1 - lax.axis_index("col")}
        self.y_peer = {"group": group + 1 - 2 * self.side}
        self.above = {"group": jnp.minimum(group + 2, count - 1)}
        self.below = {"group": jnp.maximum(group - 2, 0)}
        self.has_above = self.at < self.line - 1
        self.has_below = self.at > 0

    def meet(self):
        barrier = pltpu.get_barrier_semaphore()

        def greet(peer):
            pl.semaphore_signal(barrier, inc=1, device_id=peer, device_id_type=MESH)

        for peer in (self.x_peer, self.core_peer, self.y_peer):
            greet(peer)
        pl.when(self.has_above)(lambda: greet(self.above))
        pl.when(self.has_below)(lambda: greet(self.below))
        met = 3 + self.has_above.astype(jnp.int32) + self.has_below.astype(jnp.int32)
        pl.semaphore_wait(barrier, met)


class Chain:
    def __init__(self, place, chunks, kinds, total, came, home, add, sems, share=True):
        self.place, self.chunks, self.kinds = place, chunks, kinds
        self.total, self.came, self.home, self.add = total, came, home, add
        self.sems, self.share = sems, share

    def part_copy(self, c, k, upward):
        sent, low, high = self.sems[:3]
        p = self.kinds * c + k
        peer, which, arrived = (
            (self.place.above, 0, low) if upward else (self.place.below, 1, high)
        )
        return copy_to(
            self.total(c, k), self.came(c, k, which), sent.at[p], arrived.at[p], peer
        )

    def final_copy(self, c, k, upward, first):
        up, down, arrived = self.sems[3:6]
        p = self.kinds * c + k
        src = self.total(c, k) if first else self.home(c, k, self.place.side)
        peer, sent = (self.place.above, up) if upward else (self.place.below, down)
        return copy_to(src, self.home(c, k, self.place.side), sent.at[p], arrived.at[p], peer)

    def keep_copy(self, c, k):
        return pltpu.make_async_copy(
            self.total(c, k), self.home(c, k, self.place.side),
            self.sems[6].at[self.kinds * c + k],
        )

    def share_copy(self, c, k, first, of=None):
        p = self.kinds * c + k
        of = self.place.side if of is None else of
        src = self.total(c, k) if first else self.home(c, k, self.place.side)
        return copy_to(
            src, self.home(c, k, of), self.sems[7].at[p], self.sems[8].at[p], self.place.y_peer
        )

    def step(self, u, hop=1):
        at, line, root, deep = self.place.at, self.place.line, self.place.root, self.place.deep
        behind = jnp.where(at < root, at, jnp.where(at > root, line - 1 - at, deep))
        self.inward(u - hop * behind)
        self.outward(u - hop * (deep + jnp.abs(at - root)))

    def kinds_of(self, p):
        live = (p >= 0) & (p < self.kinds * self.chunks)
        if self.kinds == 1:
            return [(live, p, 0)]
        p = jnp.maximum(p, 0)
        return [
            (live & (lax.rem(p, self.kinds) == k), lax.div(p, self.kinds), k)
            for k in range(self.kinds)
        ]

    def inward(self, piece):
        at, line, root = self.place.at, self.place.line, self.place.root
        for live, c, k in self.kinds_of(piece):

            @pl.when(live & (at < root))
            def _():
                @pl.when(self.place.has_below)
                def _():
                    self.part_copy(c, k, True).wait_recv()
                    self.add(c, k, 0)

                self.part_copy(c, k, True).start()

            @pl.when(live & (at > root))
            def _():
                @pl.when(self.place.has_above)
                def _():
                    self.part_copy(c, k, False).wait_recv()
                    self.add(c, k, 1)

                self.part_copy(c, k, False).start()

            @pl.when(live & (at == root))
            def _():
                if root > 0:
                    self.part_copy(c, k, True).wait_recv()
                    self.add(c, k, 0)
                if root < line - 1:
                    self.part_copy(c, k, False).wait_recv()
                    self.add(c, k, 1)
                if root > 0:
                    self.final_copy(c, k, False, True).start()
                if root < line - 1:
                    self.final_copy(c, k, True, True).start()
                if self.share:
                    self.share_copy(c, k, True).start()
                self.keep_copy(c, k).start()

    def outward(self, piece):
        at, root = self.place.at, self.place.root
        for live, c, k in self.kinds_of(piece):

            @pl.when(live & (at != root))
            def _():
                self.final_copy(c, k, True, False).wait_recv()

                @pl.when((at > root) & self.place.has_above)
                def _():
                    self.final_copy(c, k, True, False).start()

                @pl.when((at < root) & self.place.has_below)
                def _():
                    self.final_copy(c, k, False, False).start()

                if self.share:
                    self.share_copy(c, k, False).start()

    def steps(self, hop=1):
        return self.kinds * self.chunks + 2 * hop * self.place.deep

    def drain(self):
        at, line, root = self.place.at, self.place.line, self.place.root

        @pl.loop(0, self.chunks)
        def _(c):
            for k in range(self.kinds):
                if self.share:
                    self.share_copy(c, k, False, 1 - self.place.side).wait_recv()
                    self.share_copy(c, k, False).wait_send()

                @pl.when(at == root)
                def _():
                    self.keep_copy(c, k).wait()
                    if root > 0:
                        self.final_copy(c, k, False, True).wait_send()
                    if root < line - 1:
                        self.final_copy(c, k, True, True).wait_send()

                @pl.when(at < root)
                def _():
                    self.part_copy(c, k, True).wait_send()

                    @pl.when(self.place.has_below)
                    def _():
                        self.final_copy(c, k, False, False).wait_send()

                @pl.when(at > root)
                def _():
                    self.part_copy(c, k, False).wait_send()

                    @pl.when(self.place.has_above)
                    def _():
                        self.final_copy(c, k, True, False).wait_send()


def chain_semaphores(pieces):
    return [pltpu.SemaphoreType.DMA((pieces,)) for _ in range(9)]


def ffn_kernel(
    count, chunks, h_ref, top_ref, early_ref, gate_ref, up_ref, down_ref,
    pair_grads_ref, down_grads_ref, late_pair_ref, late_down_ref, pair_came_ref, down_came_ref,
    branch_ref, branch_out_ref, back_ref,
    h_all, h_turned, sent, came, top_sent, top_came, grad_part, w_pair, w_down, acc_branch, acc_back, parts, inner_turned,
    pair_total, down_total, pair_stage, down_stage, reduce_recv,
    gather_send, gather_recv, x_send, x_recv, top_send, top_recv, late_sem, load_sem, weight_sem, fold_send, fold_recv,
    *chain_sems,
):
    place = Place(count)
    rows, width = h_ref.shape
    tokens = h_all.shape[0]
    tiles = tokens // TILE
    wide = w_down.shape[0] // chunks
    side = place.side

    def weight_copies(j):
        cols = tile(side * chunks + j, wide)
        return (
            pltpu.make_async_copy(
                gate_ref.at[:, cols], w_pair.at[j, :, pl.ds(0, wide)], weight_sem.at[0, j]
            ),
            pltpu.make_async_copy(
                up_ref.at[:, cols], w_pair.at[j, :, pl.ds(wide, wide)], weight_sem.at[1, j]
            ),
            pltpu.make_async_copy(
                down_ref.at[cols, :], w_down.at[tile(j, wide), :], weight_sem.at[2, j]
            ),
        )

    @pl.loop(0, chunks)
    def _(j):
        for copy in weight_copies(j):
            copy.start()

    place.meet()

    def slot(i):
        return pl.ds(i * rows, rows)

    to_y = copy_to(h_ref, h_all.at[slot(2)], gather_send.at[0], gather_recv.at[0], place.y_peer)
    to_core = copy_to(
        h_ref, h_all.at[slot(1)], gather_send.at[1], gather_recv.at[1], place.core_peer
    )
    forward = copy_to(
        h_all.at[slot(2)], h_all.at[slot(3)], gather_send.at[2], gather_recv.at[2],
        place.core_peer,
    )
    to_y.start()
    to_core.start()

    def top_exchange(j):
        n = j - EARLY
        return copy_to(
            top_sent.at[n], top_came.at[n], top_send.at[n], top_recv.at[n], place.x_peer
        )

    def top_project(j):
        @pl.loop(0, tiles)
        def _(i):
            top_sent[j - EARLY, tile(i), :] = nt(
                top_ref[tile(i), :], w_down[tile(j, wide), :]
            ).astype(BF16)

        top_exchange(j).start()

    def exchange(j):
        return copy_to(
            sent.at[lax.rem(j, 3)], came.at[j], x_send.at[j], x_recv.at[j], place.x_peer
        )

    def first_half(i):
        at_rows = pl.ds(2 * i * rows, 2 * rows)
        n = i * chunks
        return copy_to(
            sent.at[0, at_rows, :], came.at[0, at_rows, :], x_send.at[n], x_recv.at[n],
            place.x_peer,
        )

    def project_half(i):
        for n in range(2):
            at_rows = slot(2 * i + n)
            sent[0, at_rows, :] = nn(h_all[at_rows, :], w_pair[0]).astype(BF16)
        first_half(i).start()

    def project(j):
        for copy in weight_copies(j)[:2]:
            copy.wait()

        @pl.loop(0, tiles)
        def _(i):
            sent[lax.rem(j, 3), tile(i), :] = nn(h_all[tile(i), :], w_pair[j]).astype(BF16)

    def work(j):
        @pl.when(j == 0)
        def _():
            first_half(0).wait_recv()
            first_half(1).wait_recv()

        @pl.when(j > 0)
        def _():
            exchange(j).wait_recv()

        @pl.when(j < EARLY)
        def _():
            grad_part[...] = early_ref[:, tile(j, wide)].astype(F32)

        @pl.when(j >= EARLY)
        def _():
            top_exchange(j).wait_recv()
            grad_part[...] = top_sent[j - EARLY].astype(F32) + top_came[j - EARLY].astype(F32)

        @pl.loop(0, tiles)
        def _(i):
            at_rows = tile(i)
            pair = sent[lax.rem(j, 3), at_rows, :].astype(F32) + came[j, at_rows, :].astype(F32)
            gate, up = pair[:, :wide], pair[:, wide:]
            grad = grad_part[at_rows, :]
            sig = 1.0 / (1.0 + jnp.exp(-gate))
            silu = gate * sig
            parts[at_rows, pl.ds(0, wide)] = (
                grad * up * (sig * (1.0 + gate * (1.0 - sig)))
            ).astype(BF16)
            parts[at_rows, pl.ds(wide, wide)] = (grad * silu).astype(BF16)
            inner = (silu * up).astype(BF16)
            inner_turned[:, at_rows] = inner.T
            acc_branch[at_rows, :] += nn(inner, w_down[tile(j, wide), :])
            acc_back[at_rows, :] += nt(parts[at_rows, :], w_pair[j])

    def gradients(j):
        @pl.loop(0, width // TILE)
        def _(i):
            pair = nn(h_turned[tile(i), :], parts[...])
            pair_total[j, 0, tile(i), :] = pair[:, :wide].astype(BF16)
            pair_total[j, 1, tile(i), :] = pair[:, wide:].astype(BF16)
            down_total[j, :, tile(i)] = nn(inner_turned[...], top_ref[:, tile(i)]).astype(BF16)

    def total(c, k):
        return down_total.at[c] if k == 2 else pair_total.at[c, k]

    def landed(c, k, which):
        return down_came_ref.at[which, c] if k == 2 else pair_came_ref.at[which, c, k]

    def home(c, k, of):
        at_cols = tile(of * chunks + c, wide)
        return down_grads_ref.at[at_cols, :] if k == 2 else pair_grads_ref.at[k, :, at_cols]

    def add(c, k, which):
        stage = (down_stage if k == 2 else pair_stage).at[which]
        copy = pltpu.make_async_copy(landed(c, k, which), stage, load_sem.at[which])
        copy.start()
        copy.wait()
        into = total(c, k)

        @pl.loop(0, into.shape[0] // wide)
        def _(i):
            at_rows = tile(i, wide)
            into[at_rows, :] = (
                into[at_rows, :].astype(F32) + stage[at_rows, :].astype(F32)
            ).astype(BF16)

    ours = chunks - LATE
    chain = Chain(place, ours, 3, total, landed, home, add, chain_sems)

    def late_copies(c):
        return (
            pltpu.make_async_copy(pair_total.at[c], late_pair_ref.at[c - ours], late_sem.at[0, c - ours]),
            pltpu.make_async_copy(down_total.at[c], late_down_ref.at[c - ours], late_sem.at[1, c - ours]),
        )

    h_all[slot(0), :] = h_ref[...]
    for copy in weight_copies(0)[:2]:
        copy.wait()
    to_core.wait_recv()
    project_half(0)

    @pl.loop(0, chunks)
    def _(j):
        weight_copies(j)[2].wait()

    @pl.loop(EARLY, min(EARLY + AHEAD, chunks))
    def _(j):
        top_project(j)

    acc_branch[...] = jnp.zeros_like(acc_branch)
    acc_back[...] = jnp.zeros_like(acc_back)
    to_y.wait_recv()
    forward.start()
    forward.wait_recv()
    project_half(1)
    project(1)

    @pl.loop(0, tiles)
    def _(i):
        h_turned[:, tile(i)] = h_all[tile(i), :].T

    first_half(0).wait_send()
    first_half(1).wait_send()
    exchange(1).start()

    @pl.loop(0, chunks)
    def _(t):
        work(t)
        chain.step(3 * t - 1, HOP)
        gradients(t)

        @pl.when(t >= ours)
        def _():
            for copy in late_copies(t):
                copy.start()

        chain.step(3 * t, HOP)

        @pl.when(t + 2 < chunks)
        def _():
            @pl.when(t >= 2)
            def _():
                exchange(t - 1).wait_send()

            project(t + 2)
            exchange(t + 2).start()

        @pl.when((t + AHEAD >= EARLY + AHEAD) & (t + AHEAD < chunks))
        def _():
            top_project(t + AHEAD)

        chain.step(3 * t + 1, HOP)

    chain.step(3 * chunks - 1, HOP)

    def fold_source(n, i):
        if i == 2:
            return w_down.at[slot(0), :]
        return h_all.at[slot(2 * n + i), :]

    def fold(n, i):
        return copy_to(
            fold_source(n, i), reduce_recv.at[n, i], fold_send.at[n, i], fold_recv.at[n, i],
            place.y_peer if i == 2 else place.core_peer,
        )

    to_y.wait_send()
    to_core.wait_send()
    forward.wait_send()
    for n, acc in enumerate((acc_back, acc_branch)):
        for i in (1, 0):
            fold_source(n, i)[...] = acc[slot(2 * i + 1), :].astype(BF16)
            fold(n, i).start()
    fold(0, 1).wait_recv()
    fold_source(0, 2)[...] = (acc_back[slot(2), :] + reduce_recv[0, 1].astype(F32)).astype(BF16)
    fold(0, 2).start()
    chain.step(3 * chunks, HOP)
    fold(1, 0).wait_recv()
    fold(1, 1).wait_recv()
    branch_ref[...] = acc_branch[slot(0), :] + reduce_recv[1, 0].astype(F32)
    branch_out_ref[...] = (acc_branch[slot(2), :] + reduce_recv[1, 1].astype(F32)).astype(BF16)
    fold(0, 0).wait_recv()
    fold(0, 2).wait_recv()
    back_ref[...] = (
        acc_back[slot(0), :] + reduce_recv[0, 0].astype(F32) + reduce_recv[0, 2].astype(F32)
    )

    @pl.loop(3 * chunks + 1, max(3 * chunks + 1, chain.steps(HOP)))
    def _(u):
        chain.step(u, HOP)

    @pl.loop(ours, chunks)
    def _(c):
        for copy in late_copies(c):
            copy.wait()

    chain.drain()

    @pl.loop(max(chunks - 3, 0), chunks)
    def _(j):
        exchange(j).wait_send()

    @pl.loop(EARLY, chunks)
    def _(j):
        top_exchange(j).wait_send()

    for n, i in ((0, 0), (0, 1), (0, 2), (1, 0), (1, 1)):
        fold(n, i).wait_send()


def ffn(h, top, early, w_gate, w_up, w_down):
    count = lax.axis_size("group")
    rows, width = h.shape
    hidden = w_gate.shape[1] // 2
    wide = WIDE
    chunks = hidden // wide
    tokens = 4 * rows
    anywhere = pl.BlockSpec(memory_space=pl.ANY)
    local = pl.BlockSpec(memory_space=pltpu.VMEM)
    dma = pltpu.SemaphoreType.DMA
    pieces = 3 * (chunks - LATE)
    flops = 2 * tokens * width * hidden * 8
    return pl.pallas_call(
        functools.partial(ffn_kernel, count, chunks),
        out_shape=(
            jax.ShapeDtypeStruct((2, width, 2 * hidden), BF16),
            jax.ShapeDtypeStruct((2 * hidden, width), BF16),
            jax.ShapeDtypeStruct((LATE, 2, width, wide), BF16),
            jax.ShapeDtypeStruct((LATE, wide, width), BF16),
            jax.ShapeDtypeStruct((2, chunks - LATE, 2, width, wide), BF16),
            jax.ShapeDtypeStruct((2, chunks - LATE, wide, width), BF16),
            jax.ShapeDtypeStruct((rows, width), F32),
            jax.ShapeDtypeStruct((rows, width), BF16),
            jax.ShapeDtypeStruct((rows, width), F32),
        ),
        in_specs=[local, local, local, anywhere, anywhere, anywhere],
        out_specs=(anywhere,) * 6 + (local,) * 3,
        scratch_shapes=[
            pltpu.VMEM((tokens, width), BF16),
            pltpu.VMEM((width, tokens), BF16),
            pltpu.VMEM((3, tokens, 2 * wide), BF16),
            pltpu.VMEM((chunks, tokens, 2 * wide), BF16),
            pltpu.VMEM((chunks - EARLY, tokens, wide), BF16),
            pltpu.VMEM((chunks - EARLY, tokens, wide), BF16),
            pltpu.VMEM((tokens, wide), F32),
            pltpu.VMEM((chunks, width, 2 * wide), BF16),
            pltpu.VMEM((hidden, width), BF16),
            pltpu.VMEM((tokens, width), F32),
            pltpu.VMEM((tokens, width), F32),
            pltpu.VMEM((tokens, 2 * wide), BF16),
            pltpu.VMEM((wide, tokens), BF16),
            pltpu.VMEM((chunks, 2, width, wide), BF16),
            pltpu.VMEM((chunks, wide, width), BF16),
            pltpu.VMEM((2, width, wide), BF16),
            pltpu.VMEM((2, wide, width), BF16),
            pltpu.VMEM((2, 3, rows, width), BF16),
            dma((3,)), dma((3,)), dma((chunks + 1,)), dma((chunks + 1,)),
            dma((chunks - EARLY,)), dma((chunks - EARLY,)),
            dma((2, LATE)), dma((2,)), dma((3, chunks)), dma((2, 3)), dma((2, 3)),
            *chain_semaphores(pieces),
        ],
        compiler_params=pltpu.CompilerParams(
            collective_id=1, has_side_effects=True, vmem_limit_bytes=63 << 20
        ),
        cost_estimate=pl.CostEstimate(
            flops=flops, bytes_accessed=200 << 20, transcendentals=tokens * hidden
        ),
    )(h, top, early, w_gate, w_up, w_down)


ROWS = 128


def sigmoid(v):
    return 1.0 / (1.0 + jnp.exp(-v))


def column(values):
    return jnp.broadcast_to(values, (values.shape[0], 128))


def front_kernel(
    count, heads, kv_heads, tok_ref, top_ref, norm_ref, second_ref, q_gain_ref, k_gain_ref,
    cos_ref, sin_ref, at_ref, start_ref, key_at_ref, w_gates_ref, wq_ref, wk_ref, wv_ref, wo_ref,
    wd_ref,
    h_ref, resid_ref, inv_two_ref, hat_ref, inv_one_ref, normed_ref, tops_ref, early_ref,
    raw_ref, sig_ref, q_ref, k_ref, v_ref, log_ref, attended_ref, gated_ref,
    wq, wk, wv, wo, wd, kv_send, kv_came, q_send, q_came, gates, early_send, early_came,
    ss_send, ss_came, fold_src, fold_dst, acc,
    w_sem, n_send, n_recv, t_send, t_recv, p_send, p_recv, e_send, e_recv, g_send, g_recv,
    s_send, s_recv,
):
    place = Place(count)
    rows, width = tok_ref.shape
    tokens = 2 * rows
    row_at = lax.axis_index("row")
    side = place.side
    hd = 128
    qw, kw = heads * hd, kv_heads * hd
    hidden = wd_ref.shape[0] // 2
    scale = hd**-0.5

    loads = []
    for i, at in enumerate((row_at, 1 - row_at)):
        q_cols, k_cols = tile(at, qw), tile(at, kw)
        loads += [
            pltpu.make_async_copy(wk_ref.at[:, k_cols], wk.at[i], w_sem.at[i, 0]),
            pltpu.make_async_copy(wv_ref.at[:, k_cols], wv.at[i], w_sem.at[i, 1]),
            pltpu.make_async_copy(wq_ref.at[:, q_cols], wq.at[i], w_sem.at[i, 2]),
            pltpu.make_async_copy(wo_ref.at[q_cols, :], wo.at[i], w_sem.at[i, 3]),
        ]
    down_rows = pl.ds(pl.multiple_of(side * hidden, WIDE), wd.shape[0])
    loads.append(pltpu.make_async_copy(wd_ref.at[down_rows, :], wd, w_sem.at[0, 4]))
    for copy in loads:
        copy.start()
    place.meet()

    def slot(i):
        return pl.ds(i * rows, rows)

    def spread(ref, sends, recvs):
        own, core, pair, both = (ref.at[slot(i), :] for i in range(4))
        return (
            copy_to(own, core, sends.at[0], recvs.at[0], place.core_peer),
            copy_to(own, pair, sends.at[1], recvs.at[1], place.y_peer),
            copy_to(pair, both, sends.at[2], recvs.at[2], place.core_peer),
        )

    tops_ref[slot(0), :] = top_ref[...]
    tops = spread(tops_ref, t_send, t_recv)
    tops[0].start()
    tops[1].start()

    def squares(n):
        return copy_to(ss_send.at[n], ss_came.at[n], s_send.at[n], s_recv.at[n], place.x_peer)

    x = tok_ref[...].astype(F32)
    ss_send[0] = column(jnp.sum(x * x, axis=1, keepdims=True))
    squares(0).start()

    def early(i):
        return copy_to(
            early_send.at[slot(i), :], early_came.at[slot(i), :], e_send.at[i], e_recv.at[i],
            place.x_peer,
        )

    def early_start(i):
        early_send[slot(i), :] = nt(tops_ref[slot(i), :], wd[...]).astype(BF16)
        early(i).start()

    loads[-1].wait()
    early_start(0)
    squares(0).wait()
    inv_one = lax.rsqrt((ss_send[0] + ss_came[0]) / (2 * width) + EPS)
    inv_one_ref[...] = inv_one
    hat = tok_ref[...].astype(F32) * inv_one[:, :1]
    hat_ref[...] = hat
    normed_ref[slot(0), :] = (hat * norm_ref[...]).astype(BF16)
    normed = spread(normed_ref, n_send, n_recv)
    normed[0].start()
    normed[1].start()

    kv_copy = copy_to(kv_send, kv_came, p_send.at[0], p_recv.at[0], place.x_peer)
    q_copy = copy_to(q_send, q_came, p_send.at[1], p_recv.at[1], place.x_peer)
    for copy in loads[:-1]:
        copy.wait()
    for i in range(2):
        if i == 1:
            normed[0].wait_recv()
        rows_in = normed_ref[slot(i), :]
        kv_send[slot(i), pl.ds(0, kw)] = nn(rows_in, wk[1]).astype(BF16)
        kv_send[slot(i), pl.ds(kw, kw)] = nn(rows_in, wv[1]).astype(BF16)
    kv_copy.start()
    for i in range(2):
        rows_in = normed_ref[slot(i), :]
        q_send[slot(i), pl.ds(0, qw)] = nn(rows_in, wq[1]).astype(BF16)
        part = nn(rows_in, w_gates_ref[...])
        gates[slot(i), :] = part
        q_send[slot(i), pl.ds(qw, 128)] = part.astype(BF16)
    q_copy.start()
    for i in range(2):
        rows_in = normed_ref[slot(i), :]
        raw_ref[slot(i), pl.ds(0, qw)] = nn(rows_in, wq[0])
        raw_ref[slot(i), pl.ds(qw, kw)] = nn(rows_in, wk[0])
        raw_ref[slot(i), pl.ds(qw + kw, kw)] = nn(rows_in, wv[0])

    def turn(values, gain, at_rows):
        inverse = lax.rsqrt(jnp.mean(values * values, axis=1, keepdims=True) + EPS)
        scaled = values * inverse * gain
        return scaled * cos_ref[at_rows, :] + pltpu.roll(scaled, 64, axis=1) * sin_ref[at_rows, :]

    tops[1].wait_recv()
    tops[2].start()
    normed[1].wait_recv()
    normed[2].start()
    tops[0].wait_recv()
    kv_copy.wait_recv()

    @pl.loop(0, tokens // ROWS)
    def _(i):
        at_rows = tile(i, ROWS)
        for n in range(kv_heads):
            cols = pl.ds(qw + n * hd, hd)
            key = raw_ref[at_rows, cols] + kv_came[at_rows, pl.ds(n * hd, hd)].astype(F32)
            raw_ref[at_rows, cols] = key
            k_ref[at_rows, pl.ds(n * hd, hd)] = turn(key, k_gain_ref[...], at_rows).astype(BF16)
            cols = pl.ds(qw + kw + n * hd, hd)
            value = raw_ref[at_rows, cols] + kv_came[at_rows, pl.ds(kw + n * hd, hd)].astype(F32)
            raw_ref[at_rows, cols] = value
            v_ref[at_rows, pl.ds(n * hd, hd)] = value.astype(BF16)

    q_copy.wait_recv()
    early_start(1)

    @pl.loop(0, tokens // ROWS)
    def _(i):
        at_rows = tile(i, ROWS)
        other = q_came[at_rows, pl.ds(qw, 128)].astype(F32)
        logit = gates[at_rows, :] + pltpu.roll(other, 128 - heads, axis=1)
        sig_ref[at_rows, :] = sigmoid(logit)
        for n in range(heads):
            cols = pl.ds(n * hd, hd)
            query = raw_ref[at_rows, cols] + q_came[at_rows, cols].astype(F32)
            raw_ref[at_rows, cols] = query
            q_ref[at_rows, cols] = turn(query, q_gain_ref[...], at_rows).astype(BF16)

    def head_copy(n):
        cols = pl.ds(n * hd, hd)
        return copy_to(
            gated_ref.at[0, :, cols], gated_ref.at[1, :, cols], g_send.at[n], g_recv.at[n],
            place.x_peer,
        )

    for n in range(heads):
        cols = pl.ds(n * hd, hd)
        kv = pl.ds(n * kv_heads // heads * hd, hd)

        @pl.loop(0, tokens // ROWS)
        def _(i):
            at_rows = tile(i, ROWS)
            scores = nt(q_ref[at_rows, cols], k_ref[:, kv]) * scale
            key_at = key_at_ref[:1, :]
            allowed = (key_at <= at_ref[at_rows, :1]) & (key_at >= start_ref[at_rows, :1])
            scores = jnp.where(allowed, scores, NEGATIVE)
            top = jnp.max(scores, axis=1, keepdims=True)
            raised = jnp.exp(scores - top)
            total = jnp.sum(raised, axis=1, keepdims=True)
            result = nn((raised / total).astype(BF16), v_ref[:, kv])
            log_ref[n, at_rows, :] = column(top + jnp.log(total))
            attended_ref[at_rows, cols] = result
            gated_ref[0, at_rows, cols] = (result * sig_ref[at_rows, n : n + 1]).astype(BF16)

        head_copy(n).start()
        if n == 0:
            tops[2].wait_recv()
            early_start(2)
        if n == 2:
            early_start(3)

    for i in (1, 0):
        acc[slot(i), :] = nn(gated_ref[0, slot(i), :], wo[0])
    for n in range(heads):
        head_copy(n).wait_recv()
    fold = copy_to(fold_src, fold_dst, s_send.at[2], s_recv.at[2], place.core_peer)
    fold_src[...] = (acc[slot(1), :] + nn(gated_ref[1, slot(1), :], wo[1])).astype(BF16)
    fold.start()
    acc[slot(0), :] += nn(gated_ref[1, slot(0), :], wo[1])
    fold.wait_recv()
    resid = tok_ref[...].astype(F32) + acc[slot(0), :] + fold_dst[...].astype(F32)
    resid_ref[...] = resid
    ss_send[1] = column(jnp.sum(resid * resid, axis=1, keepdims=True))
    squares(1).start()
    for i in range(4):
        early(i).wait_recv()
        early_ref[slot(i), :] = (
            early_send[slot(i), :].astype(F32) + early_came[slot(i), :].astype(F32)
        ).astype(BF16)
    squares(1).wait()
    inv_two = lax.rsqrt((ss_send[1] + ss_came[1]) / (2 * width) + EPS)
    inv_two_ref[...] = inv_two
    h_ref[...] = (resid_ref[...] * inv_two[:, :1] * second_ref[...]).astype(BF16)

    normed[2].wait_recv()
    for copy in (*tops, *normed, kv_copy, q_copy, fold):
        copy.wait_send()
    for i in range(4):
        early(i).wait_send()
    for n in range(heads):
        head_copy(n).wait_send()


def front(
    tok, top, norm_gain, ffn_gain, q_gain, k_gain, cos, sin, at, start, key_at, w_gates,
    wq, wk, wv, wo, wd,
):
    count = lax.axis_size("group")
    rows, width = tok.shape
    tokens = 2 * rows
    hd = 128
    heads, kv_heads = wq.shape[1] // 2 // hd, wk.shape[1] // 2 // hd
    qw, kw = heads * hd, kv_heads * hd
    early = EARLY * WIDE
    local = pl.BlockSpec(memory_space=pltpu.VMEM)
    anywhere = pl.BlockSpec(memory_space=pl.ANY)
    dma = pltpu.SemaphoreType.DMA
    struct = jax.ShapeDtypeStruct
    return pl.pallas_call(
        functools.partial(front_kernel, count, heads, kv_heads),
        out_shape=(
            struct((rows, width), BF16),
            struct((rows, width), F32),
            struct((rows, 128), F32),
            struct((rows, width), F32),
            struct((rows, 128), F32),
            struct((4 * rows, width), BF16),
            struct((4 * rows, width), BF16),
            struct((4 * rows, early), BF16),
            struct((tokens, qw + 2 * kw), F32),
            struct((tokens, 128), F32),
            struct((tokens, qw), BF16),
            struct((tokens, kw), BF16),
            struct((tokens, kw), BF16),
            struct((heads, tokens, 128), F32),
            struct((tokens, qw), F32),
            struct((2, tokens, qw), BF16),
        ),
        in_specs=[local] * 12 + [anywhere] * 5,
        out_specs=(local,) * 16,
        scratch_shapes=[
            pltpu.VMEM((2, width, qw), BF16),
            pltpu.VMEM((2, width, kw), BF16),
            pltpu.VMEM((2, width, kw), BF16),
            pltpu.VMEM((2, qw, width), BF16),
            pltpu.VMEM((early, width), BF16),
            pltpu.VMEM((tokens, 2 * kw), BF16),
            pltpu.VMEM((tokens, 2 * kw), BF16),
            pltpu.VMEM((tokens, qw + 128), BF16),
            pltpu.VMEM((tokens, qw + 128), BF16),
            pltpu.VMEM((tokens, 128), F32),
            pltpu.VMEM((4 * rows, early), BF16),
            pltpu.VMEM((4 * rows, early), BF16),
            pltpu.VMEM((2, rows, 128), F32),
            pltpu.VMEM((2, rows, 128), F32),
            pltpu.VMEM((rows, width), BF16),
            pltpu.VMEM((rows, width), BF16),
            pltpu.VMEM((tokens, width), F32),
            dma((2, 5)), dma((3,)), dma((3,)), dma((3,)), dma((3,)), dma((2,)), dma((2,)),
            dma((4,)), dma((4,)), dma((heads,)), dma((heads,)), dma((3,)), dma((3,)),
        ],
        compiler_params=pltpu.CompilerParams(
            collective_id=3, has_side_effects=True, vmem_limit_bytes=60 << 20
        ),
        cost_estimate=pl.CostEstimate(
            flops=6 * tokens * width * (qw + kw) * 4, bytes_accessed=40 << 20,
            transcendentals=heads * tokens * tokens,
        ),
    )(
        tok, top, norm_gain, ffn_gain, q_gain, k_gain, cos, sin, at, start, key_at, w_gates,
        wq, wk, wv, wo, wd,
    )


MISC = 88


def tn(a, b):
    return lax.dot_general(a, b, (((0,), (0,)), ((), ())), preferred_element_type=F32)


def rear_kernel(
    count, heads, kv_heads, back_ref, resid_ref, inv_two_ref, second_ref, top_ref, raw_ref,
    sig_ref, q_ref, k_ref, v_ref, log_ref, attended_ref, cos_ref, sin_ref, at_ref, start_ref,
    key_at_ref, q_gain_ref, k_gain_ref, turned_ref, gated_ref, w_gates_ref, hat_ref, inv_one_ref,
    norm_ref, wq_ref, wk_ref, wv_ref, wo_ref, late_pair_ref, late_down_ref, pair_in, down_in,
    grads_ref, input_ref, sums_ref, pair_grads_ref, down_grads_ref,
    w_main, wo, branch, dg_own, dg_send, dg_came, dk, dv, gates, gates_came, own, came, across,
    total, landed, misc, misc_came, misc_landed, misc_home, acc, fold_src, fold_dst, in_send,
    in_came, late_pair, late_down, late_pair_came, late_down_came,
    w_sem, late_sem, b_send, b_recv, d_send, d_recv, x_send, x_recv, y_send, y_recv, s_send, s_recv,
    *chain_sems,
):
    place = Place(count)
    row_at = lax.axis_index("row")
    side = place.side
    rows, width = back_ref.shape
    tokens = 2 * rows
    hd = 128
    cols = 2 * hd
    qw = heads * hd
    parts = heads // 2 + kv_heads
    high = gated_ref.shape[0]
    pieces = total.shape[0]
    scale = hd**-0.5

    loads = []
    for i, at in enumerate((row_at, 1 - row_at)):
        for n in range(kv_heads):
            q_cols, k_cols = tile(at * kv_heads + n, cols), tile(at * kv_heads + n, hd)
            first, second = w_main.at[i * parts + 2 * n], w_main.at[i * parts + 2 * n + 1]
            loads += [
                pltpu.make_async_copy(wq_ref.at[:, q_cols], first, w_sem.at[i, n, 0]),
                pltpu.make_async_copy(
                    wk_ref.at[:, k_cols], second.at[:, pl.ds(0, hd)], w_sem.at[i, n, 1]
                ),
                pltpu.make_async_copy(
                    wv_ref.at[:, k_cols], second.at[:, pl.ds(hd, hd)], w_sem.at[i, n, 2]
                ),
            ]
        loads.append(pltpu.make_async_copy(wo_ref.at[tile(at, qw), :], wo.at[i], w_sem.at[i, 0, 3]))
    for copy in loads:
        copy.start()
    late_loads = (
        pltpu.make_async_copy(late_pair_ref, late_pair, late_sem.at[0]),
        pltpu.make_async_copy(late_down_ref, late_down, late_sem.at[1]),
    )
    for copy in late_loads:
        copy.start()
    place.meet()

    def late_total(c, k):
        return late_down.at[c] if k == 2 else late_pair.at[c, k]

    def late_landed(c, k, which):
        return late_down_came.at[which, c] if k == 2 else late_pair_came.at[which, c, k]

    def late_home(c, k, of):
        chunks = down_grads_ref.shape[0] // 2 // WIDE
        at_cols = tile(of * chunks + chunks - LATE + c, WIDE)
        return down_grads_ref.at[at_cols, :] if k == 2 else pair_grads_ref.at[k, :, at_cols]

    def late_add(c, k, which):
        into, came_in = late_total(c, k), late_landed(c, k, which)
        into[...] = (into[...].astype(F32) + came_in[...].astype(F32)).astype(BF16)

    late = Chain(
        place, LATE, 3, late_total, late_landed, late_home, late_add, chain_sems[18:]
    )
    def slot(i):
        return pl.ds(i * rows, rows)

    def inner_copy(n):
        return copy_to(in_send.at[n], in_came.at[n], s_send.at[n], s_recv.at[n], place.x_peer)

    def store_row(at, values):
        for i in range(width // 128):
            misc[at + i : at + i + 1, :] = values[:, i * 128 : (i + 1) * 128]

    misc[...] = jnp.zeros_like(misc)
    grad = back_ref[...]
    in_send[0] = column(jnp.sum(grad * second_ref[...] * resid_ref[...], axis=1, keepdims=True))
    inner_copy(0).start()
    for copy in late_loads:
        copy.wait()
    late.step(0, HOP)
    inv_two = inv_two_ref[:, :1]
    store_row(8, jnp.sum(back_ref[...] * resid_ref[...] * inv_two, axis=0, keepdims=True))
    inner_copy(0).wait()
    inner = (in_send[0, :, :1] + in_came[0, :, :1]) * inv_two * inv_two * inv_two / (2 * width)
    d_resid = (
        top_ref[...].astype(F32)
        + inv_two * (back_ref[...] * second_ref[...])
        - resid_ref[...] * inner
    )
    input_ref[...] = d_resid
    branch[slot(0), :] = d_resid.astype(BF16)
    to_core = copy_to(
        branch.at[slot(0), :], branch.at[slot(1), :], b_send.at[0], b_recv.at[0], place.core_peer
    )
    to_pair = copy_to(
        branch.at[slot(0), :], branch.at[slot(2), :], b_send.at[1], b_recv.at[1], place.y_peer
    )
    forward = copy_to(
        branch.at[slot(2), :], branch.at[slot(3), :], b_send.at[2], b_recv.at[2],
        place.core_peer,
    )
    to_core.start()
    to_pair.start()
    late.step(1, HOP)

    def dg_copy(n):
        at_cols = pl.ds(n * cols, cols)
        return copy_to(
            dg_send.at[:, at_cols], dg_came.at[:, at_cols], d_send.at[n], d_recv.at[n],
            place.x_peer,
        )

    for copy in loads:
        copy.wait()
    halves_of = heads // 2
    dg_send[slot(0), :] = nt(branch[slot(0), :], wo[1]).astype(BF16)
    to_core.wait_recv()
    dg_send[slot(1), :] = nt(branch[slot(1), :], wo[1]).astype(BF16)
    for n in range(halves_of):
        dg_copy(n).start()
    late.step(2, HOP)
    for i in range(2):
        dg_own[slot(i), :] = nt(branch[slot(i), :], wo[0])
    dk[...] = jnp.zeros_like(dk)
    dv[...] = jnp.zeros_like(dv)
    gates[...] = jnp.zeros_like(gates)

    def unturn(values, at_rows):
        return values * cos_ref[at_rows, :] - pltpu.roll(values, 64, axis=1) * sin_ref[at_rows, :]

    def norm_back(values, raw, gain, at_rows, into):
        normed = unturn(values, at_rows)
        inverse = lax.rsqrt(jnp.mean(raw * raw, axis=1, keepdims=True) + EPS)
        misc[into : into + 1, :] += jnp.sum(normed * raw * inverse, axis=0, keepdims=True)
        scaled = normed * gain
        inner = jnp.mean(scaled * raw, axis=1, keepdims=True)
        return inverse * scaled - raw * (inverse * inverse * inverse * inner)

    lane = lax.broadcasted_iota(jnp.int32, (ROWS, 128), 1)

    def head(n):
        at_cols = pl.ds(n * hd, hd)
        kv = n * kv_heads // heads
        kv_cols = pl.ds(kv * hd, hd)

        @pl.loop(0, tokens // ROWS)
        def _(i):
            at_rows = tile(i, ROWS)
            query = q_ref[at_rows, at_cols]
            d_gated = dg_own[at_rows, at_cols] + dg_came[at_rows, at_cols].astype(F32)
            sig = sig_ref[at_rows, n : n + 1]
            d_att = (d_gated * sig).astype(BF16)
            d_logit = jnp.sum(d_gated * attended_ref[at_rows, at_cols], axis=1, keepdims=True)
            d_logit = d_logit * sig * (1.0 - sig)
            gates[at_rows, :] = jnp.where(lane == n, d_logit.astype(BF16), gates[at_rows, :])
            scores = nt(query, k_ref[:, kv_cols]) * scale
            key_at = key_at_ref[:1, :]
            allowed = (key_at <= at_ref[at_rows, :1]) & (key_at >= start_ref[at_rows, :1])
            probs = jnp.exp(jnp.where(allowed, scores, NEGATIVE) - log_ref[n, at_rows, :1])
            d_probs = nt(d_att, v_ref[:, kv_cols])
            mean = jnp.sum(d_probs * probs, axis=1, keepdims=True)
            d_scores = (probs * (d_probs - mean)).astype(BF16)
            dv[:, kv_cols] += tn(probs.astype(BF16), d_att)
            dk[:, kv_cols] += tn(d_scores, query)
            d_query = nn(d_scores, k_ref[:, kv_cols]) * scale
            own[2 * (n // 2), at_rows, pl.ds(n % 2 * hd, hd)] = norm_back(
                d_query, raw_ref[at_rows, at_cols], q_gain_ref[...], at_rows, 80
            ).astype(BF16)

    def key_value(n):
        kv_cols = pl.ds(n * hd, hd)

        @pl.loop(0, tokens // ROWS)
        def _(i):
            at_rows = tile(i, ROWS)
            raw = raw_ref[at_rows, pl.ds(qw + n * hd, hd)]
            own[2 * n + 1, at_rows, pl.ds(0, hd)] = norm_back(
                dk[at_rows, kv_cols] * scale, raw, k_gain_ref[...], at_rows, 81
            ).astype(BF16)
            own[2 * n + 1, at_rows, pl.ds(hd, hd)] = dv[at_rows, kv_cols].astype(BF16)

    def over_x(j):
        return copy_to(own.at[j], came.at[j], x_send.at[j], x_recv.at[j], place.x_peer)

    def over_y(j, mine):
        src = own.at[j] if mine else came.at[j]
        return copy_to(src, across.at[j], y_send.at[j], y_recv.at[j], place.y_peer)

    def send_chunk(j):
        over_x(j).start()

        @pl.when(side == 1)
        def _():
            over_y(j, True).start()

    def take_chunk(j):
        over_x(j).wait_recv()

        @pl.when(side == 0)
        def _():
            over_y(j, False).start()

    def add(c, k, which):
        total[c] = (total[c].astype(F32) + landed[which, c].astype(F32)).astype(BF16)

    chain = Chain(
        place, pieces, 1,
        lambda c, k: total.at[c],
        lambda c, k, which: landed.at[which, c],
        lambda c, k, of: grads_ref.at[of * pieces + c],
        add, chain_sems[:9],
    )

    def add_misc(c, k, which):
        misc[...] += misc_landed[which]

    small = Chain(
        place, 1, 1,
        lambda c, k: misc,
        lambda c, k, which: misc_landed.at[which],
        lambda c, k, of: misc_home,
        add_misc, chain_sems[9:18], share=False,
    )

    left = 3 * LATE
    outs = pieces - 2 * parts

    def step(u):
        if u < late.steps(HOP):
            late.step(u, HOP)
        if u >= left:
            chain.step(u - left, HOP)

    def out_piece(t):
        total[t] = nn(gated_ref[...], branch[:, pl.ds(t * cols, cols)]).astype(BF16)

    def block(j):
        over_y(j, True).wait_recv()
        first = jnp.where(side == 0, own[j], came[j])
        for i in range(2):
            at_rows = pl.ds(i * high, high)
            total[outs + 2 * j + i] = (
                nn(turned_ref[at_rows, pl.ds(0, tokens)], first)
                + nn(turned_ref[at_rows, pl.ds(tokens, tokens)], across[j])
            ).astype(BF16)

    def gates_copy():
        return copy_to(gates, gates_came, s_send.at[2], s_recv.at[2], place.x_peer)

    step(3)
    for n in range(kv_heads):
        dg_copy(n).wait_recv()
        head(2 * n)
        head(2 * n + 1)
        key_value(n)
        send_chunk(2 * n)
        send_chunk(2 * n + 1)
        if n == 0:
            to_pair.wait_recv()
            forward.start()
            step(4)
    gates_copy().start()

    def back_own(j):
        acc[...] += nt(own[j], w_main[j])

    def back_came(j):
        take_chunk(j)
        acc[...] += nt(came[j], w_main[parts + j])

    step(5)
    acc[...] = jnp.zeros_like(acc)
    for j in range(parts):
        back_own(j)
    step(6)
    back_came(0)
    step(7)
    back_came(1)
    for u in range(8, left):
        step(u)
    forward.wait_recv()
    for t in range(outs):
        out_piece(t)
        step(left + t)
        if t + 2 < parts:
            back_came(t + 2)
    at = left + outs

    gates_copy().wait_recv()
    moved = pltpu.roll(gates_came[...].astype(F32), heads, axis=1)
    both = (gates[...].astype(F32) + moved).astype(BF16)
    acc[...] += nt(both, w_gates_ref[...])
    fold = copy_to(fold_src, fold_dst, s_send.at[3], s_recv.at[3], place.core_peer)
    fold_src[...] = acc[rows:, :].astype(BF16)
    fold.start()
    block(0)
    step(at)
    gate_grads = nn(turned_ref[:, pl.ds(0, tokens)], both).T
    for i in range(width // 128):
        misc[16 + 8 * i : 24 + 8 * i, :] = gate_grads[:8, i * 128 : (i + 1) * 128]

    def misc_copy(n, peer):
        return copy_to(misc, misc_came.at[n], s_send.at[4 + n], s_recv.at[4 + n], peer)

    row_of = lax.broadcasted_iota(jnp.int32, (MISC, 128), 0)
    fold.wait_recv()
    grad = acc[:rows, :] + fold_dst[...].astype(F32)
    found = grad * hat_ref[...]
    in_send[1] = column(jnp.sum(found * norm_ref[...], axis=1, keepdims=True))
    inner_copy(1).start()
    acc[:rows, :] = grad
    store_row(0, jnp.sum(found, axis=0, keepdims=True))
    misc_copy(0, place.core_peer).start()
    step(at + 1)
    block(1)
    step(at + 2)
    misc_copy(0, place.core_peer).wait()
    misc[...] += jnp.where((row_of < 16) | (row_of >= 80), misc_came[0], 0.0)
    misc_copy(1, place.x_peer).start()
    step(at + 3)
    block(2)
    step(at + 4)
    misc_copy(1, place.x_peer).wait()
    misc[...] += jnp.where(row_of >= 80, misc_came[1], 0.0)
    misc_copy(2, place.y_peer).start()
    inner_copy(1).wait()
    inner = (in_send[1, :, :1] + in_came[1, :, :1]) / (2 * width)
    input_ref[...] += inv_one_ref[:, :1] * (acc[:rows, :] * norm_ref[...] - hat_ref[...] * inner)
    step(at + 5)
    block(3)
    misc_copy(2, place.y_peer).wait()
    misc[...] += misc_came[2]
    small.step(0)
    step(at + 6)
    small.step(1)
    step(at + 7)

    @pl.loop(pieces, chain.steps(HOP))
    def _(u):
        if late.steps(HOP) > left + pieces:
            late.step(u + left, HOP)
        small.step(u - pieces + 2)
        chain.step(u, HOP)

    @pl.loop(chain.steps(HOP) - pieces + 2, small.steps())
    def _(u):
        small.step(u)

    small.drain()
    sums_ref[...] = misc_home[...]
    chain.drain()
    late.drain()
    for copy in (to_core, to_pair, forward, gates_copy(), fold):
        copy.wait_send()
    for n in range(halves_of):
        dg_copy(n).wait_send()
    for j in range(parts):
        over_x(j).wait_send()
        over_y(j, True).wait_send()


def rear(
    back, resid, inv_two, ffn_gain, top, raw, sig, query, keys, values, log, attended, cos, sin,
    at, start, key_at, q_gain, k_gain, turned, gated, w_gates, hat, inv_one, norm_gain,
    wq, wk, wv, wo, late_pair, late_down, pair_sum, down_sum,
):
    count = lax.axis_size("group")
    rows, width = back.shape
    tokens = 2 * rows
    hd = 128
    heads, kv_heads = query.shape[1] // hd, keys.shape[1] // hd
    qw, kw = heads * hd, kv_heads * hd
    cols = 2 * hd
    parts = heads // 2 + kv_heads
    high = gated.shape[0]
    pieces = 2 * parts + width // cols
    anywhere = pl.BlockSpec(memory_space=pl.ANY)
    local = pl.BlockSpec(memory_space=pltpu.VMEM)
    dma = pltpu.SemaphoreType.DMA
    struct = jax.ShapeDtypeStruct
    return pl.pallas_call(
        functools.partial(rear_kernel, count, heads, kv_heads),
        out_shape=(
            struct((2 * pieces, high, cols), BF16),
            struct((rows, width), F32),
            struct((MISC, 128), F32),
            struct(pair_sum.shape, BF16),
            struct(down_sum.shape, BF16),
        ),
        in_specs=[local] * 25 + [anywhere] * 8,
        out_specs=(anywhere, local, local, anywhere, anywhere),
        input_output_aliases={31: 3, 32: 4},
        scratch_shapes=[
            pltpu.VMEM((2 * parts, width, cols), BF16),
            pltpu.VMEM((2, qw, width), BF16),
            pltpu.VMEM((4 * rows, width), BF16),
            pltpu.VMEM((tokens, qw), F32),
            pltpu.VMEM((tokens, qw), BF16),
            pltpu.VMEM((tokens, qw), BF16),
            pltpu.VMEM((tokens, kw), F32),
            pltpu.VMEM((tokens, kw), F32),
            pltpu.VMEM((tokens, 128), BF16),
            pltpu.VMEM((tokens, 128), BF16),
            pltpu.VMEM((parts, tokens, cols), BF16),
            pltpu.VMEM((parts, tokens, cols), BF16),
            pltpu.VMEM((parts, tokens, cols), BF16),
            pltpu.VMEM((pieces, high, cols), BF16),
            pltpu.VMEM((2, pieces, high, cols), BF16),
            pltpu.VMEM((MISC, 128), F32),
            pltpu.VMEM((3, MISC, 128), F32),
            pltpu.VMEM((2, MISC, 128), F32),
            pltpu.VMEM((MISC, 128), F32),
            pltpu.VMEM((tokens, width), F32),
            pltpu.VMEM((rows, width), BF16),
            pltpu.VMEM((rows, width), BF16),
            pltpu.VMEM((2, rows, 128), F32),
            pltpu.VMEM((2, rows, 128), F32),
            pltpu.VMEM(late_pair.shape, BF16),
            pltpu.VMEM(late_down.shape, BF16),
            pltpu.VMEM((2,) + late_pair.shape, BF16),
            pltpu.VMEM((2,) + late_down.shape, BF16),
            dma((2, kv_heads, 4)), dma((2,)), dma((3,)), dma((3,)), dma((heads // 2,)), dma((heads // 2,)),
            dma((parts,)), dma((parts,)), dma((parts,)), dma((parts,)), dma((7,)), dma((7,)),
            *chain_semaphores(pieces), *chain_semaphores(1), *chain_semaphores(3 * LATE),
        ],
        compiler_params=pltpu.CompilerParams(
            collective_id=2, has_side_effects=True, vmem_limit_bytes=60 << 20
        ),
        cost_estimate=pl.CostEstimate(
            flops=2 * tokens * width * (qw + 2 * kw) * 6, bytes_accessed=100 << 20,
            transcendentals=heads * tokens * tokens,
        ),
    )(
        back, resid, inv_two, ffn_gain, top, raw, sig, query, keys, values, log, attended, cos,
        sin, at, start, key_at, q_gain, k_gain, turned, gated, w_gates, hat, inv_one, norm_gain,
        wq, wk, wv, wo, late_pair, late_down, pair_sum, down_sum,
    )


def body(
    tokens, lengths, norm_gain, w_query, w_key, w_value, w_head_gate, query_gain, key_gain,
    w_out, ffn_gain, w_gate, w_up, w_down, grad_out,
):
    rows, d_loc = tokens.shape
    group_tok = 2 * rows
    head_dim = query_gain.shape[0]
    q_half = w_query.shape[1] // 2
    kv_half = w_key.shape[1] // 2
    gate_half = w_head_gate.shape[1] // 2
    row_at = lax.axis_index("row")
    col_at = lax.axis_index("col")
    side = lax.axis_index("group") % 2

    steps = jnp.arange(rows, dtype=jnp.int32)
    index = jnp.concatenate([col_at * rows + steps, (1 - col_at) * rows + steps])
    place = places(lengths, index)[1]
    cosines, sines = rope_tables(place, head_dim)
    signed = jnp.concatenate([-sines[:, : head_dim // 2], sines[:, head_dim // 2 :]], axis=1)
    positions = (
        jnp.broadcast_to(index[:, None], (group_tok, 128)),
        jnp.broadcast_to((index - place)[:, None], (group_tok, 128)),
        jnp.broadcast_to(index[None], (8, group_tok)),
    )
    w_gates = jnp.pad(
        jnp.concatenate(halves(w_head_gate, 1, row_at), axis=1),
        ((0, 0), (0, 128 - 2 * gate_half)),
    )
    gains = (query_gain[None], key_gain[None])
    (
        normed_two, resid, inverse_two, hat, inverse_one, permuted_pair, grad_all, early_grad,
        raw, gate_sigmoid, query, keys, values, logsum, attended, gated_both,
    ) = front(
        tokens, grad_out, norm_gain[None], ffn_gain[None], *gains, cosines, signed, *positions,
        w_gates, w_query, w_key, w_value, w_out, w_down,
    )
    turned = permuted_pair.T
    gated, gated_came = gated_both[0], gated_both[1]
    first_side = side == 0
    gated_pair = jnp.concatenate(
        [
            jnp.where(first_side, gated, gated_came),
            swap_groups(jnp.where(first_side, gated_came, gated)),
        ]
    ).T

    pair_sum, down_sum, late_pair, late_down, _, _, branch, branch_out, d_normed_two = ffn(
        normed_two, grad_all, early_grad, w_gate, w_up, w_down
    )
    output = (resid + branch + swap_groups(branch_out).astype(F32)).astype(BF16)

    grads, input_grad, sums, pair_sum, down_sum = rear(
        d_normed_two, resid, inverse_two, ffn_gain[None], grad_out, raw, gate_sigmoid, query,
        keys, values, logsum, attended, cosines, signed, *positions, *gains, turned, gated_pair,
        w_gates, hat, inverse_one, norm_gain[None], w_query, w_key, w_value, w_out,
        late_pair, late_down, pair_sum, down_sum,
    )
    grad_norm_gain = sums[:8].reshape(d_loc)
    grad_ffn_gain = sums[8:16].reshape(d_loc)
    grad_gates = sums[16:80].reshape(8, 2 * gate_half, 128).transpose(1, 0, 2)
    grad_gates = grad_gates.reshape(2 * gate_half, d_loc)
    grad_head_gate = ordered(grad_gates[:gate_half], grad_gates[gate_half:], 0, row_at).T

    grads = grads.reshape(2, -1, q_half, 256)
    count = d_loc // 256
    out_sum = grads[:, :count].transpose(0, 2, 1, 3).reshape(2 * q_half, d_loc)
    grad_out_full = ordered(*jnp.split(out_sum, 2, axis=0), 0, row_at).astype(F32)
    chunks = grads[:, count:].reshape(2, kv_half // head_dim, 2, 2, q_half, 256)

    def collect(at, start, size):
        def side_of(n):
            pieces = [
                chunks[n, i, at, :, :, start : start + size].reshape(d_loc, size)
                for i in range(chunks.shape[1])
            ]
            return jnp.concatenate(pieces, axis=1)

        return ordered(side_of(0), side_of(1), 1, row_at).astype(F32)

    return (
        output,
        input_grad,
        grad_norm_gain,
        collect(0, 0, 256),
        collect(1, 0, 128),
        collect(1, 128, 128),
        grad_head_gate,
        sums[80],
        sums[81],
        grad_out_full,
        grad_ffn_gain,
        pair_sum[0].astype(F32),
        pair_sum[1].astype(F32),
        down_sum.astype(F32),
    )


def solution(mesh):
    shards = P(("group", "col"), "row")
    in_specs = (
        shards,
        P("group"),
        P("row"),
        P("row", "col"),
        P("row", "col"),
        P("row", "col"),
        P("row", "col"),
        P(),
        P(),
        P("col", "row"),
        P("row"),
        P("row", "col"),
        P("row", "col"),
        P("col", "row"),
        shards,
    )
    out_specs = (
        shards,
        shards,
        P("row"),
        P("row", "col"),
        P("row", "col"),
        P("row", "col"),
        P("row", "col"),
        P(),
        P(),
        P("col", "row"),
        P("row"),
        P("row", "col"),
        P("row", "col"),
        P("col", "row"),
    )
    return jax.shard_map(body, mesh=mesh, in_specs=in_specs, out_specs=out_specs, check_vma=False)
```

```python
import functools

import jax
import jax.numpy as jnp
from jax import lax
from jax.experimental import pallas as pl
from jax.experimental.pallas import tpu as pltpu
from jax.sharding import PartitionSpec as P

EPS = 1e-06
THETA = 1000000.0
NEGATIVE = -1e30
MESH = pl.DeviceIdType.MESH
F32 = jnp.float32
BF16 = jnp.bfloat16


def swap_groups(values):
    count = lax.axis_size("group")
    return lax.ppermute(values, "group", [(i, i ^ 1) for i in range(count)])


def halves(values, axis, at):
    low, high = jnp.split(values, 2, axis=axis)
    first = at == 0
    return jnp.where(first, low, high), jnp.where(first, high, low)


def ordered(own, other, axis, at):
    first = at == 0
    return jnp.concatenate(
        [jnp.where(first, own, other), jnp.where(first, other, own)], axis=axis
    )


def places(lengths_group, index):
    ends = jnp.cumsum(lengths_group)
    passed = (index[:, None] >= ends[None, :]).astype(jnp.int32)
    segment = jnp.sum(passed, axis=1)
    place = index - jnp.sum(passed * lengths_group[None, :], axis=1)
    return (segment, place)


def rope_tables(place, width):
    half = width // 2
    freq = THETA ** (-(jnp.arange(half, dtype=F32) * 2.0 / width))
    angle = place.astype(F32)[:, None] * freq[None, :]
    cosines = jnp.concatenate([jnp.cos(angle), jnp.cos(angle)], axis=1)
    sines = jnp.concatenate([jnp.sin(angle), jnp.sin(angle)], axis=1)
    return (cosines, sines)


TILE = 256
HOP = 2
WIDE = 128
EARLY = 6
AHEAD = 2
LATE = 3


def nt(a, b):
    return lax.dot_general(a, b, (((1,), (1,)), ((), ())), preferred_element_type=F32)


def nn(a, b):
    return jnp.dot(a, b, preferred_element_type=F32)


def copy_to(src, dst, send_sem, recv_sem, peer):
    return pltpu.make_async_remote_copy(
        src_ref=src, dst_ref=dst, send_sem=send_sem, recv_sem=recv_sem,
        device_id=peer, device_id_type=MESH,
    )


def tile(i, size=TILE):
    return pl.ds(pl.multiple_of(i * size, size), size)


class Place:
    def __init__(self, count):
        group = lax.axis_index("group")
        self.line = count // 2
        self.root = (self.line - 1) // 2
        self.deep = max(self.root, self.line - 1 - self.root)
        self.at = group // 2
        self.side = group % 2
        self.x_peer = {"row": 1 - lax.axis_index("row")}
        self.core_peer = {"col": 1 - lax.axis_index("col")}
        self.y_peer = {"group": group + 1 - 2 * self.side}
        self.above = {"group": jnp.minimum(group + 2, count - 1)}
        self.below = {"group": jnp.maximum(group - 2, 0)}
        self.has_above = self.at < self.line - 1
        self.has_below = self.at > 0

    def meet(self):
        barrier = pltpu.get_barrier_semaphore()

        def greet(peer):
            pl.semaphore_signal(barrier, inc=1, device_id=peer, device_id_type=MESH)

        for peer in (self.x_peer, self.core_peer, self.y_peer):
            greet(peer)
        pl.when(self.has_above)(lambda: greet(self.above))
        pl.when(self.has_below)(lambda: greet(self.below))
        met = 3 + self.has_above.astype(jnp.int32) + self.has_below.astype(jnp.int32)
        pl.semaphore_wait(barrier, met)


class Chain:
    def __init__(self, place, chunks, kinds, total, came, home, add, sems, share=True):
        self.place, self.chunks, self.kinds = place, chunks, kinds
        self.total, self.came, self.home, self.add = total, came, home, add
        self.sems, self.share = sems, share

    def part_copy(self, c, k, upward):
        sent, low, high = self.sems[:3]
        p = self.kinds * c + k
        peer, which, arrived = (
            (self.place.above, 0, low) if upward else (self.place.below, 1, high)
        )
        return copy_to(
            self.total(c, k), self.came(c, k, which), sent.at[p], arrived.at[p], peer
        )

    def final_copy(self, c, k, upward, first):
        up, down, arrived = self.sems[3:6]
        p = self.kinds * c + k
        src = self.total(c, k) if first else self.home(c, k, self.place.side)
        peer, sent = (self.place.above, up) if upward else (self.place.below, down)
        return copy_to(src, self.home(c, k, self.place.side), sent.at[p], arrived.at[p], peer)

    def keep_copy(self, c, k):
        return pltpu.make_async_copy(
            self.total(c, k), self.home(c, k, self.place.side),
            self.sems[6].at[self.kinds * c + k],
        )

    def share_copy(self, c, k, first, of=None):
        p = self.kinds * c + k
        of = self.place.side if of is None else of
        src = self.total(c, k) if first else self.home(c, k, self.place.side)
        return copy_to(
            src, self.home(c, k, of), self.sems[7].at[p], self.sems[8].at[p], self.place.y_peer
        )

    def step(self, u, hop=1):
        at, line, root, deep = self.place.at, self.place.line, self.place.root, self.place.deep
        behind = jnp.where(at < root, at, jnp.where(at > root, line - 1 - at, deep))
        self.inward(u - hop * behind)
        self.outward(u - hop * (deep + jnp.abs(at - root)))

    def kinds_of(self, p):
        live = (p >= 0) & (p < self.kinds * self.chunks)
        if self.kinds == 1:
            return [(live, p, 0)]
        p = jnp.maximum(p, 0)
        return [
            (live & (lax.rem(p, self.kinds) == k), lax.div(p, self.kinds), k)
            for k in range(self.kinds)
        ]

    def inward(self, piece):
        at, line, root = self.place.at, self.place.line, self.place.root
        for live, c, k in self.kinds_of(piece):

            @pl.when(live & (at < root))
            def _():
                @pl.when(self.place.has_below)
                def _():
                    self.part_copy(c, k, True).wait_recv()
                    self.add(c, k, 0)

                self.part_copy(c, k, True).start()

            @pl.when(live & (at > root))
            def _():
                @pl.when(self.place.has_above)
                def _():
                    self.part_copy(c, k, False).wait_recv()
                    self.add(c, k, 1)

                self.part_copy(c, k, False).start()

            @pl.when(live & (at == root))
            def _():
                if root > 0:
                    self.part_copy(c, k, True).wait_recv()
                    self.add(c, k, 0)
                if root < line - 1:
                    self.part_copy(c, k, False).wait_recv()
                    self.add(c, k, 1)
                if root > 0:
                    self.final_copy(c, k, False, True).start()
                if root < line - 1:
                    self.final_copy(c, k, True, True).start()
                if self.share:
                    self.share_copy(c, k, True).start()
                self.keep_copy(c, k).start()

    def outward(self, piece):
        at, root = self.place.at, self.place.root
        for live, c, k in self.kinds_of(piece):

            @pl.when(live & (at != root))
            def _():
                self.final_copy(c, k, True, False).wait_recv()

                @pl.when((at > root) & self.place.has_above)
                def _():
                    self.final_copy(c, k, True, False).start()

                @pl.when((at < root) & self.place.has_below)
                def _():
                    self.final_copy(c, k, False, False).start()

                if self.share:
                    self.share_copy(c, k, False).start()

    def steps(self, hop=1):
        return self.kinds * self.chunks + 2 * hop * self.place.deep

    def drain(self):
        at, line, root = self.place.at, self.place.line, self.place.root

        @pl.loop(0, self.chunks)
        def _(c):
            for k in range(self.kinds):
                if self.share:
                    self.share_copy(c, k, False, 1 - self.place.side).wait_recv()
                    self.share_copy(c, k, False).wait_send()

                @pl.when(at == root)
                def _():
                    self.keep_copy(c, k).wait()
                    if root > 0:
                        self.final_copy(c, k, False, True).wait_send()
                    if root < line - 1:
                        self.final_copy(c, k, True, True).wait_send()

                @pl.when(at < root)
                def _():
                    self.part_copy(c, k, True).wait_send()

                    @pl.when(self.place.has_below)
                    def _():
                        self.final_copy(c, k, False, False).wait_send()

                @pl.when(at > root)
                def _():
                    self.part_copy(c, k, False).wait_send()

                    @pl.when(self.place.has_above)
                    def _():
                        self.final_copy(c, k, True, False).wait_send()


def chain_semaphores(pieces):
    return [pltpu.SemaphoreType.DMA((pieces,)) for _ in range(9)]


def ffn_kernel(
    count, chunks, h_ref, top_ref, early_ref, gate_ref, up_ref, down_ref,
    pair_grads_ref, down_grads_ref, late_pair_ref, late_down_ref, pair_came_ref, down_came_ref,
    branch_ref, branch_out_ref, back_ref,
    h_all, h_turned, sent, came, top_sent, top_came, grad_part, w_pair, w_down, acc_branch, acc_back, parts, inner_turned,
    pair_total, down_total, pair_stage, down_stage, reduce_recv,
    gather_send, gather_recv, x_send, x_recv, top_send, top_recv, late_sem, load_sem, weight_sem, fold_send, fold_recv,
    *chain_sems,
):
    place = Place(count)
    rows, width = h_ref.shape
    tokens = h_all.shape[0]
    tiles = tokens // TILE
    wide = w_down.shape[0] // chunks
    side = place.side

    def weight_copies(j):
        cols = tile(side * chunks + j, wide)
        return (
            pltpu.make_async_copy(
                gate_ref.at[:, cols], w_pair.at[j, :, pl.ds(0, wide)], weight_sem.at[0, j]
            ),
            pltpu.make_async_copy(
                up_ref.at[:, cols], w_pair.at[j, :, pl.ds(wide, wide)], weight_sem.at[1, j]
            ),
            pltpu.make_async_copy(
                down_ref.at[cols, :], w_down.at[tile(j, wide), :], weight_sem.at[2, j]
            ),
        )

    @pl.loop(0, chunks)
    def _(j):
        for copy in weight_copies(j):
            copy.start()

    place.meet()

    def slot(i):
        return pl.ds(i * rows, rows)

    to_y = copy_to(h_ref, h_all.at[slot(2)], gather_send.at[0], gather_recv.at[0], place.y_peer)
    to_core = copy_to(
        h_ref, h_all.at[slot(1)], gather_send.at[1], gather_recv.at[1], place.core_peer
    )
    forward = copy_to(
        h_all.at[slot(2)], h_all.at[slot(3)], gather_send.at[2], gather_recv.at[2],
        place.core_peer,
    )
    to_y.start()
    to_core.start()

    def top_exchange(j):
        n = j - EARLY
        return copy_to(
            top_sent.at[n], top_came.at[n], top_send.at[n], top_recv.at[n], place.x_peer
        )

    def top_project(j):
        @pl.loop(0, tiles)
        def _(i):
            top_sent[j - EARLY, tile(i), :] = nt(
                top_ref[tile(i), :], w_down[tile(j, wide), :]
            ).astype(BF16)

        top_exchange(j).start()

    def exchange(j):
        return copy_to(
            sent.at[lax.rem(j, 3)], came.at[j], x_send.at[j], x_recv.at[j], place.x_peer
        )

    def first_half(i):
        at_rows = pl.ds(2 * i * rows, 2 * rows)
        n = i * chunks
        return copy_to(
            sent.at[0, at_rows, :], came.at[0, at_rows, :], x_send.at[n], x_recv.at[n],
            place.x_peer,
        )

    def project_half(i):
        for n in range(2):
            at_rows = slot(2 * i + n)
            sent[0, at_rows, :] = nn(h_all[at_rows, :], w_pair[0]).astype(BF16)
        first_half(i).start()

    def project(j):
        for copy in weight_copies(j)[:2]:
            copy.wait()

        @pl.loop(0, tiles)
        def _(i):
            sent[lax.rem(j, 3), tile(i), :] = nn(h_all[tile(i), :], w_pair[j]).astype(BF16)

    def work(j):
        @pl.when(j == 0)
        def _():
            first_half(0).wait_recv()
            first_half(1).wait_recv()

        @pl.when(j > 0)
        def _():
            exchange(j).wait_recv()

        @pl.when(j < EARLY)
        def _():
            grad_part[...] = early_ref[:, tile(j, wide)].astype(F32)

        @pl.when(j >= EARLY)
        def _():
            top_exchange(j).wait_recv()
            grad_part[...] = top_sent[j - EARLY].astype(F32) + top_came[j - EARLY].astype(F32)

        @pl.loop(0, tiles)
        def _(i):
            at_rows = tile(i)
            pair = sent[lax.rem(j, 3), at_rows, :].astype(F32) + came[j, at_rows, :].astype(F32)
            gate, up = pair[:, :wide], pair[:, wide:]
            grad = grad_part[at_rows, :]
            sig = 1.0 / (1.0 + jnp.exp(-gate))
            silu = gate * sig
            parts[at_rows, pl.ds(0, wide)] = (
                grad * up * (sig * (1.0 + gate * (1.0 - sig)))
            ).astype(BF16)
            parts[at_rows, pl.ds(wide, wide)] = (grad * silu).astype(BF16)
            inner = (silu * up).astype(BF16)
            inner_turned[:, at_rows] = inner.T
            acc_branch[at_rows, :] += nn(inner, w_down[tile(j, wide), :])
            acc_back[at_rows, :] += nt(parts[at_rows, :], w_pair[j])

    def gradients(j):
        @pl.loop(0, width // TILE)
        def _(i):
            pair = nn(h_turned[tile(i), :], parts[...])
            pair_total[j, 0, tile(i), :] = pair[:, :wide].astype(BF16)
            pair_total[j, 1, tile(i), :] = pair[:, wide:].astype(BF16)
            down_total[j, :, tile(i)] = nn(inner_turned[...], top_ref[:, tile(i)]).astype(BF16)

    def total(c, k):
        return down_total.at[c] if k == 2 else pair_total.at[c, k]

    def landed(c, k, which):
        return down_came_ref.at[which, c] if k == 2 else pair_came_ref.at[which, c, k]

    def home(c, k, of):
        at_cols = tile(of * chunks + c, wide)
        return down_grads_ref.at[at_cols, :] if k == 2 else pair_grads_ref.at[k, :, at_cols]

    def add(c, k, which):
        stage = (down_stage if k == 2 else pair_stage).at[which]
        copy = pltpu.make_async_copy(landed(c, k, which), stage, load_sem.at[which])
        copy.start()
        copy.wait()
        into = total(c, k)

        @pl.loop(0, into.shape[0] // wide)
        def _(i):
            at_rows = tile(i, wide)
            into[at_rows, :] = (
                into[at_rows, :].astype(F32) + stage[at_rows, :].astype(F32)
            ).astype(BF16)

    ours = chunks - LATE
    chain = Chain(place, ours, 3, total, landed, home, add, chain_sems)

    def late_copies(c):
        return (
            pltpu.make_async_copy(pair_total.at[c], late_pair_ref.at[c - ours], late_sem.at[0, c - ours]),
            pltpu.make_async_copy(down_total.at[c], late_down_ref.at[c - ours], late_sem.at[1, c - ours]),
        )

    h_all[slot(0), :] = h_ref[...]
    for copy in weight_copies(0)[:2]:
        copy.wait()
    to_core.wait_recv()
    project_half(0)

    @pl.loop(0, chunks)
    def _(j):
        weight_copies(j)[2].wait()

    @pl.loop(EARLY, min(EARLY + AHEAD, chunks))
    def _(j):
        top_project(j)

    acc_branch[...] = jnp.zeros_like(acc_branch)
    acc_back[...] = jnp.zeros_like(acc_back)
    to_y.wait_recv()
    forward.start()
    forward.wait_recv()
    project_half(1)
    project(1)

    @pl.loop(0, tiles)
    def _(i):
        h_turned[:, tile(i)] = h_all[tile(i), :].T

    first_half(0).wait_send()
    first_half(1).wait_send()
    exchange(1).start()

    @pl.loop(0, chunks)
    def _(t):
        work(t)
        chain.step(3 * t - 1, HOP)
        gradients(t)

        @pl.when(t >= ours)
        def _():
            for copy in late_copies(t):
                copy.start()

        chain.step(3 * t, HOP)

        @pl.when(t + 2 < chunks)
        def _():
            @pl.when(t >= 2)
            def _():
                exchange(t - 1).wait_send()

            project(t + 2)
            exchange(t + 2).start()

        @pl.when((t + AHEAD >= EARLY + AHEAD) & (t + AHEAD < chunks))
        def _():
            top_project(t + AHEAD)

        chain.step(3 * t + 1, HOP)

    chain.step(3 * chunks - 1, HOP)

    def fold_source(n, i):
        if i == 2:
            return w_down.at[slot(0), :]
        return h_all.at[slot(2 * n + i), :]

    def fold(n, i):
        return copy_to(
            fold_source(n, i), reduce_recv.at[n, i], fold_send.at[n, i], fold_recv.at[n, i],
            place.y_peer if i == 2 else place.core_peer,
        )

    to_y.wait_send()
    to_core.wait_send()
    forward.wait_send()
    for n, acc in enumerate((acc_back, acc_branch)):
        for i in (1, 0):
            fold_source(n, i)[...] = acc[slot(2 * i + 1), :].astype(BF16)
            fold(n, i).start()
    fold(0, 1).wait_recv()
    fold_source(0, 2)[...] = (acc_back[slot(2), :] + reduce_recv[0, 1].astype(F32)).astype(BF16)
    fold(0, 2).start()
    chain.step(3 * chunks, HOP)
    fold(1, 0).wait_recv()
    fold(1, 1).wait_recv()
    branch_ref[...] = acc_branch[slot(0), :] + reduce_recv[1, 0].astype(F32)
    branch_out_ref[...] = (acc_branch[slot(2), :] + reduce_recv[1, 1].astype(F32)).astype(BF16)
    fold(0, 0).wait_recv()
    fold(0, 2).wait_recv()
    back_ref[...] = (
        acc_back[slot(0), :] + reduce_recv[0, 0].astype(F32) + reduce_recv[0, 2].astype(F32)
    )

    @pl.loop(3 * chunks + 1, max(3 * chunks + 1, chain.steps(HOP)))
    def _(u):
        chain.step(u, HOP)

    @pl.loop(ours, chunks)
    def _(c):
        for copy in late_copies(c):
            copy.wait()

    chain.drain()

    @pl.loop(max(chunks - 3, 0), chunks)
    def _(j):
        exchange(j).wait_send()

    @pl.loop(EARLY, chunks)
    def _(j):
        top_exchange(j).wait_send()

    for n, i in ((0, 0), (0, 1), (0, 2), (1, 0), (1, 1)):
        fold(n, i).wait_send()


def ffn(h, top, early, w_gate, w_up, w_down):
    count = lax.axis_size("group")
    rows, width = h.shape
    hidden = w_gate.shape[1] // 2
    wide = WIDE
    chunks = hidden // wide
    tokens = 4 * rows
    anywhere = pl.BlockSpec(memory_space=pl.ANY)
    local = pl.BlockSpec(memory_space=pltpu.VMEM)
    dma = pltpu.SemaphoreType.DMA
    pieces = 3 * (chunks - LATE)
    flops = 2 * tokens * width * hidden * 8
    return pl.pallas_call(
        functools.partial(ffn_kernel, count, chunks),
        out_shape=(
            jax.ShapeDtypeStruct((2, width, 2 * hidden), BF16),
            jax.ShapeDtypeStruct((2 * hidden, width), BF16),
            jax.ShapeDtypeStruct((LATE, 2, width, wide), BF16),
            jax.ShapeDtypeStruct((LATE, wide, width), BF16),
            jax.ShapeDtypeStruct((2, chunks - LATE, 2, width, wide), BF16),
            jax.ShapeDtypeStruct((2, chunks - LATE, wide, width), BF16),
            jax.ShapeDtypeStruct((rows, width), F32),
            jax.ShapeDtypeStruct((rows, width), BF16),
            jax.ShapeDtypeStruct((rows, width), F32),
        ),
        in_specs=[local, local, local, anywhere, anywhere, anywhere],
        out_specs=(anywhere,) * 6 + (local,) * 3,
        scratch_shapes=[
            pltpu.VMEM((tokens, width), BF16),
            pltpu.VMEM((width, tokens), BF16),
            pltpu.VMEM((3, tokens, 2 * wide), BF16),
            pltpu.VMEM((chunks, tokens, 2 * wide), BF16),
            pltpu.VMEM((chunks - EARLY, tokens, wide), BF16),
            pltpu.VMEM((chunks - EARLY, tokens, wide), BF16),
            pltpu.VMEM((tokens, wide), F32),
            pltpu.VMEM((chunks, width, 2 * wide), BF16),
            pltpu.VMEM((hidden, width), BF16),
            pltpu.VMEM((tokens, width), F32),
            pltpu.VMEM((tokens, width), F32),
            pltpu.VMEM((tokens, 2 * wide), BF16),
            pltpu.VMEM((wide, tokens), BF16),
            pltpu.VMEM((chunks, 2, width, wide), BF16),
            pltpu.VMEM((chunks, wide, width), BF16),
            pltpu.VMEM((2, width, wide), BF16),
            pltpu.VMEM((2, wide, width), BF16),
            pltpu.VMEM((2, 3, rows, width), BF16),
            dma((3,)), dma((3,)), dma((chunks + 1,)), dma((chunks + 1,)),
            dma((chunks - EARLY,)), dma((chunks - EARLY,)),
            dma((2, LATE)), dma((2,)), dma((3, chunks)), dma((2, 3)), dma((2, 3)),
            *chain_semaphores(pieces),
        ],
        compiler_params=pltpu.CompilerParams(
            collective_id=1, has_side_effects=True, vmem_limit_bytes=63 << 20
        ),
        cost_estimate=pl.CostEstimate(
            flops=flops, bytes_accessed=200 << 20, transcendentals=tokens * hidden
        ),
    )(h, top, early, w_gate, w_up, w_down)


ROWS = 128


def sigmoid(v):
    return 1.0 / (1.0 + jnp.exp(-v))


def each_tile(start, count, size=160):
    def run(step):
        @pl.loop(0, count // size)
        def _(i):
            step(pl.ds(pl.multiple_of(start + i * size, 32), size))

    return run


def column(values):
    return jnp.broadcast_to(values, (values.shape[0], 128))


def front_kernel(
    count, heads, kv_heads, tok_ref, top_ref, norm_ref, second_ref, q_gain_ref, k_gain_ref,
    cos_ref, sin_ref, at_ref, start_ref, key_at_ref, w_gates_ref, wq_ref, wk_ref, wv_ref, wo_ref,
    wd_ref,
    h_ref, resid_ref, inv_two_ref, hat_ref, inv_one_ref, turned_ref, tops_ref, early_ref,
    raw_ref, sig_ref, q_ref, k_ref, v_ref, log_ref, attended_ref, gated_ref,
    normed_all, wq, wk, wv, wo, wd, kv_send, kv_came, q_send, q_came, gates, early_send, early_came,
    ss_send, ss_came, fold_src, fold_dst, acc,
    w_sem, n_send, n_recv, t_send, t_recv, p_send, p_recv, e_send, e_recv, g_send, g_recv,
    s_send, s_recv,
):
    place = Place(count)
    rows, width = tok_ref.shape
    tokens = 2 * rows
    row_at = lax.axis_index("row")
    side = place.side
    hd = 128
    qw, kw = heads * hd, kv_heads * hd
    hidden = wd_ref.shape[0] // 2
    scale = hd**-0.5

    loads = []
    for i, at in enumerate((row_at, 1 - row_at)):
        q_cols, k_cols = tile(at, qw), tile(at, kw)
        loads += [
            pltpu.make_async_copy(wk_ref.at[:, k_cols], wk.at[i], w_sem.at[i, 0]),
            pltpu.make_async_copy(wv_ref.at[:, k_cols], wv.at[i], w_sem.at[i, 1]),
            pltpu.make_async_copy(wq_ref.at[:, q_cols], wq.at[i], w_sem.at[i, 2]),
            pltpu.make_async_copy(wo_ref.at[q_cols, :], wo.at[i], w_sem.at[i, 3]),
        ]
    down_rows = pl.ds(pl.multiple_of(side * hidden, WIDE), wd.shape[0])
    loads.append(pltpu.make_async_copy(wd_ref.at[down_rows, :], wd, w_sem.at[0, 4]))
    for copy in loads:
        copy.start()
    place.meet()

    def slot(i):
        return pl.ds(i * rows, rows)

    def spread(ref, sends, recvs):
        own, core, pair, both = (ref.at[slot(i), :] for i in range(4))
        return (
            copy_to(own, core, sends.at[0], recvs.at[0], place.core_peer),
            copy_to(own, pair, sends.at[1], recvs.at[1], place.y_peer),
            copy_to(pair, both, sends.at[2], recvs.at[2], place.core_peer),
        )

    tops_ref[slot(0), :] = top_ref[...]
    tops = spread(tops_ref, t_send, t_recv)
    tops[0].start()
    tops[1].start()

    def squares(n):
        return copy_to(ss_send.at[n], ss_came.at[n], s_send.at[n], s_recv.at[n], place.x_peer)

    x = tok_ref[...].astype(F32)
    ss_send[0] = column(jnp.sum(x * x, axis=1, keepdims=True))
    squares(0).start()

    def early(i):
        return copy_to(
            early_send.at[slot(i), :], early_came.at[slot(i), :], e_send.at[i], e_recv.at[i],
            place.x_peer,
        )

    def early_start(i):
        @each_tile(i * rows, rows)
        def _(at_rows):
            early_send[at_rows, :] = nt(tops_ref[at_rows, :], wd[...]).astype(BF16)

        early(i).start()

    loads[-1].wait()
    early_start(0)
    squares(0).wait()
    inv_one = lax.rsqrt((ss_send[0] + ss_came[0]) / (2 * width) + EPS)
    inv_one_ref[...] = inv_one
    hat = tok_ref[...].astype(F32) * inv_one[:, :1]
    hat_ref[...] = hat
    normed_all[slot(0), :] = (hat * norm_ref[...]).astype(BF16)
    normed = spread(normed_all, n_send, n_recv)
    normed[0].start()
    normed[1].start()

    kv_copy = copy_to(kv_send, kv_came, p_send.at[0], p_recv.at[0], place.x_peer)
    q_copy = copy_to(q_send, q_came, p_send.at[1], p_recv.at[1], place.x_peer)
    for copy in loads[:-1]:
        copy.wait()
    for i in range(2):
        if i == 1:
            normed[0].wait_recv()

        @each_tile(i * rows, rows)
        def _(at_rows):
            rows_in = normed_all[at_rows, :]
            kv_send[at_rows, pl.ds(0, kw)] = nn(rows_in, wk[1]).astype(BF16)
            kv_send[at_rows, pl.ds(kw, kw)] = nn(rows_in, wv[1]).astype(BF16)

    kv_copy.start()

    @each_tile(0, tokens)
    def _(at_rows):
        rows_in = normed_all[at_rows, :]
        q_send[at_rows, pl.ds(0, qw)] = nn(rows_in, wq[1]).astype(BF16)
        part = nn(rows_in, w_gates_ref[...])
        gates[at_rows, :] = part
        q_send[at_rows, pl.ds(qw, 128)] = part.astype(BF16)

    q_copy.start()

    @each_tile(0, tokens)
    def _(at_rows):
        rows_in = normed_all[at_rows, :]
        raw_ref[at_rows, pl.ds(0, qw)] = nn(rows_in, wq[0])
        raw_ref[at_rows, pl.ds(qw, kw)] = nn(rows_in, wk[0])
        raw_ref[at_rows, pl.ds(qw + kw, kw)] = nn(rows_in, wv[0])


    def turn(values, gain, at_rows):
        inverse = lax.rsqrt(jnp.mean(values * values, axis=1, keepdims=True) + EPS)
        scaled = values * inverse * gain
        return scaled * cos_ref[at_rows, :] + pltpu.roll(scaled, 64, axis=1) * sin_ref[at_rows, :]

    tops[1].wait_recv()
    tops[2].start()
    normed[1].wait_recv()
    normed[2].start()
    tops[0].wait_recv()
    kv_copy.wait_recv()

    @pl.loop(0, tokens // ROWS)
    def _(i):
        at_rows = tile(i, ROWS)
        for n in range(kv_heads):
            cols = pl.ds(qw + n * hd, hd)
            key = raw_ref[at_rows, cols] + kv_came[at_rows, pl.ds(n * hd, hd)].astype(F32)
            raw_ref[at_rows, cols] = key
            k_ref[at_rows, pl.ds(n * hd, hd)] = turn(key, k_gain_ref[...], at_rows).astype(BF16)
            cols = pl.ds(qw + kw + n * hd, hd)
            value = raw_ref[at_rows, cols] + kv_came[at_rows, pl.ds(kw + n * hd, hd)].astype(F32)
            raw_ref[at_rows, cols] = value
            v_ref[at_rows, pl.ds(n * hd, hd)] = value.astype(BF16)

    q_copy.wait_recv()
    early_start(1)

    @pl.loop(0, tokens // ROWS)
    def _(i):
        at_rows = tile(i, ROWS)
        other = q_came[at_rows, pl.ds(qw, 128)].astype(F32)
        logit = gates[at_rows, :] + pltpu.roll(other, 128 - heads, axis=1)
        sig_ref[at_rows, :] = sigmoid(logit)
        for n in range(heads):
            cols = pl.ds(n * hd, hd)
            query = raw_ref[at_rows, cols] + q_came[at_rows, cols].astype(F32)
            raw_ref[at_rows, cols] = query
            q_ref[at_rows, cols] = turn(query, q_gain_ref[...], at_rows).astype(BF16)

    def head_copy(n):
        cols = pl.ds(n * hd, hd)
        return copy_to(
            gated_ref.at[0, :, cols], gated_ref.at[1, :, cols], g_send.at[n], g_recv.at[n],
            place.x_peer,
        )

    for n in range(heads):
        cols = pl.ds(n * hd, hd)
        kv = pl.ds(n * kv_heads // heads * hd, hd)

        @pl.loop(0, tokens // ROWS)
        def _(i):
            at_rows = tile(i, ROWS)
            scores = nt(q_ref[at_rows, cols], k_ref[:, kv]) * scale
            key_at = key_at_ref[:1, :]
            allowed = (key_at <= at_ref[at_rows, :1]) & (key_at >= start_ref[at_rows, :1])
            scores = jnp.where(allowed, scores, NEGATIVE)
            top = jnp.max(scores, axis=1, keepdims=True)
            raised = jnp.exp(scores - top)
            total = jnp.sum(raised, axis=1, keepdims=True)
            result = nn((raised / total).astype(BF16), v_ref[:, kv])
            log_ref[n, at_rows, :] = column(top + jnp.log(total))
            attended_ref[at_rows, cols] = result
            gated_ref[0, at_rows, cols] = (result * sig_ref[at_rows, n : n + 1]).astype(BF16)

        head_copy(n).start()
        if n == 0:
            tops[2].wait_recv()
            early_start(2)
        if n == 2:
            early_start(3)

    @each_tile(0, tokens)
    def _(at_rows):
        acc[at_rows, :] = nn(gated_ref[0, at_rows, :], wo[0])

    def turn_rows(first, last):
        @pl.loop(first, last)
        def _(i):
            turned_ref[:, tile(i, ROWS)] = normed_all[tile(i, ROWS), :].T

    turn_rows(0, tokens // ROWS)
    for n in range(heads):
        head_copy(n).wait_recv()
    fold = copy_to(fold_src, fold_dst, s_send.at[2], s_recv.at[2], place.core_peer)

    @each_tile(0, rows)
    def _(at_rows):
        there = pl.ds(pl.multiple_of(at_rows.start + rows, 32), at_rows.size)
        fold_src[at_rows, :] = (acc[there, :] + nn(gated_ref[1, there, :], wo[1])).astype(BF16)

    fold.start()

    @each_tile(0, rows)
    def _(at_rows):
        acc[at_rows, :] += nn(gated_ref[1, at_rows, :], wo[1])

    normed[2].wait_recv()
    fold.wait_recv()
    resid = tok_ref[...].astype(F32) + acc[slot(0), :] + fold_dst[...].astype(F32)
    resid_ref[...] = resid
    ss_send[1] = column(jnp.sum(resid * resid, axis=1, keepdims=True))
    squares(1).start()
    turn_rows(tokens // ROWS, 2 * tokens // ROWS)
    for i in range(4):
        early(i).wait_recv()
        early_ref[slot(i), :] = (
            early_send[slot(i), :].astype(F32) + early_came[slot(i), :].astype(F32)
        ).astype(BF16)
    squares(1).wait()
    inv_two = lax.rsqrt((ss_send[1] + ss_came[1]) / (2 * width) + EPS)
    inv_two_ref[...] = inv_two
    h_ref[...] = (resid_ref[...] * inv_two[:, :1] * second_ref[...]).astype(BF16)

    for copy in (*tops, *normed, kv_copy, q_copy, fold):
        copy.wait_send()
    for i in range(4):
        early(i).wait_send()
    for n in range(heads):
        head_copy(n).wait_send()


def front(
    tok, top, norm_gain, ffn_gain, q_gain, k_gain, cos, sin, at, start, key_at, w_gates,
    wq, wk, wv, wo, wd,
):
    count = lax.axis_size("group")
    rows, width = tok.shape
    tokens = 2 * rows
    hd = 128
    heads, kv_heads = wq.shape[1] // 2 // hd, wk.shape[1] // 2 // hd
    qw, kw = heads * hd, kv_heads * hd
    early = EARLY * WIDE
    local = pl.BlockSpec(memory_space=pltpu.VMEM)
    anywhere = pl.BlockSpec(memory_space=pl.ANY)
    dma = pltpu.SemaphoreType.DMA
    struct = jax.ShapeDtypeStruct
    return pl.pallas_call(
        functools.partial(front_kernel, count, heads, kv_heads),
        out_shape=(
            struct((rows, width), BF16),
            struct((rows, width), F32),
            struct((rows, 128), F32),
            struct((rows, width), F32),
            struct((rows, 128), F32),
            struct((width, 4 * rows), BF16),
            struct((4 * rows, width), BF16),
            struct((4 * rows, early), BF16),
            struct((tokens, qw + 2 * kw), F32),
            struct((tokens, 128), F32),
            struct((tokens, qw), BF16),
            struct((tokens, kw), BF16),
            struct((tokens, kw), BF16),
            struct((heads, tokens, 128), F32),
            struct((tokens, qw), F32),
            struct((2, tokens, qw), BF16),
        ),
        in_specs=[local] * 12 + [anywhere] * 5,
        out_specs=(local,) * 16,
        scratch_shapes=[
            pltpu.VMEM((4 * rows, width), BF16),
            pltpu.VMEM((2, width, qw), BF16),
            pltpu.VMEM((2, width, kw), BF16),
            pltpu.VMEM((2, width, kw), BF16),
            pltpu.VMEM((2, qw, width), BF16),
            pltpu.VMEM((early, width), BF16),
            pltpu.VMEM((tokens, 2 * kw), BF16),
            pltpu.VMEM((tokens, 2 * kw), BF16),
            pltpu.VMEM((tokens, qw + 128), BF16),
            pltpu.VMEM((tokens, qw + 128), BF16),
            pltpu.VMEM((tokens, 128), F32),
            pltpu.VMEM((4 * rows, early), BF16),
            pltpu.VMEM((4 * rows, early), BF16),
            pltpu.VMEM((2, rows, 128), F32),
            pltpu.VMEM((2, rows, 128), F32),
            pltpu.VMEM((rows, width), BF16),
            pltpu.VMEM((rows, width), BF16),
            pltpu.VMEM((tokens, width), F32),
            dma((2, 5)), dma((3,)), dma((3,)), dma((3,)), dma((3,)), dma((2,)), dma((2,)),
            dma((4,)), dma((4,)), dma((heads,)), dma((heads,)), dma((3,)), dma((3,)),
        ],
        compiler_params=pltpu.CompilerParams(
            collective_id=3, has_side_effects=True, vmem_limit_bytes=60 << 20
        ),
        cost_estimate=pl.CostEstimate(
            flops=6 * tokens * width * (qw + kw) * 4, bytes_accessed=40 << 20,
            transcendentals=heads * tokens * tokens,
        ),
    )(
        tok, top, norm_gain, ffn_gain, q_gain, k_gain, cos, sin, at, start, key_at, w_gates,
        wq, wk, wv, wo, wd,
    )


MISC = 88


def tn(a, b):
    return lax.dot_general(a, b, (((0,), (0,)), ((), ())), preferred_element_type=F32)


def rear_kernel(
    count, heads, kv_heads, back_ref, resid_ref, inv_two_ref, second_ref, top_ref, raw_ref,
    sig_ref, q_ref, k_ref, v_ref, log_ref, attended_ref, cos_ref, sin_ref, at_ref, start_ref,
    key_at_ref, q_gain_ref, k_gain_ref, turned_ref, gated_ref, w_gates_ref, hat_ref, inv_one_ref,
    norm_ref, wq_ref, wk_ref, wv_ref, wo_ref, late_pair_ref, late_down_ref, pair_in, down_in,
    grads_ref, input_ref, sums_ref, pair_grads_ref, down_grads_ref,
    w_main, wo, branch, block_src, dg_own, dg_send, dg_came, dk, dv, gates, gates_came, own, came, across,
    total, landed, misc, misc_came, misc_landed, misc_home, acc, fold_src, fold_dst, in_send,
    in_came, late_pair, late_down, late_pair_came, late_down_came,
    w_sem, late_sem, b_send, b_recv, d_send, d_recv, x_send, x_recv, y_send, y_recv, s_send, s_recv,
    *chain_sems,
):
    place = Place(count)
    row_at = lax.axis_index("row")
    side = place.side
    rows, width = back_ref.shape
    tokens = 2 * rows
    hd = 128
    cols = 2 * hd
    qw = heads * hd
    parts = heads // 2 + kv_heads
    high = gated_ref.shape[0]
    pieces = total.shape[0]
    scale = hd**-0.5

    loads = []
    for i, at in enumerate((row_at, 1 - row_at)):
        for n in range(kv_heads):
            q_cols, k_cols = tile(at * kv_heads + n, cols), tile(at * kv_heads + n, hd)
            first, second = w_main.at[i * parts + 2 * n], w_main.at[i * parts + 2 * n + 1]
            loads += [
                pltpu.make_async_copy(wq_ref.at[:, q_cols], first, w_sem.at[i, n, 0]),
                pltpu.make_async_copy(
                    wk_ref.at[:, k_cols], second.at[:, pl.ds(0, hd)], w_sem.at[i, n, 1]
                ),
                pltpu.make_async_copy(
                    wv_ref.at[:, k_cols], second.at[:, pl.ds(hd, hd)], w_sem.at[i, n, 2]
                ),
            ]
        loads.append(pltpu.make_async_copy(wo_ref.at[tile(at, qw), :], wo.at[i], w_sem.at[i, 0, 3]))
    for copy in loads:
        copy.start()
    late_loads = (
        pltpu.make_async_copy(late_pair_ref, late_pair, late_sem.at[0]),
        pltpu.make_async_copy(late_down_ref, late_down, late_sem.at[1]),
    )
    for copy in late_loads:
        copy.start()
    place.meet()

    def late_total(c, k):
        return late_down.at[c] if k == 2 else late_pair.at[c, k]

    def late_landed(c, k, which):
        return late_down_came.at[which, c] if k == 2 else late_pair_came.at[which, c, k]

    def late_home(c, k, of):
        chunks = down_grads_ref.shape[0] // 2 // WIDE
        at_cols = tile(of * chunks + chunks - LATE + c, WIDE)
        return down_grads_ref.at[at_cols, :] if k == 2 else pair_grads_ref.at[k, :, at_cols]

    def late_add(c, k, which):
        into, came_in = late_total(c, k), late_landed(c, k, which)
        into[...] = (into[...].astype(F32) + came_in[...].astype(F32)).astype(BF16)

    late = Chain(
        place, LATE, 3, late_total, late_landed, late_home, late_add, chain_sems[18:]
    )
    def slot(i):
        return pl.ds(i * rows, rows)

    def inner_copy(n):
        return copy_to(in_send.at[n], in_came.at[n], s_send.at[n], s_recv.at[n], place.x_peer)

    def store_row(at, values):
        for i in range(width // 128):
            misc[at + i : at + i + 1, :] = values[:, i * 128 : (i + 1) * 128]

    misc[...] = jnp.zeros_like(misc)
    grad = back_ref[...]
    in_send[0] = column(jnp.sum(grad * second_ref[...] * resid_ref[...], axis=1, keepdims=True))
    inner_copy(0).start()
    for copy in late_loads:
        copy.wait()
    late.step(0, HOP)
    inv_two = inv_two_ref[:, :1]
    store_row(8, jnp.sum(back_ref[...] * resid_ref[...] * inv_two, axis=0, keepdims=True))
    inner_copy(0).wait()
    inner = (in_send[0, :, :1] + in_came[0, :, :1]) * inv_two * inv_two * inv_two / (2 * width)
    d_resid = (
        top_ref[...].astype(F32)
        + inv_two * (back_ref[...] * second_ref[...])
        - resid_ref[...] * inner
    )
    input_ref[...] = d_resid
    branch[slot(0), :] = d_resid.astype(BF16)
    to_core = copy_to(
        branch.at[slot(0), :], branch.at[slot(1), :], b_send.at[0], b_recv.at[0], place.core_peer
    )
    to_pair = copy_to(
        branch.at[slot(0), :], branch.at[slot(2), :], b_send.at[1], b_recv.at[1], place.y_peer
    )
    forward = copy_to(
        branch.at[slot(2), :], branch.at[slot(3), :], b_send.at[2], b_recv.at[2],
        place.core_peer,
    )
    to_core.start()
    to_pair.start()
    late.step(1, HOP)

    def dg_copy(n):
        at_cols = pl.ds(n * cols, cols)
        return copy_to(
            dg_send.at[:, at_cols], dg_came.at[:, at_cols], d_send.at[n], d_recv.at[n],
            place.x_peer,
        )

    for copy in loads:
        copy.wait()
    halves_of = heads // 2
    for i in range(2):
        if i == 1:
            to_core.wait_recv()

        @each_tile(i * rows, rows)
        def _(at_rows):
            dg_send[at_rows, :] = nt(branch[at_rows, :], wo[1]).astype(BF16)

    for n in range(halves_of):
        dg_copy(n).start()
    late.step(2, HOP)

    @each_tile(0, tokens)
    def _(at_rows):
        dg_own[at_rows, :] = nt(branch[at_rows, :], wo[0])

    dk[...] = jnp.zeros_like(dk)
    dv[...] = jnp.zeros_like(dv)
    gates[...] = jnp.zeros_like(gates)

    def unturn(values, at_rows):
        return values * cos_ref[at_rows, :] - pltpu.roll(values, 64, axis=1) * sin_ref[at_rows, :]

    def norm_back(values, raw, gain, at_rows, into):
        normed = unturn(values, at_rows)
        inverse = lax.rsqrt(jnp.mean(raw * raw, axis=1, keepdims=True) + EPS)
        misc[into : into + 1, :] += jnp.sum(normed * raw * inverse, axis=0, keepdims=True)
        scaled = normed * gain
        inner = jnp.mean(scaled * raw, axis=1, keepdims=True)
        return inverse * scaled - raw * (inverse * inverse * inverse * inner)

    lane = lax.broadcasted_iota(jnp.int32, (ROWS, 128), 1)

    def head(n):
        at_cols = pl.ds(n * hd, hd)
        kv = n * kv_heads // heads
        kv_cols = pl.ds(kv * hd, hd)

        @pl.loop(0, tokens // ROWS)
        def _(i):
            at_rows = tile(i, ROWS)
            query = q_ref[at_rows, at_cols]
            d_gated = dg_own[at_rows, at_cols] + dg_came[at_rows, at_cols].astype(F32)
            sig = sig_ref[at_rows, n : n + 1]
            d_att = (d_gated * sig).astype(BF16)
            d_logit = jnp.sum(d_gated * attended_ref[at_rows, at_cols], axis=1, keepdims=True)
            d_logit = d_logit * sig * (1.0 - sig)
            gates[at_rows, :] = jnp.where(lane == n, d_logit.astype(BF16), gates[at_rows, :])
            scores = nt(query, k_ref[:, kv_cols]) * scale
            key_at = key_at_ref[:1, :]
            allowed = (key_at <= at_ref[at_rows, :1]) & (key_at >= start_ref[at_rows, :1])
            probs = jnp.exp(jnp.where(allowed, scores, NEGATIVE) - log_ref[n, at_rows, :1])
            d_probs = nt(d_att, v_ref[:, kv_cols])
            mean = jnp.sum(d_probs * probs, axis=1, keepdims=True)
            d_scores = (probs * (d_probs - mean)).astype(BF16)
            dv[:, kv_cols] += tn(probs.astype(BF16), d_att)
            dk[:, kv_cols] += tn(d_scores, query)
            d_query = nn(d_scores, k_ref[:, kv_cols]) * scale
            own[2 * (n // 2), at_rows, pl.ds(n % 2 * hd, hd)] = norm_back(
                d_query, raw_ref[at_rows, at_cols], q_gain_ref[...], at_rows, 80
            ).astype(BF16)

    def key_value(n):
        kv_cols = pl.ds(n * hd, hd)

        @pl.loop(0, tokens // ROWS)
        def _(i):
            at_rows = tile(i, ROWS)
            raw = raw_ref[at_rows, pl.ds(qw + n * hd, hd)]
            own[2 * n + 1, at_rows, pl.ds(0, hd)] = norm_back(
                dk[at_rows, kv_cols] * scale, raw, k_gain_ref[...], at_rows, 81
            ).astype(BF16)
            own[2 * n + 1, at_rows, pl.ds(hd, hd)] = dv[at_rows, kv_cols].astype(BF16)

    def over_x(j):
        return copy_to(own.at[j], came.at[j], x_send.at[j], x_recv.at[j], place.x_peer)

    def over_y(j, mine):
        src = own.at[j] if mine else came.at[j]
        return copy_to(src, across.at[j], y_send.at[j], y_recv.at[j], place.y_peer)

    def send_chunk(j):
        over_x(j).start()

        @pl.when(side == 1)
        def _():
            over_y(j, True).start()

    def take_chunk(j):
        over_x(j).wait_recv()

        @pl.when(side == 0)
        def _():
            over_y(j, False).start()

    def add(c, k, which):
        total[c] = (total[c].astype(F32) + landed[which, c].astype(F32)).astype(BF16)

    chain = Chain(
        place, pieces, 1,
        lambda c, k: total.at[c],
        lambda c, k, which: landed.at[which, c],
        lambda c, k, of: grads_ref.at[of * pieces + c],
        add, chain_sems[:9],
    )

    def add_misc(c, k, which):
        misc[...] += misc_landed[which]

    small = Chain(
        place, 1, 1,
        lambda c, k: misc,
        lambda c, k, which: misc_landed.at[which],
        lambda c, k, of: misc_home,
        add_misc, chain_sems[9:18], share=False,
    )

    left = 3 * LATE
    outs = pieces - 2 * parts

    def step(u):
        if u < late.steps(HOP):
            late.step(u, HOP)
        if u >= left:
            chain.step(u - left, HOP)

    def out_piece(t):
        total[t] = nn(gated_ref[...], branch[:, pl.ds(t * cols, cols)]).astype(BF16)

    def block(j):
        over_y(j, True).wait_recv()
        block_src[...] = jnp.where(side == 0, own[j], came[j])
        for i in range(2):

            @each_tile(0, high, TILE)
            def _(at_rows):
                there = pl.ds(pl.multiple_of(at_rows.start + i * high, TILE), at_rows.size)
                total[outs + 2 * j + i, at_rows, :] = (
                    nn(turned_ref[there, pl.ds(0, tokens)], block_src[...])
                    + nn(turned_ref[there, pl.ds(tokens, tokens)], across[j])
                ).astype(BF16)

    def gates_copy():
        return copy_to(gates, gates_came, s_send.at[2], s_recv.at[2], place.x_peer)

    step(3)
    for n in range(kv_heads):
        dg_copy(n).wait_recv()
        head(2 * n)
        head(2 * n + 1)
        key_value(n)
        send_chunk(2 * n)
        send_chunk(2 * n + 1)
        if n == 0:
            to_pair.wait_recv()
            forward.start()
            step(4)
    gates_copy().start()

    def back_came(j):
        take_chunk(j)

        @each_tile(0, tokens)
        def _(at_rows):
            acc[at_rows, :] += nt(came[j, at_rows, :], w_main[parts + j])


    step(5)

    @each_tile(0, tokens)
    def _(at_rows):
        found = nt(own[0, at_rows, :], w_main[0])
        for j in range(1, parts):
            found += nt(own[j, at_rows, :], w_main[j])
        acc[at_rows, :] = found

    step(6)
    back_came(0)
    step(7)
    back_came(1)
    for u in range(8, left):
        step(u)
    forward.wait_recv()
    for t in range(outs):
        out_piece(t)
        step(left + t)
        if t + 2 < parts:
            back_came(t + 2)
    at = left + outs

    gates_copy().wait()
    moved = pltpu.roll(gates_came[...].astype(F32), heads, axis=1)
    both = (gates[...].astype(F32) + moved).astype(BF16)
    gates[...] = both

    @each_tile(0, tokens)
    def _(at_rows):
        acc[at_rows, :] += nt(gates[at_rows, :], w_gates_ref[...])

    fold = copy_to(fold_src, fold_dst, s_send.at[3], s_recv.at[3], place.core_peer)
    fold_src[...] = acc[rows:, :].astype(BF16)
    fold.start()
    block(0)
    step(at)
    gate_grads = nn(turned_ref[:, pl.ds(0, tokens)], both).T
    for i in range(width // 128):
        misc[16 + 8 * i : 24 + 8 * i, :] = gate_grads[:8, i * 128 : (i + 1) * 128]

    def misc_copy(n, peer):
        return copy_to(misc, misc_came.at[n], s_send.at[4 + n], s_recv.at[4 + n], peer)

    row_of = lax.broadcasted_iota(jnp.int32, (MISC, 128), 0)
    fold.wait_recv()
    grad = acc[:rows, :] + fold_dst[...].astype(F32)
    found = grad * hat_ref[...]
    in_send[1] = column(jnp.sum(found * norm_ref[...], axis=1, keepdims=True))
    inner_copy(1).start()
    acc[:rows, :] = grad
    store_row(0, jnp.sum(found, axis=0, keepdims=True))
    misc_copy(0, place.core_peer).start()
    step(at + 1)
    block(1)
    step(at + 2)
    misc_copy(0, place.core_peer).wait()
    misc[...] += jnp.where((row_of < 16) | (row_of >= 80), misc_came[0], 0.0)
    misc_copy(1, place.x_peer).start()
    step(at + 3)
    block(2)
    step(at + 4)
    misc_copy(1, place.x_peer).wait()
    misc[...] += jnp.where(row_of >= 80, misc_came[1], 0.0)
    misc_copy(2, place.y_peer).start()
    inner_copy(1).wait()
    inner = (in_send[1, :, :1] + in_came[1, :, :1]) / (2 * width)
    input_ref[...] += inv_one_ref[:, :1] * (acc[:rows, :] * norm_ref[...] - hat_ref[...] * inner)
    step(at + 5)
    block(3)
    misc_copy(2, place.y_peer).wait()
    misc[...] += misc_came[2]
    small.step(0)
    step(at + 6)
    small.step(1)
    step(at + 7)

    @pl.loop(pieces, chain.steps(HOP))
    def _(u):
        if late.steps(HOP) > left + pieces:
            late.step(u + left, HOP)
        small.step(u - pieces + 2)
        chain.step(u, HOP)

    @pl.loop(chain.steps(HOP) - pieces + 2, small.steps())
    def _(u):
        small.step(u)

    small.drain()
    sums_ref[...] = misc_home[...]
    chain.drain()
    late.drain()
    for copy in (to_core, to_pair, forward, fold):
        copy.wait_send()
    for n in range(halves_of):
        dg_copy(n).wait_send()
    for j in range(parts):
        over_x(j).wait_send()
        over_y(j, True).wait_send()


def rear(
    back, resid, inv_two, ffn_gain, top, raw, sig, query, keys, values, log, attended, cos, sin,
    at, start, key_at, q_gain, k_gain, turned, gated, w_gates, hat, inv_one, norm_gain,
    wq, wk, wv, wo, late_pair, late_down, pair_sum, down_sum,
):
    count = lax.axis_size("group")
    rows, width = back.shape
    tokens = 2 * rows
    hd = 128
    heads, kv_heads = query.shape[1] // hd, keys.shape[1] // hd
    qw, kw = heads * hd, kv_heads * hd
    cols = 2 * hd
    parts = heads // 2 + kv_heads
    high = gated.shape[0]
    pieces = 2 * parts + width // cols
    anywhere = pl.BlockSpec(memory_space=pl.ANY)
    local = pl.BlockSpec(memory_space=pltpu.VMEM)
    dma = pltpu.SemaphoreType.DMA
    struct = jax.ShapeDtypeStruct
    return pl.pallas_call(
        functools.partial(rear_kernel, count, heads, kv_heads),
        out_shape=(
            struct((2 * pieces, high, cols), BF16),
            struct((rows, width), F32),
            struct((MISC, 128), F32),
            struct(pair_sum.shape, BF16),
            struct(down_sum.shape, BF16),
        ),
        in_specs=[local] * 25 + [anywhere] * 8,
        out_specs=(anywhere, local, local, anywhere, anywhere),
        input_output_aliases={31: 3, 32: 4},
        scratch_shapes=[
            pltpu.VMEM((2 * parts, width, cols), BF16),
            pltpu.VMEM((2, qw, width), BF16),
            pltpu.VMEM((4 * rows, width), BF16),
            pltpu.VMEM((tokens, cols), BF16),
            pltpu.VMEM((tokens, qw), F32),
            pltpu.VMEM((tokens, qw), BF16),
            pltpu.VMEM((tokens, qw), BF16),
            pltpu.VMEM((tokens, kw), F32),
            pltpu.VMEM((tokens, kw), F32),
            pltpu.VMEM((tokens, 128), BF16),
            pltpu.VMEM((tokens, 128), BF16),
            pltpu.VMEM((parts, tokens, cols), BF16),
            pltpu.VMEM((parts, tokens, cols), BF16),
            pltpu.VMEM((parts, tokens, cols), BF16),
            pltpu.VMEM((pieces, high, cols), BF16),
            pltpu.VMEM((2, pieces, high, cols), BF16),
            pltpu.VMEM((MISC, 128), F32),
            pltpu.VMEM((3, MISC, 128), F32),
            pltpu.VMEM((2, MISC, 128), F32),
            pltpu.VMEM((MISC, 128), F32),
            pltpu.VMEM((tokens, width), F32),
            pltpu.VMEM((rows, width), BF16),
            pltpu.VMEM((rows, width), BF16),
            pltpu.VMEM((2, rows, 128), F32),
            pltpu.VMEM((2, rows, 128), F32),
            pltpu.VMEM(late_pair.shape, BF16),
            pltpu.VMEM(late_down.shape, BF16),
            pltpu.VMEM((2,) + late_pair.shape, BF16),
            pltpu.VMEM((2,) + late_down.shape, BF16),
            dma((2, kv_heads, 4)), dma((2,)), dma((3,)), dma((3,)), dma((heads // 2,)), dma((heads // 2,)),
            dma((parts,)), dma((parts,)), dma((parts,)), dma((parts,)), dma((7,)), dma((7,)),
            *chain_semaphores(pieces), *chain_semaphores(1), *chain_semaphores(3 * LATE),
        ],
        compiler_params=pltpu.CompilerParams(
            collective_id=2, has_side_effects=True, vmem_limit_bytes=60 << 20
        ),
        cost_estimate=pl.CostEstimate(
            flops=2 * tokens * width * (qw + 2 * kw) * 6, bytes_accessed=100 << 20,
            transcendentals=heads * tokens * tokens,
        ),
    )(
        back, resid, inv_two, ffn_gain, top, raw, sig, query, keys, values, log, attended, cos,
        sin, at, start, key_at, q_gain, k_gain, turned, gated, w_gates, hat, inv_one, norm_gain,
        wq, wk, wv, wo, late_pair, late_down, pair_sum, down_sum,
    )


def assemble_kernel(parts, outs, grads_ref, q_ref, k_ref, v_ref, o_ref, wide, sems):
    row_at = lax.axis_index("row")
    pieces = outs + 2 * parts
    high = grads_ref.shape[1]
    copies = []

    def move(src, dst):
        copies.append(pltpu.make_async_copy(src, dst, sems.at[len(copies)]))
        copies[-1].start()

    for s in range(2):
        at = row_at if s == 0 else 1 - row_at
        for p in range(pieces):
            n = s * pieces + p
            wide[n] = grads_ref[n].astype(F32)
            if p < outs:
                rows, cols = tile(at, high), pl.ds(p * 256, 256)
                move(wide.at[n], o_ref.at[rows, cols])
            else:
                j, i = (p - outs) // 2, (p - outs) % 2
                rows, head = pl.ds(i * high, high), at * (parts // 2) + j // 2
                if j % 2 == 0:
                    move(wide.at[n], q_ref.at[rows, tile(head, 256)])
                else:
                    for m, ref in enumerate((k_ref, v_ref)):
                        half = wide.at[n, :, pl.ds(m * 128, 128)]
                        move(half, ref.at[rows, tile(head, 128)])
    for copy in copies:
        copy.wait()


def assemble(grads, q_shape, k_shape, o_shape, head_dim):
    parts = q_shape[1] // 2 // head_dim // 2 + k_shape[1] // 2 // head_dim
    outs = grads.shape[0] // 2 - 2 * parts
    anywhere = pl.BlockSpec(memory_space=pl.ANY)
    struct = jax.ShapeDtypeStruct
    count = 2 * (outs + 3 * parts)
    return pl.pallas_call(
        functools.partial(assemble_kernel, parts, outs),
        out_shape=(
            struct(q_shape, F32), struct(k_shape, F32), struct(k_shape, F32), struct(o_shape, F32),
        ),
        in_specs=[pl.BlockSpec(memory_space=pltpu.VMEM)],
        out_specs=(anywhere,) * 4,
        scratch_shapes=[
            pltpu.VMEM(grads.shape, F32),
            pltpu.SemaphoreType.DMA((count,)),
        ],
        compiler_params=pltpu.CompilerParams(vmem_limit_bytes=40 << 20),
    )(grads)


def body(
    tokens, lengths, norm_gain, w_query, w_key, w_value, w_head_gate, query_gain, key_gain,
    w_out, ffn_gain, w_gate, w_up, w_down, grad_out,
):
    rows, d_loc = tokens.shape
    group_tok = 2 * rows
    head_dim = query_gain.shape[0]
    gate_half = w_head_gate.shape[1] // 2
    row_at = lax.axis_index("row")
    col_at = lax.axis_index("col")
    side = lax.axis_index("group") % 2

    steps = jnp.arange(rows, dtype=jnp.int32)
    index = jnp.concatenate([col_at * rows + steps, (1 - col_at) * rows + steps])
    place = places(lengths, index)[1]
    cosines, sines = rope_tables(place, head_dim)
    signed = jnp.concatenate([-sines[:, : head_dim // 2], sines[:, head_dim // 2 :]], axis=1)
    positions = (
        jnp.broadcast_to(index[:, None], (group_tok, 128)),
        jnp.broadcast_to((index - place)[:, None], (group_tok, 128)),
        jnp.broadcast_to(index[None], (8, group_tok)),
    )
    w_gates = jnp.pad(
        jnp.concatenate(halves(w_head_gate, 1, row_at), axis=1),
        ((0, 0), (0, 128 - 2 * gate_half)),
    )
    gains = (query_gain[None], key_gain[None])
    (
        normed_two, resid, inverse_two, hat, inverse_one, turned, grad_all, early_grad,
        raw, gate_sigmoid, query, keys, values, logsum, attended, gated_both,
    ) = front(
        tokens, grad_out, norm_gain[None], ffn_gain[None], *gains, cosines, signed, *positions,
        w_gates, w_query, w_key, w_value, w_out, w_down,
    )
    gated, gated_came = gated_both[0], gated_both[1]
    first_side = side == 0
    gated_pair = jnp.concatenate(
        [
            jnp.where(first_side, gated, gated_came),
            swap_groups(jnp.where(first_side, gated_came, gated)),
        ]
    ).T

    pair_sum, down_sum, late_pair, late_down, _, _, branch, branch_out, d_normed_two = ffn(
        normed_two, grad_all, early_grad, w_gate, w_up, w_down
    )
    output = (resid + branch + swap_groups(branch_out).astype(F32)).astype(BF16)

    grads, input_grad, sums, pair_sum, down_sum = rear(
        d_normed_two, resid, inverse_two, ffn_gain[None], grad_out, raw, gate_sigmoid, query,
        keys, values, logsum, attended, cosines, signed, *positions, *gains, turned, gated_pair,
        w_gates, hat, inverse_one, norm_gain[None], w_query, w_key, w_value, w_out,
        late_pair, late_down, pair_sum, down_sum,
    )
    grad_norm_gain = sums[:8].reshape(d_loc)
    grad_ffn_gain = sums[8:16].reshape(d_loc)
    grad_gates = sums[16:80].reshape(8, 2 * gate_half, 128).transpose(1, 0, 2)
    grad_gates = grad_gates.reshape(2 * gate_half, d_loc)
    grad_head_gate = ordered(grad_gates[:gate_half], grad_gates[gate_half:], 0, row_at).T

    grad_query, grad_key, grad_value, grad_out_w = assemble(
        grads, w_query.shape, w_key.shape, w_out.shape, head_dim
    )
    return (
        output,
        input_grad,
        grad_norm_gain,
        grad_query,
        grad_key,
        grad_value,
        grad_head_gate,
        sums[80],
        sums[81],
        grad_out_w,
        grad_ffn_gain,
        pair_sum[0].astype(F32),
        pair_sum[1].astype(F32),
        down_sum.astype(F32),
    )


def solution(mesh):
    shards = P(("group", "col"), "row")
    in_specs = (
        shards,
        P("group"),
        P("row"),
        P("row", "col"),
        P("row", "col"),
        P("row", "col"),
        P("row", "col"),
        P(),
        P(),
        P("col", "row"),
        P("row"),
        P("row", "col"),
        P("row", "col"),
        P("col", "row"),
        shards,
    )
    out_specs = (
        shards,
        shards,
        P("row"),
        P("row", "col"),
        P("row", "col"),
        P("row", "col"),
        P("row", "col"),
        P(),
        P(),
        P("col", "row"),
        P("row"),
        P("row", "col"),
        P("row", "col"),
        P("col", "row"),
    )
    return jax.shard_map(body, mesh=mesh, in_specs=in_specs, out_specs=out_specs, check_vma=False)
```

```python
import functools

import jax
import jax.numpy as jnp
from jax import lax
from jax.experimental import pallas as pl
from jax.experimental.pallas import tpu as pltpu
from jax.sharding import PartitionSpec as P

EPS = 1e-06
THETA = 1000000.0
NEGATIVE = -1e30
MESH = pl.DeviceIdType.MESH
F32 = jnp.float32
BF16 = jnp.bfloat16


def swap_groups(values):
    count = lax.axis_size("group")
    return lax.ppermute(values, "group", [(i, i ^ 1) for i in range(count)])


def halves(values, axis, at):
    low, high = jnp.split(values, 2, axis=axis)
    first = at == 0
    return jnp.where(first, low, high), jnp.where(first, high, low)


def ordered(own, other, axis, at):
    first = at == 0
    return jnp.concatenate(
        [jnp.where(first, own, other), jnp.where(first, other, own)], axis=axis
    )


def places(lengths_group, index):
    ends = jnp.cumsum(lengths_group)
    passed = (index[:, None] >= ends[None, :]).astype(jnp.int32)
    segment = jnp.sum(passed, axis=1)
    place = index - jnp.sum(passed * lengths_group[None, :], axis=1)
    return (segment, place)


def rope_tables(place, width):
    half = width // 2
    freq = THETA ** (-(jnp.arange(half, dtype=F32) * 2.0 / width))
    angle = place.astype(F32)[:, None] * freq[None, :]
    cosines = jnp.concatenate([jnp.cos(angle), jnp.cos(angle)], axis=1)
    sines = jnp.concatenate([jnp.sin(angle), jnp.sin(angle)], axis=1)
    return (cosines, sines)


TILE = 256
HOP = 2
WIDE = 128
EARLY = 6
AHEAD = 2
LATE = 3


def nt(a, b):
    return lax.dot_general(a, b, (((1,), (1,)), ((), ())), preferred_element_type=F32)


def nn(a, b):
    return jnp.dot(a, b, preferred_element_type=F32)


def copy_to(src, dst, send_sem, recv_sem, peer):
    return pltpu.make_async_remote_copy(
        src_ref=src, dst_ref=dst, send_sem=send_sem, recv_sem=recv_sem,
        device_id=peer, device_id_type=MESH,
    )


def tile(i, size=TILE):
    return pl.ds(pl.multiple_of(i * size, size), size)


class Place:
    def __init__(self, count):
        group = lax.axis_index("group")
        self.line = count // 2
        self.root = (self.line - 1) // 2
        self.deep = max(self.root, self.line - 1 - self.root)
        self.at = group // 2
        self.side = group % 2
        self.x_peer = {"row": 1 - lax.axis_index("row")}
        self.core_peer = {"col": 1 - lax.axis_index("col")}
        self.y_peer = {"group": group + 1 - 2 * self.side}
        self.above = {"group": jnp.minimum(group + 2, count - 1)}
        self.below = {"group": jnp.maximum(group - 2, 0)}
        self.has_above = self.at < self.line - 1
        self.has_below = self.at > 0

    def meet(self):
        barrier = pltpu.get_barrier_semaphore()

        def greet(peer):
            pl.semaphore_signal(barrier, inc=1, device_id=peer, device_id_type=MESH)

        for peer in (self.x_peer, self.core_peer, self.y_peer):
            greet(peer)
        pl.when(self.has_above)(lambda: greet(self.above))
        pl.when(self.has_below)(lambda: greet(self.below))
        met = 3 + self.has_above.astype(jnp.int32) + self.has_below.astype(jnp.int32)
        pl.semaphore_wait(barrier, met)


class Chain:
    def __init__(self, place, chunks, kinds, total, came, home, add, sems, share=True):
        self.place, self.chunks, self.kinds = place, chunks, kinds
        self.total, self.came, self.home, self.add = total, came, home, add
        self.sems, self.share = sems, share

    def part_copy(self, c, k, upward):
        sent, low, high = self.sems[:3]
        p = self.kinds * c + k
        peer, which, arrived = (
            (self.place.above, 0, low) if upward else (self.place.below, 1, high)
        )
        return copy_to(
            self.total(c, k), self.came(c, k, which), sent.at[p], arrived.at[p], peer
        )

    def final_copy(self, c, k, upward, first):
        up, down, arrived = self.sems[3:6]
        p = self.kinds * c + k
        src = self.total(c, k) if first else self.home(c, k, self.place.side)
        peer, sent = (self.place.above, up) if upward else (self.place.below, down)
        return copy_to(src, self.home(c, k, self.place.side), sent.at[p], arrived.at[p], peer)

    def keep_copy(self, c, k):
        return pltpu.make_async_copy(
            self.total(c, k), self.home(c, k, self.place.side),
            self.sems[6].at[self.kinds * c + k],
        )

    def share_copy(self, c, k, first, of=None):
        p = self.kinds * c + k
        of = self.place.side if of is None else of
        src = self.total(c, k) if first else self.home(c, k, self.place.side)
        return copy_to(
            src, self.home(c, k, of), self.sems[7].at[p], self.sems[8].at[p], self.place.y_peer
        )

    def step(self, u, hop=1):
        at, line, root, deep = self.place.at, self.place.line, self.place.root, self.place.deep
        behind = jnp.where(at < root, at, jnp.where(at > root, line - 1 - at, deep))
        self.inward(u - hop * behind)
        self.outward(u - hop * (deep + jnp.abs(at - root)))

    def kinds_of(self, p):
        live = (p >= 0) & (p < self.kinds * self.chunks)
        if self.kinds == 1:
            return [(live, p, 0)]
        p = jnp.maximum(p, 0)
        return [
            (live & (lax.rem(p, self.kinds) == k), lax.div(p, self.kinds), k)
            for k in range(self.kinds)
        ]

    def inward(self, piece):
        at, line, root = self.place.at, self.place.line, self.place.root
        for live, c, k in self.kinds_of(piece):

            @pl.when(live & (at < root))
            def _():
                @pl.when(self.place.has_below)
                def _():
                    self.part_copy(c, k, True).wait_recv()
                    self.add(c, k, 0)

                self.part_copy(c, k, True).start()

            @pl.when(live & (at > root))
            def _():
                @pl.when(self.place.has_above)
                def _():
                    self.part_copy(c, k, False).wait_recv()
                    self.add(c, k, 1)

                self.part_copy(c, k, False).start()

            @pl.when(live & (at == root))
            def _():
                if root > 0:
                    self.part_copy(c, k, True).wait_recv()
                    self.add(c, k, 0)
                if root < line - 1:
                    self.part_copy(c, k, False).wait_recv()
                    self.add(c, k, 1)
                if root > 0:
                    self.final_copy(c, k, False, True).start()
                if root < line - 1:
                    self.final_copy(c, k, True, True).start()
                if self.share:
                    self.share_copy(c, k, True).start()
                self.keep_copy(c, k).start()

    def outward(self, piece):
        at, root = self.place.at, self.place.root
        for live, c, k in self.kinds_of(piece):

            @pl.when(live & (at != root))
            def _():
                self.final_copy(c, k, True, False).wait_recv()

                @pl.when((at > root) & self.place.has_above)
                def _():
                    self.final_copy(c, k, True, False).start()

                @pl.when((at < root) & self.place.has_below)
                def _():
                    self.final_copy(c, k, False, False).start()

                if self.share:
                    self.share_copy(c, k, False).start()

    def steps(self, hop=1):
        return self.kinds * self.chunks + 2 * hop * self.place.deep

    def drain(self):
        at, line, root = self.place.at, self.place.line, self.place.root

        @pl.loop(0, self.chunks)
        def _(c):
            for k in range(self.kinds):
                if self.share:
                    self.share_copy(c, k, False, 1 - self.place.side).wait_recv()
                    self.share_copy(c, k, False).wait_send()

                @pl.when(at == root)
                def _():
                    self.keep_copy(c, k).wait()
                    if root > 0:
                        self.final_copy(c, k, False, True).wait_send()
                    if root < line - 1:
                        self.final_copy(c, k, True, True).wait_send()

                @pl.when(at < root)
                def _():
                    self.part_copy(c, k, True).wait_send()

                    @pl.when(self.place.has_below)
                    def _():
                        self.final_copy(c, k, False, False).wait_send()

                @pl.when(at > root)
                def _():
                    self.part_copy(c, k, False).wait_send()

                    @pl.when(self.place.has_above)
                    def _():
                        self.final_copy(c, k, True, False).wait_send()


def chain_semaphores(pieces):
    return [pltpu.SemaphoreType.DMA((pieces,)) for _ in range(9)]


def ffn_kernel(
    count, chunks, h_ref, top_ref, early_ref, gate_ref, up_ref, down_ref,
    pair_grads_ref, down_grads_ref, late_pair_ref, late_down_ref, pair_came_ref, down_came_ref,
    branch_ref, branch_out_ref, back_ref,
    h_all, h_turned, sent, came, top_sent, top_came, grad_part, w_pair, w_down, acc_branch, acc_back, parts, inner_turned,
    pair_total, down_total, pair_stage, down_stage, reduce_recv,
    gather_send, gather_recv, x_send, x_recv, top_send, top_recv, late_sem, load_sem, weight_sem, fold_send, fold_recv,
    *chain_sems,
):
    place = Place(count)
    rows, width = h_ref.shape
    tokens = h_all.shape[0]
    tiles = tokens // TILE
    wide = w_down.shape[0] // chunks
    side = place.side

    def weight_copies(j):
        cols = tile(side * chunks + j, wide)
        return (
            pltpu.make_async_copy(
                gate_ref.at[:, cols], w_pair.at[j, :, pl.ds(0, wide)], weight_sem.at[0, j]
            ),
            pltpu.make_async_copy(
                up_ref.at[:, cols], w_pair.at[j, :, pl.ds(wide, wide)], weight_sem.at[1, j]
            ),
            pltpu.make_async_copy(
                down_ref.at[cols, :], w_down.at[tile(j, wide), :], weight_sem.at[2, j]
            ),
        )

    @pl.loop(0, chunks)
    def _(j):
        for copy in weight_copies(j):
            copy.start()

    place.meet()

    def slot(i):
        return pl.ds(i * rows, rows)

    to_y = copy_to(h_ref, h_all.at[slot(2)], gather_send.at[0], gather_recv.at[0], place.y_peer)
    to_core = copy_to(
        h_ref, h_all.at[slot(1)], gather_send.at[1], gather_recv.at[1], place.core_peer
    )
    forward = copy_to(
        h_all.at[slot(2)], h_all.at[slot(3)], gather_send.at[2], gather_recv.at[2],
        place.core_peer,
    )
    to_y.start()
    to_core.start()

    def top_exchange(j):
        n = j - EARLY
        return copy_to(
            top_sent.at[n], top_came.at[n], top_send.at[n], top_recv.at[n], place.x_peer
        )

    def top_project(j):
        @pl.loop(0, tiles)
        def _(i):
            top_sent[j - EARLY, tile(i), :] = nt(
                top_ref[tile(i), :], w_down[tile(j, wide), :]
            ).astype(BF16)

        top_exchange(j).start()

    def exchange(j):
        return copy_to(
            sent.at[lax.rem(j, 3)], came.at[j], x_send.at[j], x_recv.at[j], place.x_peer
        )

    def first_half(i):
        at_rows = pl.ds(2 * i * rows, 2 * rows)
        n = i * chunks
        return copy_to(
            sent.at[0, at_rows, :], came.at[0, at_rows, :], x_send.at[n], x_recv.at[n],
            place.x_peer,
        )

    def project_half(i):
        for n in range(2):
            at_rows = slot(2 * i + n)
            sent[0, at_rows, :] = nn(h_all[at_rows, :], w_pair[0]).astype(BF16)
        first_half(i).start()

    def project(j):
        for copy in weight_copies(j)[:2]:
            copy.wait()

        @pl.loop(0, tiles)
        def _(i):
            sent[lax.rem(j, 3), tile(i), :] = nn(h_all[tile(i), :], w_pair[j]).astype(BF16)

    def work(j):
        @pl.when(j == 0)
        def _():
            first_half(0).wait_recv()
            first_half(1).wait_recv()

        @pl.when(j > 0)
        def _():
            exchange(j).wait_recv()

        @pl.when(j < EARLY)
        def _():
            grad_part[...] = early_ref[:, tile(j, wide)].astype(F32)

        @pl.when(j >= EARLY)
        def _():
            top_exchange(j).wait_recv()
            grad_part[...] = top_sent[j - EARLY].astype(F32) + top_came[j - EARLY].astype(F32)

        @pl.loop(0, tiles)
        def _(i):
            at_rows = tile(i)
            pair = sent[lax.rem(j, 3), at_rows, :].astype(F32) + came[j, at_rows, :].astype(F32)
            gate, up = pair[:, :wide], pair[:, wide:]
            grad = grad_part[at_rows, :]
            sig = 1.0 / (1.0 + jnp.exp(-gate))
            silu = gate * sig
            parts[at_rows, pl.ds(0, wide)] = (
                grad * up * (sig * (1.0 + gate * (1.0 - sig)))
            ).astype(BF16)
            parts[at_rows, pl.ds(wide, wide)] = (grad * silu).astype(BF16)
            inner = (silu * up).astype(BF16)
            inner_turned[:, at_rows] = inner.T
            acc_branch[at_rows, :] += nn(inner, w_down[tile(j, wide), :])
            acc_back[at_rows, :] += nt(parts[at_rows, :], w_pair[j])

    def gradients(j):
        @pl.loop(0, width // TILE)
        def _(i):
            pair = nn(h_turned[tile(i), :], parts[...])
            pair_total[j, 0, tile(i), :] = pair[:, :wide].astype(BF16)
            pair_total[j, 1, tile(i), :] = pair[:, wide:].astype(BF16)
            down_total[j, :, tile(i)] = nn(inner_turned[...], top_ref[:, tile(i)]).astype(BF16)

    def total(c, k):
        return down_total.at[c] if k == 2 else pair_total.at[c, k]

    def landed(c, k, which):
        return down_came_ref.at[which, c] if k == 2 else pair_came_ref.at[which, c, k]

    def home(c, k, of):
        at_cols = tile(of * chunks + c, wide)
        return down_grads_ref.at[at_cols, :] if k == 2 else pair_grads_ref.at[k, :, at_cols]

    def add(c, k, which):
        stage = (down_stage if k == 2 else pair_stage).at[which]
        copy = pltpu.make_async_copy(landed(c, k, which), stage, load_sem.at[which])
        copy.start()
        copy.wait()
        into = total(c, k)

        @pl.loop(0, into.shape[0] // wide)
        def _(i):
            at_rows = tile(i, wide)
            into[at_rows, :] = (
                into[at_rows, :].astype(F32) + stage[at_rows, :].astype(F32)
            ).astype(BF16)

    ours = chunks - LATE
    chain = Chain(place, ours, 3, total, landed, home, add, chain_sems)

    def late_copies(c):
        return (
            pltpu.make_async_copy(pair_total.at[c], late_pair_ref.at[c - ours], late_sem.at[0, c - ours]),
            pltpu.make_async_copy(down_total.at[c], late_down_ref.at[c - ours], late_sem.at[1, c - ours]),
        )

    h_all[slot(0), :] = h_ref[...]
    for copy in weight_copies(0)[:2]:
        copy.wait()
    to_core.wait_recv()
    project_half(0)

    @pl.loop(0, chunks)
    def _(j):
        weight_copies(j)[2].wait()

    @pl.loop(EARLY, min(EARLY + AHEAD, chunks))
    def _(j):
        top_project(j)

    acc_branch[...] = jnp.zeros_like(acc_branch)
    acc_back[...] = jnp.zeros_like(acc_back)
    to_y.wait_recv()
    forward.start()
    forward.wait_recv()
    project_half(1)
    project(1)

    @pl.loop(0, tiles)
    def _(i):
        h_turned[:, tile(i)] = h_all[tile(i), :].T

    first_half(0).wait_send()
    first_half(1).wait_send()
    exchange(1).start()

    @pl.loop(0, chunks)
    def _(t):
        work(t)
        chain.step(3 * t - 1, HOP)
        gradients(t)

        @pl.when(t >= ours)
        def _():
            for copy in late_copies(t):
                copy.start()

        chain.step(3 * t, HOP)

        @pl.when(t + 2 < chunks)
        def _():
            @pl.when(t >= 2)
            def _():
                exchange(t - 1).wait_send()

            project(t + 2)
            exchange(t + 2).start()

        @pl.when((t + AHEAD >= EARLY + AHEAD) & (t + AHEAD < chunks))
        def _():
            top_project(t + AHEAD)

        chain.step(3 * t + 1, HOP)

    chain.step(3 * chunks - 1, HOP)

    def fold_source(n, i):
        if i == 2:
            return w_down.at[slot(0), :]
        return h_all.at[slot(2 * n + i), :]

    def fold(n, i):
        return copy_to(
            fold_source(n, i), reduce_recv.at[n, i], fold_send.at[n, i], fold_recv.at[n, i],
            place.y_peer if i == 2 else place.core_peer,
        )

    to_y.wait_send()
    to_core.wait_send()
    forward.wait_send()
    for n, acc in enumerate((acc_back, acc_branch)):
        for i in (1, 0):
            fold_source(n, i)[...] = acc[slot(2 * i + 1), :].astype(BF16)
            fold(n, i).start()
    fold(0, 1).wait_recv()
    fold_source(0, 2)[...] = (acc_back[slot(2), :] + reduce_recv[0, 1].astype(F32)).astype(BF16)
    fold(0, 2).start()
    chain.step(3 * chunks, HOP)
    fold(1, 0).wait_recv()
    fold(1, 1).wait_recv()
    branch_ref[...] = acc_branch[slot(0), :] + reduce_recv[1, 0].astype(F32)
    branch_out_ref[...] = (acc_branch[slot(2), :] + reduce_recv[1, 1].astype(F32)).astype(BF16)
    fold(0, 0).wait_recv()
    fold(0, 2).wait_recv()
    back_ref[...] = (
        acc_back[slot(0), :] + reduce_recv[0, 0].astype(F32) + reduce_recv[0, 2].astype(F32)
    )

    @pl.loop(3 * chunks + 1, max(3 * chunks + 1, chain.steps(HOP)))
    def _(u):
        chain.step(u, HOP)

    @pl.loop(ours, chunks)
    def _(c):
        for copy in late_copies(c):
            copy.wait()

    chain.drain()

    @pl.loop(max(chunks - 3, 0), chunks)
    def _(j):
        exchange(j).wait_send()

    @pl.loop(EARLY, chunks)
    def _(j):
        top_exchange(j).wait_send()

    for n, i in ((0, 0), (0, 1), (0, 2), (1, 0), (1, 1)):
        fold(n, i).wait_send()


def ffn(h, top, early, w_gate, w_up, w_down):
    count = lax.axis_size("group")
    rows, width = h.shape
    hidden = w_gate.shape[1] // 2
    wide = WIDE
    chunks = hidden // wide
    tokens = 4 * rows
    anywhere = pl.BlockSpec(memory_space=pl.ANY)
    local = pl.BlockSpec(memory_space=pltpu.VMEM)
    dma = pltpu.SemaphoreType.DMA
    pieces = 3 * (chunks - LATE)
    flops = 2 * tokens * width * hidden * 8
    return pl.pallas_call(
        functools.partial(ffn_kernel, count, chunks),
        out_shape=(
            jax.ShapeDtypeStruct((2, width, 2 * hidden), BF16),
            jax.ShapeDtypeStruct((2 * hidden, width), BF16),
            jax.ShapeDtypeStruct((LATE, 2, width, wide), BF16),
            jax.ShapeDtypeStruct((LATE, wide, width), BF16),
            jax.ShapeDtypeStruct((2, chunks - LATE, 2, width, wide), BF16),
            jax.ShapeDtypeStruct((2, chunks - LATE, wide, width), BF16),
            jax.ShapeDtypeStruct((rows, width), F32),
            jax.ShapeDtypeStruct((rows, width), BF16),
            jax.ShapeDtypeStruct((rows, width), F32),
        ),
        in_specs=[local, local, local, anywhere, anywhere, anywhere],
        out_specs=(anywhere,) * 6 + (local,) * 3,
        scratch_shapes=[
            pltpu.VMEM((tokens, width), BF16),
            pltpu.VMEM((width, tokens), BF16),
            pltpu.VMEM((3, tokens, 2 * wide), BF16),
            pltpu.VMEM((chunks, tokens, 2 * wide), BF16),
            pltpu.VMEM((chunks - EARLY, tokens, wide), BF16),
            pltpu.VMEM((chunks - EARLY, tokens, wide), BF16),
            pltpu.VMEM((tokens, wide), F32),
            pltpu.VMEM((chunks, width, 2 * wide), BF16),
            pltpu.VMEM((hidden, width), BF16),
            pltpu.VMEM((tokens, width), F32),
            pltpu.VMEM((tokens, width), F32),
            pltpu.VMEM((tokens, 2 * wide), BF16),
            pltpu.VMEM((wide, tokens), BF16),
            pltpu.VMEM((chunks, 2, width, wide), BF16),
            pltpu.VMEM((chunks, wide, width), BF16),
            pltpu.VMEM((2, width, wide), BF16),
            pltpu.VMEM((2, wide, width), BF16),
            pltpu.VMEM((2, 3, rows, width), BF16),
            dma((3,)), dma((3,)), dma((chunks + 1,)), dma((chunks + 1,)),
            dma((chunks - EARLY,)), dma((chunks - EARLY,)),
            dma((2, LATE)), dma((2,)), dma((3, chunks)), dma((2, 3)), dma((2, 3)),
            *chain_semaphores(pieces),
        ],
        compiler_params=pltpu.CompilerParams(
            collective_id=1, has_side_effects=True, vmem_limit_bytes=63 << 20
        ),
        cost_estimate=pl.CostEstimate(
            flops=flops, bytes_accessed=200 << 20, transcendentals=tokens * hidden
        ),
    )(h, top, early, w_gate, w_up, w_down)


ROWS = 128


def sigmoid(v):
    return 1.0 / (1.0 + jnp.exp(-v))


def each_tile(start, count, size=160):
    def run(step):
        @pl.loop(0, count // size)
        def _(i):
            step(pl.ds(pl.multiple_of(start + i * size, 32), size))

    return run


def column(values):
    return jnp.broadcast_to(values, (values.shape[0], 128))


def front_kernel(
    count, heads, kv_heads, tok_ref, top_ref, norm_ref, second_ref, q_gain_ref, k_gain_ref,
    cos_ref, sin_ref, at_ref, start_ref, key_at_ref, w_gates_ref, wq_ref, wk_ref, wv_ref, wo_ref,
    wd_ref,
    h_ref, resid_ref, inv_two_ref, hat_ref, inv_one_ref, turned_ref, tops_ref, early_ref,
    raw_ref, sig_ref, q_ref, k_ref, v_ref, log_ref, attended_ref, gated_ref,
    normed_all, wq, wk, wv, wo, wd, kv_send, kv_came, q_send, q_came, gates, early_send, early_came,
    ss_send, ss_came, fold_src, fold_dst, acc,
    w_sem, n_send, n_recv, t_send, t_recv, p_send, p_recv, e_send, e_recv, g_send, g_recv,
    s_send, s_recv,
):
    place = Place(count)
    rows, width = tok_ref.shape
    tokens = 2 * rows
    row_at = lax.axis_index("row")
    side = place.side
    hd = 128
    qw, kw = heads * hd, kv_heads * hd
    hidden = wd_ref.shape[0] // 2
    scale = hd**-0.5

    loads = []
    for i, at in enumerate((row_at, 1 - row_at)):
        q_cols, k_cols = tile(at, qw), tile(at, kw)
        loads += [
            pltpu.make_async_copy(wk_ref.at[:, k_cols], wk.at[i], w_sem.at[i, 0]),
            pltpu.make_async_copy(wv_ref.at[:, k_cols], wv.at[i], w_sem.at[i, 1]),
            pltpu.make_async_copy(wq_ref.at[:, q_cols], wq.at[i], w_sem.at[i, 2]),
            pltpu.make_async_copy(wo_ref.at[q_cols, :], wo.at[i], w_sem.at[i, 3]),
        ]
    down_rows = pl.ds(pl.multiple_of(side * hidden, WIDE), wd.shape[0])
    loads.append(pltpu.make_async_copy(wd_ref.at[down_rows, :], wd, w_sem.at[0, 4]))
    for copy in loads:
        copy.start()
    place.meet()

    def slot(i):
        return pl.ds(i * rows, rows)

    def spread(ref, sends, recvs):
        own, core, pair, both = (ref.at[slot(i), :] for i in range(4))
        return (
            copy_to(own, core, sends.at[0], recvs.at[0], place.core_peer),
            copy_to(own, pair, sends.at[1], recvs.at[1], place.y_peer),
            copy_to(pair, both, sends.at[2], recvs.at[2], place.core_peer),
        )

    tops_ref[slot(0), :] = top_ref[...]
    tops = spread(tops_ref, t_send, t_recv)
    tops[0].start()
    tops[1].start()

    def squares(n):
        return copy_to(ss_send.at[n], ss_came.at[n], s_send.at[n], s_recv.at[n], place.x_peer)

    x = tok_ref[...].astype(F32)
    ss_send[0] = column(jnp.sum(x * x, axis=1, keepdims=True))
    squares(0).start()

    def early(i):
        return copy_to(
            early_send.at[slot(i), :], early_came.at[slot(i), :], e_send.at[i], e_recv.at[i],
            place.x_peer,
        )

    def early_start(i):
        @each_tile(i * rows, rows)
        def _(at_rows):
            early_send[at_rows, :] = nt(tops_ref[at_rows, :], wd[...]).astype(BF16)

        early(i).start()

    loads[-1].wait()
    early_start(0)
    squares(0).wait()
    inv_one = lax.rsqrt((ss_send[0] + ss_came[0]) / (2 * width) + EPS)
    inv_one_ref[...] = inv_one
    hat = tok_ref[...].astype(F32) * inv_one[:, :1]
    hat_ref[...] = hat
    normed_all[slot(0), :] = (hat * norm_ref[...]).astype(BF16)
    normed = spread(normed_all, n_send, n_recv)
    normed[0].start()
    normed[1].start()

    kv_copy = copy_to(kv_send, kv_came, p_send.at[0], p_recv.at[0], place.x_peer)
    q_copy = copy_to(q_send, q_came, p_send.at[1], p_recv.at[1], place.x_peer)
    for copy in loads[:-1]:
        copy.wait()
    for i in range(2):
        if i == 1:
            normed[0].wait_recv()

        @each_tile(i * rows, rows)
        def _(at_rows):
            rows_in = normed_all[at_rows, :]
            kv_send[at_rows, pl.ds(0, kw)] = nn(rows_in, wk[1]).astype(BF16)
            kv_send[at_rows, pl.ds(kw, kw)] = nn(rows_in, wv[1]).astype(BF16)

    kv_copy.start()

    @each_tile(0, tokens)
    def _(at_rows):
        rows_in = normed_all[at_rows, :]
        q_send[at_rows, pl.ds(0, qw)] = nn(rows_in, wq[1]).astype(BF16)
        part = nn(rows_in, w_gates_ref[...])
        gates[at_rows, :] = part
        q_send[at_rows, pl.ds(qw, 128)] = part.astype(BF16)

    q_copy.start()

    @each_tile(0, tokens)
    def _(at_rows):
        rows_in = normed_all[at_rows, :]
        raw_ref[at_rows, pl.ds(0, qw)] = nn(rows_in, wq[0])
        raw_ref[at_rows, pl.ds(qw, kw)] = nn(rows_in, wk[0])
        raw_ref[at_rows, pl.ds(qw + kw, kw)] = nn(rows_in, wv[0])


    def turn(values, gain, at_rows):
        inverse = lax.rsqrt(jnp.mean(values * values, axis=1, keepdims=True) + EPS)
        scaled = values * inverse * gain
        return scaled * cos_ref[at_rows, :] + pltpu.roll(scaled, 64, axis=1) * sin_ref[at_rows, :]

    tops[1].wait_recv()
    tops[2].start()
    normed[1].wait_recv()
    normed[2].start()
    tops[0].wait_recv()
    kv_copy.wait_recv()

    @pl.loop(0, tokens // ROWS)
    def _(i):
        at_rows = tile(i, ROWS)
        for n in range(kv_heads):
            cols = pl.ds(qw + n * hd, hd)
            key = raw_ref[at_rows, cols] + kv_came[at_rows, pl.ds(n * hd, hd)].astype(F32)
            raw_ref[at_rows, cols] = key
            k_ref[at_rows, pl.ds(n * hd, hd)] = turn(key, k_gain_ref[...], at_rows).astype(BF16)
            cols = pl.ds(qw + kw + n * hd, hd)
            value = raw_ref[at_rows, cols] + kv_came[at_rows, pl.ds(kw + n * hd, hd)].astype(F32)
            raw_ref[at_rows, cols] = value
            v_ref[at_rows, pl.ds(n * hd, hd)] = value.astype(BF16)

    q_copy.wait_recv()
    early_start(1)

    @pl.loop(0, tokens // ROWS)
    def _(i):
        at_rows = tile(i, ROWS)
        other = q_came[at_rows, pl.ds(qw, 128)].astype(F32)
        logit = gates[at_rows, :] + pltpu.roll(other, 128 - heads, axis=1)
        sig_ref[at_rows, :] = sigmoid(logit)
        for n in range(heads):
            cols = pl.ds(n * hd, hd)
            query = raw_ref[at_rows, cols] + q_came[at_rows, cols].astype(F32)
            raw_ref[at_rows, cols] = query
            q_ref[at_rows, cols] = turn(query, q_gain_ref[...], at_rows).astype(BF16)

    def head_copy(n):
        cols = pl.ds(n * hd, hd)
        return copy_to(
            gated_ref.at[0, :, cols], gated_ref.at[1, :, cols], g_send.at[n], g_recv.at[n],
            place.x_peer,
        )

    for n in range(heads):
        cols = pl.ds(n * hd, hd)
        kv = pl.ds(n * kv_heads // heads * hd, hd)

        @pl.loop(0, tokens // ROWS)
        def _(i):
            at_rows = tile(i, ROWS)
            scores = nt(q_ref[at_rows, cols], k_ref[:, kv]) * scale
            key_at = key_at_ref[:1, :]
            allowed = (key_at <= at_ref[at_rows, :1]) & (key_at >= start_ref[at_rows, :1])
            scores = jnp.where(allowed, scores, NEGATIVE)
            top = jnp.max(scores, axis=1, keepdims=True)
            raised = jnp.exp(scores - top)
            total = jnp.sum(raised, axis=1, keepdims=True)
            result = nn((raised / total).astype(BF16), v_ref[:, kv])
            log_ref[n, at_rows, :] = column(top + jnp.log(total))
            attended_ref[at_rows, cols] = result
            gated_ref[0, at_rows, cols] = (result * sig_ref[at_rows, n : n + 1]).astype(BF16)

        head_copy(n).start()
        if n == 0:
            tops[2].wait_recv()
            early_start(2)
        if n == 2:
            early_start(3)

    @each_tile(0, tokens)
    def _(at_rows):
        acc[at_rows, :] = nn(gated_ref[0, at_rows, :], wo[0])

    def turn_rows(first, last):
        @pl.loop(first, last)
        def _(i):
            turned_ref[:, tile(i, ROWS)] = normed_all[tile(i, ROWS), :].T

    turn_rows(0, tokens // ROWS)
    for n in range(heads):
        head_copy(n).wait_recv()
    fold = copy_to(fold_src, fold_dst, s_send.at[2], s_recv.at[2], place.core_peer)

    @each_tile(0, rows)
    def _(at_rows):
        there = pl.ds(pl.multiple_of(at_rows.start + rows, 32), at_rows.size)
        fold_src[at_rows, :] = (acc[there, :] + nn(gated_ref[1, there, :], wo[1])).astype(BF16)

    fold.start()

    @each_tile(0, rows)
    def _(at_rows):
        acc[at_rows, :] += nn(gated_ref[1, at_rows, :], wo[1])

    normed[2].wait_recv()
    fold.wait_recv()
    resid = tok_ref[...].astype(F32) + acc[slot(0), :] + fold_dst[...].astype(F32)
    resid_ref[...] = resid
    ss_send[1] = column(jnp.sum(resid * resid, axis=1, keepdims=True))
    squares(1).start()
    turn_rows(tokens // ROWS, 2 * tokens // ROWS)
    for i in range(4):
        early(i).wait_recv()
        early_ref[slot(i), :] = (
            early_send[slot(i), :].astype(F32) + early_came[slot(i), :].astype(F32)
        ).astype(BF16)
    squares(1).wait()
    inv_two = lax.rsqrt((ss_send[1] + ss_came[1]) / (2 * width) + EPS)
    inv_two_ref[...] = inv_two
    h_ref[...] = (resid_ref[...] * inv_two[:, :1] * second_ref[...]).astype(BF16)

    for copy in (*tops, *normed, kv_copy, q_copy, fold):
        copy.wait_send()
    for i in range(4):
        early(i).wait_send()
    for n in range(heads):
        head_copy(n).wait_send()


def front(
    tok, top, norm_gain, ffn_gain, q_gain, k_gain, cos, sin, at, start, key_at, w_gates,
    wq, wk, wv, wo, wd,
):
    count = lax.axis_size("group")
    rows, width = tok.shape
    tokens = 2 * rows
    hd = 128
    heads, kv_heads = wq.shape[1] // 2 // hd, wk.shape[1] // 2 // hd
    qw, kw = heads * hd, kv_heads * hd
    early = EARLY * WIDE
    local = pl.BlockSpec(memory_space=pltpu.VMEM)
    anywhere = pl.BlockSpec(memory_space=pl.ANY)
    dma = pltpu.SemaphoreType.DMA
    struct = jax.ShapeDtypeStruct
    return pl.pallas_call(
        functools.partial(front_kernel, count, heads, kv_heads),
        out_shape=(
            struct((rows, width), BF16),
            struct((rows, width), F32),
            struct((rows, 128), F32),
            struct((rows, width), F32),
            struct((rows, 128), F32),
            struct((width, 4 * rows), BF16),
            struct((4 * rows, width), BF16),
            struct((4 * rows, early), BF16),
            struct((tokens, qw + 2 * kw), F32),
            struct((tokens, 128), F32),
            struct((tokens, qw), BF16),
            struct((tokens, kw), BF16),
            struct((tokens, kw), BF16),
            struct((heads, tokens, 128), F32),
            struct((tokens, qw), F32),
            struct((2, tokens, qw), BF16),
        ),
        in_specs=[local] * 12 + [anywhere] * 5,
        out_specs=(local,) * 16,
        scratch_shapes=[
            pltpu.VMEM((4 * rows, width), BF16),
            pltpu.VMEM((2, width, qw), BF16),
            pltpu.VMEM((2, width, kw), BF16),
            pltpu.VMEM((2, width, kw), BF16),
            pltpu.VMEM((2, qw, width), BF16),
            pltpu.VMEM((early, width), BF16),
            pltpu.VMEM((tokens, 2 * kw), BF16),
            pltpu.VMEM((tokens, 2 * kw), BF16),
            pltpu.VMEM((tokens, qw + 128), BF16),
            pltpu.VMEM((tokens, qw + 128), BF16),
            pltpu.VMEM((tokens, 128), F32),
            pltpu.VMEM((4 * rows, early), BF16),
            pltpu.VMEM((4 * rows, early), BF16),
            pltpu.VMEM((2, rows, 128), F32),
            pltpu.VMEM((2, rows, 128), F32),
            pltpu.VMEM((rows, width), BF16),
            pltpu.VMEM((rows, width), BF16),
            pltpu.VMEM((tokens, width), F32),
            dma((2, 5)), dma((3,)), dma((3,)), dma((3,)), dma((3,)), dma((2,)), dma((2,)),
            dma((4,)), dma((4,)), dma((heads,)), dma((heads,)), dma((3,)), dma((3,)),
        ],
        compiler_params=pltpu.CompilerParams(
            collective_id=3, has_side_effects=True, vmem_limit_bytes=60 << 20
        ),
        cost_estimate=pl.CostEstimate(
            flops=6 * tokens * width * (qw + kw) * 4, bytes_accessed=40 << 20,
            transcendentals=heads * tokens * tokens,
        ),
    )(
        tok, top, norm_gain, ffn_gain, q_gain, k_gain, cos, sin, at, start, key_at, w_gates,
        wq, wk, wv, wo, wd,
    )


MISC = 88


def tn(a, b):
    return lax.dot_general(a, b, (((0,), (0,)), ((), ())), preferred_element_type=F32)


def rear_kernel(
    count, heads, kv_heads, back_ref, resid_ref, inv_two_ref, second_ref, top_ref, raw_ref,
    sig_ref, q_ref, k_ref, v_ref, log_ref, attended_ref, cos_ref, sin_ref, at_ref, start_ref,
    key_at_ref, q_gain_ref, k_gain_ref, turned_ref, gated_ref, w_gates_ref, hat_ref, inv_one_ref,
    norm_ref, wq_ref, wk_ref, wv_ref, wo_ref, late_pair_ref, late_down_ref, pair_in, down_in,
    grads_ref, input_ref, sums_ref, pair_grads_ref, down_grads_ref,
    w_main, wo, branch, block_src, dg_own, dg_send, dg_came, dk, dv, gates, gates_came, own, came, across,
    total, landed, misc, misc_came, misc_landed, misc_home, acc, fold_src, fold_dst, in_send,
    in_came, late_pair, late_down, late_pair_came, late_down_came,
    w_sem, late_sem, b_send, b_recv, d_send, d_recv, x_send, x_recv, y_send, y_recv, s_send, s_recv,
    *chain_sems,
):
    place = Place(count)
    row_at = lax.axis_index("row")
    side = place.side
    rows, width = back_ref.shape
    tokens = 2 * rows
    hd = 128
    cols = 2 * hd
    qw = heads * hd
    parts = heads // 2 + kv_heads
    high = gated_ref.shape[0]
    pieces = total.shape[0]
    scale = hd**-0.5

    loads = []
    for i, at in enumerate((row_at, 1 - row_at)):
        for n in range(kv_heads):
            q_cols, k_cols = tile(at * kv_heads + n, cols), tile(at * kv_heads + n, hd)
            first, second = w_main.at[i * parts + 2 * n], w_main.at[i * parts + 2 * n + 1]
            loads += [
                pltpu.make_async_copy(wq_ref.at[:, q_cols], first, w_sem.at[i, n, 0]),
                pltpu.make_async_copy(
                    wk_ref.at[:, k_cols], second.at[:, pl.ds(0, hd)], w_sem.at[i, n, 1]
                ),
                pltpu.make_async_copy(
                    wv_ref.at[:, k_cols], second.at[:, pl.ds(hd, hd)], w_sem.at[i, n, 2]
                ),
            ]
        loads.append(pltpu.make_async_copy(wo_ref.at[tile(at, qw), :], wo.at[i], w_sem.at[i, 0, 3]))
    for copy in loads:
        copy.start()
    late_loads = (
        pltpu.make_async_copy(late_pair_ref, late_pair, late_sem.at[0]),
        pltpu.make_async_copy(late_down_ref, late_down, late_sem.at[1]),
    )
    for copy in late_loads:
        copy.start()
    place.meet()

    def late_total(c, k):
        return late_down.at[c] if k == 2 else late_pair.at[c, k]

    def late_landed(c, k, which):
        return late_down_came.at[which, c] if k == 2 else late_pair_came.at[which, c, k]

    def late_home(c, k, of):
        chunks = down_grads_ref.shape[0] // 2 // WIDE
        at_cols = tile(of * chunks + chunks - LATE + c, WIDE)
        return down_grads_ref.at[at_cols, :] if k == 2 else pair_grads_ref.at[k, :, at_cols]

    def late_add(c, k, which):
        into, came_in = late_total(c, k), late_landed(c, k, which)
        into[...] = (into[...].astype(F32) + came_in[...].astype(F32)).astype(BF16)

    late = Chain(
        place, LATE, 3, late_total, late_landed, late_home, late_add, chain_sems[18:]
    )
    def slot(i):
        return pl.ds(i * rows, rows)

    def inner_copy(n):
        return copy_to(in_send.at[n], in_came.at[n], s_send.at[n], s_recv.at[n], place.x_peer)

    def store_row(at, values):
        for i in range(width // 128):
            misc[at + i : at + i + 1, :] = values[:, i * 128 : (i + 1) * 128]

    misc[...] = jnp.zeros_like(misc)
    grad = back_ref[...]
    in_send[0] = column(jnp.sum(grad * second_ref[...] * resid_ref[...], axis=1, keepdims=True))
    inner_copy(0).start()
    for copy in late_loads:
        copy.wait()
    late.step(0, 1)
    inv_two = inv_two_ref[:, :1]
    store_row(8, jnp.sum(back_ref[...] * resid_ref[...] * inv_two, axis=0, keepdims=True))
    inner_copy(0).wait()
    inner = (in_send[0, :, :1] + in_came[0, :, :1]) * inv_two * inv_two * inv_two / (2 * width)
    d_resid = (
        top_ref[...].astype(F32)
        + inv_two * (back_ref[...] * second_ref[...])
        - resid_ref[...] * inner
    )
    input_ref[...] = d_resid
    branch[slot(0), :] = d_resid.astype(BF16)
    to_core = copy_to(
        branch.at[slot(0), :], branch.at[slot(1), :], b_send.at[0], b_recv.at[0], place.core_peer
    )
    to_pair = copy_to(
        branch.at[slot(0), :], branch.at[slot(2), :], b_send.at[1], b_recv.at[1], place.y_peer
    )
    forward = copy_to(
        branch.at[slot(2), :], branch.at[slot(3), :], b_send.at[2], b_recv.at[2],
        place.core_peer,
    )
    to_core.start()
    to_pair.start()
    late.step(1, 1)

    def dg_copy(n):
        at_cols = pl.ds(n * cols, cols)
        return copy_to(
            dg_send.at[:, at_cols], dg_came.at[:, at_cols], d_send.at[n], d_recv.at[n],
            place.x_peer,
        )

    for copy in loads:
        copy.wait()
    halves_of = heads // 2
    for i in range(2):
        if i == 1:
            to_core.wait_recv()

        @each_tile(i * rows, rows)
        def _(at_rows):
            dg_send[at_rows, :] = nt(branch[at_rows, :], wo[1]).astype(BF16)

    for n in range(halves_of):
        dg_copy(n).start()
    late.step(2, 1)

    @each_tile(0, tokens)
    def _(at_rows):
        dg_own[at_rows, :] = nt(branch[at_rows, :], wo[0])

    dk[...] = jnp.zeros_like(dk)
    dv[...] = jnp.zeros_like(dv)
    gates[...] = jnp.zeros_like(gates)

    def unturn(values, at_rows):
        return values * cos_ref[at_rows, :] - pltpu.roll(values, 64, axis=1) * sin_ref[at_rows, :]

    def norm_back(values, raw, gain, at_rows, into):
        normed = unturn(values, at_rows)
        inverse = lax.rsqrt(jnp.mean(raw * raw, axis=1, keepdims=True) + EPS)
        misc[into : into + 1, :] += jnp.sum(normed * raw * inverse, axis=0, keepdims=True)
        scaled = normed * gain
        inner = jnp.mean(scaled * raw, axis=1, keepdims=True)
        return inverse * scaled - raw * (inverse * inverse * inverse * inner)

    lane = lax.broadcasted_iota(jnp.int32, (ROWS, 128), 1)

    def head(n):
        at_cols = pl.ds(n * hd, hd)
        kv = n * kv_heads // heads
        kv_cols = pl.ds(kv * hd, hd)

        @pl.loop(0, tokens // ROWS)
        def _(i):
            at_rows = tile(i, ROWS)
            query = q_ref[at_rows, at_cols]
            d_gated = dg_own[at_rows, at_cols] + dg_came[at_rows, at_cols].astype(F32)
            sig = sig_ref[at_rows, n : n + 1]
            d_att = (d_gated * sig).astype(BF16)
            d_logit = jnp.sum(d_gated * attended_ref[at_rows, at_cols], axis=1, keepdims=True)
            d_logit = d_logit * sig * (1.0 - sig)
            gates[at_rows, :] = jnp.where(lane == n, d_logit.astype(BF16), gates[at_rows, :])
            scores = nt(query, k_ref[:, kv_cols]) * scale
            key_at = key_at_ref[:1, :]
            allowed = (key_at <= at_ref[at_rows, :1]) & (key_at >= start_ref[at_rows, :1])
            probs = jnp.exp(jnp.where(allowed, scores, NEGATIVE) - log_ref[n, at_rows, :1])
            d_probs = nt(d_att, v_ref[:, kv_cols])
            mean = jnp.sum(d_probs * probs, axis=1, keepdims=True)
            d_scores = (probs * (d_probs - mean)).astype(BF16)
            dv[:, kv_cols] += tn(probs.astype(BF16), d_att)
            dk[:, kv_cols] += tn(d_scores, query)
            d_query = nn(d_scores, k_ref[:, kv_cols]) * scale
            own[2 * (n // 2), at_rows, pl.ds(n % 2 * hd, hd)] = norm_back(
                d_query, raw_ref[at_rows, at_cols], q_gain_ref[...], at_rows, 80
            ).astype(BF16)

    def key_value(n):
        kv_cols = pl.ds(n * hd, hd)

        @pl.loop(0, tokens // ROWS)
        def _(i):
            at_rows = tile(i, ROWS)
            raw = raw_ref[at_rows, pl.ds(qw + n * hd, hd)]
            own[2 * n + 1, at_rows, pl.ds(0, hd)] = norm_back(
                dk[at_rows, kv_cols] * scale, raw, k_gain_ref[...], at_rows, 81
            ).astype(BF16)
            own[2 * n + 1, at_rows, pl.ds(hd, hd)] = dv[at_rows, kv_cols].astype(BF16)

    def over_x(j):
        return copy_to(own.at[j], came.at[j], x_send.at[j], x_recv.at[j], place.x_peer)

    def over_y(j, mine):
        src = own.at[j] if mine else came.at[j]
        return copy_to(src, across.at[j], y_send.at[j], y_recv.at[j], place.y_peer)

    def send_chunk(j):
        over_x(j).start()

        @pl.when(side == 1)
        def _():
            over_y(j, True).start()

    def take_chunk(j):
        over_x(j).wait_recv()

        @pl.when(side == 0)
        def _():
            over_y(j, False).start()

    def add(c, k, which):
        total[c] = (total[c].astype(F32) + landed[which, c].astype(F32)).astype(BF16)

    chain = Chain(
        place, pieces, 1,
        lambda c, k: total.at[c],
        lambda c, k, which: landed.at[which, c],
        lambda c, k, of: grads_ref.at[of * pieces + c],
        add, chain_sems[:9],
    )

    def add_misc(c, k, which):
        misc[...] += misc_landed[which]

    small = Chain(
        place, 1, 1,
        lambda c, k: misc,
        lambda c, k, which: misc_landed.at[which],
        lambda c, k, of: misc_home,
        add_misc, chain_sems[9:18], share=False,
    )

    left = 3 * LATE
    outs = pieces - 2 * parts

    def step(u):
        if u < late.steps(1):
            late.step(u, 1)
        if u >= left:
            chain.step(u - left, 1)

    def out_piece(t):
        total[t] = nn(gated_ref[...], branch[:, pl.ds(t * cols, cols)]).astype(BF16)

    def block(j):
        over_y(j, True).wait_recv()
        block_src[...] = jnp.where(side == 0, own[j], came[j])
        for i in range(2):

            @each_tile(0, high, TILE)
            def _(at_rows):
                there = pl.ds(pl.multiple_of(at_rows.start + i * high, TILE), at_rows.size)
                total[outs + 2 * j + i, at_rows, :] = (
                    nn(turned_ref[there, pl.ds(0, tokens)], block_src[...])
                    + nn(turned_ref[there, pl.ds(tokens, tokens)], across[j])
                ).astype(BF16)

    def gates_copy():
        return copy_to(gates, gates_came, s_send.at[2], s_recv.at[2], place.x_peer)

    step(3)
    for n in range(kv_heads):
        dg_copy(n).wait_recv()
        head(2 * n)
        head(2 * n + 1)
        key_value(n)
        send_chunk(2 * n)
        send_chunk(2 * n + 1)
        if n == 0:
            to_pair.wait_recv()
            forward.start()
            step(4)
    gates_copy().start()

    def back_came(j):
        take_chunk(j)

        @each_tile(0, tokens)
        def _(at_rows):
            acc[at_rows, :] += nt(came[j, at_rows, :], w_main[parts + j])


    step(5)

    @each_tile(0, tokens)
    def _(at_rows):
        found = nt(own[0, at_rows, :], w_main[0])
        for j in range(1, parts):
            found += nt(own[j, at_rows, :], w_main[j])
        acc[at_rows, :] = found

    step(6)
    back_came(0)
    step(7)
    back_came(1)
    for u in range(8, left):
        step(u)
    forward.wait_recv()
    for t in range(outs):
        out_piece(t)
        step(left + t)
        if t + 2 < parts:
            back_came(t + 2)
    at = left + outs

    gates_copy().wait()
    moved = pltpu.roll(gates_came[...].astype(F32), heads, axis=1)
    both = (gates[...].astype(F32) + moved).astype(BF16)
    gates[...] = both

    @each_tile(0, tokens)
    def _(at_rows):
        acc[at_rows, :] += nt(gates[at_rows, :], w_gates_ref[...])

    fold = copy_to(fold_src, fold_dst, s_send.at[3], s_recv.at[3], place.core_peer)
    fold_src[...] = acc[rows:, :].astype(BF16)
    fold.start()
    block(0)
    step(at)
    gate_grads = nn(turned_ref[:, pl.ds(0, tokens)], both).T
    for i in range(width // 128):
        misc[16 + 8 * i : 24 + 8 * i, :] = gate_grads[:8, i * 128 : (i + 1) * 128]

    def misc_copy(n, peer):
        return copy_to(misc, misc_came.at[n], s_send.at[4 + n], s_recv.at[4 + n], peer)

    row_of = lax.broadcasted_iota(jnp.int32, (MISC, 128), 0)
    fold.wait_recv()
    grad = acc[:rows, :] + fold_dst[...].astype(F32)
    found = grad * hat_ref[...]
    in_send[1] = column(jnp.sum(found * norm_ref[...], axis=1, keepdims=True))
    inner_copy(1).start()
    acc[:rows, :] = grad
    store_row(0, jnp.sum(found, axis=0, keepdims=True))
    misc_copy(0, place.core_peer).start()
    step(at + 1)
    block(1)
    step(at + 2)
    misc_copy(0, place.core_peer).wait()
    misc[...] += jnp.where((row_of < 16) | (row_of >= 80), misc_came[0], 0.0)
    misc_copy(1, place.x_peer).start()
    step(at + 3)
    block(2)
    step(at + 4)
    misc_copy(1, place.x_peer).wait()
    misc[...] += jnp.where(row_of >= 80, misc_came[1], 0.0)
    misc_copy(2, place.y_peer).start()
    inner_copy(1).wait()
    inner = (in_send[1, :, :1] + in_came[1, :, :1]) / (2 * width)
    input_ref[...] += inv_one_ref[:, :1] * (acc[:rows, :] * norm_ref[...] - hat_ref[...] * inner)
    step(at + 5)
    block(3)
    misc_copy(2, place.y_peer).wait()
    misc[...] += misc_came[2]
    small.step(0)
    step(at + 6)
    small.step(1)
    step(at + 7)

    @pl.loop(pieces, chain.steps(1))
    def _(u):
        if late.steps(1) > left + pieces:
            late.step(u + left, 1)
        small.step(u - pieces + 2)
        chain.step(u, 1)

    @pl.loop(chain.steps(1) - pieces + 2, small.steps())
    def _(u):
        small.step(u)

    small.drain()
    sums_ref[...] = misc_home[...]
    chain.drain()
    late.drain()
    for copy in (to_core, to_pair, forward, fold):
        copy.wait_send()
    for n in range(halves_of):
        dg_copy(n).wait_send()
    for j in range(parts):
        over_x(j).wait_send()
        over_y(j, True).wait_send()


def rear(
    back, resid, inv_two, ffn_gain, top, raw, sig, query, keys, values, log, attended, cos, sin,
    at, start, key_at, q_gain, k_gain, turned, gated, w_gates, hat, inv_one, norm_gain,
    wq, wk, wv, wo, late_pair, late_down, pair_sum, down_sum,
):
    count = lax.axis_size("group")
    rows, width = back.shape
    tokens = 2 * rows
    hd = 128
    heads, kv_heads = query.shape[1] // hd, keys.shape[1] // hd
    qw, kw = heads * hd, kv_heads * hd
    cols = 2 * hd
    parts = heads // 2 + kv_heads
    high = gated.shape[0]
    pieces = 2 * parts + width // cols
    anywhere = pl.BlockSpec(memory_space=pl.ANY)
    local = pl.BlockSpec(memory_space=pltpu.VMEM)
    dma = pltpu.SemaphoreType.DMA
    struct = jax.ShapeDtypeStruct
    return pl.pallas_call(
        functools.partial(rear_kernel, count, heads, kv_heads),
        out_shape=(
            struct((2 * pieces, high, cols), BF16),
            struct((rows, width), F32),
            struct((MISC, 128), F32),
            struct(pair_sum.shape, BF16),
            struct(down_sum.shape, BF16),
        ),
        in_specs=[local] * 25 + [anywhere] * 8,
        out_specs=(anywhere, local, local, anywhere, anywhere),
        input_output_aliases={31: 3, 32: 4},
        scratch_shapes=[
            pltpu.VMEM((2 * parts, width, cols), BF16),
            pltpu.VMEM((2, qw, width), BF16),
            pltpu.VMEM((4 * rows, width), BF16),
            pltpu.VMEM((tokens, cols), BF16),
            pltpu.VMEM((tokens, qw), F32),
            pltpu.VMEM((tokens, qw), BF16),
            pltpu.VMEM((tokens, qw), BF16),
            pltpu.VMEM((tokens, kw), F32),
            pltpu.VMEM((tokens, kw), F32),
            pltpu.VMEM((tokens, 128), BF16),
            pltpu.VMEM((tokens, 128), BF16),
            pltpu.VMEM((parts, tokens, cols), BF16),
            pltpu.VMEM((parts, tokens, cols), BF16),
            pltpu.VMEM((parts, tokens, cols), BF16),
            pltpu.VMEM((pieces, high, cols), BF16),
            pltpu.VMEM((2, pieces, high, cols), BF16),
            pltpu.VMEM((MISC, 128), F32),
            pltpu.VMEM((3, MISC, 128), F32),
            pltpu.VMEM((2, MISC, 128), F32),
            pltpu.VMEM((MISC, 128), F32),
            pltpu.VMEM((tokens, width), F32),
            pltpu.VMEM((rows, width), BF16),
            pltpu.VMEM((rows, width), BF16),
            pltpu.VMEM((2, rows, 128), F32),
            pltpu.VMEM((2, rows, 128), F32),
            pltpu.VMEM(late_pair.shape, BF16),
            pltpu.VMEM(late_down.shape, BF16),
            pltpu.VMEM((2,) + late_pair.shape, BF16),
            pltpu.VMEM((2,) + late_down.shape, BF16),
            dma((2, kv_heads, 4)), dma((2,)), dma((3,)), dma((3,)), dma((heads // 2,)), dma((heads // 2,)),
            dma((parts,)), dma((parts,)), dma((parts,)), dma((parts,)), dma((7,)), dma((7,)),
            *chain_semaphores(pieces), *chain_semaphores(1), *chain_semaphores(3 * LATE),
        ],
        compiler_params=pltpu.CompilerParams(
            collective_id=2, has_side_effects=True, vmem_limit_bytes=60 << 20
        ),
        cost_estimate=pl.CostEstimate(
            flops=2 * tokens * width * (qw + 2 * kw) * 6, bytes_accessed=100 << 20,
            transcendentals=heads * tokens * tokens,
        ),
    )(
        back, resid, inv_two, ffn_gain, top, raw, sig, query, keys, values, log, attended, cos,
        sin, at, start, key_at, q_gain, k_gain, turned, gated, w_gates, hat, inv_one, norm_gain,
        wq, wk, wv, wo, late_pair, late_down, pair_sum, down_sum,
    )


def assemble_kernel(parts, outs, grads_ref, q_ref, k_ref, v_ref, o_ref, wide, sems):
    row_at = lax.axis_index("row")
    pieces = outs + 2 * parts
    high = grads_ref.shape[1]
    copies = []

    def move(src, dst):
        copies.append(pltpu.make_async_copy(src, dst, sems.at[len(copies)]))
        copies[-1].start()

    for s in range(2):
        at = row_at if s == 0 else 1 - row_at
        for p in range(pieces):
            n = s * pieces + p
            wide[n] = grads_ref[n].astype(F32)
            if p < outs:
                rows, cols = tile(at, high), pl.ds(p * 256, 256)
                move(wide.at[n], o_ref.at[rows, cols])
            else:
                j, i = (p - outs) // 2, (p - outs) % 2
                rows, head = pl.ds(i * high, high), at * (parts // 2) + j // 2
                if j % 2 == 0:
                    move(wide.at[n], q_ref.at[rows, tile(head, 256)])
                else:
                    for m, ref in enumerate((k_ref, v_ref)):
                        half = wide.at[n, :, pl.ds(m * 128, 128)]
                        move(half, ref.at[rows, tile(head, 128)])
    for copy in copies:
        copy.wait()


def assemble(grads, q_shape, k_shape, o_shape, head_dim):
    parts = q_shape[1] // 2 // head_dim // 2 + k_shape[1] // 2 // head_dim
    outs = grads.shape[0] // 2 - 2 * parts
    anywhere = pl.BlockSpec(memory_space=pl.ANY)
    struct = jax.ShapeDtypeStruct
    count = 2 * (outs + 3 * parts)
    return pl.pallas_call(
        functools.partial(assemble_kernel, parts, outs),
        out_shape=(
            struct(q_shape, F32), struct(k_shape, F32), struct(k_shape, F32), struct(o_shape, F32),
        ),
        in_specs=[pl.BlockSpec(memory_space=pltpu.VMEM)],
        out_specs=(anywhere,) * 4,
        scratch_shapes=[
            pltpu.VMEM(grads.shape, F32),
            pltpu.SemaphoreType.DMA((count,)),
        ],
        compiler_params=pltpu.CompilerParams(vmem_limit_bytes=40 << 20),
    )(grads)


def body(
    tokens, lengths, norm_gain, w_query, w_key, w_value, w_head_gate, query_gain, key_gain,
    w_out, ffn_gain, w_gate, w_up, w_down, grad_out,
):
    rows, d_loc = tokens.shape
    group_tok = 2 * rows
    head_dim = query_gain.shape[0]
    gate_half = w_head_gate.shape[1] // 2
    row_at = lax.axis_index("row")
    col_at = lax.axis_index("col")
    side = lax.axis_index("group") % 2

    steps = jnp.arange(rows, dtype=jnp.int32)
    index = jnp.concatenate([col_at * rows + steps, (1 - col_at) * rows + steps])
    place = places(lengths, index)[1]
    cosines, sines = rope_tables(place, head_dim)
    signed = jnp.concatenate([-sines[:, : head_dim // 2], sines[:, head_dim // 2 :]], axis=1)
    positions = (
        jnp.broadcast_to(index[:, None], (group_tok, 128)),
        jnp.broadcast_to((index - place)[:, None], (group_tok, 128)),
        jnp.broadcast_to(index[None], (8, group_tok)),
    )
    w_gates = jnp.pad(
        jnp.concatenate(halves(w_head_gate, 1, row_at), axis=1),
        ((0, 0), (0, 128 - 2 * gate_half)),
    )
    gains = (query_gain[None], key_gain[None])
    (
        normed_two, resid, inverse_two, hat, inverse_one, turned, grad_all, early_grad,
        raw, gate_sigmoid, query, keys, values, logsum, attended, gated_both,
    ) = front(
        tokens, grad_out, norm_gain[None], ffn_gain[None], *gains, cosines, signed, *positions,
        w_gates, w_query, w_key, w_value, w_out, w_down,
    )
    gated, gated_came = gated_both[0], gated_both[1]
    first_side = side == 0
    gated_pair = jnp.concatenate(
        [
            jnp.where(first_side, gated, gated_came),
            swap_groups(jnp.where(first_side, gated_came, gated)),
        ]
    ).T

    pair_sum, down_sum, late_pair, late_down, _, _, branch, branch_out, d_normed_two = ffn(
        normed_two, grad_all, early_grad, w_gate, w_up, w_down
    )
    output = (resid + branch + swap_groups(branch_out).astype(F32)).astype(BF16)

    grads, input_grad, sums, pair_sum, down_sum = rear(
        d_normed_two, resid, inverse_two, ffn_gain[None], grad_out, raw, gate_sigmoid, query,
        keys, values, logsum, attended, cosines, signed, *positions, *gains, turned, gated_pair,
        w_gates, hat, inverse_one, norm_gain[None], w_query, w_key, w_value, w_out,
        late_pair, late_down, pair_sum, down_sum,
    )
    grad_norm_gain = sums[:8].reshape(d_loc)
    grad_ffn_gain = sums[8:16].reshape(d_loc)
    grad_gates = sums[16:80].reshape(8, 2 * gate_half, 128).transpose(1, 0, 2)
    grad_gates = grad_gates.reshape(2 * gate_half, d_loc)
    grad_head_gate = ordered(grad_gates[:gate_half], grad_gates[gate_half:], 0, row_at).T

    grad_query, grad_key, grad_value, grad_out_w = assemble(
        grads, w_query.shape, w_key.shape, w_out.shape, head_dim
    )
    return (
        output,
        input_grad,
        grad_norm_gain,
        grad_query,
        grad_key,
        grad_value,
        grad_head_gate,
        sums[80],
        sums[81],
        grad_out_w,
        grad_ffn_gain,
        pair_sum[0].astype(F32),
        pair_sum[1].astype(F32),
        down_sum.astype(F32),
    )


def solution(mesh):
    shards = P(("group", "col"), "row")
    in_specs = (
        shards,
        P("group"),
        P("row"),
        P("row", "col"),
        P("row", "col"),
        P("row", "col"),
        P("row", "col"),
        P(),
        P(),
        P("col", "row"),
        P("row"),
        P("row", "col"),
        P("row", "col"),
        P("col", "row"),
        shards,
    )
    out_specs = (
        shards,
        shards,
        P("row"),
        P("row", "col"),
        P("row", "col"),
        P("row", "col"),
        P("row", "col"),
        P(),
        P(),
        P("col", "row"),
        P("row"),
        P("row", "col"),
        P("row", "col"),
        P("col", "row"),
    )
    return jax.shard_map(body, mesh=mesh, in_specs=in_specs, out_specs=out_specs, check_vma=False)
```

```python
import functools

import jax
import jax.numpy as jnp
from jax import lax
from jax.experimental import pallas as pl
from jax.experimental.pallas import tpu as pltpu
from jax.sharding import PartitionSpec as P

EPS = 1e-06
THETA = 1000000.0
NEGATIVE = -1e30
MESH = pl.DeviceIdType.MESH
F32 = jnp.float32
BF16 = jnp.bfloat16


def swap_groups(values):
    count = lax.axis_size("group")
    return lax.ppermute(values, "group", [(i, i ^ 1) for i in range(count)])


def halves(values, axis, at):
    low, high = jnp.split(values, 2, axis=axis)
    first = at == 0
    return jnp.where(first, low, high), jnp.where(first, high, low)


def ordered(own, other, axis, at):
    first = at == 0
    return jnp.concatenate(
        [jnp.where(first, own, other), jnp.where(first, other, own)], axis=axis
    )


def places(lengths_group, index):
    ends = jnp.cumsum(lengths_group)
    passed = (index[:, None] >= ends[None, :]).astype(jnp.int32)
    segment = jnp.sum(passed, axis=1)
    place = index - jnp.sum(passed * lengths_group[None, :], axis=1)
    return (segment, place)


def rope_tables(place, width):
    half = width // 2
    freq = THETA ** (-(jnp.arange(half, dtype=F32) * 2.0 / width))
    angle = place.astype(F32)[:, None] * freq[None, :]
    cosines = jnp.concatenate([jnp.cos(angle), jnp.cos(angle)], axis=1)
    sines = jnp.concatenate([jnp.sin(angle), jnp.sin(angle)], axis=1)
    return (cosines, sines)


TILE = 256
HOP = 2
WIDE = 128
EARLY = 6
AHEAD = 2
LATE = 3


def nt(a, b):
    return lax.dot_general(a, b, (((1,), (1,)), ((), ())), preferred_element_type=F32)


def nn(a, b):
    return jnp.dot(a, b, preferred_element_type=F32)


def copy_to(src, dst, send_sem, recv_sem, peer):
    return pltpu.make_async_remote_copy(
        src_ref=src, dst_ref=dst, send_sem=send_sem, recv_sem=recv_sem,
        device_id=peer, device_id_type=MESH,
    )


def tile(i, size=TILE):
    return pl.ds(pl.multiple_of(i * size, size), size)


class Place:
    def __init__(self, count):
        group = lax.axis_index("group")
        self.line = count // 2
        self.root = (self.line - 1) // 2
        self.deep = max(self.root, self.line - 1 - self.root)
        self.at = group // 2
        self.side = group % 2
        self.x_peer = {"row": 1 - lax.axis_index("row")}
        self.core_peer = {"col": 1 - lax.axis_index("col")}
        self.y_peer = {"group": group + 1 - 2 * self.side}
        self.above = {"group": jnp.minimum(group + 2, count - 1)}
        self.below = {"group": jnp.maximum(group - 2, 0)}
        self.has_above = self.at < self.line - 1
        self.has_below = self.at > 0

    def meet(self):
        barrier = pltpu.get_barrier_semaphore()

        def greet(peer):
            pl.semaphore_signal(barrier, inc=1, device_id=peer, device_id_type=MESH)

        for peer in (self.x_peer, self.core_peer, self.y_peer):
            greet(peer)
        pl.when(self.has_above)(lambda: greet(self.above))
        pl.when(self.has_below)(lambda: greet(self.below))
        met = 3 + self.has_above.astype(jnp.int32) + self.has_below.astype(jnp.int32)
        pl.semaphore_wait(barrier, met)


class Chain:
    def __init__(self, place, chunks, kinds, total, came, home, add, sems, share=True):
        self.place, self.chunks, self.kinds = place, chunks, kinds
        self.total, self.came, self.home, self.add = total, came, home, add
        self.sems, self.share = sems, share

    def part_copy(self, c, k, upward):
        sent, low, high = self.sems[:3]
        p = self.kinds * c + k
        peer, which, arrived = (
            (self.place.above, 0, low) if upward else (self.place.below, 1, high)
        )
        return copy_to(
            self.total(c, k), self.came(c, k, which), sent.at[p], arrived.at[p], peer
        )

    def final_copy(self, c, k, upward, first):
        up, down, arrived = self.sems[3:6]
        p = self.kinds * c + k
        src = self.total(c, k) if first else self.home(c, k, self.place.side)
        peer, sent = (self.place.above, up) if upward else (self.place.below, down)
        return copy_to(src, self.home(c, k, self.place.side), sent.at[p], arrived.at[p], peer)

    def keep_copy(self, c, k):
        return pltpu.make_async_copy(
            self.total(c, k), self.home(c, k, self.place.side),
            self.sems[6].at[self.kinds * c + k],
        )

    def share_copy(self, c, k, first, of=None):
        p = self.kinds * c + k
        of = self.place.side if of is None else of
        src = self.total(c, k) if first else self.home(c, k, self.place.side)
        return copy_to(
            src, self.home(c, k, of), self.sems[7].at[p], self.sems[8].at[p], self.place.y_peer
        )

    def step(self, u, hop=1):
        at, line, root, deep = self.place.at, self.place.line, self.place.root, self.place.deep
        behind = jnp.where(at < root, at, jnp.where(at > root, line - 1 - at, deep))
        self.inward(u - hop * behind)
        self.outward(u - hop * (deep + jnp.abs(at - root)))

    def kinds_of(self, p):
        live = (p >= 0) & (p < self.kinds * self.chunks)
        if self.kinds == 1:
            return [(live, p, 0)]
        p = jnp.maximum(p, 0)
        return [
            (live & (lax.rem(p, self.kinds) == k), lax.div(p, self.kinds), k)
            for k in range(self.kinds)
        ]

    def inward(self, piece):
        at, line, root = self.place.at, self.place.line, self.place.root
        for live, c, k in self.kinds_of(piece):

            @pl.when(live & (at < root))
            def _():
                @pl.when(self.place.has_below)
                def _():
                    self.part_copy(c, k, True).wait_recv()
                    self.add(c, k, 0)

                self.part_copy(c, k, True).start()

            @pl.when(live & (at > root))
            def _():
                @pl.when(self.place.has_above)
                def _():
                    self.part_copy(c, k, False).wait_recv()
                    self.add(c, k, 1)

                self.part_copy(c, k, False).start()

            @pl.when(live & (at == root))
            def _():
                if root > 0:
                    self.part_copy(c, k, True).wait_recv()
                    self.add(c, k, 0)
                if root < line - 1:
                    self.part_copy(c, k, False).wait_recv()
                    self.add(c, k, 1)
                if root > 0:
                    self.final_copy(c, k, False, True).start()
                if root < line - 1:
                    self.final_copy(c, k, True, True).start()
                if self.share:
                    self.share_copy(c, k, True).start()
                self.keep_copy(c, k).start()

    def outward(self, piece):
        at, root = self.place.at, self.place.root
        for live, c, k in self.kinds_of(piece):

            @pl.when(live & (at != root))
            def _():
                self.final_copy(c, k, True, False).wait_recv()

                @pl.when((at > root) & self.place.has_above)
                def _():
                    self.final_copy(c, k, True, False).start()

                @pl.when((at < root) & self.place.has_below)
                def _():
                    self.final_copy(c, k, False, False).start()

                if self.share:
                    self.share_copy(c, k, False).start()

    def steps(self, hop=1):
        return self.kinds * self.chunks + 2 * hop * self.place.deep

    def drain(self):
        at, line, root = self.place.at, self.place.line, self.place.root

        @pl.loop(0, self.chunks)
        def _(c):
            for k in range(self.kinds):
                if self.share:
                    self.share_copy(c, k, False, 1 - self.place.side).wait_recv()
                    self.share_copy(c, k, False).wait_send()

                @pl.when(at == root)
                def _():
                    self.keep_copy(c, k).wait()
                    if root > 0:
                        self.final_copy(c, k, False, True).wait_send()
                    if root < line - 1:
                        self.final_copy(c, k, True, True).wait_send()

                @pl.when(at < root)
                def _():
                    self.part_copy(c, k, True).wait_send()

                    @pl.when(self.place.has_below)
                    def _():
                        self.final_copy(c, k, False, False).wait_send()

                @pl.when(at > root)
                def _():
                    self.part_copy(c, k, False).wait_send()

                    @pl.when(self.place.has_above)
                    def _():
                        self.final_copy(c, k, True, False).wait_send()


def chain_semaphores(pieces):
    return [pltpu.SemaphoreType.DMA((pieces,)) for _ in range(9)]


def ffn_kernel(
    count, chunks, h_ref, top_ref, early_ref, gate_ref, up_ref, down_ref,
    pair_grads_ref, down_grads_ref, late_pair_ref, late_down_ref, pair_came_ref, down_came_ref,
    branch_ref, branch_out_ref, back_ref,
    h_all, h_turned, sent, came, top_sent, top_came, grad_part, w_pair, w_down, acc_branch, acc_back, parts, inner_turned,
    pair_total, down_total, pair_stage, down_stage, reduce_recv,
    gather_send, gather_recv, x_send, x_recv, top_send, top_recv, late_sem, load_sem, weight_sem, fold_send, fold_recv,
    *chain_sems,
):
    place = Place(count)
    rows, width = h_ref.shape
    tokens = h_all.shape[0]
    tiles = tokens // TILE
    wide = w_down.shape[0] // chunks
    side = place.side

    def weight_copies(j):
        cols = tile(side * chunks + j, wide)
        return (
            pltpu.make_async_copy(
                gate_ref.at[:, cols], w_pair.at[j, :, pl.ds(0, wide)], weight_sem.at[0, j]
            ),
            pltpu.make_async_copy(
                up_ref.at[:, cols], w_pair.at[j, :, pl.ds(wide, wide)], weight_sem.at[1, j]
            ),
            pltpu.make_async_copy(
                down_ref.at[cols, :], w_down.at[tile(j, wide), :], weight_sem.at[2, j]
            ),
        )

    @pl.loop(0, chunks)
    def _(j):
        for copy in weight_copies(j):
            copy.start()

    place.meet()

    def slot(i):
        return pl.ds(i * rows, rows)

    to_y = copy_to(h_ref, h_all.at[slot(2)], gather_send.at[0], gather_recv.at[0], place.y_peer)
    to_core = copy_to(
        h_ref, h_all.at[slot(1)], gather_send.at[1], gather_recv.at[1], place.core_peer
    )
    forward = copy_to(
        h_all.at[slot(2)], h_all.at[slot(3)], gather_send.at[2], gather_recv.at[2],
        place.core_peer,
    )
    to_y.start()
    to_core.start()

    def top_exchange(j):
        n = j - EARLY
        return copy_to(
            top_sent.at[n], top_came.at[n], top_send.at[n], top_recv.at[n], place.x_peer
        )

    def top_project(j):
        @pl.loop(0, tiles)
        def _(i):
            top_sent[j - EARLY, tile(i), :] = nt(
                top_ref[tile(i), :], w_down[tile(j, wide), :]
            ).astype(BF16)

        top_exchange(j).start()

    def exchange(j):
        return copy_to(
            sent.at[lax.rem(j, 3)], came.at[j], x_send.at[j], x_recv.at[j], place.x_peer
        )

    def first_half(i):
        at_rows = pl.ds(2 * i * rows, 2 * rows)
        n = i * chunks
        return copy_to(
            sent.at[0, at_rows, :], came.at[0, at_rows, :], x_send.at[n], x_recv.at[n],
            place.x_peer,
        )

    def project_half(i):
        for n in range(2):
            at_rows = slot(2 * i + n)
            sent[0, at_rows, :] = nn(h_all[at_rows, :], w_pair[0]).astype(BF16)
        first_half(i).start()

    def project(j):
        for copy in weight_copies(j)[:2]:
            copy.wait()

        @pl.loop(0, tiles)
        def _(i):
            sent[lax.rem(j, 3), tile(i), :] = nn(h_all[tile(i), :], w_pair[j]).astype(BF16)

    def work(j):
        @pl.when(j == 0)
        def _():
            first_half(0).wait_recv()
            first_half(1).wait_recv()

        @pl.when(j > 0)
        def _():
            exchange(j).wait_recv()

        @pl.when(j < EARLY)
        def _():
            grad_part[...] = early_ref[:, tile(j, wide)].astype(F32)

        @pl.when(j >= EARLY)
        def _():
            top_exchange(j).wait_recv()
            grad_part[...] = top_sent[j - EARLY].astype(F32) + top_came[j - EARLY].astype(F32)

        @pl.loop(0, tiles)
        def _(i):
            at_rows = tile(i)
            pair = sent[lax.rem(j, 3), at_rows, :].astype(F32) + came[j, at_rows, :].astype(F32)
            gate, up = pair[:, :wide], pair[:, wide:]
            grad = grad_part[at_rows, :]
            sig = 1.0 / (1.0 + jnp.exp(-gate))
            silu = gate * sig
            parts[at_rows, pl.ds(0, wide)] = (
                grad * up * (sig * (1.0 + gate * (1.0 - sig)))
            ).astype(BF16)
            parts[at_rows, pl.ds(wide, wide)] = (grad * silu).astype(BF16)
            inner = (silu * up).astype(BF16)
            inner_turned[:, at_rows] = inner.T
            acc_branch[at_rows, :] += nn(inner, w_down[tile(j, wide), :])
            acc_back[at_rows, :] += nt(parts[at_rows, :], w_pair[j])

    def gradients(j):
        @pl.loop(0, width // TILE)
        def _(i):
            pair = nn(h_turned[tile(i), :], parts[...])
            pair_total[j, 0, tile(i), :] = pair[:, :wide].astype(BF16)
            pair_total[j, 1, tile(i), :] = pair[:, wide:].astype(BF16)
            down_total[j, :, tile(i)] = nn(inner_turned[...], top_ref[:, tile(i)]).astype(BF16)

    def total(c, k):
        return down_total.at[c] if k == 2 else pair_total.at[c, k]

    def landed(c, k, which):
        return down_came_ref.at[which, c] if k == 2 else pair_came_ref.at[which, c, k]

    def home(c, k, of):
        at_cols = tile(of * chunks + c, wide)
        return down_grads_ref.at[at_cols, :] if k == 2 else pair_grads_ref.at[k, :, at_cols]

    def add(c, k, which):
        stage = (down_stage if k == 2 else pair_stage).at[which]
        copy = pltpu.make_async_copy(landed(c, k, which), stage, load_sem.at[which])
        copy.start()
        copy.wait()
        into = total(c, k)

        @pl.loop(0, into.shape[0] // wide)
        def _(i):
            at_rows = tile(i, wide)
            into[at_rows, :] = (
                into[at_rows, :].astype(F32) + stage[at_rows, :].astype(F32)
            ).astype(BF16)

    ours = chunks - LATE
    chain = Chain(place, ours, 3, total, landed, home, add, chain_sems)

    def late_copies(c):
        return (
            pltpu.make_async_copy(pair_total.at[c], late_pair_ref.at[c - ours], late_sem.at[0, c - ours]),
            pltpu.make_async_copy(down_total.at[c], late_down_ref.at[c - ours], late_sem.at[1, c - ours]),
        )

    h_all[slot(0), :] = h_ref[...]
    for copy in weight_copies(0)[:2]:
        copy.wait()
    to_core.wait_recv()
    project_half(0)

    @pl.loop(0, chunks)
    def _(j):
        weight_copies(j)[2].wait()

    @pl.loop(EARLY, min(EARLY + AHEAD, chunks))
    def _(j):
        top_project(j)

    acc_branch[...] = jnp.zeros_like(acc_branch)
    acc_back[...] = jnp.zeros_like(acc_back)
    to_y.wait_recv()
    forward.start()
    forward.wait_recv()
    project_half(1)
    project(1)

    @pl.loop(0, tiles)
    def _(i):
        h_turned[:, tile(i)] = h_all[tile(i), :].T

    first_half(0).wait_send()
    first_half(1).wait_send()
    exchange(1).start()

    @pl.loop(0, chunks)
    def _(t):
        work(t)
        chain.step(3 * t - 1, HOP)
        gradients(t)

        @pl.when(t >= ours)
        def _():
            for copy in late_copies(t):
                copy.start()

        chain.step(3 * t, HOP)

        @pl.when(t + 2 < chunks)
        def _():
            @pl.when(t >= 2)
            def _():
                exchange(t - 1).wait_send()

            project(t + 2)
            exchange(t + 2).start()

        @pl.when((t + AHEAD >= EARLY + AHEAD) & (t + AHEAD < chunks))
        def _():
            top_project(t + AHEAD)

        chain.step(3 * t + 1, HOP)

    chain.step(3 * chunks - 1, HOP)

    def fold_source(n, i):
        if i == 2:
            return w_down.at[slot(0), :]
        return h_all.at[slot(2 * n + i), :]

    def fold(n, i):
        return copy_to(
            fold_source(n, i), reduce_recv.at[n, i], fold_send.at[n, i], fold_recv.at[n, i],
            place.y_peer if i == 2 else place.core_peer,
        )

    to_y.wait_send()
    to_core.wait_send()
    forward.wait_send()
    for n, acc in enumerate((acc_back, acc_branch)):
        for i in (1, 0):
            fold_source(n, i)[...] = acc[slot(2 * i + 1), :].astype(BF16)
            fold(n, i).start()
    fold(0, 1).wait_recv()
    fold_source(0, 2)[...] = (acc_back[slot(2), :] + reduce_recv[0, 1].astype(F32)).astype(BF16)
    fold(0, 2).start()
    chain.step(3 * chunks, HOP)
    fold(1, 0).wait_recv()
    fold(1, 1).wait_recv()
    branch_ref[...] = acc_branch[slot(0), :] + reduce_recv[1, 0].astype(F32)
    branch_out_ref[...] = (acc_branch[slot(2), :] + reduce_recv[1, 1].astype(F32)).astype(BF16)
    fold(0, 0).wait_recv()
    fold(0, 2).wait_recv()
    back_ref[...] = (
        acc_back[slot(0), :] + reduce_recv[0, 0].astype(F32) + reduce_recv[0, 2].astype(F32)
    )

    @pl.loop(3 * chunks + 1, max(3 * chunks + 1, chain.steps(HOP)))
    def _(u):
        chain.step(u, HOP)

    @pl.loop(ours, chunks)
    def _(c):
        for copy in late_copies(c):
            copy.wait()

    chain.drain()

    @pl.loop(max(chunks - 3, 0), chunks)
    def _(j):
        exchange(j).wait_send()

    @pl.loop(EARLY, chunks)
    def _(j):
        top_exchange(j).wait_send()

    for n, i in ((0, 0), (0, 1), (0, 2), (1, 0), (1, 1)):
        fold(n, i).wait_send()


def ffn(h, top, early, w_gate, w_up, w_down):
    count = lax.axis_size("group")
    rows, width = h.shape
    hidden = w_gate.shape[1] // 2
    wide = WIDE
    chunks = hidden // wide
    tokens = 4 * rows
    anywhere = pl.BlockSpec(memory_space=pl.ANY)
    local = pl.BlockSpec(memory_space=pltpu.VMEM)
    dma = pltpu.SemaphoreType.DMA
    pieces = 3 * (chunks - LATE)
    flops = 2 * tokens * width * hidden * 8
    return pl.pallas_call(
        functools.partial(ffn_kernel, count, chunks),
        out_shape=(
            jax.ShapeDtypeStruct((2, width, 2 * hidden), BF16),
            jax.ShapeDtypeStruct((2 * hidden, width), BF16),
            jax.ShapeDtypeStruct((LATE, 2, width, wide), BF16),
            jax.ShapeDtypeStruct((LATE, wide, width), BF16),
            jax.ShapeDtypeStruct((2, chunks - LATE, 2, width, wide), BF16),
            jax.ShapeDtypeStruct((2, chunks - LATE, wide, width), BF16),
            jax.ShapeDtypeStruct((rows, width), F32),
            jax.ShapeDtypeStruct((rows, width), BF16),
            jax.ShapeDtypeStruct((rows, width), F32),
        ),
        in_specs=[local, local, local, anywhere, anywhere, anywhere],
        out_specs=(anywhere,) * 6 + (local,) * 3,
        scratch_shapes=[
            pltpu.VMEM((tokens, width), BF16),
            pltpu.VMEM((width, tokens), BF16),
            pltpu.VMEM((3, tokens, 2 * wide), BF16),
            pltpu.VMEM((chunks, tokens, 2 * wide), BF16),
            pltpu.VMEM((chunks - EARLY, tokens, wide), BF16),
            pltpu.VMEM((chunks - EARLY, tokens, wide), BF16),
            pltpu.VMEM((tokens, wide), F32),
            pltpu.VMEM((chunks, width, 2 * wide), BF16),
            pltpu.VMEM((hidden, width), BF16),
            pltpu.VMEM((tokens, width), F32),
            pltpu.VMEM((tokens, width), F32),
            pltpu.VMEM((tokens, 2 * wide), BF16),
            pltpu.VMEM((wide, tokens), BF16),
            pltpu.VMEM((chunks, 2, width, wide), BF16),
            pltpu.VMEM((chunks, wide, width), BF16),
            pltpu.VMEM((2, width, wide), BF16),
            pltpu.VMEM((2, wide, width), BF16),
            pltpu.VMEM((2, 3, rows, width), BF16),
            dma((3,)), dma((3,)), dma((chunks + 1,)), dma((chunks + 1,)),
            dma((chunks - EARLY,)), dma((chunks - EARLY,)),
            dma((2, LATE)), dma((2,)), dma((3, chunks)), dma((2, 3)), dma((2, 3)),
            *chain_semaphores(pieces),
        ],
        compiler_params=pltpu.CompilerParams(
            collective_id=1, has_side_effects=True, vmem_limit_bytes=63 << 20
        ),
        cost_estimate=pl.CostEstimate(
            flops=flops, bytes_accessed=200 << 20, transcendentals=tokens * hidden
        ),
    )(h, top, early, w_gate, w_up, w_down)


ROWS = 128


def sigmoid(v):
    return 1.0 / (1.0 + jnp.exp(-v))


def each_tile(start, count, size=160):
    def run(step):
        @pl.loop(0, count // size)
        def _(i):
            step(pl.ds(pl.multiple_of(start + i * size, 32), size))

    return run


def column(values):
    return jnp.broadcast_to(values, (values.shape[0], 128))


def front_kernel(
    count, heads, kv_heads, tok_ref, top_ref, norm_ref, second_ref, q_gain_ref, k_gain_ref,
    cos_ref, sin_ref, at_ref, start_ref, key_at_ref, w_gates_ref, wq_ref, wk_ref, wv_ref, wo_ref,
    wd_ref,
    h_ref, resid_ref, inv_two_ref, hat_ref, inv_one_ref, turned_ref, tops_ref, early_ref,
    raw_ref, sig_ref, q_ref, k_ref, v_ref, log_ref, attended_ref, gated_ref,
    normed_all, wq, wk, wv, wo, wd, kv_send, kv_came, q_send, q_came, gates, early_send, early_came,
    ss_send, ss_came, fold_src, fold_dst, acc,
    w_sem, n_send, n_recv, t_send, t_recv, p_send, p_recv, e_send, e_recv, g_send, g_recv,
    s_send, s_recv,
):
    place = Place(count)
    rows, width = tok_ref.shape
    tokens = 2 * rows
    row_at = lax.axis_index("row")
    side = place.side
    hd = 128
    qw, kw = heads * hd, kv_heads * hd
    hidden = wd_ref.shape[0] // 2
    scale = hd**-0.5

    loads = []
    for i, at in enumerate((row_at, 1 - row_at)):
        q_cols, k_cols = tile(at, qw), tile(at, kw)
        loads += [
            pltpu.make_async_copy(wk_ref.at[:, k_cols], wk.at[i], w_sem.at[i, 0]),
            pltpu.make_async_copy(wv_ref.at[:, k_cols], wv.at[i], w_sem.at[i, 1]),
            pltpu.make_async_copy(wq_ref.at[:, q_cols], wq.at[i], w_sem.at[i, 2]),
            pltpu.make_async_copy(wo_ref.at[q_cols, :], wo.at[i], w_sem.at[i, 3]),
        ]
    down_rows = pl.ds(pl.multiple_of(side * hidden, WIDE), wd.shape[0])
    loads.append(pltpu.make_async_copy(wd_ref.at[down_rows, :], wd, w_sem.at[0, 4]))
    for copy in loads:
        copy.start()
    place.meet()

    def slot(i):
        return pl.ds(i * rows, rows)

    def spread(ref, sends, recvs):
        own, core, pair, both = (ref.at[slot(i), :] for i in range(4))
        return (
            copy_to(own, core, sends.at[0], recvs.at[0], place.core_peer),
            copy_to(own, pair, sends.at[1], recvs.at[1], place.y_peer),
            copy_to(pair, both, sends.at[2], recvs.at[2], place.core_peer),
        )

    tops_ref[slot(0), :] = top_ref[...]
    tops = spread(tops_ref, t_send, t_recv)
    tops[0].start()
    tops[1].start()

    def squares(n):
        return copy_to(ss_send.at[n], ss_came.at[n], s_send.at[n], s_recv.at[n], place.x_peer)

    x = tok_ref[...].astype(F32)
    ss_send[0] = column(jnp.sum(x * x, axis=1, keepdims=True))
    squares(0).start()

    def early(i):
        return copy_to(
            early_send.at[slot(i), :], early_came.at[slot(i), :], e_send.at[i], e_recv.at[i],
            place.x_peer,
        )

    def early_start(i):
        @each_tile(i * rows, rows)
        def _(at_rows):
            early_send[at_rows, :] = nt(tops_ref[at_rows, :], wd[...]).astype(BF16)

        early(i).start()

    loads[-1].wait()
    early_start(0)
    squares(0).wait()
    inv_one = lax.rsqrt((ss_send[0] + ss_came[0]) / (2 * width) + EPS)
    inv_one_ref[...] = inv_one
    hat = tok_ref[...].astype(F32) * inv_one[:, :1]
    hat_ref[...] = hat
    normed_all[slot(0), :] = (hat * norm_ref[...]).astype(BF16)
    normed = spread(normed_all, n_send, n_recv)
    normed[0].start()
    normed[1].start()

    kv_copy = copy_to(kv_send, kv_came, p_send.at[0], p_recv.at[0], place.x_peer)
    q_copy = copy_to(q_send, q_came, p_send.at[1], p_recv.at[1], place.x_peer)
    for copy in loads[:-1]:
        copy.wait()
    for i in range(2):
        if i == 1:
            normed[0].wait_recv()

        @each_tile(i * rows, rows)
        def _(at_rows):
            rows_in = normed_all[at_rows, :]
            kv_send[at_rows, pl.ds(0, kw)] = nn(rows_in, wk[1]).astype(BF16)
            kv_send[at_rows, pl.ds(kw, kw)] = nn(rows_in, wv[1]).astype(BF16)

    kv_copy.start()

    @each_tile(0, tokens)
    def _(at_rows):
        rows_in = normed_all[at_rows, :]
        q_send[at_rows, pl.ds(0, qw)] = nn(rows_in, wq[1]).astype(BF16)
        part = nn(rows_in, w_gates_ref[...])
        gates[at_rows, :] = part
        q_send[at_rows, pl.ds(qw, 128)] = part.astype(BF16)

    q_copy.start()

    @each_tile(0, tokens)
    def _(at_rows):
        rows_in = normed_all[at_rows, :]
        raw_ref[at_rows, pl.ds(0, qw)] = nn(rows_in, wq[0])
        raw_ref[at_rows, pl.ds(qw, kw)] = nn(rows_in, wk[0])
        raw_ref[at_rows, pl.ds(qw + kw, kw)] = nn(rows_in, wv[0])


    def turn(values, gain, at_rows):
        inverse = lax.rsqrt(jnp.mean(values * values, axis=1, keepdims=True) + EPS)
        scaled = values * inverse * gain
        return scaled * cos_ref[at_rows, :] + pltpu.roll(scaled, 64, axis=1) * sin_ref[at_rows, :]

    tops[1].wait_recv()
    tops[2].start()
    normed[1].wait_recv()
    normed[2].start()
    tops[0].wait_recv()
    kv_copy.wait_recv()

    @pl.loop(0, tokens // ROWS)
    def _(i):
        at_rows = tile(i, ROWS)
        for n in range(kv_heads):
            cols = pl.ds(qw + n * hd, hd)
            key = raw_ref[at_rows, cols] + kv_came[at_rows, pl.ds(n * hd, hd)].astype(F32)
            raw_ref[at_rows, cols] = key
            k_ref[at_rows, pl.ds(n * hd, hd)] = turn(key, k_gain_ref[...], at_rows).astype(BF16)
            cols = pl.ds(qw + kw + n * hd, hd)
            value = raw_ref[at_rows, cols] + kv_came[at_rows, pl.ds(kw + n * hd, hd)].astype(F32)
            raw_ref[at_rows, cols] = value
            v_ref[at_rows, pl.ds(n * hd, hd)] = value.astype(BF16)

    q_copy.wait_recv()
    early_start(1)

    @pl.loop(0, tokens // ROWS)
    def _(i):
        at_rows = tile(i, ROWS)
        other = q_came[at_rows, pl.ds(qw, 128)].astype(F32)
        logit = gates[at_rows, :] + pltpu.roll(other, 128 - heads, axis=1)
        sig_ref[at_rows, :] = sigmoid(logit)
        for n in range(heads):
            cols = pl.ds(n * hd, hd)
            query = raw_ref[at_rows, cols] + q_came[at_rows, cols].astype(F32)
            raw_ref[at_rows, cols] = query
            q_ref[at_rows, cols] = turn(query, q_gain_ref[...], at_rows).astype(BF16)

    def head_copy(n):
        cols = pl.ds(n * hd, hd)
        return copy_to(
            gated_ref.at[0, :, cols], gated_ref.at[1, :, cols], g_send.at[n], g_recv.at[n],
            place.x_peer,
        )

    for n in range(heads):
        cols = pl.ds(n * hd, hd)
        kv = pl.ds(n * kv_heads // heads * hd, hd)

        @pl.loop(0, tokens // ROWS)
        def _(i):
            at_rows = tile(i, ROWS)
            scores = nt(q_ref[at_rows, cols], k_ref[:, kv]) * scale
            key_at = key_at_ref[:1, :]
            allowed = (key_at <= at_ref[at_rows, :1]) & (key_at >= start_ref[at_rows, :1])
            scores = jnp.where(allowed, scores, NEGATIVE)
            top = jnp.max(scores, axis=1, keepdims=True)
            raised = jnp.exp(scores - top)
            total = jnp.sum(raised, axis=1, keepdims=True)
            result = nn((raised / total).astype(BF16), v_ref[:, kv])
            log_ref[n, at_rows, :] = column(top + jnp.log(total))
            attended_ref[at_rows, cols] = result
            gated_ref[0, at_rows, cols] = (result * sig_ref[at_rows, n : n + 1]).astype(BF16)

        head_copy(n).start()

    @each_tile(0, tokens)
    def _(at_rows):
        acc[at_rows, :] = nn(gated_ref[0, at_rows, :], wo[0])

    def turn_rows(first, last):
        @pl.loop(first, last)
        def _(i):
            turned_ref[:, tile(i, ROWS)] = normed_all[tile(i, ROWS), :].T

    turn_rows(0, tokens // ROWS)
    for n in range(heads):
        head_copy(n).wait_recv()
    fold = copy_to(fold_src, fold_dst, s_send.at[2], s_recv.at[2], place.core_peer)

    @each_tile(0, rows)
    def _(at_rows):
        there = pl.ds(pl.multiple_of(at_rows.start + rows, 32), at_rows.size)
        fold_src[at_rows, :] = (acc[there, :] + nn(gated_ref[1, there, :], wo[1])).astype(BF16)

    fold.start()
    tops[2].wait_recv()
    early_start(2)
    early_start(3)

    @each_tile(0, rows)
    def _(at_rows):
        acc[at_rows, :] += nn(gated_ref[1, at_rows, :], wo[1])

    normed[2].wait_recv()
    fold.wait_recv()
    resid = tok_ref[...].astype(F32) + acc[slot(0), :] + fold_dst[...].astype(F32)
    resid_ref[...] = resid
    ss_send[1] = column(jnp.sum(resid * resid, axis=1, keepdims=True))
    squares(1).start()
    turn_rows(tokens // ROWS, 2 * tokens // ROWS)
    for i in range(4):
        early(i).wait_recv()
        early_ref[slot(i), :] = (
            early_send[slot(i), :].astype(F32) + early_came[slot(i), :].astype(F32)
        ).astype(BF16)
    squares(1).wait()
    inv_two = lax.rsqrt((ss_send[1] + ss_came[1]) / (2 * width) + EPS)
    inv_two_ref[...] = inv_two
    h_ref[...] = (resid_ref[...] * inv_two[:, :1] * second_ref[...]).astype(BF16)

    for copy in (*tops, *normed, kv_copy, q_copy, fold):
        copy.wait_send()
    for i in range(4):
        early(i).wait_send()
    for n in range(heads):
        head_copy(n).wait_send()


def front(
    tok, top, norm_gain, ffn_gain, q_gain, k_gain, cos, sin, at, start, key_at, w_gates,
    wq, wk, wv, wo, wd,
):
    count = lax.axis_size("group")
    rows, width = tok.shape
    tokens = 2 * rows
    hd = 128
    heads, kv_heads = wq.shape[1] // 2 // hd, wk.shape[1] // 2 // hd
    qw, kw = heads * hd, kv_heads * hd
    early = EARLY * WIDE
    local = pl.BlockSpec(memory_space=pltpu.VMEM)
    anywhere = pl.BlockSpec(memory_space=pl.ANY)
    dma = pltpu.SemaphoreType.DMA
    struct = jax.ShapeDtypeStruct
    return pl.pallas_call(
        functools.partial(front_kernel, count, heads, kv_heads),
        out_shape=(
            struct((rows, width), BF16),
            struct((rows, width), F32),
            struct((rows, 128), F32),
            struct((rows, width), F32),
            struct((rows, 128), F32),
            struct((width, 4 * rows), BF16),
            struct((4 * rows, width), BF16),
            struct((4 * rows, early), BF16),
            struct((tokens, qw + 2 * kw), F32),
            struct((tokens, 128), F32),
            struct((tokens, qw), BF16),
            struct((tokens, kw), BF16),
            struct((tokens, kw), BF16),
            struct((heads, tokens, 128), F32),
            struct((tokens, qw), F32),
            struct((2, tokens, qw), BF16),
        ),
        in_specs=[local] * 12 + [anywhere] * 5,
        out_specs=(local,) * 16,
        scratch_shapes=[
            pltpu.VMEM((4 * rows, width), BF16),
            pltpu.VMEM((2, width, qw), BF16),
            pltpu.VMEM((2, width, kw), BF16),
            pltpu.VMEM((2, width, kw), BF16),
            pltpu.VMEM((2, qw, width), BF16),
            pltpu.VMEM((early, width), BF16),
            pltpu.VMEM((tokens, 2 * kw), BF16),
            pltpu.VMEM((tokens, 2 * kw), BF16),
            pltpu.VMEM((tokens, qw + 128), BF16),
            pltpu.VMEM((tokens, qw + 128), BF16),
            pltpu.VMEM((tokens, 128), F32),
            pltpu.VMEM((4 * rows, early), BF16),
            pltpu.VMEM((4 * rows, early), BF16),
            pltpu.VMEM((2, rows, 128), F32),
            pltpu.VMEM((2, rows, 128), F32),
            pltpu.VMEM((rows, width), BF16),
            pltpu.VMEM((rows, width), BF16),
            pltpu.VMEM((tokens, width), F32),
            dma((2, 5)), dma((3,)), dma((3,)), dma((3,)), dma((3,)), dma((2,)), dma((2,)),
            dma((4,)), dma((4,)), dma((heads,)), dma((heads,)), dma((3,)), dma((3,)),
        ],
        compiler_params=pltpu.CompilerParams(
            collective_id=3, has_side_effects=True, vmem_limit_bytes=60 << 20
        ),
        cost_estimate=pl.CostEstimate(
            flops=6 * tokens * width * (qw + kw) * 4, bytes_accessed=40 << 20,
            transcendentals=heads * tokens * tokens,
        ),
    )(
        tok, top, norm_gain, ffn_gain, q_gain, k_gain, cos, sin, at, start, key_at, w_gates,
        wq, wk, wv, wo, wd,
    )


MISC = 88


def tn(a, b):
    return lax.dot_general(a, b, (((0,), (0,)), ((), ())), preferred_element_type=F32)


def rear_kernel(
    count, heads, kv_heads, back_ref, resid_ref, inv_two_ref, second_ref, top_ref, raw_ref,
    sig_ref, q_ref, k_ref, v_ref, log_ref, attended_ref, cos_ref, sin_ref, at_ref, start_ref,
    key_at_ref, q_gain_ref, k_gain_ref, turned_ref, gated_ref, w_gates_ref, hat_ref, inv_one_ref,
    norm_ref, wq_ref, wk_ref, wv_ref, wo_ref, late_pair_ref, late_down_ref, pair_in, down_in,
    grads_ref, input_ref, sums_ref, pair_grads_ref, down_grads_ref,
    w_main, wo, branch, block_src, dg_own, dg_send, dg_came, dk, dv, gates, gates_came, own, came, across,
    total, landed, misc, misc_came, misc_landed, misc_home, acc, fold_src, fold_dst, in_send,
    in_came, late_pair, late_down, late_pair_came, late_down_came,
    w_sem, late_sem, b_send, b_recv, d_send, d_recv, x_send, x_recv, y_send, y_recv, s_send, s_recv,
    *chain_sems,
):
    place = Place(count)
    row_at = lax.axis_index("row")
    side = place.side
    rows, width = back_ref.shape
    tokens = 2 * rows
    hd = 128
    cols = 2 * hd
    qw = heads * hd
    parts = heads // 2 + kv_heads
    high = gated_ref.shape[0]
    pieces = total.shape[0]
    scale = hd**-0.5

    loads = []
    for i, at in enumerate((row_at, 1 - row_at)):
        for n in range(kv_heads):
            q_cols, k_cols = tile(at * kv_heads + n, cols), tile(at * kv_heads + n, hd)
            first, second = w_main.at[i * parts + 2 * n], w_main.at[i * parts + 2 * n + 1]
            loads += [
                pltpu.make_async_copy(wq_ref.at[:, q_cols], first, w_sem.at[i, n, 0]),
                pltpu.make_async_copy(
                    wk_ref.at[:, k_cols], second.at[:, pl.ds(0, hd)], w_sem.at[i, n, 1]
                ),
                pltpu.make_async_copy(
                    wv_ref.at[:, k_cols], second.at[:, pl.ds(hd, hd)], w_sem.at[i, n, 2]
                ),
            ]
        loads.append(pltpu.make_async_copy(wo_ref.at[tile(at, qw), :], wo.at[i], w_sem.at[i, 0, 3]))
    for copy in loads:
        copy.start()
    late_loads = (
        pltpu.make_async_copy(late_pair_ref, late_pair, late_sem.at[0]),
        pltpu.make_async_copy(late_down_ref, late_down, late_sem.at[1]),
    )
    for copy in late_loads:
        copy.start()
    place.meet()

    def late_total(c, k):
        return late_down.at[c] if k == 2 else late_pair.at[c, k]

    def late_landed(c, k, which):
        return late_down_came.at[which, c] if k == 2 else late_pair_came.at[which, c, k]

    def late_home(c, k, of):
        chunks = down_grads_ref.shape[0] // 2 // WIDE
        at_cols = tile(of * chunks + chunks - LATE + c, WIDE)
        return down_grads_ref.at[at_cols, :] if k == 2 else pair_grads_ref.at[k, :, at_cols]

    def late_add(c, k, which):
        into, came_in = late_total(c, k), late_landed(c, k, which)
        into[...] = (into[...].astype(F32) + came_in[...].astype(F32)).astype(BF16)

    late = Chain(
        place, LATE, 3, late_total, late_landed, late_home, late_add, chain_sems[18:]
    )
    def slot(i):
        return pl.ds(i * rows, rows)

    def inner_copy(n):
        return copy_to(in_send.at[n], in_came.at[n], s_send.at[n], s_recv.at[n], place.x_peer)

    def store_row(at, values):
        for i in range(width // 128):
            misc[at + i : at + i + 1, :] = values[:, i * 128 : (i + 1) * 128]

    misc[...] = jnp.zeros_like(misc)
    grad = back_ref[...]
    in_send[0] = column(jnp.sum(grad * second_ref[...] * resid_ref[...], axis=1, keepdims=True))
    inner_copy(0).start()
    for copy in late_loads:
        copy.wait()
    late.step(0, 1)
    inv_two = inv_two_ref[:, :1]
    store_row(8, jnp.sum(back_ref[...] * resid_ref[...] * inv_two, axis=0, keepdims=True))
    inner_copy(0).wait()
    inner = (in_send[0, :, :1] + in_came[0, :, :1]) * inv_two * inv_two * inv_two / (2 * width)
    d_resid = (
        top_ref[...].astype(F32)
        + inv_two * (back_ref[...] * second_ref[...])
        - resid_ref[...] * inner
    )
    input_ref[...] = d_resid
    branch[slot(0), :] = d_resid.astype(BF16)
    to_core = copy_to(
        branch.at[slot(0), :], branch.at[slot(1), :], b_send.at[0], b_recv.at[0], place.core_peer
    )
    to_pair = copy_to(
        branch.at[slot(0), :], branch.at[slot(2), :], b_send.at[1], b_recv.at[1], place.y_peer
    )
    forward = copy_to(
        branch.at[slot(2), :], branch.at[slot(3), :], b_send.at[2], b_recv.at[2],
        place.core_peer,
    )
    to_core.start()
    to_pair.start()
    late.step(1, 1)

    def dg_copy(n):
        at_cols = pl.ds(n * cols, cols)
        return copy_to(
            dg_send.at[:, at_cols], dg_came.at[:, at_cols], d_send.at[n], d_recv.at[n],
            place.x_peer,
        )

    for copy in loads:
        copy.wait()
    halves_of = heads // 2
    for i in range(2):
        if i == 1:
            to_core.wait_recv()

        @each_tile(i * rows, rows)
        def _(at_rows):
            dg_send[at_rows, :] = nt(branch[at_rows, :], wo[1]).astype(BF16)

    for n in range(halves_of):
        dg_copy(n).start()
    late.step(2, 1)

    @each_tile(0, tokens)
    def _(at_rows):
        dg_own[at_rows, :] = nt(branch[at_rows, :], wo[0])

    dk[...] = jnp.zeros_like(dk)
    dv[...] = jnp.zeros_like(dv)
    gates[...] = jnp.zeros_like(gates)

    def unturn(values, at_rows):
        return values * cos_ref[at_rows, :] - pltpu.roll(values, 64, axis=1) * sin_ref[at_rows, :]

    def norm_back(values, raw, gain, at_rows, into):
        normed = unturn(values, at_rows)
        inverse = lax.rsqrt(jnp.mean(raw * raw, axis=1, keepdims=True) + EPS)
        misc[into : into + 1, :] += jnp.sum(normed * raw * inverse, axis=0, keepdims=True)
        scaled = normed * gain
        inner = jnp.mean(scaled * raw, axis=1, keepdims=True)
        return inverse * scaled - raw * (inverse * inverse * inverse * inner)

    lane = lax.broadcasted_iota(jnp.int32, (ROWS, 128), 1)

    def head(n):
        at_cols = pl.ds(n * hd, hd)
        kv = n * kv_heads // heads
        kv_cols = pl.ds(kv * hd, hd)

        @pl.loop(0, tokens // ROWS)
        def _(i):
            at_rows = tile(i, ROWS)
            query = q_ref[at_rows, at_cols]
            d_gated = dg_own[at_rows, at_cols] + dg_came[at_rows, at_cols].astype(F32)
            sig = sig_ref[at_rows, n : n + 1]
            d_att = (d_gated * sig).astype(BF16)
            d_logit = jnp.sum(d_gated * attended_ref[at_rows, at_cols], axis=1, keepdims=True)
            d_logit = d_logit * sig * (1.0 - sig)
            gates[at_rows, :] = jnp.where(lane == n, d_logit.astype(BF16), gates[at_rows, :])
            scores = nt(query, k_ref[:, kv_cols]) * scale
            key_at = key_at_ref[:1, :]
            allowed = (key_at <= at_ref[at_rows, :1]) & (key_at >= start_ref[at_rows, :1])
            probs = jnp.exp(jnp.where(allowed, scores, NEGATIVE) - log_ref[n, at_rows, :1])
            d_probs = nt(d_att, v_ref[:, kv_cols])
            mean = jnp.sum(d_probs * probs, axis=1, keepdims=True)
            d_scores = (probs * (d_probs - mean)).astype(BF16)
            dv[:, kv_cols] += tn(probs.astype(BF16), d_att)
            dk[:, kv_cols] += tn(d_scores, query)
            d_query = nn(d_scores, k_ref[:, kv_cols]) * scale
            own[2 * (n // 2), at_rows, pl.ds(n % 2 * hd, hd)] = norm_back(
                d_query, raw_ref[at_rows, at_cols], q_gain_ref[...], at_rows, 80
            ).astype(BF16)

    def key_value(n):
        kv_cols = pl.ds(n * hd, hd)

        @pl.loop(0, tokens // ROWS)
        def _(i):
            at_rows = tile(i, ROWS)
            raw = raw_ref[at_rows, pl.ds(qw + n * hd, hd)]
            own[2 * n + 1, at_rows, pl.ds(0, hd)] = norm_back(
                dk[at_rows, kv_cols] * scale, raw, k_gain_ref[...], at_rows, 81
            ).astype(BF16)
            own[2 * n + 1, at_rows, pl.ds(hd, hd)] = dv[at_rows, kv_cols].astype(BF16)

    def over_x(j):
        return copy_to(own.at[j], came.at[j], x_send.at[j], x_recv.at[j], place.x_peer)

    def over_y(j, mine):
        src = own.at[j] if mine else came.at[j]
        return copy_to(src, across.at[j], y_send.at[j], y_recv.at[j], place.y_peer)

    def send_chunk(j):
        over_x(j).start()

        @pl.when(side == 1)
        def _():
            over_y(j, True).start()

    def take_chunk(j):
        over_x(j).wait_recv()

        @pl.when(side == 0)
        def _():
            over_y(j, False).start()

    def add(c, k, which):
        total[c] = (total[c].astype(F32) + landed[which, c].astype(F32)).astype(BF16)

    chain = Chain(
        place, pieces, 1,
        lambda c, k: total.at[c],
        lambda c, k, which: landed.at[which, c],
        lambda c, k, of: grads_ref.at[of * pieces + c],
        add, chain_sems[:9],
    )

    def add_misc(c, k, which):
        misc[...] += misc_landed[which]

    small = Chain(
        place, 1, 1,
        lambda c, k: misc,
        lambda c, k, which: misc_landed.at[which],
        lambda c, k, of: misc_home,
        add_misc, chain_sems[9:18], share=False,
    )

    left = 3 * LATE
    outs = pieces - 2 * parts

    def step(u):
        if u < late.steps(1):
            late.step(u, 1)
        if u >= left:
            chain.step(u - left, 1)

    def out_piece(t):
        total[t] = nn(gated_ref[...], branch[:, pl.ds(t * cols, cols)]).astype(BF16)

    def block(j):
        over_y(j, True).wait_recv()
        block_src[...] = jnp.where(side == 0, own[j], came[j])
        for i in range(2):

            @each_tile(0, high, TILE)
            def _(at_rows):
                there = pl.ds(pl.multiple_of(at_rows.start + i * high, TILE), at_rows.size)
                total[outs + 2 * j + i, at_rows, :] = (
                    nn(turned_ref[there, pl.ds(0, tokens)], block_src[...])
                    + nn(turned_ref[there, pl.ds(tokens, tokens)], across[j])
                ).astype(BF16)

    def gates_copy():
        return copy_to(gates, gates_came, s_send.at[2], s_recv.at[2], place.x_peer)

    step(3)
    for n in range(kv_heads):
        dg_copy(n).wait_recv()
        head(2 * n)
        head(2 * n + 1)
        key_value(n)
        send_chunk(2 * n)
        send_chunk(2 * n + 1)
        if n == 0:
            to_pair.wait_recv()
            forward.start()
            step(4)
    gates_copy().start()

    def back_came(j):
        take_chunk(j)

        @each_tile(0, tokens)
        def _(at_rows):
            acc[at_rows, :] += nt(came[j, at_rows, :], w_main[parts + j])


    step(5)

    @each_tile(0, tokens)
    def _(at_rows):
        found = nt(own[0, at_rows, :], w_main[0])
        for j in range(1, parts):
            found += nt(own[j, at_rows, :], w_main[j])
        acc[at_rows, :] = found

    step(6)
    back_came(0)
    step(7)
    back_came(1)
    for u in range(8, left):
        step(u)
    forward.wait_recv()
    for t in range(outs):
        out_piece(t)
        step(left + t)
        if t + 2 < parts:
            back_came(t + 2)
    at = left + outs

    gates_copy().wait()
    moved = pltpu.roll(gates_came[...].astype(F32), heads, axis=1)
    both = (gates[...].astype(F32) + moved).astype(BF16)
    gates[...] = both

    @each_tile(0, tokens)
    def _(at_rows):
        acc[at_rows, :] += nt(gates[at_rows, :], w_gates_ref[...])

    fold = copy_to(fold_src, fold_dst, s_send.at[3], s_recv.at[3], place.core_peer)
    fold_src[...] = acc[rows:, :].astype(BF16)
    fold.start()
    block(0)
    step(at)
    gate_grads = nn(turned_ref[:, pl.ds(0, tokens)], both).T
    for i in range(width // 128):
        misc[16 + 8 * i : 24 + 8 * i, :] = gate_grads[:8, i * 128 : (i + 1) * 128]

    def misc_copy(n, peer):
        return copy_to(misc, misc_came.at[n], s_send.at[4 + n], s_recv.at[4 + n], peer)

    row_of = lax.broadcasted_iota(jnp.int32, (MISC, 128), 0)
    fold.wait_recv()
    grad = acc[:rows, :] + fold_dst[...].astype(F32)
    found = grad * hat_ref[...]
    in_send[1] = column(jnp.sum(found * norm_ref[...], axis=1, keepdims=True))
    inner_copy(1).start()
    acc[:rows, :] = grad
    store_row(0, jnp.sum(found, axis=0, keepdims=True))
    misc_copy(0, place.core_peer).start()
    step(at + 1)
    block(1)
    step(at + 2)
    misc_copy(0, place.core_peer).wait()
    misc[...] += jnp.where((row_of < 16) | (row_of >= 80), misc_came[0], 0.0)
    misc_copy(1, place.x_peer).start()
    step(at + 3)
    block(2)
    step(at + 4)
    misc_copy(1, place.x_peer).wait()
    misc[...] += jnp.where(row_of >= 80, misc_came[1], 0.0)
    misc_copy(2, place.y_peer).start()
    inner_copy(1).wait()
    inner = (in_send[1, :, :1] + in_came[1, :, :1]) / (2 * width)
    input_ref[...] += inv_one_ref[:, :1] * (acc[:rows, :] * norm_ref[...] - hat_ref[...] * inner)
    step(at + 5)
    block(3)
    misc_copy(2, place.y_peer).wait()
    misc[...] += misc_came[2]
    small.step(0)
    step(at + 6)
    small.step(1)
    step(at + 7)

    @pl.loop(pieces, chain.steps(1))
    def _(u):
        if late.steps(1) > left + pieces:
            late.step(u + left, 1)
        small.step(u - pieces + 2)
        chain.step(u, 1)

    @pl.loop(chain.steps(1) - pieces + 2, small.steps())
    def _(u):
        small.step(u)

    small.drain()
    sums_ref[...] = misc_home[...]
    chain.drain()
    late.drain()
    for copy in (to_core, to_pair, forward, fold):
        copy.wait_send()
    for n in range(halves_of):
        dg_copy(n).wait_send()
    for j in range(parts):
        over_x(j).wait_send()
        over_y(j, True).wait_send()


def rear(
    back, resid, inv_two, ffn_gain, top, raw, sig, query, keys, values, log, attended, cos, sin,
    at, start, key_at, q_gain, k_gain, turned, gated, w_gates, hat, inv_one, norm_gain,
    wq, wk, wv, wo, late_pair, late_down, pair_sum, down_sum,
):
    count = lax.axis_size("group")
    rows, width = back.shape
    tokens = 2 * rows
    hd = 128
    heads, kv_heads = query.shape[1] // hd, keys.shape[1] // hd
    qw, kw = heads * hd, kv_heads * hd
    cols = 2 * hd
    parts = heads // 2 + kv_heads
    high = gated.shape[0]
    pieces = 2 * parts + width // cols
    anywhere = pl.BlockSpec(memory_space=pl.ANY)
    local = pl.BlockSpec(memory_space=pltpu.VMEM)
    dma = pltpu.SemaphoreType.DMA
    struct = jax.ShapeDtypeStruct
    return pl.pallas_call(
        functools.partial(rear_kernel, count, heads, kv_heads),
        out_shape=(
            struct((2 * pieces, high, cols), BF16),
            struct((rows, width), F32),
            struct((MISC, 128), F32),
            struct(pair_sum.shape, BF16),
            struct(down_sum.shape, BF16),
        ),
        in_specs=[local] * 25 + [anywhere] * 8,
        out_specs=(anywhere, local, local, anywhere, anywhere),
        input_output_aliases={31: 3, 32: 4},
        scratch_shapes=[
            pltpu.VMEM((2 * parts, width, cols), BF16),
            pltpu.VMEM((2, qw, width), BF16),
            pltpu.VMEM((4 * rows, width), BF16),
            pltpu.VMEM((tokens, cols), BF16),
            pltpu.VMEM((tokens, qw), F32),
            pltpu.VMEM((tokens, qw), BF16),
            pltpu.VMEM((tokens, qw), BF16),
            pltpu.VMEM((tokens, kw), F32),
            pltpu.VMEM((tokens, kw), F32),
            pltpu.VMEM((tokens, 128), BF16),
            pltpu.VMEM((tokens, 128), BF16),
            pltpu.VMEM((parts, tokens, cols), BF16),
            pltpu.VMEM((parts, tokens, cols), BF16),
            pltpu.VMEM((parts, tokens, cols), BF16),
            pltpu.VMEM((pieces, high, cols), BF16),
            pltpu.VMEM((2, pieces, high, cols), BF16),
            pltpu.VMEM((MISC, 128), F32),
            pltpu.VMEM((3, MISC, 128), F32),
            pltpu.VMEM((2, MISC, 128), F32),
            pltpu.VMEM((MISC, 128), F32),
            pltpu.VMEM((tokens, width), F32),
            pltpu.VMEM((rows, width), BF16),
            pltpu.VMEM((rows, width), BF16),
            pltpu.VMEM((2, rows, 128), F32),
            pltpu.VMEM((2, rows, 128), F32),
            pltpu.VMEM(late_pair.shape, BF16),
            pltpu.VMEM(late_down.shape, BF16),
            pltpu.VMEM((2,) + late_pair.shape, BF16),
            pltpu.VMEM((2,) + late_down.shape, BF16),
            dma((2, kv_heads, 4)), dma((2,)), dma((3,)), dma((3,)), dma((heads // 2,)), dma((heads // 2,)),
            dma((parts,)), dma((parts,)), dma((parts,)), dma((parts,)), dma((7,)), dma((7,)),
            *chain_semaphores(pieces), *chain_semaphores(1), *chain_semaphores(3 * LATE),
        ],
        compiler_params=pltpu.CompilerParams(
            collective_id=2, has_side_effects=True, vmem_limit_bytes=60 << 20
        ),
        cost_estimate=pl.CostEstimate(
            flops=2 * tokens * width * (qw + 2 * kw) * 6, bytes_accessed=100 << 20,
            transcendentals=heads * tokens * tokens,
        ),
    )(
        back, resid, inv_two, ffn_gain, top, raw, sig, query, keys, values, log, attended, cos,
        sin, at, start, key_at, q_gain, k_gain, turned, gated, w_gates, hat, inv_one, norm_gain,
        wq, wk, wv, wo, late_pair, late_down, pair_sum, down_sum,
    )


def assemble_kernel(parts, outs, grads_ref, q_ref, k_ref, v_ref, o_ref, wide, sems):
    row_at = lax.axis_index("row")
    pieces = outs + 2 * parts
    high = grads_ref.shape[1]
    copies = []

    def move(src, dst):
        copies.append(pltpu.make_async_copy(src, dst, sems.at[len(copies)]))
        copies[-1].start()

    for s in range(2):
        at = row_at if s == 0 else 1 - row_at
        for p in range(pieces):
            n = s * pieces + p
            wide[n] = grads_ref[n].astype(F32)
            if p < outs:
                rows, cols = tile(at, high), pl.ds(p * 256, 256)
                move(wide.at[n], o_ref.at[rows, cols])
            else:
                j, i = (p - outs) // 2, (p - outs) % 2
                rows, head = pl.ds(i * high, high), at * (parts // 2) + j // 2
                if j % 2 == 0:
                    move(wide.at[n], q_ref.at[rows, tile(head, 256)])
                else:
                    for m, ref in enumerate((k_ref, v_ref)):
                        half = wide.at[n, :, pl.ds(m * 128, 128)]
                        move(half, ref.at[rows, tile(head, 128)])
    for copy in copies:
        copy.wait()


def assemble(grads, q_shape, k_shape, o_shape, head_dim):
    parts = q_shape[1] // 2 // head_dim // 2 + k_shape[1] // 2 // head_dim
    outs = grads.shape[0] // 2 - 2 * parts
    anywhere = pl.BlockSpec(memory_space=pl.ANY)
    struct = jax.ShapeDtypeStruct
    count = 2 * (outs + 3 * parts)
    return pl.pallas_call(
        functools.partial(assemble_kernel, parts, outs),
        out_shape=(
            struct(q_shape, F32), struct(k_shape, F32), struct(k_shape, F32), struct(o_shape, F32),
        ),
        in_specs=[pl.BlockSpec(memory_space=pltpu.VMEM)],
        out_specs=(anywhere,) * 4,
        scratch_shapes=[
            pltpu.VMEM(grads.shape, F32),
            pltpu.SemaphoreType.DMA((count,)),
        ],
        compiler_params=pltpu.CompilerParams(vmem_limit_bytes=40 << 20),
    )(grads)


def body(
    tokens, lengths, norm_gain, w_query, w_key, w_value, w_head_gate, query_gain, key_gain,
    w_out, ffn_gain, w_gate, w_up, w_down, grad_out,
):
    rows, d_loc = tokens.shape
    group_tok = 2 * rows
    head_dim = query_gain.shape[0]
    gate_half = w_head_gate.shape[1] // 2
    row_at = lax.axis_index("row")
    col_at = lax.axis_index("col")
    side = lax.axis_index("group") % 2

    steps = jnp.arange(rows, dtype=jnp.int32)
    index = jnp.concatenate([col_at * rows + steps, (1 - col_at) * rows + steps])
    place = places(lengths, index)[1]
    cosines, sines = rope_tables(place, head_dim)
    signed = jnp.concatenate([-sines[:, : head_dim // 2], sines[:, head_dim // 2 :]], axis=1)
    positions = (
        jnp.broadcast_to(index[:, None], (group_tok, 128)),
        jnp.broadcast_to((index - place)[:, None], (group_tok, 128)),
        jnp.broadcast_to(index[None], (8, group_tok)),
    )
    w_gates = jnp.pad(
        jnp.concatenate(halves(w_head_gate, 1, row_at), axis=1),
        ((0, 0), (0, 128 - 2 * gate_half)),
    )
    gains = (query_gain[None], key_gain[None])
    (
        normed_two, resid, inverse_two, hat, inverse_one, turned, grad_all, early_grad,
        raw, gate_sigmoid, query, keys, values, logsum, attended, gated_both,
    ) = front(
        tokens, grad_out, norm_gain[None], ffn_gain[None], *gains, cosines, signed, *positions,
        w_gates, w_query, w_key, w_value, w_out, w_down,
    )
    gated, gated_came = gated_both[0], gated_both[1]
    first_side = side == 0
    gated_pair = jnp.concatenate(
        [
            jnp.where(first_side, gated, gated_came),
            swap_groups(jnp.where(first_side, gated_came, gated)),
        ]
    ).T

    pair_sum, down_sum, late_pair, late_down, _, _, branch, branch_out, d_normed_two = ffn(
        normed_two, grad_all, early_grad, w_gate, w_up, w_down
    )
    output = (resid + branch + swap_groups(branch_out).astype(F32)).astype(BF16)

    grads, input_grad, sums, pair_sum, down_sum = rear(
        d_normed_two, resid, inverse_two, ffn_gain[None], grad_out, raw, gate_sigmoid, query,
        keys, values, logsum, attended, cosines, signed, *positions, *gains, turned, gated_pair,
        w_gates, hat, inverse_one, norm_gain[None], w_query, w_key, w_value, w_out,
        late_pair, late_down, pair_sum, down_sum,
    )
    grad_norm_gain = sums[:8].reshape(d_loc)
    grad_ffn_gain = sums[8:16].reshape(d_loc)
    grad_gates = sums[16:80].reshape(8, 2 * gate_half, 128).transpose(1, 0, 2)
    grad_gates = grad_gates.reshape(2 * gate_half, d_loc)
    grad_head_gate = ordered(grad_gates[:gate_half], grad_gates[gate_half:], 0, row_at).T

    grad_query, grad_key, grad_value, grad_out_w = assemble(
        grads, w_query.shape, w_key.shape, w_out.shape, head_dim
    )
    return (
        output,
        input_grad,
        grad_norm_gain,
        grad_query,
        grad_key,
        grad_value,
        grad_head_gate,
        sums[80],
        sums[81],
        grad_out_w,
        grad_ffn_gain,
        pair_sum[0].astype(F32),
        pair_sum[1].astype(F32),
        down_sum.astype(F32),
    )


def solution(mesh):
    shards = P(("group", "col"), "row")
    in_specs = (
        shards,
        P("group"),
        P("row"),
        P("row", "col"),
        P("row", "col"),
        P("row", "col"),
        P("row", "col"),
        P(),
        P(),
        P("col", "row"),
        P("row"),
        P("row", "col"),
        P("row", "col"),
        P("col", "row"),
        shards,
    )
    out_specs = (
        shards,
        shards,
        P("row"),
        P("row", "col"),
        P("row", "col"),
        P("row", "col"),
        P("row", "col"),
        P(),
        P(),
        P("col", "row"),
        P("row"),
        P("row", "col"),
        P("row", "col"),
        P("col", "row"),
    )
    return jax.shard_map(body, mesh=mesh, in_specs=in_specs, out_specs=out_specs, check_vma=False)
```
